32 devices in a mesh: wide: 8 (over y, x, core), narrow: 4 (over z).
Axes of the slice: x: 2, y: 2, z: 4, core: 2. Of those that a mesh axis runs over, the one named last changes fastest.
Arguments:
- tokens: bfloat16 [32, 256, 1536], P(('wide', 'narrow')), may hold values from -6 to 6
- cotangent: bfloat16 [32, 256, 1536], P(('wide', 'narrow')), may hold values from -6 to 6
- thresholds: float32 [32, 2], P(('wide', 'narrow')), may hold values from 0.5 to 4
- attn_norm_gain: bfloat16 [1536], P('narrow'), may hold values from 0.25 to 1.75
- attn_norm_shift: bfloat16 [1536], P('narrow'), may hold values from -4 to 4
- query_weight: bfloat16 [1536, 512], P('narrow'), may hold values from -0.15625 to 0.15625
- key_weight: bfloat16 [1536, 512], P('narrow'), may hold values from -0.15625 to 0.15625
- value_weight: bfloat16 [1536, 1536], P('narrow'), may hold values from -0.15625 to 0.15625
- relative_weight: bfloat16 [192, 512], P('narrow'), may hold values from -0.4375 to 0.4375
- content_bias: bfloat16 [512], P('narrow'), may hold values from -3 to 3
- position_bias: bfloat16 [512], P('narrow'), may hold values from -3 to 3
- out_weight: bfloat16 [1536, 1536], P('narrow'), may hold values from -1.25 to 1.25
- out_bias: bfloat16 [1536], P('narrow'), may hold values from -4 to 4
- mlp_norm_gain: bfloat16 [1536], P('narrow'), may hold values from 0.25 to 1.75
- mlp_norm_shift: bfloat16 [1536], P('narrow'), may hold values from -4 to 4
- inner_weight: bfloat16 [1536, 3072], P('narrow'), may hold values from -0.15625 to 0.15625
- inner_bias: bfloat16 [3072], P('narrow'), may hold values from -4 to 4
- outer_weight: bfloat16 [3072, 1536], P('narrow'), may hold values from -0.109375 to 0.109375
- outer_bias: bfloat16 [1536], P('narrow'), may hold values from -4 to 4
Outputs:
- layer_out: bfloat16 [32, 256, 1536], P(('wide', 'narrow'))
- tokens_grad: bfloat16 [32, 256, 1536], P(('wide', 'narrow'))
- attn_norm_gain_grad: float32 [1536], P('narrow')
- attn_norm_shift_grad: float32 [1536], P('narrow')
- query_weight_grad: float32 [1536, 512], P('narrow')
- key_weight_grad: float32 [1536, 512], P('narrow')
- value_weight_grad: float32 [1536, 1536], P('narrow')
- relative_weight_grad: float32 [192, 512], P('narrow')
- content_bias_grad: float32 [512], P('narrow')
- position_bias_grad: float32 [512], P('narrow')
- out_weight_grad: float32 [1536, 1536], P('narrow')
- out_bias_grad: float32 [1536], P('narrow')
- mlp_norm_gain_grad: float32 [1536], P('narrow')
- mlp_norm_shift_grad: float32 [1536], P('narrow')
- inner_weight_grad: float32 [1536, 3072], P('narrow')
- inner_bias_grad: float32 [3072], P('narrow')
- outer_weight_grad: float32 [3072, 1536], P('narrow')
- outer_bias_grad: float32 [1536], P('narrow')
The draws below stay inside these ranges and needn't reach their ends.
All inputs are finite; a program needn't handle non-finite values.
Results may differ from the reference program's by a relative error of at most 0.023.
Values may be sent and summed in bfloat16 or wider, within the bound.
A program may use at most 256 MiB of HBM per device.

```python
import math
import jax
import jax.numpy as jnp
from jax import lax

D = 1536
H = 8
KEY = 64
VAL = 192
FF = 3072
F = 192
LEN = 256
WIN = 128
SEQS = 32


def level_of(rng, extent, pieces, smallest, top_value):
    def one(dim, blocks):
        draws = jax.random.uniform(jax.random.fold_in(jax.random.fold_in(rng, 6), dim), (blocks,), jnp.float32, smallest / len(pieces), top_value / len(pieces))
        return jnp.repeat(jnp.exp(draws), extent[dim] // blocks).reshape((-1,) + (1,) * (len(extent) - dim - 1))

    factor_of = one(*pieces[0])
    for cut in pieces[1:]:
        factor_of = factor_of * one(*cut)
    return factor_of


def bell_draw(stream_key, shape, width, limit, cuts=(), held_as=jnp.bfloat16):
    result = jax.random.normal(stream_key, shape, jnp.float32) * width
    if len(cuts) > 0:
        result = level_of(stream_key, shape, cuts, -0.22, 0.18) * result
    return jnp.clip(result, min=-limit, max=limit).astype(held_as)


def setup_inputs(seed: int = 0) -> dict:
    seeds = jax.random.split(jax.random.key(seed), 20)
    tokens = bell_draw(seeds[0], (SEQS, LEN, D), 1.0, 6.0, ((0, 32),))
    cotangent = bell_draw(seeds[1], (SEQS, LEN, D), 1.0, 6.0, ((0, 32),))
    thresholds = jnp.clip(jnp.exp(math.log(4.0) - 2.0794415 * jax.random.uniform(seeds[2], (SEQS, LEN // WIN), jnp.float32) ** level_of(seeds[2], (SEQS, LEN // WIN), ((0, 32),), -0.2, 0.2)), 0.5, 4.0)
    attn_norm_gain = jnp.clip(1.0 + 0.15 * jax.random.normal(seeds[3], (D,), jnp.float32), 0.25, 1.75).astype(jnp.bfloat16)
    attn_norm_shift = bell_draw(seeds[4], (D,), 0.3, 4.0, ((0, 4),))
    query_weight = bell_draw(seeds[5], (D, H * KEY), D ** -0.5, 0.15625, ((0, 4),))
    key_weight = bell_draw(seeds[6], (D, H * KEY), D ** -0.5, 0.15625, ((0, 4),))
    value_weight = bell_draw(seeds[7], (D, H * VAL), D ** -0.5, 0.15625, ((0, 4),))
    relative_weight = bell_draw(seeds[8], (F, H * KEY), F ** -0.5, 0.4375, ((0, 4),))
    content_bias = bell_draw(seeds[9], (H * KEY,), 0.2, 3.0, ((0, 4),))
    position_bias = bell_draw(seeds[10], (H * KEY,), 0.2, 3.0, ((0, 4),))
    out_weight = bell_draw(seeds[11], (H * VAL, D), (max(1, 4 * D // LEN)) ** -0.5, 1.25, ((0, 4),))
    out_bias = bell_draw(seeds[12], (D,), 0.3, 4.0, ((0, 4),))
    mlp_norm_gain = jnp.clip(1.0 + 0.15 * jax.random.normal(seeds[13], (D,), jnp.float32), 0.25, 1.75).astype(jnp.bfloat16)
    mlp_norm_shift = bell_draw(seeds[14], (D,), 0.3, 4.0, ((0, 4),))
    inner_weight = bell_draw(seeds[15], (D, FF), D ** -0.5, 0.15625, ((0, 4),))
    inner_bias = bell_draw(seeds[16], (FF,), 0.3, 4.0, ((0, 4),))
    outer_weight = bell_draw(seeds[17], (FF, D), FF ** -0.5, 0.109375, ((0, 4),))
    outer_bias = bell_draw(seeds[18], (D,), 0.3, 4.0, ((0, 4),))
    return {"tokens": tokens, "cotangent": cotangent, "thresholds": thresholds, "attn_norm_gain": attn_norm_gain, "attn_norm_shift": attn_norm_shift, "query_weight": query_weight, "key_weight": key_weight, "value_weight": value_weight, "relative_weight": relative_weight, "content_bias": content_bias, "position_bias": position_bias, "out_weight": out_weight, "out_bias": out_bias, "mlp_norm_gain": mlp_norm_gain, "mlp_norm_shift": mlp_norm_shift, "inner_weight": inner_weight, "inner_bias": inner_bias, "outer_weight": outer_weight, "outer_bias": outer_bias}


@jax.custom_vjp
def low(v):
    return lax.optimization_barrier(v.astype(jnp.bfloat16)).astype(jnp.float32)

@jax.custom_vjp
def low_back(v):
    return v

def low_keep(v):
    return (low(v), None)

def low_pass(kept, grad):
    return (grad,)

def back_keep(v):
    return (v, None)

def back_low(kept, grad):
    return (low(grad),)
low.defvjp(low_keep, low_pass)
low_back.defvjp(back_keep, back_low)
EPSILON = 1e-05
HIGHEST = lax.Precision.HIGHEST

def basis_table(length, features):
    family = features // 6
    offsets = jnp.arange(2 * length - 1, dtype=jnp.float32) - (length - 1)
    distance = jnp.abs(offsets)[:, None]
    halves = 2.0 ** jnp.linspace(3.0, math.log2(length), family, dtype=jnp.float32)
    decays = jnp.exp(-math.log(2.0) / halves[None, :] * distance)
    widths = 2.0 ** jnp.arange(1, family + 1, dtype=jnp.float32) - 1.0
    central = jnp.where(widths[None, :] > distance, 1.0, 0.0).astype(jnp.float32)
    centers = jnp.linspace(0.0, float(length), family, dtype=jnp.float32)
    spread = length / family
    bump_rows = jnp.exp(-0.5 * ((distance - centers[None, :]) / spread) ** 2)
    positive = jnp.concatenate([decays, central, bump_rows], axis=1)
    return jnp.concatenate([positive, jnp.sign(offsets)[:, None] * positive], axis=1)

def shift_offsets(raw_scores, length):
    leading = raw_scores.shape[:-2]
    padded = jnp.pad(raw_scores, [(0, 0)] * len(leading) + [(0, 0), (0, 1)])
    flatten = padded.reshape(leading + (2 * length * length,))
    window = flatten[..., length - 1:length - 1 + length * (2 * length - 1)]
    return window.reshape(leading + (length, 2 * length - 1))[..., :length]

def layer_norm(values, gain, shift):
    center = values - lax.optimization_barrier(jnp.mean(values, axis=-1, keepdims=True))
    spread = lax.optimization_barrier(jnp.mean(center * center, axis=-1, keepdims=True))
    return center * lax.rsqrt(spread + EPSILON) * gain + shift

def product(left, right):
    return jnp.dot(left, right, precision=HIGHEST)

def one_sequence(params, tokens, basis):
    attn_gain, attn_shift, query_weight, key_weight, value_weight, relative_weight, content_bias, position_bias, out_weight, out_bias, mlp_gain, mlp_shift, inner_weight, inner_bias, outer_weight, outer_bias = params
    length = tokens.shape[0]
    normed = low(layer_norm(tokens, attn_gain, attn_shift))
    queries = low_back(product(normed, query_weight) * KEY ** (-0.5))
    content_query = low(queries + content_bias).reshape(length, H, KEY)
    position_query = low(queries + position_bias).reshape(length, H, KEY)
    key_rows = low(low_back(product(normed, key_weight))).reshape(length, H, KEY)
    value_rows = low(low_back(product(normed, value_weight))).reshape(length, H, VAL)
    rel_keys = low(low_back(product(low(basis), relative_weight))).reshape(2 * length - 1, H, KEY)
    content = jnp.einsum('ihe,jhe->hij', content_query, key_rows, precision=HIGHEST)
    raw_scores = jnp.einsum('ihe,the->hit', position_query, rel_keys, precision=HIGHEST)
    logits = low_back(content + shift_offsets(raw_scores, length))
    attention = low(jax.nn.softmax(logits, axis=-1))
    mixed_heads = jnp.einsum('hij,jhd->ihd', attention, value_rows, precision=HIGHEST)
    mixed_heads = low(low_back(mixed_heads.reshape(length, H * VAL)))
    hidden = tokens + low_back(product(mixed_heads, out_weight) + out_bias)
    normed_mid = low(layer_norm(hidden, mlp_gain, mlp_shift))
    inner_pre = low_back(product(normed_mid, inner_weight) + inner_bias)
    active = low(jax.nn.gelu(inner_pre, approximate=False))
    return hidden + low_back(product(active, outer_weight) + outer_bias)

def reference(tokens, cotangent, thresholds, attn_norm_gain, attn_norm_shift, query_weight, key_weight, value_weight, relative_weight, content_bias, position_bias, out_weight, out_bias, mlp_norm_gain, mlp_norm_shift, inner_weight, inner_bias, outer_weight, outer_bias):
    params = tuple((weight.astype(jnp.float32) for weight in (attn_norm_gain, attn_norm_shift, query_weight, key_weight, value_weight, relative_weight, content_bias, position_bias, out_weight, out_bias, mlp_norm_gain, mlp_norm_shift, inner_weight, inner_bias, outer_weight, outer_bias)))
    basis = basis_table(LEN, F)
    group = 1
    while group * 2 <= max(1, 4096 // LEN) and SEQS % (group * 2) == 0:
        group = group * 2
    rounds = SEQS // group
    bases = jnp.broadcast_to(basis, (group,) + basis.shape)
    token_blocks = tokens.reshape(rounds, group, LEN, D)
    grad_blocks = cotangent.reshape(rounds, group, LEN, D)
    limit_blocks = thresholds.reshape(rounds, group, LEN // WIN)

    def forward(weights, inputs):
        return jax.vmap(one_sequence, in_axes=(None, 0, 0))(weights, inputs, bases)

    def section(totals, item):
        block_tokens, block_grads, block_limits = item
        outputs, pull = jax.vjp(forward, params, block_tokens.astype(jnp.float32))
        clip_limit = jnp.repeat(block_limits, WIN, axis=1)[:, :, None]
        clipped = jnp.clip(block_grads.astype(jnp.float32), -clip_limit, clip_limit)
        weight_grads, input_grads = pull(clipped)
        totals = tuple((total + piece for total, piece in zip(totals, weight_grads)))
        return (totals, (outputs.astype(jnp.bfloat16), input_grads.astype(jnp.bfloat16)))
    initial = tuple((jnp.zeros(weight.shape, jnp.float32) for weight in params))
    sums, (outputs, input_grads) = lax.scan(section, initial, (token_blocks, grad_blocks, limit_blocks))
    layer_out = outputs.reshape(SEQS, LEN, D)
    tokens_grad = input_grads.reshape(SEQS, LEN, D)
    return (layer_out, tokens_grad, sums[0], sums[1], sums[2], sums[3], sums[4], sums[5], sums[6], sums[7], sums[8], sums[9], sums[10], sums[11], sums[12], sums[13], sums[14], sums[15])
```

```python
import math
import types

import jax
import jax.numpy as jnp
from jax import lax
from jax.experimental import pallas as pl
from jax.experimental.pallas import tpu as pltpu
from jax.sharding import PartitionSpec as P

H = 8
KEY = 64
VAL = 192
F = 192
WIN = 128


EPSILON = 1e-05


def basis_table(length, features):
    family = features // 6
    offsets = jnp.arange(2 * length - 1, dtype=jnp.float32) - (length - 1)
    distance = jnp.abs(offsets)[:, None]
    halves = 2.0 ** jnp.linspace(3.0, math.log2(length), family, dtype=jnp.float32)
    decays = jnp.exp(-math.log(2.0) / halves[None, :] * distance)
    widths = 2.0 ** jnp.arange(1, family + 1, dtype=jnp.float32) - 1.0
    central = jnp.where(widths[None, :] > distance, 1.0, 0.0).astype(jnp.float32)
    centers = jnp.linspace(0.0, float(length), family, dtype=jnp.float32)
    spread = length / family
    bump_rows = jnp.exp(-0.5 * ((distance - centers[None, :]) / spread) ** 2)
    positive = jnp.concatenate([decays, central, bump_rows], axis=1)
    return jnp.concatenate([positive, jnp.sign(offsets)[:, None] * positive], axis=1)


def shift_offsets(raw_scores, length):
    leading = raw_scores.shape[:-2]
    padded = jnp.pad(raw_scores, [(0, 0)] * len(leading) + [(0, 0), (0, 1)])
    flatten = padded.reshape(leading + (2 * length * length,))
    window = flatten[..., length - 1 : length - 1 + length * (2 * length - 1)]
    return window.reshape(leading + (length, 2 * length - 1))[..., :length]


def unshift_offsets(grad_scores, length):
    leading = grad_scores.shape[:-2]
    widened = jnp.pad(grad_scores, [(0, 0)] * len(leading) + [(0, 0), (0, length - 1)])
    flatten = widened.reshape(leading + (length * (2 * length - 1),))
    flatten = jnp.pad(flatten, [(0, 0)] * len(leading) + [(length - 1, 1)])
    return flatten.reshape(leading + (length, 2 * length))[..., : 2 * length - 1]


def layer_norm(values, gain, shift):
    center = values - jnp.mean(values, axis=-1, keepdims=True)
    spread = jnp.mean(center * center, axis=-1, keepdims=True)
    return center * lax.rsqrt(spread + EPSILON) * gain + shift


def gelu_exact(values):
    return jax.nn.gelu(values, approximate=False)


def column_sums(values):
    return jnp.sum(values.astype(jnp.float32), axis=0)


WIDE = "wide"
DEPTH = "narrow"


def spread_rows(shard):
    return lax.all_gather(shard, DEPTH, axis=0, tiled=True)


def sum_columns(part):
    low = part.astype(jnp.bfloat16)
    return lax.psum_scatter(low, WIDE, scatter_dimension=1, tiled=True).astype(jnp.float32)


def sum_rows(part):
    low = part.astype(jnp.bfloat16)
    return lax.psum_scatter(low, DEPTH, scatter_dimension=0, tiled=True).astype(jnp.float32)


def spread_columns(part):
    low = part.astype(jnp.bfloat16)
    return lax.all_gather(low, WIDE, axis=1, tiled=True).astype(jnp.float32)


def per_device_generic(
    tokens,
    cotangent,
    thresholds,
    attn_norm_gain,
    attn_norm_shift,
    query_weight,
    key_weight,
    value_weight,
    relative_weight,
    content_bias,
    position_bias,
    out_weight,
    out_bias,
    mlp_norm_gain,
    mlp_norm_shift,
    inner_weight,
    inner_bias,
    outer_weight,
    outer_bias,
):
    seq_count, length, model_width = tokens.shape
    row_count = seq_count * length
    span = 2 * length - 1
    query_scale = KEY ** (-0.5)
    (
        attn_gain,
        attn_shift,
        query_full,
        key_full,
        value_full,
        relative_full,
        content_full,
        position_full,
        exit_full,
        exit_bias,
    ) = (
        spread_rows(attn_norm_gain),
        spread_rows(attn_norm_shift),
        spread_rows(query_weight),
        spread_rows(key_weight),
        spread_rows(value_weight),
        spread_rows(relative_weight),
        spread_rows(content_bias),
        spread_rows(position_bias),
        spread_rows(out_weight),
        spread_rows(out_bias),
    )
    mlp_gain, mlp_shift, inner_full, inner_offset, outer_full, outer_offset = (
        spread_rows(mlp_norm_gain),
        spread_rows(mlp_norm_shift),
        spread_rows(inner_weight),
        spread_rows(inner_bias),
        spread_rows(outer_weight),
        spread_rows(outer_bias),
    )
    flat_tokens = tokens.reshape(row_count, model_width).astype(jnp.float32)
    attn_gain_f = attn_gain.astype(jnp.float32)
    attn_shift_f = attn_shift.astype(jnp.float32)
    normed = layer_norm(flat_tokens, attn_gain_f, attn_shift_f).astype(jnp.bfloat16)
    queries = jnp.dot(normed, query_full, preferred_element_type=jnp.float32) * query_scale
    content_query = (
        (queries + content_full.astype(jnp.float32))
        .astype(jnp.bfloat16)
        .reshape(seq_count, length, H, KEY)
    )
    position_query = (
        (queries + position_full.astype(jnp.float32))
        .astype(jnp.bfloat16)
        .reshape(seq_count, length, H, KEY)
    )
    key_rows = (
        jnp.dot(normed, key_full, preferred_element_type=jnp.float32)
        .astype(jnp.bfloat16)
        .reshape(seq_count, length, H, KEY)
    )
    value_rows = (
        jnp.dot(normed, value_full, preferred_element_type=jnp.float32)
        .astype(jnp.bfloat16)
        .reshape(seq_count, length, H, VAL)
    )
    basis = basis_table(length, F).astype(jnp.bfloat16)
    rel_keys = (
        jnp.dot(basis, relative_full, preferred_element_type=jnp.float32)
        .astype(jnp.bfloat16)
        .reshape(span, H, KEY)
    )

    def attention_logits():
        content = jnp.einsum(
            "bihe,bjhe->bhij", content_query, key_rows, preferred_element_type=jnp.float32
        )
        raw_scores = jnp.einsum(
            "bihe,the->bhit", position_query, rel_keys, preferred_element_type=jnp.float32
        )
        return content + shift_offsets(raw_scores, length)

    logits = attention_logits()
    row_peak = jnp.max(logits, axis=-1, keepdims=True)
    log_total = row_peak + jnp.log(jnp.sum(jnp.exp(logits - row_peak), axis=-1, keepdims=True))
    attention = jnp.exp(logits - log_total).astype(jnp.bfloat16)
    mixed_heads = jnp.einsum(
        "bhij,bjhd->bihd", attention, value_rows, preferred_element_type=jnp.float32
    )
    mixed_heads = mixed_heads.astype(jnp.bfloat16).reshape(row_count, H * VAL)
    hidden = flat_tokens + (
        jnp.dot(mixed_heads, exit_full, preferred_element_type=jnp.float32)
        + exit_bias.astype(jnp.float32)
    )
    mlp_gain_f = mlp_gain.astype(jnp.float32)
    mlp_shift_f = mlp_shift.astype(jnp.float32)
    normed_mid = layer_norm(hidden, mlp_gain_f, mlp_shift_f).astype(jnp.bfloat16)
    inner_pre = jnp.dot(
        normed_mid, inner_full, preferred_element_type=jnp.float32
    ) + inner_offset.astype(jnp.float32)
    active, gelu_pull = jax.vjp(gelu_exact, inner_pre)
    active_low = active.astype(jnp.bfloat16)
    result = hidden + (
        jnp.dot(active_low, outer_full, preferred_element_type=jnp.float32)
        + outer_offset.astype(jnp.float32)
    )
    layer_out = result.astype(jnp.bfloat16).reshape(seq_count, length, model_width)
    clip_limit = jnp.repeat(thresholds, WIN, axis=1).reshape(row_count, 1)
    clipped = jnp.clip(
        cotangent.reshape(row_count, model_width).astype(jnp.float32), -clip_limit, clip_limit
    )
    mlp_gain, mlp_shift, inner_full, inner_offset, outer_full, outer_offset = (
        spread_rows(mlp_norm_gain),
        spread_rows(mlp_norm_shift),
        spread_rows(inner_weight),
        spread_rows(inner_bias),
        spread_rows(outer_weight),
        spread_rows(outer_bias),
    )
    mlp_gain_f = mlp_gain.astype(jnp.float32)
    outer_delta = clipped.astype(jnp.bfloat16)
    outer_bias_grad = column_sums(outer_delta)
    outer_weight_grad = jnp.einsum(
        "nk,nm->km", active_low, outer_delta, preferred_element_type=jnp.float32
    )
    active_delta = jnp.einsum(
        "nm,km->nk", outer_delta, outer_full, preferred_element_type=jnp.float32
    )
    (inner_grad_pre,) = gelu_pull(active_delta)
    inner_delta = inner_grad_pre.astype(jnp.bfloat16)
    inner_bias_grad = column_sums(inner_delta)
    inner_weight_grad = jnp.einsum(
        "nd,nf->df", normed_mid, inner_delta, preferred_element_type=jnp.float32
    )
    mid_delta = jnp.einsum("nf,df->nd", inner_delta, inner_full, preferred_element_type=jnp.float32)
    norm_out, norm_pull = jax.vjp(layer_norm, hidden, mlp_gain_f, mlp_shift_f)
    hidden_part, mlp_gain_grad, mlp_shift_grad = norm_pull(mid_delta)
    hidden_delta = clipped + hidden_part
    (
        attn_gain,
        attn_shift,
        query_full,
        key_full,
        value_full,
        relative_full,
        content_full,
        position_full,
        exit_full,
        exit_bias,
    ) = (
        spread_rows(attn_norm_gain),
        spread_rows(attn_norm_shift),
        spread_rows(query_weight),
        spread_rows(key_weight),
        spread_rows(value_weight),
        spread_rows(relative_weight),
        spread_rows(content_bias),
        spread_rows(position_bias),
        spread_rows(out_weight),
        spread_rows(out_bias),
    )
    attn_gain_f = attn_gain.astype(jnp.float32)
    branch_delta = hidden_delta.astype(jnp.bfloat16)
    out_bias_grad = column_sums(branch_delta)
    out_weight_grad = jnp.einsum(
        "nk,nd->kd", mixed_heads, branch_delta, preferred_element_type=jnp.float32
    )
    mixed_delta = jnp.einsum(
        "nd,kd->nk", branch_delta, exit_full, preferred_element_type=jnp.float32
    )
    mixed_delta = mixed_delta.astype(jnp.bfloat16).reshape(seq_count, length, H, VAL)
    logits = attention_logits()
    soft_rows = jnp.exp(logits - log_total)
    attention = soft_rows.astype(jnp.bfloat16)
    attention_delta = jnp.einsum(
        "bihd,bjhd->bhij", mixed_delta, value_rows, preferred_element_type=jnp.float32
    )
    value_delta = jnp.einsum(
        "bhij,bihd->bjhd", attention, mixed_delta, preferred_element_type=jnp.float32
    )
    value_delta = value_delta.astype(jnp.bfloat16).reshape(row_count, H * VAL)
    logit_delta = soft_rows * (
        attention_delta - jnp.sum(soft_rows * attention_delta, axis=-1, keepdims=True)
    )
    logit_delta = logit_delta.astype(jnp.bfloat16)
    content_delta = jnp.einsum(
        "bhij,bjhe->bihe", logit_delta, key_rows, preferred_element_type=jnp.float32
    )
    key_delta = jnp.einsum(
        "bhij,bihe->bjhe", logit_delta, content_query, preferred_element_type=jnp.float32
    )
    key_delta = key_delta.astype(jnp.bfloat16).reshape(row_count, H * KEY)
    offset_delta = unshift_offsets(logit_delta, length)
    position_delta = jnp.einsum(
        "bhit,the->bihe", offset_delta, rel_keys, preferred_element_type=jnp.float32
    )
    rel_delta = jnp.einsum(
        "bhit,bihe->the", offset_delta, position_query, preferred_element_type=jnp.float32
    )
    rel_delta = rel_delta.astype(jnp.bfloat16).reshape(span, H * KEY)
    relative_weight_grad = jnp.einsum(
        "tf,tk->fk", basis, rel_delta, preferred_element_type=jnp.float32
    )
    content_delta = content_delta.reshape(row_count, H * KEY)
    position_delta = position_delta.reshape(row_count, H * KEY)
    content_bias_grad = jnp.sum(content_delta, axis=0)
    position_bias_grad = jnp.sum(position_delta, axis=0)
    query_delta = (content_delta + position_delta).astype(jnp.bfloat16) * jnp.asarray(
        query_scale, jnp.bfloat16
    )
    query_weight_grad = jnp.einsum(
        "nd,nk->dk", normed, query_delta, preferred_element_type=jnp.float32
    )
    key_weight_grad = jnp.einsum("nd,nk->dk", normed, key_delta, preferred_element_type=jnp.float32)
    value_weight_grad = jnp.einsum(
        "nd,nk->dk", normed, value_delta, preferred_element_type=jnp.float32
    )
    normed_delta = (
        jnp.einsum("nk,dk->nd", query_delta, query_full, preferred_element_type=jnp.float32)
        + jnp.einsum("nk,dk->nd", key_delta, key_full, preferred_element_type=jnp.float32)
        + jnp.einsum("nk,dk->nd", value_delta, value_full, preferred_element_type=jnp.float32)
    )
    first_out, first_pull = jax.vjp(layer_norm, flat_tokens, attn_gain_f, attn_shift_f)
    tokens_part, attn_gain_grad, attn_shift_grad = first_pull(normed_delta)
    tokens_grad = (
        (hidden_delta + tokens_part).astype(jnp.bfloat16).reshape(seq_count, length, model_width)
    )
    (
        query_weight_grad,
        key_weight_grad,
        value_weight_grad,
        relative_weight_grad,
        out_weight_grad,
        inner_weight_grad,
        outer_weight_grad,
    ) = (
        sum_columns(query_weight_grad),
        sum_columns(key_weight_grad),
        sum_columns(value_weight_grad),
        sum_columns(relative_weight_grad),
        sum_columns(out_weight_grad),
        sum_columns(inner_weight_grad),
        sum_columns(outer_weight_grad),
    )
    (
        query_weight_grad,
        key_weight_grad,
        value_weight_grad,
        relative_weight_grad,
        out_weight_grad,
        inner_weight_grad,
        outer_weight_grad,
        attn_gain_grad,
        attn_shift_grad,
        content_bias_grad,
        position_bias_grad,
        out_bias_grad,
        mlp_gain_grad,
        mlp_shift_grad,
        inner_bias_grad,
        outer_bias_grad,
    ) = (
        sum_rows(query_weight_grad),
        sum_rows(key_weight_grad),
        sum_rows(value_weight_grad),
        sum_rows(relative_weight_grad),
        sum_rows(out_weight_grad),
        sum_rows(inner_weight_grad),
        sum_rows(outer_weight_grad),
        sum_rows(attn_gain_grad),
        sum_rows(attn_shift_grad),
        sum_rows(content_bias_grad),
        sum_rows(position_bias_grad),
        sum_rows(out_bias_grad),
        sum_rows(mlp_gain_grad),
        sum_rows(mlp_shift_grad),
        sum_rows(inner_bias_grad),
        sum_rows(outer_bias_grad),
    )
    (
        query_weight_grad,
        key_weight_grad,
        value_weight_grad,
        relative_weight_grad,
        out_weight_grad,
        inner_weight_grad,
        outer_weight_grad,
    ) = (
        spread_columns(query_weight_grad),
        spread_columns(key_weight_grad),
        spread_columns(value_weight_grad),
        spread_columns(relative_weight_grad),
        spread_columns(out_weight_grad),
        spread_columns(inner_weight_grad),
        spread_columns(outer_weight_grad),
    )
    (
        attn_gain_grad,
        attn_shift_grad,
        content_bias_grad,
        position_bias_grad,
        out_bias_grad,
        mlp_gain_grad,
        mlp_shift_grad,
        inner_bias_grad,
        outer_bias_grad,
    ) = lax.psum(
        (
            attn_gain_grad,
            attn_shift_grad,
            content_bias_grad,
            position_bias_grad,
            out_bias_grad,
            mlp_gain_grad,
            mlp_shift_grad,
            inner_bias_grad,
            outer_bias_grad,
        ),
        WIDE,
    )
    return (
        layer_out,
        tokens_grad,
        attn_gain_grad,
        attn_shift_grad,
        query_weight_grad,
        key_weight_grad,
        value_weight_grad,
        relative_weight_grad,
        content_bias_grad,
        position_bias_grad,
        out_weight_grad,
        out_bias_grad,
        mlp_gain_grad,
        mlp_shift_grad,
        inner_weight_grad,
        inner_bias_grad,
        outer_weight_grad,
        outer_bias_grad,
    )


MESH = pl.DeviceIdType.MESH
NARROW = 4


def position():
    w = lax.axis_index(WIDE)
    z = lax.axis_index(DEPTH)
    c = lax.rem(w, 2)
    p = lax.div(w, 2)
    x = lax.rem(p, 2)
    y = lax.div(p, 2)
    chip = (lambda q: q * 2 + c)
    return types.SimpleNamespace(
        w=w,
        z=z,
        c=c,
        p=p,
        x=x,
        y=y,
        px=p + 1 - 2 * x,
        py=p + 2 - 4 * y,
        pd=3 - p,
        sib=(w + 1 - 2 * c, z),
        xn=(chip(p + 1 - 2 * x), z),
        yn=(chip(p + 2 - 4 * y), z),
    )


def meet(partners):
    barrier = pltpu.get_barrier_semaphore()
    for partner in partners:
        pl.semaphore_signal(barrier, inc=1, device_id=partner, device_id_type=MESH)
    pl.semaphore_wait(barrier, len(partners))


def remote(src, dst, send, recv, target):
    return pltpu.make_async_remote_copy(
        src_ref=src,
        dst_ref=dst,
        send_sem=send,
        recv_sem=recv,
        device_id=target,
        device_id_type=MESH,
    )


def gather_kernel(count, *refs):
    shards = refs[:count]
    rel, small = refs[count : count + 2]
    fulls = refs[count + 2 : 2 * count + 2]
    rel_full, small_full = refs[2 * count + 2 : 2 * count + 4]
    stage = refs[2 * count + 4 : 3 * count + 6]
    zr, xr, yr, fxr, fyr, sr, snd, own, misc_s, misc_r = refs[3 * count + 6 :]
    at = position()
    w, z, c, p = at.w, at.z, at.c, at.p
    me = (w, z)
    depth = [(w, lax.rem(z + d, NARROW)) for d in range(1, NARROW)]
    meet([at.sib, at.xn, at.yn] + depth)

    def block(m, zz, pp, half=None):
        full = fulls[m]
        rows, cols = full.shape[1] // 4, full.shape[2] // 2
        start = pp * rows
        if half is not None:
            rows = rows // 2
            start = start + half * rows
        return full.at[
            zz, pl.ds(pl.multiple_of(start, 8), rows), pl.ds(pl.multiple_of(c * cols, 128), cols)
        ]

    def send(m, ref, recv, target):
        remote(ref, ref, snd.at[m], recv, target).start()

    for d in (1, 3, 2):
        for k, (src, dst) in enumerate(((rel, rel_full), (small, small_full))):
            remote(src, dst.at[z], misc_s.at[k], misc_r.at[k], depth[d - 1]).start()
    for m in range(count):
        shard = shards[m]
        rows, cols = shard.shape[0] // 4, shard.shape[1] // 2
        piece = shard.at[
            pl.ds(pl.multiple_of(p * rows, 8), rows), pl.ds(pl.multiple_of(c * cols, 128), cols)
        ]
        for d in (1, 3, 2):
            remote(piece, block(m, z, p), snd.at[m], zr.at[m, d - 1], depth[d - 1]).start()
    local = [
        (pltpu.make_async_copy(src, mid, own.at[k]), pltpu.make_async_copy(mid, dst.at[z], own.at[k]))
        for k, (src, mid, dst) in enumerate(
            zip((*shards, rel, small), stage, (*fulls, rel_full, small_full))
        )
    ]
    for first, _ in local:
        first.start()
    for first, second in local:
        first.wait()
        second.start()

    def arrive(ref, recv):
        remote(ref, ref, recv, recv, me).wait_recv()

    def spread(m, d):
        zz = lax.rem(z + NARROW - d, NARROW)
        mine = block(m, zz, p)
        arrive(mine, zr.at[m, d - 1])
        send(m, mine, xr.at[m, d - 1], at.xn)
        send(m, mine, yr.at[m, d - 1], at.yn)
        send(m, mine, sr.at[m], at.sib)

    def forward(m, d):
        zz = lax.rem(z + NARROW - d, NARROW)
        arrive(block(m, zz, at.px), xr.at[m, d - 1])
        send(m, block(m, zz, at.px, 0), fxr.at[m, d - 1], at.yn)
        send(m, block(m, zz, at.px), sr.at[m], at.sib)
        arrive(block(m, zz, at.py), yr.at[m, d - 1])
        send(m, block(m, zz, at.py, 1), fyr.at[m, d - 1], at.xn)
        send(m, block(m, zz, at.py), sr.at[m], at.sib)

    def finish(m, d):
        zz = lax.rem(z + NARROW - d, NARROW)
        arrive(block(m, zz, at.pd, 0), fxr.at[m, d - 1])
        arrive(block(m, zz, at.pd, 1), fyr.at[m, d - 1])
        send(m, block(m, zz, at.pd), sr.at[m], at.sib)

    units = [(m, d) for m in range(count) for d in (1, 3, 2)]
    total = len(units)
    for u in range(total + 4):
        if u < total:
            spread(*units[u])
        if 0 <= u - 2 < total:
            forward(*units[u - 2])
        if 0 <= u - 4 < total:
            finish(*units[u - 4])
    for m in range(count):
        cols = fulls[m].shape[2] // 2
        theirs = fulls[m].at[pl.ds(0, 3), :, pl.ds(0, cols)]
        arrive(theirs, sr.at[m])
        sent = fulls[m].at[pl.ds(0, 3)]
        remote(sent, sent, snd.at[m], snd.at[m], me).wait_send()
    for k, full in enumerate((rel_full, small_full)):
        others = full.at[pl.ds(0, 3)]
        arrive(others, misc_r.at[k])
        remote(others, others, misc_s.at[k], misc_s.at[k], me).wait_send()
    for _, second in local:
        second.wait()


HBM = pl.BlockSpec(memory_space=pltpu.HBM)
DMA = pltpu.SemaphoreType.DMA


def gather_weights(shards, rel, small):
    count = len(shards)
    outs = pl.pallas_call(
        lambda *refs: gather_kernel(count, *refs),
        out_shape=tuple(
            jax.ShapeDtypeStruct((NARROW,) + a.shape, a.dtype) for a in (*shards, rel, small)
        ),
        in_specs=[HBM] * (count + 2),
        out_specs=(HBM,) * (count + 2),
        scratch_shapes=[pltpu.VMEM(a.shape, a.dtype) for a in (*shards, rel, small)]
        + [
            DMA((count, 3)),
            DMA((count, 3)),
            DMA((count, 3)),
            DMA((count, 3)),
            DMA((count, 3)),
            DMA((count,)),
            DMA((count,)),
            DMA((count + 2,)),
            DMA((2,)),
            DMA((2,)),
        ],
        compiler_params=pltpu.CompilerParams(
            collective_id=1, has_side_effects=True, vmem_limit_bytes=24 << 20
        ),
        name="gather_weights",
    )(*shards, rel, small)
    fulls = [a.reshape(a.shape[0] * a.shape[1], a.shape[2]) for a in outs[:count]]
    return fulls, outs[count].reshape(-1, rel.shape[1]), outs[count + 1]


def pair_kernel(lefts, rights, *refs):
    n = lefts + rights
    ins, outs, stage = refs[:n], refs[n : 2 * n], refs[2 * n : 3 * n]
    snd, rcv, own = refs[3 * n :]
    at = position()
    c = at.c
    meet([at.sib])
    copies = []
    for k in range(n):
        src, dst = ins[k], outs[k]
        if k < lefts:
            mine, theirs = src, src
        else:
            cols = src.shape[1] // 2
            mine = src.at[:, pl.ds(pl.multiple_of(c * cols, 128), cols)]
            theirs = src.at[:, pl.ds(pl.multiple_of((1 - c) * cols, 128), cols)]
        away = remote(theirs, dst.at[c], snd.at[k], rcv.at[k], at.sib)
        away.start()
        first = pltpu.make_async_copy(mine, stage[k], own.at[k])
        first.start()
        second = pltpu.make_async_copy(stage[k], dst.at[c], own.at[k])
        copies.append((away, first, second))
    for _, first, second in copies:
        first.wait()
        second.start()
    for away, _, second in copies:
        away.wait()
        second.wait()


def pair_exchange(lefts, rights):
    n = len(lefts) + len(rights)
    shapes = [(2,) + a.shape for a in lefts] + [(2, a.shape[0], a.shape[1] // 2) for a in rights]
    outs = pl.pallas_call(
        lambda *refs: pair_kernel(len(lefts), len(rights), *refs),
        out_shape=tuple(jax.ShapeDtypeStruct(s, jnp.bfloat16) for s in shapes),
        in_specs=[HBM] * n,
        out_specs=(HBM,) * n,
        scratch_shapes=[pltpu.VMEM(s[1:], jnp.bfloat16) for s in shapes]
        + [DMA((n,)), DMA((n,)), DMA((n,))],
        compiler_params=pltpu.CompilerParams(
            collective_id=2, has_side_effects=True, vmem_limit_bytes=24 << 20
        ),
        name="pair_exchange",
    )(*lefts, *rights)
    outs = [a.reshape(-1, a.shape[-1]) for a in outs]
    return outs[: len(lefts)], outs[len(lefts) :]


def reduce_kernel(count, *refs):
    grads = refs[:count]
    extra = refs[count]
    outs = refs[count + 1 : 2 * count + 1]
    extra_out = refs[2 * count + 1]
    rest = refs[2 * count + 2 :]
    take = iter(rest)
    keep = [next(take) for _ in range(count)]
    got1 = [next(take) for _ in range(count)]
    got2 = [next(take) for _ in range(count)]
    got3 = [next(take) for _ in range(count)]
    last = [next(take) for _ in range(count)]
    extra_in, extra_keep, extra_got, extra_sum = (next(take) for _ in range(4))
    (ld, s1, r1, s2, r2, s3, r3, s4, r4, lo, es, er, el) = take
    at = position()
    w, z, c, p, x, y = at.w, at.z, at.c, at.p, at.x, at.y
    me = (w, z)
    depth = [(w, lax.rem(z + d, NARROW)) for d in range(1, NARROW)]
    meet([at.sib, at.xn, at.yn] + depth)

    def half(m, h, mine):
        g = grads[m]
        if h == 0:
            return g.at[:, :, x if mine else 1 - x, 0]
        return g.at[:, y if mine else 1 - y, :, 1]

    def stage1(m):
        for h, target in ((0, at.xn), (1, at.yn)):
            remote(half(m, h, False), got1[m].at[h], s1.at[m, h], r1.at[m, h], target).start()
            pltpu.make_async_copy(half(m, h, True), keep[m].at[h], ld.at[m, h]).start()

    def wait_local(ref, sem):
        pltpu.make_async_copy(ref, ref, sem).wait()

    def arrive(ref, recv):
        remote(ref, ref, recv, recv, me).wait_recv()

    def left(ref, sem):
        remote(ref, ref, sem, sem, me).wait_send()

    def stage2(m):
        for h, target, mine in ((0, at.yn, y), (1, at.xn, x)):
            arrive(got1[m].at[h], r1.at[m, h])
            wait_local(keep[m].at[h], ld.at[m, h])

            def add(k, _, h=h):
                zz, o = lax.div(k, 2), lax.rem(k, 2)
                total = keep[m][h, zz, o].astype(jnp.float32) + got1[m][h, zz, o].astype(
                    jnp.float32
                )
                keep[m][h, zz, o] = total.astype(jnp.bfloat16)
                return 0

            lax.fori_loop(0, 8, add, 0)
            remote(
                keep[m].at[h, :, 1 - mine], got2[m].at[h], s2.at[m, h], r2.at[m, h], target
            ).start()

    def stage3(m):
        for h, mine in ((0, y), (1, x)):
            arrive(got2[m].at[h], r2.at[m, h])

            def add(zz, _, h=h, mine=mine):
                total = keep[m][h, zz, mine].astype(jnp.float32) + got2[m][h, zz].astype(
                    jnp.float32
                )
                got2[m][h, zz] = total.astype(jnp.bfloat16)
                return 0

            lax.fori_loop(0, 4, add, 0)
        for d in (1, 3, 2):
            zz = lax.rem(z + d, NARROW)
            remote(
                got2[m].at[:, zz], got3[m].at[d - 1], s3.at[m, d - 1], r3.at[m, d - 1], depth[d - 1]
            ).start()

    def piece(m, pp, half=None):
        out = outs[m]
        rows, cols = out.shape[0] // 4, out.shape[1] // 2
        start = pp * rows
        if half is not None:
            rows = rows // 2
            start = start + half * rows
        return out.at[
            pl.ds(pl.multiple_of(start, 8), rows), pl.ds(pl.multiple_of(c * cols, 128), cols)
        ]

    def stage4(m):
        for d in (1, 3, 2):
            arrive(got3[m].at[d - 1], r3.at[m, d - 1])
        rows = last[m].shape[0] // 2
        for h in range(2):
            total = got2[m][h, z].astype(jnp.float32)
            for d in range(3):
                total = total + got3[m][d, h].astype(jnp.float32)
            last[m][pl.ds(h * rows, rows), :] = total.astype(jnp.bfloat16)
        mine = piece(m, p)
        remote(last[m], mine, s4.at[m], r4.at[m, 0], at.xn).start()
        remote(last[m], mine, s4.at[m], r4.at[m, 1], at.yn).start()
        remote(last[m], mine, s4.at[m], r4.at[m, 4], at.sib).start()
        pltpu.make_async_copy(last[m], mine, lo.at[m]).start()

    def stage5(m):
        arrive(piece(m, at.px), r4.at[m, 0])
        part = piece(m, at.px, 0)
        remote(part, part, s4.at[m], r4.at[m, 2], at.yn).start()
        part = piece(m, at.px)
        remote(part, part, s4.at[m], r4.at[m, 4], at.sib).start()
        arrive(piece(m, at.py), r4.at[m, 1])
        part = piece(m, at.py, 1)
        remote(part, part, s4.at[m], r4.at[m, 3], at.xn).start()
        part = piece(m, at.py)
        remote(part, part, s4.at[m], r4.at[m, 4], at.sib).start()

    def stage6(m):
        arrive(piece(m, at.pd, 0), r4.at[m, 2])
        arrive(piece(m, at.pd, 1), r4.at[m, 3])
        part = piece(m, at.pd)
        remote(part, part, s4.at[m], r4.at[m, 4], at.sib).start()

    def extra_start():
        cp = pltpu.make_async_copy(extra, extra_in, el.at[0])
        cp.start()
        cp.wait()
        extra_keep[0] = extra_in[...]
        remote(extra_keep.at[0], extra_got.at[0], es.at[0], er.at[0], at.sib).start()

    def extra_step(k):
        arrive(extra_got.at[k], er.at[k])
        extra_keep[k + 1] = extra_keep[k] + extra_got[k]
        if k < 2:
            target = (at.xn, at.yn)[k]
            remote(
                extra_keep.at[k + 1], extra_got.at[k + 1], es.at[k + 1], er.at[k + 1], target
            ).start()
        else:
            for d in (1, 3, 2):
                zz = lax.rem(z + d, NARROW)
                remote(
                    extra_keep.at[3, zz],
                    extra_sum.at[d - 1],
                    es.at[2 + d],
                    er.at[2 + d],
                    depth[d - 1],
                ).start()

    def extra_end():
        total = extra_keep[3, z]
        for d in (1, 3, 2):
            arrive(extra_sum.at[d - 1], er.at[2 + d])
            total = total + extra_sum[d - 1]
        extra_in[0] = total
        cp = pltpu.make_async_copy(extra_in.at[0], extra_out, el.at[1])
        cp.start()
        cp.wait()

    stage1(0)
    if count > 1:
        stage1(1)
    extra_start()
    for u in range(count + 5):
        if u < count:
            stage2(u)
            if u + 2 < count:
                stage1(u + 2)
        if u < 3:
            extra_step(u)
        if 0 <= u - 1 < count:
            stage3(u - 1)
        if 0 <= u - 2 < count:
            stage4(u - 2)
        if 0 <= u - 3 < count:
            stage5(u - 3)
        if 0 <= u - 4 < count:
            stage6(u - 4)
        if u == 4:
            extra_end()
    for m in range(count):
        cols = outs[m].shape[1] // 2
        arrive(outs[m].at[:, pl.ds(0, cols)], r4.at[m, 4])
        wait_local(last[m], lo.at[m])
        for h in range(2):
            left(got1[m].at[h], s1.at[m, h])
            left(got2[m].at[h], s2.at[m, h])
        for d in range(3):
            left(got3[m].at[d], s3.at[m, d])
        left(outs[m].at[:, pl.ds(0, cols)], s4.at[m])
        rows = outs[m].shape[0] // 4
        left(outs[m].at[pl.ds(0, 3 * rows), pl.ds(0, cols)], s4.at[m])
    for k in range(3):
        left(extra_got.at[k], es.at[k])
    for d in range(3):
        left(extra_sum.at[d], es.at[3 + d])


def reduce_grads(grads, extra):
    count = len(grads)
    scratch = []
    views = []
    for g in grads:
        rows, cols = g.shape
        views.append(g.reshape(4, 2, 2, 2, rows // 32, cols))
    for g in grads:
        rows, cols = g.shape
        scratch.append(pltpu.VMEM((2, 4, 2, rows // 32, cols), jnp.bfloat16))
    for g in grads:
        rows, cols = g.shape
        scratch.append(pltpu.VMEM((2, 4, 2, rows // 32, cols), jnp.bfloat16))
    for g in grads:
        rows, cols = g.shape
        scratch.append(pltpu.VMEM((2, 4, rows // 32, cols), jnp.bfloat16))
    for g in grads:
        rows, cols = g.shape
        scratch.append(pltpu.VMEM((3, 2, rows // 32, cols), jnp.bfloat16))
    for g in grads:
        rows, cols = g.shape
        scratch.append(pltpu.VMEM((rows // 16, cols), jnp.bfloat16))
    scratch += [
        pltpu.VMEM(extra.shape, jnp.float32),
        pltpu.VMEM((4,) + extra.shape, jnp.float32),
        pltpu.VMEM((3,) + extra.shape, jnp.float32),
        pltpu.VMEM((3,) + extra.shape[1:], jnp.float32),
    ]
    scratch += [
        DMA((count, 2)),
        DMA((count, 2)),
        DMA((count, 2)),
        DMA((count, 2)),
        DMA((count, 2)),
        DMA((count, 3)),
        DMA((count, 3)),
        DMA((count,)),
        DMA((count, 5)),
        DMA((count,)),
        DMA((6,)),
        DMA((6,)),
        DMA((2,)),
    ]
    outs = pl.pallas_call(
        lambda *refs: reduce_kernel(count, *refs),
        out_shape=tuple(
            jax.ShapeDtypeStruct((g.shape[0] // 4, g.shape[1] * 2), jnp.bfloat16) for g in grads
        )
        + (jax.ShapeDtypeStruct(extra.shape[1:], jnp.float32),),
        in_specs=[HBM] * (count + 1),
        out_specs=(HBM,) * (count + 1),
        scratch_shapes=scratch,
        compiler_params=pltpu.CompilerParams(
            collective_id=3, has_side_effects=True, vmem_limit_bytes=58 << 20
        ),
        name="reduce_grads",
    )(*views, extra)
    return outs[:count], outs[count]


def per_device_linked(
    tokens,
    cotangent,
    thresholds,
    attn_norm_gain,
    attn_norm_shift,
    query_weight,
    key_weight,
    value_weight,
    relative_weight,
    content_bias,
    position_bias,
    out_weight,
    out_bias,
    mlp_norm_gain,
    mlp_norm_shift,
    inner_weight,
    inner_bias,
    outer_weight,
    outer_bias,
):
    seq_count, length, model_width = tokens.shape
    row_count = seq_count * length
    span = 2 * length - 1
    query_scale = KEY ** (-0.5)
    vectors = (
        attn_norm_gain,
        attn_norm_shift,
        content_bias,
        position_bias,
        out_bias,
        mlp_norm_gain,
        mlp_norm_shift,
        inner_bias,
        outer_bias,
    )
    sizes = [v.shape[0] for v in vectors]
    small = jnp.concatenate(vectors).reshape(-1, 128)
    small = jnp.pad(small, ((0, -small.shape[0] % 8), (0, 0)))
    fulls, relative_full, small_full = gather_weights(
        (query_weight, key_weight, value_weight, out_weight, inner_weight, outer_weight),
        relative_weight,
        small,
    )
    query_full, key_full, value_full, exit_full, inner_full, outer_full = fulls
    flat_small = small_full.reshape(NARROW, -1)
    spread = []
    start = 0
    for size in sizes:
        spread.append(flat_small[:, start : start + size].reshape(-1).astype(jnp.float32))
        start += size
    (
        attn_gain_f,
        attn_shift_f,
        content_f,
        position_f,
        exit_f,
        mlp_gain_f,
        mlp_shift_f,
        inner_offset_f,
        outer_offset_f,
    ) = spread
    flat_tokens = tokens.reshape(row_count, model_width).astype(jnp.float32)
    normed = layer_norm(flat_tokens, attn_gain_f, attn_shift_f).astype(jnp.bfloat16)
    queries = jnp.dot(normed, query_full, preferred_element_type=jnp.float32) * query_scale
    content_query = (
        (queries + content_f).astype(jnp.bfloat16).reshape(seq_count, length, H, KEY)
    )
    position_query = (
        (queries + position_f).astype(jnp.bfloat16).reshape(seq_count, length, H, KEY)
    )
    key_rows = (
        jnp.dot(normed, key_full, preferred_element_type=jnp.float32)
        .astype(jnp.bfloat16)
        .reshape(seq_count, length, H, KEY)
    )
    value_rows = (
        jnp.dot(normed, value_full, preferred_element_type=jnp.float32)
        .astype(jnp.bfloat16)
        .reshape(seq_count, length, H, VAL)
    )
    basis = basis_table(length, F).astype(jnp.bfloat16)
    rel_keys = (
        jnp.dot(basis, relative_full, preferred_element_type=jnp.float32)
        .astype(jnp.bfloat16)
        .reshape(span, H, KEY)
    )
    content = jnp.einsum(
        "bihe,bjhe->bhij", content_query, key_rows, preferred_element_type=jnp.float32
    )
    raw_scores = jnp.einsum(
        "bihe,the->bhit", position_query, rel_keys, preferred_element_type=jnp.float32
    )
    logits = content + shift_offsets(raw_scores, length)
    row_peak = jnp.max(logits, axis=-1, keepdims=True)
    log_total = row_peak + jnp.log(jnp.sum(jnp.exp(logits - row_peak), axis=-1, keepdims=True))
    soft_rows = jnp.exp(logits - log_total)
    attention = soft_rows.astype(jnp.bfloat16)
    mixed_heads = jnp.einsum(
        "bhij,bjhd->bihd", attention, value_rows, preferred_element_type=jnp.float32
    )
    mixed_heads = mixed_heads.astype(jnp.bfloat16).reshape(row_count, H * VAL)
    hidden = flat_tokens + (
        jnp.dot(mixed_heads, exit_full, preferred_element_type=jnp.float32) + exit_f
    )
    normed_mid = layer_norm(hidden, mlp_gain_f, mlp_shift_f).astype(jnp.bfloat16)
    inner_pre = (
        jnp.dot(normed_mid, inner_full, preferred_element_type=jnp.float32) + inner_offset_f
    )
    active, gelu_pull = jax.vjp(gelu_exact, inner_pre)
    active_low = active.astype(jnp.bfloat16)
    result = hidden + (
        jnp.dot(active_low, outer_full, preferred_element_type=jnp.float32) + outer_offset_f
    )
    layer_out = result.astype(jnp.bfloat16).reshape(seq_count, length, model_width)
    clip_limit = jnp.repeat(thresholds, WIN, axis=1).reshape(row_count, 1)
    clipped = jnp.clip(
        cotangent.reshape(row_count, model_width).astype(jnp.float32), -clip_limit, clip_limit
    )
    outer_delta = clipped.astype(jnp.bfloat16)
    outer_bias_grad = column_sums(outer_delta)
    active_delta = jnp.einsum(
        "nm,km->nk", outer_delta, outer_full, preferred_element_type=jnp.float32
    )
    (inner_grad_pre,) = gelu_pull(active_delta)
    inner_delta = inner_grad_pre.astype(jnp.bfloat16)
    inner_bias_grad = column_sums(inner_delta)
    mid_delta = jnp.einsum("nf,df->nd", inner_delta, inner_full, preferred_element_type=jnp.float32)
    _, norm_pull = jax.vjp(layer_norm, hidden, mlp_gain_f, mlp_shift_f)
    hidden_part, mlp_gain_grad, mlp_shift_grad = norm_pull(mid_delta)
    hidden_delta = clipped + hidden_part
    branch_delta = hidden_delta.astype(jnp.bfloat16)
    out_bias_grad = column_sums(branch_delta)
    mixed_delta = jnp.einsum(
        "nd,kd->nk", branch_delta, exit_full, preferred_element_type=jnp.float32
    )
    mixed_delta = mixed_delta.astype(jnp.bfloat16).reshape(seq_count, length, H, VAL)
    attention_delta = jnp.einsum(
        "bihd,bjhd->bhij", mixed_delta, value_rows, preferred_element_type=jnp.float32
    )
    value_delta = jnp.einsum(
        "bhij,bihd->bjhd", attention, mixed_delta, preferred_element_type=jnp.float32
    )
    value_delta = value_delta.astype(jnp.bfloat16).reshape(row_count, H * VAL)
    logit_delta = soft_rows * (
        attention_delta - jnp.sum(soft_rows * attention_delta, axis=-1, keepdims=True)
    )
    logit_delta = logit_delta.astype(jnp.bfloat16)
    content_delta = jnp.einsum(
        "bhij,bjhe->bihe", logit_delta, key_rows, preferred_element_type=jnp.float32
    )
    key_delta = jnp.einsum(
        "bhij,bihe->bjhe", logit_delta, content_query, preferred_element_type=jnp.float32
    )
    key_delta = key_delta.astype(jnp.bfloat16).reshape(row_count, H * KEY)
    offset_delta = unshift_offsets(logit_delta, length)
    position_delta = jnp.einsum(
        "bhit,the->bihe", offset_delta, rel_keys, preferred_element_type=jnp.float32
    )
    rel_delta = jnp.einsum(
        "bhit,bihe->the", offset_delta, position_query, preferred_element_type=jnp.float32
    )
    rel_delta = rel_delta.astype(jnp.bfloat16).reshape(span, H * KEY)
    relative_weight_grad = jnp.einsum(
        "tf,tk->fk", basis, rel_delta, preferred_element_type=jnp.float32
    )
    content_delta = content_delta.reshape(row_count, H * KEY)
    position_delta = position_delta.reshape(row_count, H * KEY)
    content_bias_grad = jnp.sum(content_delta, axis=0)
    position_bias_grad = jnp.sum(position_delta, axis=0)
    query_delta = (content_delta + position_delta).astype(jnp.bfloat16) * jnp.asarray(
        query_scale, jnp.bfloat16
    )
    normed_delta = (
        jnp.einsum("nk,dk->nd", query_delta, query_full, preferred_element_type=jnp.float32)
        + jnp.einsum("nk,dk->nd", key_delta, key_full, preferred_element_type=jnp.float32)
        + jnp.einsum("nk,dk->nd", value_delta, value_full, preferred_element_type=jnp.float32)
    )
    _, first_pull = jax.vjp(layer_norm, flat_tokens, attn_gain_f, attn_shift_f)
    tokens_part, attn_gain_grad, attn_shift_grad = first_pull(normed_delta)
    tokens_grad = (
        (hidden_delta + tokens_part).astype(jnp.bfloat16).reshape(seq_count, length, model_width)
    )
    (xn, xm, xi, xo), (dq, dk, dv, db, di, do) = pair_exchange(
        (normed, mixed_heads, normed_mid, active_low),
        (query_delta, key_delta, value_delta, branch_delta, inner_delta, outer_delta),
    )

    def outer_product(a, b):
        return jnp.einsum("nk,nm->km", a, b, preferred_element_type=jnp.float32).astype(
            jnp.bfloat16
        )

    grads = (
        outer_product(xo, do),
        outer_product(xi, di),
        outer_product(xm, db),
        outer_product(xn, dv),
        outer_product(xn, dk),
        outer_product(xn, dq),
    )
    parts = [relative_weight_grad.reshape(NARROW, -1)] + [
        v.reshape(NARROW, -1)
        for v in (
            attn_gain_grad,
            attn_shift_grad,
            content_bias_grad,
            position_bias_grad,
            out_bias_grad,
            mlp_gain_grad,
            mlp_shift_grad,
            inner_bias_grad,
            outer_bias_grad,
        )
    ]
    widths = [v.shape[1] for v in parts]
    extra = jnp.concatenate(parts, axis=1).reshape(NARROW, -1, 128)
    extra = jnp.pad(extra, ((0, 0), (0, -extra.shape[1] % 8), (0, 0)))
    sums, extra_sum = reduce_grads(grads, extra)
    outer_g, inner_g, out_g, value_g, key_g, query_g = (a.astype(jnp.float32) for a in sums)
    flat = extra_sum.reshape(-1)
    pieces = []
    start = 0
    for width in widths:
        pieces.append(flat[start : start + width])
        start += width
    (
        relative_weight_grad,
        attn_gain_grad,
        attn_shift_grad,
        content_bias_grad,
        position_bias_grad,
        out_bias_grad,
        mlp_gain_grad,
        mlp_shift_grad,
        inner_bias_grad,
        outer_bias_grad,
    ) = pieces
    return (
        layer_out,
        tokens_grad,
        attn_gain_grad,
        attn_shift_grad,
        query_g,
        key_g,
        value_g,
        relative_weight_grad.reshape(relative_weight.shape),
        content_bias_grad,
        position_bias_grad,
        out_g,
        out_bias_grad,
        mlp_gain_grad,
        mlp_shift_grad,
        inner_g,
        inner_bias_grad,
        outer_g,
        outer_bias_grad,
    )


def solution(mesh):
    body = per_device_generic
    if mesh.shape[WIDE] == 8 and mesh.shape[DEPTH] == 4:
        body = per_device_linked
    in_specs = (
        P((WIDE, DEPTH), None, None),
        P((WIDE, DEPTH), None, None),
        P((WIDE, DEPTH), None),
        P(DEPTH),
        P(DEPTH),
        P(DEPTH, None),
        P(DEPTH, None),
        P(DEPTH, None),
        P(DEPTH, None),
        P(DEPTH),
        P(DEPTH),
        P(DEPTH, None),
        P(DEPTH),
        P(DEPTH),
        P(DEPTH),
        P(DEPTH, None),
        P(DEPTH),
        P(DEPTH, None),
        P(DEPTH),
    )
    out_specs = (
        P((WIDE, DEPTH), None, None),
        P((WIDE, DEPTH), None, None),
        P(DEPTH),
        P(DEPTH),
        P(DEPTH, None),
        P(DEPTH, None),
        P(DEPTH, None),
        P(DEPTH, None),
        P(DEPTH),
        P(DEPTH),
        P(DEPTH, None),
        P(DEPTH),
        P(DEPTH),
        P(DEPTH),
        P(DEPTH, None),
        P(DEPTH),
        P(DEPTH, None),
        P(DEPTH),
    )
    return jax.shard_map(
        body, mesh=mesh, in_specs=in_specs, out_specs=out_specs, check_vma=False
    )
```

```python
import math
import types

import jax
import jax.numpy as jnp
from jax import lax
from jax.experimental import pallas as pl
from jax.experimental.pallas import tpu as pltpu
from jax.sharding import PartitionSpec as P

H = 8
KEY = 64
VAL = 192
F = 192
WIN = 128


EPSILON = 1e-05


def basis_table(length, features):
    family = features // 6
    offsets = jnp.arange(2 * length - 1, dtype=jnp.float32) - (length - 1)
    distance = jnp.abs(offsets)[:, None]
    halves = 2.0 ** jnp.linspace(3.0, math.log2(length), family, dtype=jnp.float32)
    decays = jnp.exp(-math.log(2.0) / halves[None, :] * distance)
    widths = 2.0 ** jnp.arange(1, family + 1, dtype=jnp.float32) - 1.0
    central = jnp.where(widths[None, :] > distance, 1.0, 0.0).astype(jnp.float32)
    centers = jnp.linspace(0.0, float(length), family, dtype=jnp.float32)
    spread = length / family
    bump_rows = jnp.exp(-0.5 * ((distance - centers[None, :]) / spread) ** 2)
    positive = jnp.concatenate([decays, central, bump_rows], axis=1)
    return jnp.concatenate([positive, jnp.sign(offsets)[:, None] * positive], axis=1)


def shift_offsets(raw_scores, length):
    leading = raw_scores.shape[:-2]
    padded = jnp.pad(raw_scores, [(0, 0)] * len(leading) + [(0, 0), (0, 1)])
    flatten = padded.reshape(leading + (2 * length * length,))
    window = flatten[..., length - 1 : length - 1 + length * (2 * length - 1)]
    return window.reshape(leading + (length, 2 * length - 1))[..., :length]


def unshift_offsets(grad_scores, length):
    leading = grad_scores.shape[:-2]
    widened = jnp.pad(grad_scores, [(0, 0)] * len(leading) + [(0, 0), (0, length - 1)])
    flatten = widened.reshape(leading + (length * (2 * length - 1),))
    flatten = jnp.pad(flatten, [(0, 0)] * len(leading) + [(length - 1, 1)])
    return flatten.reshape(leading + (length, 2 * length))[..., : 2 * length - 1]


def layer_norm(values, gain, shift):
    center = values - jnp.mean(values, axis=-1, keepdims=True)
    spread = jnp.mean(center * center, axis=-1, keepdims=True)
    return center * lax.rsqrt(spread + EPSILON) * gain + shift


def gelu_exact(values):
    return jax.nn.gelu(values, approximate=False)


def column_sums(values):
    return jnp.sum(values.astype(jnp.float32), axis=0)


WIDE = "wide"
DEPTH = "narrow"


def spread_rows(shard):
    return lax.all_gather(shard, DEPTH, axis=0, tiled=True)


def sum_columns(part):
    low = part.astype(jnp.bfloat16)
    return lax.psum_scatter(low, WIDE, scatter_dimension=1, tiled=True).astype(jnp.float32)


def sum_rows(part):
    low = part.astype(jnp.bfloat16)
    return lax.psum_scatter(low, DEPTH, scatter_dimension=0, tiled=True).astype(jnp.float32)


def spread_columns(part):
    low = part.astype(jnp.bfloat16)
    return lax.all_gather(low, WIDE, axis=1, tiled=True).astype(jnp.float32)


def per_device_generic(
    tokens,
    cotangent,
    thresholds,
    attn_norm_gain,
    attn_norm_shift,
    query_weight,
    key_weight,
    value_weight,
    relative_weight,
    content_bias,
    position_bias,
    out_weight,
    out_bias,
    mlp_norm_gain,
    mlp_norm_shift,
    inner_weight,
    inner_bias,
    outer_weight,
    outer_bias,
):
    seq_count, length, model_width = tokens.shape
    row_count = seq_count * length
    span = 2 * length - 1
    query_scale = KEY ** (-0.5)
    (
        attn_gain,
        attn_shift,
        query_full,
        key_full,
        value_full,
        relative_full,
        content_full,
        position_full,
        exit_full,
        exit_bias,
    ) = (
        spread_rows(attn_norm_gain),
        spread_rows(attn_norm_shift),
        spread_rows(query_weight),
        spread_rows(key_weight),
        spread_rows(value_weight),
        spread_rows(relative_weight),
        spread_rows(content_bias),
        spread_rows(position_bias),
        spread_rows(out_weight),
        spread_rows(out_bias),
    )
    mlp_gain, mlp_shift, inner_full, inner_offset, outer_full, outer_offset = (
        spread_rows(mlp_norm_gain),
        spread_rows(mlp_norm_shift),
        spread_rows(inner_weight),
        spread_rows(inner_bias),
        spread_rows(outer_weight),
        spread_rows(outer_bias),
    )
    flat_tokens = tokens.reshape(row_count, model_width).astype(jnp.float32)
    attn_gain_f = attn_gain.astype(jnp.float32)
    attn_shift_f = attn_shift.astype(jnp.float32)
    normed = layer_norm(flat_tokens, attn_gain_f, attn_shift_f).astype(jnp.bfloat16)
    queries = jnp.dot(normed, query_full, preferred_element_type=jnp.float32) * query_scale
    content_query = (
        (queries + content_full.astype(jnp.float32))
        .astype(jnp.bfloat16)
        .reshape(seq_count, length, H, KEY)
    )
    position_query = (
        (queries + position_full.astype(jnp.float32))
        .astype(jnp.bfloat16)
        .reshape(seq_count, length, H, KEY)
    )
    key_rows = (
        jnp.dot(normed, key_full, preferred_element_type=jnp.float32)
        .astype(jnp.bfloat16)
        .reshape(seq_count, length, H, KEY)
    )
    value_rows = (
        jnp.dot(normed, value_full, preferred_element_type=jnp.float32)
        .astype(jnp.bfloat16)
        .reshape(seq_count, length, H, VAL)
    )
    basis = basis_table(length, F).astype(jnp.bfloat16)
    rel_keys = (
        jnp.dot(basis, relative_full, preferred_element_type=jnp.float32)
        .astype(jnp.bfloat16)
        .reshape(span, H, KEY)
    )

    def attention_logits():
        content = jnp.einsum(
            "bihe,bjhe->bhij", content_query, key_rows, preferred_element_type=jnp.float32
        )
        raw_scores = jnp.einsum(
            "bihe,the->bhit", position_query, rel_keys, preferred_element_type=jnp.float32
        )
        return content + shift_offsets(raw_scores, length)

    logits = attention_logits()
    row_peak = jnp.max(logits, axis=-1, keepdims=True)
    log_total = row_peak + jnp.log(jnp.sum(jnp.exp(logits - row_peak), axis=-1, keepdims=True))
    attention = jnp.exp(logits - log_total).astype(jnp.bfloat16)
    mixed_heads = jnp.einsum(
        "bhij,bjhd->bihd", attention, value_rows, preferred_element_type=jnp.float32
    )
    mixed_heads = mixed_heads.astype(jnp.bfloat16).reshape(row_count, H * VAL)
    hidden = flat_tokens + (
        jnp.dot(mixed_heads, exit_full, preferred_element_type=jnp.float32)
        + exit_bias.astype(jnp.float32)
    )
    mlp_gain_f = mlp_gain.astype(jnp.float32)
    mlp_shift_f = mlp_shift.astype(jnp.float32)
    normed_mid = layer_norm(hidden, mlp_gain_f, mlp_shift_f).astype(jnp.bfloat16)
    inner_pre = jnp.dot(
        normed_mid, inner_full, preferred_element_type=jnp.float32
    ) + inner_offset.astype(jnp.float32)
    active, gelu_pull = jax.vjp(gelu_exact, inner_pre)
    active_low = active.astype(jnp.bfloat16)
    result = hidden + (
        jnp.dot(active_low, outer_full, preferred_element_type=jnp.float32)
        + outer_offset.astype(jnp.float32)
    )
    layer_out = result.astype(jnp.bfloat16).reshape(seq_count, length, model_width)
    clip_limit = jnp.repeat(thresholds, WIN, axis=1).reshape(row_count, 1)
    clipped = jnp.clip(
        cotangent.reshape(row_count, model_width).astype(jnp.float32), -clip_limit, clip_limit
    )
    mlp_gain, mlp_shift, inner_full, inner_offset, outer_full, outer_offset = (
        spread_rows(mlp_norm_gain),
        spread_rows(mlp_norm_shift),
        spread_rows(inner_weight),
        spread_rows(inner_bias),
        spread_rows(outer_weight),
        spread_rows(outer_bias),
    )
    mlp_gain_f = mlp_gain.astype(jnp.float32)
    outer_delta = clipped.astype(jnp.bfloat16)
    outer_bias_grad = column_sums(outer_delta)
    outer_weight_grad = jnp.einsum(
        "nk,nm->km", active_low, outer_delta, preferred_element_type=jnp.float32
    )
    active_delta = jnp.einsum(
        "nm,km->nk", outer_delta, outer_full, preferred_element_type=jnp.float32
    )
    (inner_grad_pre,) = gelu_pull(active_delta)
    inner_delta = inner_grad_pre.astype(jnp.bfloat16)
    inner_bias_grad = column_sums(inner_delta)
    inner_weight_grad = jnp.einsum(
        "nd,nf->df", normed_mid, inner_delta, preferred_element_type=jnp.float32
    )
    mid_delta = jnp.einsum("nf,df->nd", inner_delta, inner_full, preferred_element_type=jnp.float32)
    norm_out, norm_pull = jax.vjp(layer_norm, hidden, mlp_gain_f, mlp_shift_f)
    hidden_part, mlp_gain_grad, mlp_shift_grad = norm_pull(mid_delta)
    hidden_delta = clipped + hidden_part
    (
        attn_gain,
        attn_shift,
        query_full,
        key_full,
        value_full,
        relative_full,
        content_full,
        position_full,
        exit_full,
        exit_bias,
    ) = (
        spread_rows(attn_norm_gain),
        spread_rows(attn_norm_shift),
        spread_rows(query_weight),
        spread_rows(key_weight),
        spread_rows(value_weight),
        spread_rows(relative_weight),
        spread_rows(content_bias),
        spread_rows(position_bias),
        spread_rows(out_weight),
        spread_rows(out_bias),
    )
    attn_gain_f = attn_gain.astype(jnp.float32)
    branch_delta = hidden_delta.astype(jnp.bfloat16)
    out_bias_grad = column_sums(branch_delta)
    out_weight_grad = jnp.einsum(
        "nk,nd->kd", mixed_heads, branch_delta, preferred_element_type=jnp.float32
    )
    mixed_delta = jnp.einsum(
        "nd,kd->nk", branch_delta, exit_full, preferred_element_type=jnp.float32
    )
    mixed_delta = mixed_delta.astype(jnp.bfloat16).reshape(seq_count, length, H, VAL)
    logits = attention_logits()
    soft_rows = jnp.exp(logits - log_total)
    attention = soft_rows.astype(jnp.bfloat16)
    attention_delta = jnp.einsum(
        "bihd,bjhd->bhij", mixed_delta, value_rows, preferred_element_type=jnp.float32
    )
    value_delta = jnp.einsum(
        "bhij,bihd->bjhd", attention, mixed_delta, preferred_element_type=jnp.float32
    )
    value_delta = value_delta.astype(jnp.bfloat16).reshape(row_count, H * VAL)
    logit_delta = soft_rows * (
        attention_delta - jnp.sum(soft_rows * attention_delta, axis=-1, keepdims=True)
    )
    logit_delta = logit_delta.astype(jnp.bfloat16)
    content_delta = jnp.einsum(
        "bhij,bjhe->bihe", logit_delta, key_rows, preferred_element_type=jnp.float32
    )
    key_delta = jnp.einsum(
        "bhij,bihe->bjhe", logit_delta, content_query, preferred_element_type=jnp.float32
    )
    key_delta = key_delta.astype(jnp.bfloat16).reshape(row_count, H * KEY)
    offset_delta = unshift_offsets(logit_delta, length)
    position_delta = jnp.einsum(
        "bhit,the->bihe", offset_delta, rel_keys, preferred_element_type=jnp.float32
    )
    rel_delta = jnp.einsum(
        "bhit,bihe->the", offset_delta, position_query, preferred_element_type=jnp.float32
    )
    rel_delta = rel_delta.astype(jnp.bfloat16).reshape(span, H * KEY)
    relative_weight_grad = jnp.einsum(
        "tf,tk->fk", basis, rel_delta, preferred_element_type=jnp.float32
    )
    content_delta = content_delta.reshape(row_count, H * KEY)
    position_delta = position_delta.reshape(row_count, H * KEY)
    content_bias_grad = jnp.sum(content_delta, axis=0)
    position_bias_grad = jnp.sum(position_delta, axis=0)
    query_delta = (content_delta + position_delta).astype(jnp.bfloat16) * jnp.asarray(
        query_scale, jnp.bfloat16
    )
    query_weight_grad = jnp.einsum(
        "nd,nk->dk", normed, query_delta, preferred_element_type=jnp.float32
    )
    key_weight_grad = jnp.einsum("nd,nk->dk", normed, key_delta, preferred_element_type=jnp.float32)
    value_weight_grad = jnp.einsum(
        "nd,nk->dk", normed, value_delta, preferred_element_type=jnp.float32
    )
    normed_delta = (
        jnp.einsum("nk,dk->nd", query_delta, query_full, preferred_element_type=jnp.float32)
        + jnp.einsum("nk,dk->nd", key_delta, key_full, preferred_element_type=jnp.float32)
        + jnp.einsum("nk,dk->nd", value_delta, value_full, preferred_element_type=jnp.float32)
    )
    first_out, first_pull = jax.vjp(layer_norm, flat_tokens, attn_gain_f, attn_shift_f)
    tokens_part, attn_gain_grad, attn_shift_grad = first_pull(normed_delta)
    tokens_grad = (
        (hidden_delta + tokens_part).astype(jnp.bfloat16).reshape(seq_count, length, model_width)
    )
    (
        query_weight_grad,
        key_weight_grad,
        value_weight_grad,
        relative_weight_grad,
        out_weight_grad,
        inner_weight_grad,
        outer_weight_grad,
    ) = (
        sum_columns(query_weight_grad),
        sum_columns(key_weight_grad),
        sum_columns(value_weight_grad),
        sum_columns(relative_weight_grad),
        sum_columns(out_weight_grad),
        sum_columns(inner_weight_grad),
        sum_columns(outer_weight_grad),
    )
    (
        query_weight_grad,
        key_weight_grad,
        value_weight_grad,
        relative_weight_grad,
        out_weight_grad,
        inner_weight_grad,
        outer_weight_grad,
        attn_gain_grad,
        attn_shift_grad,
        content_bias_grad,
        position_bias_grad,
        out_bias_grad,
        mlp_gain_grad,
        mlp_shift_grad,
        inner_bias_grad,
        outer_bias_grad,
    ) = (
        sum_rows(query_weight_grad),
        sum_rows(key_weight_grad),
        sum_rows(value_weight_grad),
        sum_rows(relative_weight_grad),
        sum_rows(out_weight_grad),
        sum_rows(inner_weight_grad),
        sum_rows(outer_weight_grad),
        sum_rows(attn_gain_grad),
        sum_rows(attn_shift_grad),
        sum_rows(content_bias_grad),
        sum_rows(position_bias_grad),
        sum_rows(out_bias_grad),
        sum_rows(mlp_gain_grad),
        sum_rows(mlp_shift_grad),
        sum_rows(inner_bias_grad),
        sum_rows(outer_bias_grad),
    )
    (
        query_weight_grad,
        key_weight_grad,
        value_weight_grad,
        relative_weight_grad,
        out_weight_grad,
        inner_weight_grad,
        outer_weight_grad,
    ) = (
        spread_columns(query_weight_grad),
        spread_columns(key_weight_grad),
        spread_columns(value_weight_grad),
        spread_columns(relative_weight_grad),
        spread_columns(out_weight_grad),
        spread_columns(inner_weight_grad),
        spread_columns(outer_weight_grad),
    )
    (
        attn_gain_grad,
        attn_shift_grad,
        content_bias_grad,
        position_bias_grad,
        out_bias_grad,
        mlp_gain_grad,
        mlp_shift_grad,
        inner_bias_grad,
        outer_bias_grad,
    ) = lax.psum(
        (
            attn_gain_grad,
            attn_shift_grad,
            content_bias_grad,
            position_bias_grad,
            out_bias_grad,
            mlp_gain_grad,
            mlp_shift_grad,
            inner_bias_grad,
            outer_bias_grad,
        ),
        WIDE,
    )
    return (
        layer_out,
        tokens_grad,
        attn_gain_grad,
        attn_shift_grad,
        query_weight_grad,
        key_weight_grad,
        value_weight_grad,
        relative_weight_grad,
        content_bias_grad,
        position_bias_grad,
        out_weight_grad,
        out_bias_grad,
        mlp_gain_grad,
        mlp_shift_grad,
        inner_weight_grad,
        inner_bias_grad,
        outer_weight_grad,
        outer_bias_grad,
    )


MESH = pl.DeviceIdType.MESH
NARROW = 4


def position():
    w = lax.axis_index(WIDE)
    z = lax.axis_index(DEPTH)
    c = lax.rem(w, 2)
    p = lax.div(w, 2)
    x = lax.rem(p, 2)
    y = lax.div(p, 2)
    chip = (lambda q: q * 2 + c)
    return types.SimpleNamespace(
        w=w,
        z=z,
        c=c,
        p=p,
        x=x,
        y=y,
        px=p + 1 - 2 * x,
        py=p + 2 - 4 * y,
        pd=3 - p,
        sib=(w + 1 - 2 * c, z),
        xn=(chip(p + 1 - 2 * x), z),
        yn=(chip(p + 2 - 4 * y), z),
    )


def meet(partners):
    barrier = pltpu.get_barrier_semaphore()
    for partner in partners:
        pl.semaphore_signal(barrier, inc=1, device_id=partner, device_id_type=MESH)
    pl.semaphore_wait(barrier, len(partners))


def remote(src, dst, send, recv, target):
    return pltpu.make_async_remote_copy(
        src_ref=src,
        dst_ref=dst,
        send_sem=send,
        recv_sem=recv,
        device_id=target,
        device_id_type=MESH,
    )


HBM = pl.BlockSpec(memory_space=pltpu.HBM)
DMA = pltpu.SemaphoreType.DMA


def dot_nn(a, b):
    return jnp.dot(a, b, preferred_element_type=jnp.float32)


def dot_nt(a, b):
    return lax.dot_general(a, b, (((1,), (1,)), ((), ())), preferred_element_type=jnp.float32)


def dot_tn(a, b):
    return lax.dot_general(a, b, (((0,), (0,)), ((), ())), preferred_element_type=jnp.float32)


def low(v):
    return v.astype(jnp.bfloat16)


def wide(v):
    return v.astype(jnp.float32)


def lanes(start, size):
    return pl.ds(pl.multiple_of(start, 128), size)


def arrive(ref, sem):
    me = (lax.axis_index(WIDE), lax.axis_index(DEPTH))
    remote(ref, ref, sem, sem, me).wait_recv()


def left(ref, sem):
    me = (lax.axis_index(WIDE), lax.axis_index(DEPTH))
    remote(ref, ref, sem, sem, me).wait_send()


def forward_refs(
    tok_h,
    cot_h,
    lim_h,
    wq,
    wk,
    wv,
    wo,
    wu,
    wi,
    rel_h,
    small_h,
    basis_h,
    flip_h,
    out_h,
    p_h,
    cq_h,
    pq_h,
    k_h,
    v_h,
    rr_h,
    md_h,
    hd_h,
    nn_h,
    fq,
    fk,
    fv,
    vec_h,
    gu0,
    gu1,
    gi0,
    gi1,
    go,
    sums_h,
    q,
    k,
    v,
    o,
    u0,
    u1,
    i0,
    i1,
    rel,
    small,
    vec,
    tok,
    normed,
    cq,
    pq,
    kr,
    vr,
    basis,
    flip,
    rk,
    rr,
    p,
    mixed,
    hidden,
    nmid,
    cot,
    od,
    odc,
    ad,
    act,
    idl,
    idc,
    hd,
    bd,
    bdc,
    md,
    lo,
    gst,
    sums,
    lim,
    zr,
    xr,
    yr,
    fxr,
    fyr,
    sr,
    snd,
    own,
    ld,
    mr,
    ms,
    ps,
    pr,
    st,
    gs,
):
    return types.SimpleNamespace(**locals())


def forward_kernel(*refs):
    t = forward_refs(*refs)
    at = position()
    w, z, c, p = at.w, at.z, at.c, at.p
    depth = [(w, lax.rem(z + d, NARROW)) for d in range(1, NARROW)]
    meet([at.sib, at.xn, at.yn] + depth)
    rows_all = t.tok.shape[0]
    width = t.tok.shape[1]

    plan = (
        (t.wq, 0, t.q),
        (t.wk, 0, t.k),
        (t.wv, 0, t.v),
        (t.wo, 0, t.o),
        (t.wu, 0, t.u0),
        (t.wu, 1, t.u1),
        (t.wi, 0, t.i0),
        (t.wi, 1, t.i1),
    )

    def block(m, zz, pp, half=None):
        full = plan[m][2]
        rows, cols = full.shape[1] // 4, full.shape[2] // 2
        start = pp * rows
        if half is not None:
            rows = rows // 2
            start = start + half * rows
        return full.at[zz, pl.ds(pl.multiple_of(start, 16), rows), lanes(c * cols, cols)]

    def send(m, ref, recv, target):
        remote(ref, ref, t.snd.at[m], recv, target).start()

    loads = [
        pltpu.make_async_copy(src, dst, t.ld.at[k])
        for k, (src, dst) in enumerate(
            (
                (t.tok_h, t.tok),
                (t.small_h, t.small.at[z]),
                (t.rel_h, t.rel.at[z]),
                (t.basis_h, t.basis),
                (t.cot_h, t.cot),
                (t.lim_h, t.lim),
                (t.flip_h, t.flip),
            )
        )
    ]
    for d in (1, 3, 2):
        for k, (src, dst) in enumerate(((t.small_h, t.small), (t.rel_h, t.rel))):
            remote(src, dst.at[z], t.ms.at[k], t.mr.at[k], depth[d - 1]).start()
    for copy in loads:
        copy.start()
    for m, (shard, part, full) in enumerate(plan):
        rows, cols = full.shape[1] // 4, full.shape[2] // 2
        piece = shard.at[
            pl.ds(pl.multiple_of(p * rows, 16), rows),
            lanes(part * full.shape[2] + c * cols, cols),
        ]
        for d in (1, 3, 2):
            remote(piece, block(m, z, p), t.snd.at[m], t.zr.at[m, d - 1], depth[d - 1]).start()
    own = []
    for m, (shard, part, full) in enumerate(plan):
        copy = pltpu.make_async_copy(
            shard.at[:, lanes(part * full.shape[2], full.shape[2])], full.at[z], t.own.at[m]
        )
        copy.start()
        own.append(copy)

    def source(d):
        return lax.rem(z + NARROW - d, NARROW)

    def spread(m, d):
        mine = block(m, source(d), p)
        arrive(mine, t.zr.at[m, d - 1])
        send(m, mine, t.xr.at[m, d - 1], at.xn)
        send(m, mine, t.yr.at[m, d - 1], at.yn)
        send(m, mine, t.sr.at[m], at.sib)

    def forward(m, d):
        zz = source(d)
        arrive(block(m, zz, at.px), t.xr.at[m, d - 1])
        send(m, block(m, zz, at.px, 0), t.fxr.at[m, d - 1], at.yn)
        send(m, block(m, zz, at.px), t.sr.at[m], at.sib)
        arrive(block(m, zz, at.py), t.yr.at[m, d - 1])
        send(m, block(m, zz, at.py, 1), t.fyr.at[m, d - 1], at.xn)
        send(m, block(m, zz, at.py), t.sr.at[m], at.sib)

    def finish(m, d):
        zz = source(d)
        arrive(block(m, zz, at.pd, 0), t.fxr.at[m, d - 1])
        arrive(block(m, zz, at.pd, 1), t.fyr.at[m, d - 1])
        send(m, block(m, zz, at.pd), t.sr.at[m], at.sib)

    units = [(m, d) for m in range(len(plan)) for d in (1, 3, 2)]
    events = []
    for u in range(len(units) + 2):
        if u < len(units):
            events.append((spread, units[u]))
        if 0 <= u - 1 < len(units):
            events.append((forward, units[u - 1]))
        if 0 <= u - 2 < len(units):
            events.append((finish, units[u - 2]))
    progress = [0]

    def pump(count):
        for _ in range(count):
            if progress[0] < len(events):
                step, unit = events[progress[0]]
                step(*unit)
                progress[0] += 1

    def complete(m):
        goal = events.index((finish, units[3 * m + 2])) + 1
        pump(goal - progress[0])
        full = plan[m][2]
        arrive(full.at[pl.ds(0, 3), :, pl.ds(0, full.shape[2] // 2)], t.sr.at[m])
        own[m].wait()

    places = ((0, 384), (384, 384), (768, 384), (1152, 384), (1536, 384), (1920, 384), (2304, 768), (3072, 128), (3200, 128))

    def vectors():
        loads[1].wait()
        loads[2].wait()
        for k, full in enumerate((t.small, t.rel)):
            arrive(full.at[pl.ds(0, 3)], t.mr.at[k])
        for r, (start, size) in enumerate(places):
            for zz in range(NARROW):
                t.vec[r : r + 1, zz * size : (zz + 1) * size] = wide(
                    t.small[zz, 0:8, start : start + size]
                )[0:1]

    def norm_rows(src, dst, gain_row):
        def one(i, _):
            rows = pl.ds(pl.multiple_of(i * 32, 32), 32)
            v = wide(src[rows, :])
            center = v - jnp.mean(v, axis=1, keepdims=True)
            var = jnp.mean(center * center, axis=1, keepdims=True)
            gain = t.vec[gain_row : gain_row + 1, 0:width]
            shift = t.vec[gain_row + 1 : gain_row + 2, 0:width]
            dst[rows, :] = low(center * lax.rsqrt(var + EPSILON) * gain + shift)
            return 0

        lax.fori_loop(0, rows_all // 32, one, 0)

    def flat(full):
        return full[...].reshape(full.shape[0] * full.shape[1], full.shape[2])

    def columns(full, start, size):
        part = full[:, :, lanes(start, size)]
        return part.reshape(full.shape[0] * full.shape[1], size)

    def make_queries():
        queries = dot_nn(t.normed[...], flat(t.q)) * (KEY ** (-0.5))
        size = H * KEY
        t.cq[...] = low(queries + t.vec[7:8, 0:size])
        t.pq[...] = low(queries + t.vec[8:9, 0:size])

    def make_keys():
        t.kr[...] = low(dot_nn(t.normed[...], flat(t.k)))
        loads[3].wait()
        table = t.rel[...].reshape(t.rel.shape[0] * t.rel.shape[1], t.rel.shape[2])
        t.rk[...] = low(dot_nn(t.basis[...], table))
        loads[6].wait()
        t.rr[...] = low(dot_nn(t.flip[...], table))

    def make_values():
        def one(n, _):
            t.vr[:, lanes(n * 512, 512)] = low(dot_nn(t.normed[...], columns(t.v, n * 512, 512)))
            return 0

        lax.fori_loop(0, 3, one, 0)

    def pair_mask(size, split):
        return lax.broadcasted_iota(jnp.int32, (rows_all, size), 1) < split

    def heads(pair):
        qs = slice(pair * 2 * KEY, (pair + 1) * 2 * KEY)
        vs = slice(pair * 2 * VAL, (pair + 1) * 2 * VAL)
        first = pair_mask(2 * KEY, KEY)
        keys, rel, vals = t.kr[:, qs], t.rk[:, qs], t.vr[:, vs]
        mixed = []
        for side in range(2):
            keep = first if side == 0 else jnp.logical_not(first)
            cq = jnp.where(keep, t.cq[:, qs], jnp.zeros_like(t.cq[:, qs]))
            pq = jnp.where(keep, t.pq[:, qs], jnp.zeros_like(t.pq[:, qs]))
            raw = dot_nt(pq, rel)
            shifted = pltpu.roll(raw, rows_all + 1, axis=1, stride=1, stride_axis=0)
            logits = dot_nt(cq, keys) + shifted[:, :rows_all]
            grown = jnp.exp(logits - jnp.max(logits, axis=1, keepdims=True))
            soft = low(grown / jnp.sum(grown, axis=1, keepdims=True))
            t.p[2 * pair + side] = soft
            mixed.append(dot_nn(soft, vals))
        t.mixed[0, :, vs] = low(jnp.where(pair_mask(2 * VAL, VAL), mixed[0], mixed[1]))

    def give(k, src, dst):
        remote(src, dst, t.ps.at[k], t.pr.at[k], at.sib).start()

    stored = []

    def store(src, dst):
        copy = pltpu.make_async_copy(src, dst, t.st.at[len(stored)])
        copy.start()
        stored.append(copy)

    def attend_out():
        def one(n, _):
            cols = lanes(n * 512, 512)
            t.hidden[:, cols] = (
                wide(t.tok[:, cols])
                + dot_nn(t.mixed[0], columns(t.o, n * 512, 512))
                + t.vec[2:3, cols]
            )
            return 0

        lax.fori_loop(0, 3, one, 0)
        norm_rows(t.hidden, t.nmid.at[0], 3)
        give(2, t.nmid.at[0], t.nmid.at[1])

    def clip_rows():
        loads[4].wait()
        loads[5].wait()

        def one(i, total):
            rows = pl.ds(pl.multiple_of(i * 32, 32), 32)
            clipped = low(clip(i * 32, wide(t.cot[rows, :])))
            t.od[rows, :] = clipped
            return total + jnp.sum(wide(clipped), axis=0, keepdims=True)

        total = lax.fori_loop(0, rows_all // 32, one, jnp.zeros((1, width), jnp.float32))
        t.sums[5:6, 0:width] = total
        half = width // 2
        t.odc[0] = t.od[:, lanes(c * half, half)]
        give(0, t.od.at[:, lanes((1 - c) * half, half)], t.odc.at[1])

    def clip(row, values):
        limit = jnp.where(row < WIN, t.lim[0:1, 0:1], t.lim[0:1, 1:2])
        return jnp.minimum(jnp.maximum(values, -limit), limit)

    def pull_active(h):
        full = (t.u0, t.u1)[h]
        half = width // 2
        delta = t.od[:, h * half : (h + 1) * half]

        def one(zz, _):
            cols = lanes(zz * 768, 768)
            part = dot_nt(delta, full[zz])
            if h == 0:
                t.ad[:, cols] = part
            else:
                t.ad[:, cols] = t.ad[:, cols] + part
            return 0

        lax.fori_loop(0, NARROW, one, 0)

    def inner(h):
        full = (t.i0, t.i1)[h]

        def one(n, _):
            local = n * 256
            cols = lanes(h * width + local, 256)
            pre = dot_nn(t.nmid[0], columns(full, local, 256)) + t.vec[6:7, cols]
            cdf = 0.5 + 0.5 * lax.erf(pre * (0.5**0.5))
            slope = cdf + pre * jnp.exp(-0.5 * pre * pre) * (2.0 * math.pi) ** -0.5
            t.act[0, :, cols] = low(pre * cdf)
            delta = low(t.ad[:, cols] * slope)
            t.idl[h, :, lanes(local, 256)] = delta
            t.sums[6:7, cols] = jnp.sum(wide(delta), axis=0, keepdims=True)
            return 0

        lax.fori_loop(0, 6, one, 0)
        cols = pl.ds(h * width, width)
        give(3 + h, t.act.at[0, :, cols], t.act.at[1, :, cols])

    def finish_out():
        def one(n, _):
            cols = lanes(n * 256, 256)
            for h, full in enumerate((t.u0, t.u1)):
                spot = lanes(h * 768 + n * 256, 256)
                t.lo[:, spot] = low(
                    t.hidden[:, spot]
                    + dot_nn(t.act[0], columns(full, n * 256, 256))
                    + t.vec[5:6, spot]
                )
            return 0

        lax.fori_loop(0, 3, one, 0)
        store(t.lo, t.out_h)

    def pull_mid():
        for zz in range(NARROW):
            t.hd[:, zz * 384 : (zz + 1) * 384] = dot_nt(t.idl[0], t.i0[zz]) + dot_nt(
                t.idl[1], t.i1[zz]
            )

        def one(i, carry):
            gain_total, shift_total, bias_total = carry
            rows = pl.ds(pl.multiple_of(i * 32, 32), 32)
            v = t.hidden[rows, :]
            center = v - jnp.mean(v, axis=1, keepdims=True)
            scale = lax.rsqrt(jnp.mean(center * center, axis=1, keepdims=True) + EPSILON)
            n = center * scale
            delta = t.hd[rows, :]
            e = delta * t.vec[3:4, 0:width]
            back = scale * (
                e
                - jnp.mean(e, axis=1, keepdims=True)
                - n * jnp.mean(e * n, axis=1, keepdims=True)
            )
            full = clip(i * 32, wide(t.cot[rows, :])) + back
            t.hd[rows, :] = full
            rounded = low(full)
            t.bd[rows, :] = rounded
            return (
                gain_total + jnp.sum(delta * n, axis=0, keepdims=True),
                shift_total + jnp.sum(delta, axis=0, keepdims=True),
                bias_total + jnp.sum(wide(rounded), axis=0, keepdims=True),
            )

        zero = jnp.zeros((1, width), jnp.float32)
        gain_total, shift_total, bias_total = lax.fori_loop(
            0, rows_all // 32, one, (zero, zero, zero)
        )
        t.sums[3:4, 0:width] = gain_total
        t.sums[4:5, 0:width] = shift_total
        t.sums[2:3, 0:width] = bias_total
        half = width // 2
        give(6, t.bd.at[:, lanes((1 - c) * half, half)], t.bdc.at[1])
        t.bdc[0] = t.bd[:, lanes(c * half, half)]
        store(t.hd, t.hd_h)

    def pull_mixed():
        for zz in range(NARROW):
            t.md[:, zz * 384 : (zz + 1) * 384] = low(dot_nt(t.bd[...], t.o[zz]))
        store(t.md, t.md_h)

    def outer_product(left_ref, right_ref, dst, start, size):
        steps = left_ref.shape[2] // 256
        right = right_ref[:, :, start : start + size].reshape(2 * rows_all, size)

        def tile(slot, n):
            return pltpu.make_async_copy(
                t.gst.at[slot, :, 0:size],
                dst.at[pl.ds(pl.multiple_of(n * 256, 256), 256)],
                t.gs.at[slot],
            )

        def one(n, _):
            slot = lax.rem(n, 2)

            @pl.when(n >= 2)
            def _():
                tile(slot, n - 2).wait()

            lhs = left_ref[:, :, lanes(n * 256, 256)].reshape(2 * rows_all, 256)
            t.gst[slot, :, 0:size] = low(dot_tn(lhs, right))
            tile(slot, n).start()
            return 0

        lax.fori_loop(0, steps, one, 0)
        tile(0, steps - 2).wait()
        tile(1, steps - 1).wait()

    t.sums[...] = jnp.zeros_like(t.sums)
    t.vec[...] = jnp.zeros_like(t.vec)
    loads[0].wait()
    vectors()
    pump(1)
    norm_rows(t.tok, t.normed, 0)
    give(1, t.normed, t.nn_h.at[1])
    store(t.normed, t.nn_h.at[0])
    pump(1)
    clip_rows()
    complete(0)
    make_queries()
    store(t.q, t.fq)
    store(t.cq, t.cq_h)
    store(t.pq, t.pq_h)
    complete(1)
    make_keys()
    store(t.k, t.fk)
    store(t.kr, t.k_h)
    store(t.rr, t.rr_h)
    complete(2)
    make_values()
    store(t.v, t.fv)
    store(t.vr, t.v_h)
    store(t.vec, t.vec_h)
    for pair in range(4):
        heads(pair)
        pump(2)
    store(t.p, t.p_h)
    give(5, t.mixed.at[0], t.mixed.at[1])
    complete(3)
    attend_out()
    complete(4)
    pull_active(0)
    complete(5)
    pull_active(1)
    complete(6)
    inner(0)
    complete(7)
    inner(1)
    give(7, t.idl.at[1 - c], t.idc.at[1])
    t.idc[0] = t.idl[c]
    finish_out()
    pull_mid()
    pull_mixed()
    arrive(t.odc.at[1], t.pr.at[0])
    for h in range(2):
        arrive(t.act.at[1, :, pl.ds(0, width)], t.pr.at[3 + h])
    outer_product(t.act, t.odc, t.gu0, 0, 384)
    outer_product(t.act, t.odc, t.gu1, 384, 384)
    arrive(t.nmid.at[1], t.pr.at[2])
    arrive(t.idc.at[1], t.pr.at[7])
    outer_product(t.nmid, t.idc, t.gi0, 0, 768)
    outer_product(t.nmid, t.idc, t.gi1, 768, 768)
    arrive(t.mixed.at[1], t.pr.at[5])
    arrive(t.bdc.at[1], t.pr.at[6])
    outer_product(t.mixed, t.bdc, t.go, 0, 768)
    store(t.sums, t.sums_h)

    arrive(t.nn_h.at[1], t.pr.at[1])
    left(t.odc.at[1], t.ps.at[0])
    left(t.normed, t.ps.at[1])
    left(t.nmid.at[0], t.ps.at[2])
    for h in range(2):
        left(t.act.at[0, :, pl.ds(0, width)], t.ps.at[3 + h])
    left(t.mixed.at[0], t.ps.at[5])
    left(t.bdc.at[1], t.ps.at[6])
    left(t.idc.at[1], t.ps.at[7])
    for k, full in enumerate((t.small, t.rel)):
        left(full.at[pl.ds(0, 3)], t.ms.at[k])
    for m, (_, _, full) in enumerate(plan):
        left(full.at[pl.ds(0, 3)], t.snd.at[m])
    for copy in stored:
        copy.wait()


def forward_pass(tokens, cotangent, limits, shards, rel, small, basis, flip):
    rows, width = tokens.shape
    bf, f32 = jnp.bfloat16, jnp.float32
    keys = H * KEY
    out_shape = (
        ((rows, width), bf),
        ((H, rows, rows), bf),
        ((rows, keys), bf),
        ((rows, keys), bf),
        ((rows, keys), bf),
        ((rows, width), bf),
        ((2 * rows, keys), bf),
        ((rows, width), bf),
        ((rows, width), f32),
        ((2, rows, width), bf),
        ((NARROW, width // 4, keys), bf),
        ((NARROW, width // 4, keys), bf),
        ((NARROW, width // 4, width), bf),
        ((16, 2 * width), f32),
        ((2 * width, width // 4), bf),
        ((2 * width, width // 4), bf),
        ((width, width // 2), bf),
        ((width, width // 2), bf),
        ((width, width // 2), bf),
        ((8, 2 * width), f32),
    )
    quarter = width // 4
    vmem = (
        ((NARROW, quarter, keys), bf),
        ((NARROW, quarter, keys), bf),
        ((NARROW, quarter, width), bf),
        ((NARROW, quarter, width), bf),
        ((NARROW, 2 * quarter, width // 2), bf),
        ((NARROW, 2 * quarter, width // 2), bf),
        ((NARROW, quarter, width), bf),
        ((NARROW, quarter, width), bf),
        ((NARROW,) + rel.shape, bf),
        ((NARROW,) + small.shape, bf),
        ((16, 2 * width), f32),
        ((rows, width), bf),
        ((rows, width), bf),
        ((rows, keys), bf),
        ((rows, keys), bf),
        ((rows, keys), bf),
        ((rows, width), bf),
        (basis.shape, bf),
        (flip.shape, bf),
        ((2 * rows, keys), bf),
        ((2 * rows, keys), bf),
        ((H, rows, rows), bf),
        ((2, rows, width), bf),
        ((rows, width), f32),
        ((2, rows, width), bf),
        ((rows, width), bf),
        ((rows, width), bf),
        ((2, rows, width // 2), bf),
        ((rows, 2 * width), f32),
        ((2, rows, 2 * width), bf),
        ((2, rows, width), bf),
        ((2, rows, width), bf),
        ((rows, width), f32),
        ((rows, width), bf),
        ((2, rows, width // 2), bf),
        ((rows, width), bf),
        ((rows, width), bf),
        ((2, rows, width // 2), bf),
        ((8, 2 * width), f32),
        ((8, 128), f32),
    )
    sems = [
        DMA((8, 3)),
        DMA((8, 3)),
        DMA((8, 3)),
        DMA((8, 3)),
        DMA((8, 3)),
        DMA((8,)),
        DMA((8,)),
        DMA((8,)),
        DMA((7,)),
        DMA((2,)),
        DMA((2,)),
        DMA((8,)),
        DMA((8,)),
        DMA((20,)),
        DMA((2,)),
    ]
    ins = (tokens, cotangent, limits, *shards, rel, small, basis, flip)
    return pl.pallas_call(
        forward_kernel,
        out_shape=tuple(jax.ShapeDtypeStruct(s, d) for s, d in out_shape),
        in_specs=[HBM] * len(ins),
        out_specs=(HBM,) * len(out_shape),
        scratch_shapes=[pltpu.VMEM(s, d) for s, d in vmem] + sems,
        compiler_params=pltpu.CompilerParams(
            collective_id=1, has_side_effects=True, vmem_limit_bytes=60 << 20
        ),
        name="forward_pass",
    )(*ins)


UNITS = 8


def backward_refs(
    gu0,
    gu1,
    gi0,
    gi1,
    go,
    p_h,
    cq_h,
    pq_h,
    k_h,
    v_h,
    rr_h,
    md_h,
    hd_h,
    tok_h,
    nn_h,
    fq_h,
    fk_h,
    fv_h,
    vec_h,
    sums_h,
    flipt_h,
    turn_h,
    ou,
    oi,
    oo,
    ov,
    ok,
    oq,
    tg_h,
    e_h,
    rg_h,
    gv,
    gk,
    gq,
    p,
    cq,
    pq,
    kr,
    vr,
    rr,
    md,
    hd,
    tok,
    nn,
    fq,
    fk,
    fv,
    vec,
    sums,
    flipt,
    turn,
    qd,
    kd,
    vd,
    qdc,
    kdc,
    vdc,
    nd,
    tg,
    rg,
    rgk,
    rgg,
    rgs,
    rgo,
    eb,
    ek,
    eg,
    es,
    eo,
    ld,
    s1,
    r1,
    l1,
    s2,
    r2,
    s3,
    r3,
    s4,
    r4,
    lo,
    ps,
    pr,
    xs,
    xr,
    ws,
    wr,
    st,
):
    return types.SimpleNamespace(**locals())


def backward_kernel(*refs):
    head = 31
    t = backward_refs(*refs[:head], *refs[head + 5 * UNITS :])
    keep, got1, got2, got3, last = (
        refs[head + k * UNITS : head + (k + 1) * UNITS] for k in range(5)
    )
    at = position()
    w, z, c, p, x, y = at.w, at.z, at.c, at.p, at.x, at.y
    depth = [(w, lax.rem(z + d, NARROW)) for d in range(1, NARROW)]
    rows_all, width = t.tok.shape
    meet([at.sib, at.xn, at.yn] + depth)

    plan = (
        (t.gu0, False, t.ou, 0, width // 2),
        (t.gu1, False, t.ou, width // 4, width // 2),
        (t.gi0, False, t.oi, 0, width),
        (t.gi1, False, t.oi, width // 2, width),
        (t.go, False, t.oo, 0, width // 2),
        (t.gv, True, t.ov, 0, width // 2),
        (t.gk, True, t.ok, 0, H * KEY // 2),
        (t.gq, True, t.oq, 0, H * KEY // 2),
    )

    def half(m, h, mine):
        g = plan[m][0]
        if h == 0:
            return g.at[:, :, x if mine else 1 - x, 0]
        return g.at[:, y if mine else 1 - y, :, 1]

    def stage1(m):
        for h, target in ((0, at.xn), (1, at.yn)):
            remote(half(m, h, False), got1[m].at[h], t.s1.at[m, h], t.r1.at[m, h], target).start()
            if not plan[m][1]:
                pltpu.make_async_copy(half(m, h, True), keep[m].at[h], t.l1.at[m, h]).start()

    def stage2(m):
        for h, target, mine in ((0, at.yn, y), (1, at.xn, x)):
            arrive(got1[m].at[h], t.r1.at[m, h])
            if not plan[m][1]:
                arrive(keep[m].at[h], t.l1.at[m, h])

            def add(k, _, h=h):
                zz, o = lax.div(k, 2), lax.rem(k, 2)
                if not plan[m][1]:
                    own = keep[m][h, zz, o]
                elif h == 0:
                    own = plan[m][0][zz, o, x, 0]
                else:
                    own = plan[m][0][zz, y, o, 1]
                keep[m][h, zz, o] = low(wide(own) + wide(got1[m][h, zz, o]))
                return 0

            lax.fori_loop(0, 2 * NARROW, add, 0)
            remote(
                keep[m].at[h, :, 1 - mine], got2[m].at[h], t.s2.at[m, h], t.r2.at[m, h], target
            ).start()

    def stage3(m):
        for h, mine in ((0, y), (1, x)):
            arrive(got2[m].at[h], t.r2.at[m, h])

            def add(zz, _, h=h, mine=mine):
                got2[m][h, zz] = low(wide(keep[m][h, zz, mine]) + wide(got2[m][h, zz]))
                return 0

            lax.fori_loop(0, NARROW, add, 0)
        for d in (1, 3, 2):
            zz = lax.rem(z + d, NARROW)
            remote(
                got2[m].at[:, zz],
                got3[m].at[d - 1],
                t.s3.at[m, d - 1],
                t.r3.at[m, d - 1],
                depth[d - 1],
            ).start()

    def piece(m, pp, part=None):
        _, _, out, start, span = plan[m]
        rows, cols = out.shape[0] // 4, last[m].shape[1]
        first = pp * rows
        if part is not None:
            rows = rows // 2
            first = first + part * rows
        return out.at[pl.ds(pl.multiple_of(first, 16), rows), lanes(c * span + start, cols)]

    def stage4(m):
        for d in (1, 3, 2):
            arrive(got3[m].at[d - 1], t.r3.at[m, d - 1])
        rows = last[m].shape[0] // 2
        for h in range(2):
            total = wide(got2[m][h, z])
            for d in range(3):
                total = total + wide(got3[m][d, h])
            last[m][h * rows : (h + 1) * rows, :] = low(total)
        mine = piece(m, p)
        remote(last[m], mine, t.s4.at[m], t.r4.at[m, 0], at.xn).start()
        remote(last[m], mine, t.s4.at[m], t.r4.at[m, 1], at.yn).start()
        remote(last[m], mine, t.s4.at[m], t.r4.at[m, 4], at.sib).start()
        pltpu.make_async_copy(last[m], mine, t.lo.at[m]).start()

    def stage5(m):
        for pp, part, slot, target in ((at.px, 0, 0, at.yn), (at.py, 1, 1, at.xn)):
            arrive(piece(m, pp), t.r4.at[m, slot])
            some = piece(m, pp, part)
            remote(some, some, t.s4.at[m], t.r4.at[m, 2 + slot], target).start()
            some = piece(m, pp)
            remote(some, some, t.s4.at[m], t.r4.at[m, 4], at.sib).start()

    def stage6(m):
        arrive(piece(m, at.pd, 0), t.r4.at[m, 2])
        arrive(piece(m, at.pd, 1), t.r4.at[m, 3])
        some = piece(m, at.pd)
        remote(some, some, t.s4.at[m], t.r4.at[m, 4], at.sib).start()

    sources = (
        (t.p_h, t.p),
        (t.v_h, t.vr),
        (t.md_h, t.md),
        (t.k_h, t.kr),
        (t.cq_h, t.cq),
        (t.pq_h, t.pq),
        (t.rr_h, t.rr),
        (t.turn_h, t.turn),
        (t.flipt_h, t.flipt),
        (t.nn_h, t.nn),
        (t.fv_h, t.fv),
        (t.fk_h, t.fk),
        (t.fq_h, t.fq),
        (t.tok_h, t.tok),
        (t.hd_h, t.hd),
        (t.vec_h, t.vec),
        (t.sums_h, t.sums),
    )
    stage1(0)
    stage1(1)
    loads = [pltpu.make_async_copy(s, d, t.ld.at[k]) for k, (s, d) in enumerate(sources)]
    for copy in loads:
        copy.start()

    def lane_mask(size, split, rows=rows_all):
        return lax.broadcasted_iota(jnp.int32, (rows, size), 1) < split

    def heads(pair):
        qs = slice(pair * 2 * KEY, (pair + 1) * 2 * KEY)
        vs = slice(pair * 2 * VAL, (pair + 1) * 2 * VAL)
        vals, mixed = t.vr[:, vs], t.md[:, vs]
        keys, rel, cq, pq = t.kr[:, qs], t.rr[:, qs], t.cq[:, qs], t.pq[:, qs]
        first = lane_mask(2 * VAL, VAL)
        parts = []
        for side in range(2):
            mask = first if side == 0 else jnp.logical_not(first)
            soft = t.p[2 * pair + side]
            pull = dot_nt(jnp.where(mask, mixed, jnp.zeros_like(mixed)), vals)
            full = wide(soft)
            delta = low(full * (pull - jnp.sum(full * pull, axis=1, keepdims=True)))
            turned = dot_nn(delta, t.turn[...])
            padded = jnp.concatenate([turned, jnp.zeros_like(turned)], axis=1)
            slid = low(pltpu.roll(padded, 2 * rows_all, axis=1, stride=1, stride_axis=0))
            parts.append(
                (
                    dot_tn(soft, mixed),
                    dot_nn(delta, keys),
                    dot_tn(delta, cq),
                    dot_nn(slid, rel),
                    dot_tn(slid, pq),
                )
            )
        t.vd[:, vs] = low(jnp.where(first, parts[0][0], parts[1][0]))
        narrow = lane_mask(2 * KEY, KEY)
        content = jnp.where(narrow, parts[0][1], parts[1][1])
        place = jnp.where(narrow, parts[0][3], parts[1][3])
        t.kd[:, qs] = low(jnp.where(narrow, parts[0][2], parts[1][2]))
        rel_delta = low(
            jnp.where(lane_mask(2 * KEY, KEY, 2 * rows_all), parts[0][4], parts[1][4])
        )
        t.qd[:, qs] = low(content + place) * jnp.asarray(KEY ** (-0.5), jnp.bfloat16)
        t.rg[:, qs] = dot_nn(t.flipt[...], rel_delta)
        t.sums[7:8, qs] = jnp.sum(content, axis=0, keepdims=True)
        keys_all = H * KEY
        there = slice(keys_all + pair * 2 * KEY, keys_all + (pair + 1) * 2 * KEY)
        t.sums[7:8, there] = jnp.sum(place, axis=0, keepdims=True)

    def trade():
        for k, (full, pair) in enumerate(((t.vd, t.vdc), (t.kd, t.kdc), (t.qd, t.qdc))):
            cols = full.shape[1] // 2
            away = full.at[:, lanes((1 - c) * cols, cols)]
            remote(away, pair.at[1], t.ps.at[k], t.pr.at[k], at.sib).start()
            pair[0] = full[:, lanes(c * cols, cols)]
        cols = t.rg.shape[1] // 2
        t.rgo[...] = low(t.rg[:, lanes((1 - c) * cols, cols)]).reshape(t.rgo.shape)
        remote(t.rgo, t.rgg.at[0], t.xs.at[0], t.xr.at[0], at.sib).start()
        t.rgk[0] = low(t.rg[:, lanes(c * cols, cols)]).reshape(t.rgo.shape)

    def outer_product(pair, dst):
        def one(zz, _):
            lhs = t.nn[:, :, lanes(zz * 384, 384)].reshape(2 * rows_all, 384)
            rhs = pair[...].reshape(2 * rows_all, pair.shape[2])
            dst[zz] = low(dot_tn(lhs, rhs)).reshape(dst.shape[1:])
            return 0

        lax.fori_loop(0, NARROW, one, 0)

    def pull_tokens():
        for zz in range(NARROW):
            t.nd[:, zz * 384 : (zz + 1) * 384] = (
                dot_nt(t.qd[...], t.fq[zz])
                + dot_nt(t.kd[...], t.fk[zz])
                + dot_nt(t.vd[...], t.fv[zz])
            )

        def one(i, carry):
            gain_total, shift_total = carry
            rows = pl.ds(pl.multiple_of(i * 32, 32), 32)
            v = wide(t.tok[rows, :])
            center = v - jnp.mean(v, axis=1, keepdims=True)
            scale = lax.rsqrt(jnp.mean(center * center, axis=1, keepdims=True) + EPSILON)
            n = center * scale
            delta = t.nd[rows, :]
            e = delta * t.vec[0:1, 0:width]
            back = scale * (
                e
                - jnp.mean(e, axis=1, keepdims=True)
                - n * jnp.mean(e * n, axis=1, keepdims=True)
            )
            t.tg[rows, :] = low(t.hd[rows, :] + back)
            return (
                gain_total + jnp.sum(delta * n, axis=0, keepdims=True),
                shift_total + jnp.sum(delta, axis=0, keepdims=True),
            )

        zero = jnp.zeros((1, width), jnp.float32)
        gain_total, shift_total = lax.fori_loop(0, rows_all // 32, one, (zero, zero))
        t.sums[0:1, 0:width] = gain_total
        t.sums[1:2, 0:width] = shift_total
        for zz in range(NARROW):
            t.eb[zz] = jnp.zeros(t.eb.shape[1:], jnp.float32)
            t.eb[zz, 0:6, 0:384] = t.sums[0:6, zz * 384 : (zz + 1) * 384]
            t.eb[zz, 6:7, :] = t.sums[6:7, zz * 768 : (zz + 1) * 768]
            t.eb[zz, 7:8, 0:128] = t.sums[7:8, zz * 128 : (zz + 1) * 128]
            t.eb[zz, 7:8, 128:256] = t.sums[7:8, 512 + zz * 128 : 512 + (zz + 1) * 128]

    def sum_steps(keep, got, over, out, sends, recvs):
        def begin():
            remote(keep.at[0], got.at[0], sends.at[0], recvs.at[0], at.sib).start()

        def step(k):
            arrive(got.at[k], recvs.at[k])
            total = wide(keep[k]) + wide(got[k])
            keep[k + 1] = total.astype(keep.dtype)
            if k < 2:
                target = (at.xn, at.yn)[k]
                remote(
                    keep.at[k + 1], got.at[k + 1], sends.at[k + 1], recvs.at[k + 1], target
                ).start()
            else:
                for d in (1, 3, 2):
                    zz = lax.rem(z + d, NARROW)
                    remote(
                        keep.at[3, zz],
                        over.at[d - 1],
                        sends.at[2 + d],
                        recvs.at[2 + d],
                        depth[d - 1],
                    ).start()

        def end():
            total = wide(keep[3, z])
            for d in (1, 3, 2):
                arrive(over.at[d - 1], recvs.at[2 + d])
                total = total + wide(over[d - 1])
            out[...] = total

        return begin, step, end

    rel_sums = sum_steps(t.rgk, t.rgg, t.rgs, t.rg.at[0:48, 0:256], t.xs, t.xr)
    row_sums = sum_steps(t.ek, t.eg, t.es, t.eo, t.ws, t.wr)

    stored = []

    def store(src, dst):
        copy = pltpu.make_async_copy(src, dst, t.st.at[len(stored)])
        copy.start()
        stored.append(copy)

    for copy in loads[:9]:
        copy.wait()
    loads[16].wait()
    heads(0)
    heads(1)
    stage2(0)
    stage1(2)
    heads(2)
    heads(3)
    trade()
    stage2(1)
    stage1(3)
    stage3(0)
    loads[9].wait()
    for k, (pair, dst) in enumerate(((t.vdc, t.gv), (t.kdc, t.gk), (t.qdc, t.gq))):
        arrive(pair.at[1], t.pr.at[k])
        outer_product(pair, dst)
    rel_sums[1](0)
    for copy in loads[10:16]:
        copy.wait()
    stage2(2)
    stage1(4)
    stage3(1)
    stage4(0)
    pull_tokens()
    store(t.tg, t.tg_h)
    t.ek[0] = t.eb[...]
    row_sums[0]()
    for u in range(3, UNITS + 5):
        if u < UNITS:
            stage2(u)
            if u + 2 < UNITS:
                stage1(u + 2)
        if u - 3 < 3:
            if u - 3 < 2:
                rel_sums[1](u - 2)
            else:
                rel_sums[2]()
            row_sums[1](u - 3)
        if u == 6:
            row_sums[2]()
            store(t.eo, t.e_h)
            store(t.rg.at[0:48, 0:256], t.rg_h.at[c])
            remote(t.rg.at[0:48, 0:256], t.rg_h.at[c], t.xs.at[6], t.xr.at[6], at.sib).start()
        if u - 1 < UNITS:
            stage3(u - 1)
        if u - 2 < UNITS:
            stage4(u - 2)
        if 0 <= u - 3 < UNITS:
            stage5(u - 3)
        if 0 <= u - 4 < UNITS:
            stage6(u - 4)

    for m in range(UNITS):
        _, _, out, _, _ = plan[m]
        cols = last[m].shape[1]
        arrive(out.at[:, pl.ds(0, cols)], t.r4.at[m, 4])
        arrive(last[m], t.lo.at[m])
        for h in range(2):
            left(got1[m].at[h], t.s1.at[m, h])
            left(got2[m].at[h], t.s2.at[m, h])
        for d in range(3):
            left(got3[m].at[d], t.s3.at[m, d])
        left(out.at[:, pl.ds(0, cols)], t.s4.at[m])
        left(out.at[pl.ds(0, 3 * (out.shape[0] // 4)), pl.ds(0, cols)], t.s4.at[m])
    for k, pair in enumerate((t.vdc, t.kdc, t.qdc)):
        left(pair.at[1], t.ps.at[k])
    for got, over, sends in ((t.rgg, t.rgs, t.xs), (t.eg, t.es, t.ws)):
        for k in range(3):
            left(got.at[k], sends.at[k])
            left(over.at[k], sends.at[3 + k])
    left(t.rg.at[0:48, 0:256], t.xs.at[6])
    arrive(t.rg_h.at[1 - c], t.xr.at[6])
    for copy in stored:
        copy.wait()


def backward_pass(grads, saved, tables):
    bf, f32 = jnp.bfloat16, jnp.float32
    tokens = saved[8]
    rows, width = tokens.shape
    keys = H * KEY
    views = [g.reshape(4, 2, 2, 2, g.shape[0] // 32, g.shape[1]) for g in grads]
    shapes = [(g.shape[0], g.shape[1]) for g in grads] + [
        (width, width // 2),
        (width, keys // 2),
        (width, keys // 2),
    ]
    out_shape = (
        ((width // 2, width), bf),
        ((width // 4, 2 * width), bf),
        ((width // 4, width), bf),
        ((width // 4, width), bf),
        ((width // 4, keys), bf),
        ((width // 4, keys), bf),
        ((rows, width), bf),
        ((8, 768), f32),
        ((2, 48, 256), f32),
    )
    vmem = []
    for lead in ((2, 4, 2), (2, 4, 2), (2, 4), (3, 2)):
        vmem += [(lead + (r // 32, n), bf) for r, n in shapes]
    vmem += [((r // 16, n), bf) for r, n in shapes]
    vmem += [((4, 2, 2, 2, r // 32, n), bf) for r, n in shapes[5:]]
    vmem += [(s.shape, s.dtype) for s in saved[:9]]
    vmem += [(s.shape, s.dtype) for s in saved[9:]]
    vmem += [(s.shape, s.dtype) for s in tables]
    vmem += [
        ((rows, keys), bf),
        ((rows, keys), bf),
        ((rows, width), bf),
        ((2, rows, keys // 2), bf),
        ((2, rows, keys // 2), bf),
        ((2, rows, width // 2), bf),
        ((rows, width), f32),
        ((rows, width), bf),
        ((F, keys), f32),
        ((4, 4, 48, 256), bf),
        ((3, 4, 48, 256), bf),
        ((3, 48, 256), bf),
        ((4, 48, 256), bf),
        ((4, 8, 768), f32),
        ((4, 4, 8, 768), f32),
        ((3, 4, 8, 768), f32),
        ((3, 8, 768), f32),
        ((8, 768), f32),
    ]
    sems = [
        DMA((17,)),
        DMA((UNITS, 2)),
        DMA((UNITS, 2)),
        DMA((UNITS, 2)),
        DMA((UNITS, 2)),
        DMA((UNITS, 2)),
        DMA((UNITS, 3)),
        DMA((UNITS, 3)),
        DMA((UNITS,)),
        DMA((UNITS, 5)),
        DMA((UNITS,)),
        DMA((3,)),
        DMA((3,)),
        DMA((7,)),
        DMA((7,)),
        DMA((6,)),
        DMA((6,)),
        DMA((3,)),
    ]
    ins = (*views, *saved, *tables)
    return pl.pallas_call(
        backward_kernel,
        out_shape=tuple(jax.ShapeDtypeStruct(s, d) for s, d in out_shape),
        in_specs=[HBM] * len(ins),
        out_specs=(HBM,) * len(out_shape),
        scratch_shapes=[pltpu.VMEM(s, d) for s, d in vmem] + sems,
        compiler_params=pltpu.CompilerParams(
            collective_id=2, has_side_effects=True, vmem_limit_bytes=60 << 20
        ),
        name="backward_pass",
    )(*ins)


def per_device_linked(
    tokens,
    cotangent,
    thresholds,
    attn_norm_gain,
    attn_norm_shift,
    query_weight,
    key_weight,
    value_weight,
    relative_weight,
    content_bias,
    position_bias,
    out_weight,
    out_bias,
    mlp_norm_gain,
    mlp_norm_shift,
    inner_weight,
    inner_bias,
    outer_weight,
    outer_bias,
):
    _, length, width = tokens.shape
    bf = jnp.bfloat16
    vectors = (
        attn_norm_gain,
        attn_norm_shift,
        out_bias,
        mlp_norm_gain,
        mlp_norm_shift,
        outer_bias,
        inner_bias,
        content_bias,
        position_bias,
    )
    small = jnp.broadcast_to(jnp.concatenate(vectors)[None, :], (8, 3328))
    limits = jnp.pad(thresholds, ((0, 7), (0, 126)))
    table = basis_table(length, F)
    empty = jnp.zeros((1, F), jnp.float32)
    basis = jnp.concatenate([table, empty]).astype(bf)
    flip = jnp.concatenate([table[::-1], empty]).astype(bf)
    turn = jnp.eye(length, dtype=bf)[::-1]
    flat_tokens = tokens.reshape(length, width)
    (
        layer_out,
        p,
        cq,
        pq,
        k,
        v,
        rr,
        md,
        hd,
        nn,
        fq,
        fk,
        fv,
        vec,
        gu0,
        gu1,
        gi0,
        gi1,
        go,
        sums,
    ) = forward_pass(
        flat_tokens,
        cotangent.reshape(length, width),
        limits,
        (query_weight, key_weight, value_weight, out_weight, outer_weight, inner_weight),
        relative_weight,
        small,
        basis,
        flip,
    )
    ou, oi, oo, ov, ok, oq, tokens_grad, rows, rel = backward_pass(
        (gu0, gu1, gi0, gi1, go),
        (p, cq, pq, k, v, rr, md, hd, flat_tokens, nn, fq, fk, fv, vec, sums),
        (flip.T, turn),
    )
    f32 = jnp.float32
    return (
        layer_out[None],
        tokens_grad[None],
        rows[0, :384],
        rows[1, :384],
        oq.astype(f32),
        ok.astype(f32),
        ov.astype(f32),
        jnp.concatenate([rel[0], rel[1]], axis=1),
        rows[7, :128],
        rows[7, 128:256],
        oo.astype(f32),
        rows[2, :384],
        rows[3, :384],
        rows[4, :384],
        oi.astype(f32),
        rows[6],
        ou.astype(f32),
        rows[5, :384],
    )


def solution(mesh):
    body = per_device_generic
    if mesh.shape[WIDE] == 8 and mesh.shape[DEPTH] == 4:
        body = per_device_linked
    in_specs = (
        P((WIDE, DEPTH), None, None),
        P((WIDE, DEPTH), None, None),
        P((WIDE, DEPTH), None),
        P(DEPTH),
        P(DEPTH),
        P(DEPTH, None),
        P(DEPTH, None),
        P(DEPTH, None),
        P(DEPTH, None),
        P(DEPTH),
        P(DEPTH),
        P(DEPTH, None),
        P(DEPTH),
        P(DEPTH),
        P(DEPTH),
        P(DEPTH, None),
        P(DEPTH),
        P(DEPTH, None),
        P(DEPTH),
    )
    out_specs = (
        P((WIDE, DEPTH), None, None),
        P((WIDE, DEPTH), None, None),
        P(DEPTH),
        P(DEPTH),
        P(DEPTH, None),
        P(DEPTH, None),
        P(DEPTH, None),
        P(DEPTH, None),
        P(DEPTH),
        P(DEPTH),
        P(DEPTH, None),
        P(DEPTH),
        P(DEPTH),
        P(DEPTH),
        P(DEPTH, None),
        P(DEPTH),
        P(DEPTH, None),
        P(DEPTH),
    )
    return jax.shard_map(
        body, mesh=mesh, in_specs=in_specs, out_specs=out_specs, check_vma=False
    )
```

```python
import functools
import math
import types

import jax
import jax.numpy as jnp
import numpy as np
from jax import lax
from jax.experimental import pallas as pl
from jax.experimental.pallas import tpu as pltpu
from jax.sharding import PartitionSpec as P

H = 8
KEY = 64
VAL = 192
F = 192
WIN = 128


EPSILON = 1e-05


def basis_table(length, features):
    family = features // 6
    offsets = jnp.arange(2 * length - 1, dtype=jnp.float32) - (length - 1)
    distance = jnp.abs(offsets)[:, None]
    halves = 2.0 ** jnp.linspace(3.0, math.log2(length), family, dtype=jnp.float32)
    decays = jnp.exp(-math.log(2.0) / halves[None, :] * distance)
    widths = 2.0 ** jnp.arange(1, family + 1, dtype=jnp.float32) - 1.0
    central = jnp.where(widths[None, :] > distance, 1.0, 0.0).astype(jnp.float32)
    centers = jnp.linspace(0.0, float(length), family, dtype=jnp.float32)
    spread = length / family
    bump_rows = jnp.exp(-0.5 * ((distance - centers[None, :]) / spread) ** 2)
    positive = jnp.concatenate([decays, central, bump_rows], axis=1)
    return jnp.concatenate([positive, jnp.sign(offsets)[:, None] * positive], axis=1)


def shift_offsets(raw_scores, length):
    leading = raw_scores.shape[:-2]
    padded = jnp.pad(raw_scores, [(0, 0)] * len(leading) + [(0, 0), (0, 1)])
    flatten = padded.reshape(leading + (2 * length * length,))
    window = flatten[..., length - 1 : length - 1 + length * (2 * length - 1)]
    return window.reshape(leading + (length, 2 * length - 1))[..., :length]


def unshift_offsets(grad_scores, length):
    leading = grad_scores.shape[:-2]
    widened = jnp.pad(grad_scores, [(0, 0)] * len(leading) + [(0, 0), (0, length - 1)])
    flatten = widened.reshape(leading + (length * (2 * length - 1),))
    flatten = jnp.pad(flatten, [(0, 0)] * len(leading) + [(length - 1, 1)])
    return flatten.reshape(leading + (length, 2 * length))[..., : 2 * length - 1]


def layer_norm(values, gain, shift):
    center = values - jnp.mean(values, axis=-1, keepdims=True)
    spread = jnp.mean(center * center, axis=-1, keepdims=True)
    return center * lax.rsqrt(spread + EPSILON) * gain + shift


def gelu_exact(values):
    return jax.nn.gelu(values, approximate=False)


def column_sums(values):
    return jnp.sum(values.astype(jnp.float32), axis=0)


WIDE = "wide"
DEPTH = "narrow"


def spread_rows(shard):
    return lax.all_gather(shard, DEPTH, axis=0, tiled=True)


def sum_columns(part):
    low = part.astype(jnp.bfloat16)
    return lax.psum_scatter(low, WIDE, scatter_dimension=1, tiled=True).astype(jnp.float32)


def sum_rows(part):
    low = part.astype(jnp.bfloat16)
    return lax.psum_scatter(low, DEPTH, scatter_dimension=0, tiled=True).astype(jnp.float32)


def spread_columns(part):
    low = part.astype(jnp.bfloat16)
    return lax.all_gather(low, WIDE, axis=1, tiled=True).astype(jnp.float32)


def per_device_generic(
    tokens,
    cotangent,
    thresholds,
    attn_norm_gain,
    attn_norm_shift,
    query_weight,
    key_weight,
    value_weight,
    relative_weight,
    content_bias,
    position_bias,
    out_weight,
    out_bias,
    mlp_norm_gain,
    mlp_norm_shift,
    inner_weight,
    inner_bias,
    outer_weight,
    outer_bias,
):
    seq_count, length, model_width = tokens.shape
    row_count = seq_count * length
    span = 2 * length - 1
    query_scale = KEY ** (-0.5)
    (
        attn_gain,
        attn_shift,
        query_full,
        key_full,
        value_full,
        relative_full,
        content_full,
        position_full,
        exit_full,
        exit_bias,
    ) = (
        spread_rows(attn_norm_gain),
        spread_rows(attn_norm_shift),
        spread_rows(query_weight),
        spread_rows(key_weight),
        spread_rows(value_weight),
        spread_rows(relative_weight),
        spread_rows(content_bias),
        spread_rows(position_bias),
        spread_rows(out_weight),
        spread_rows(out_bias),
    )
    mlp_gain, mlp_shift, inner_full, inner_offset, outer_full, outer_offset = (
        spread_rows(mlp_norm_gain),
        spread_rows(mlp_norm_shift),
        spread_rows(inner_weight),
        spread_rows(inner_bias),
        spread_rows(outer_weight),
        spread_rows(outer_bias),
    )
    flat_tokens = tokens.reshape(row_count, model_width).astype(jnp.float32)
    attn_gain_f = attn_gain.astype(jnp.float32)
    attn_shift_f = attn_shift.astype(jnp.float32)
    normed = layer_norm(flat_tokens, attn_gain_f, attn_shift_f).astype(jnp.bfloat16)
    queries = jnp.dot(normed, query_full, preferred_element_type=jnp.float32) * query_scale
    content_query = (
        (queries + content_full.astype(jnp.float32))
        .astype(jnp.bfloat16)
        .reshape(seq_count, length, H, KEY)
    )
    position_query = (
        (queries + position_full.astype(jnp.float32))
        .astype(jnp.bfloat16)
        .reshape(seq_count, length, H, KEY)
    )
    key_rows = (
        jnp.dot(normed, key_full, preferred_element_type=jnp.float32)
        .astype(jnp.bfloat16)
        .reshape(seq_count, length, H, KEY)
    )
    value_rows = (
        jnp.dot(normed, value_full, preferred_element_type=jnp.float32)
        .astype(jnp.bfloat16)
        .reshape(seq_count, length, H, VAL)
    )
    basis = basis_table(length, F).astype(jnp.bfloat16)
    rel_keys = (
        jnp.dot(basis, relative_full, preferred_element_type=jnp.float32)
        .astype(jnp.bfloat16)
        .reshape(span, H, KEY)
    )

    def attention_logits():
        content = jnp.einsum(
            "bihe,bjhe->bhij", content_query, key_rows, preferred_element_type=jnp.float32
        )
        raw_scores = jnp.einsum(
            "bihe,the->bhit", position_query, rel_keys, preferred_element_type=jnp.float32
        )
        return content + shift_offsets(raw_scores, length)

    logits = attention_logits()
    row_peak = jnp.max(logits, axis=-1, keepdims=True)
    log_total = row_peak + jnp.log(jnp.sum(jnp.exp(logits - row_peak), axis=-1, keepdims=True))
    attention = jnp.exp(logits - log_total).astype(jnp.bfloat16)
    mixed_heads = jnp.einsum(
        "bhij,bjhd->bihd", attention, value_rows, preferred_element_type=jnp.float32
    )
    mixed_heads = mixed_heads.astype(jnp.bfloat16).reshape(row_count, H * VAL)
    hidden = flat_tokens + (
        jnp.dot(mixed_heads, exit_full, preferred_element_type=jnp.float32)
        + exit_bias.astype(jnp.float32)
    )
    mlp_gain_f = mlp_gain.astype(jnp.float32)
    mlp_shift_f = mlp_shift.astype(jnp.float32)
    normed_mid = layer_norm(hidden, mlp_gain_f, mlp_shift_f).astype(jnp.bfloat16)
    inner_pre = jnp.dot(
        normed_mid, inner_full, preferred_element_type=jnp.float32
    ) + inner_offset.astype(jnp.float32)
    active, gelu_pull = jax.vjp(gelu_exact, inner_pre)
    active_low = active.astype(jnp.bfloat16)
    result = hidden + (
        jnp.dot(active_low, outer_full, preferred_element_type=jnp.float32)
        + outer_offset.astype(jnp.float32)
    )
    layer_out = result.astype(jnp.bfloat16).reshape(seq_count, length, model_width)
    clip_limit = jnp.repeat(thresholds, WIN, axis=1).reshape(row_count, 1)
    clipped = jnp.clip(
        cotangent.reshape(row_count, model_width).astype(jnp.float32), -clip_limit, clip_limit
    )
    mlp_gain, mlp_shift, inner_full, inner_offset, outer_full, outer_offset = (
        spread_rows(mlp_norm_gain),
        spread_rows(mlp_norm_shift),
        spread_rows(inner_weight),
        spread_rows(inner_bias),
        spread_rows(outer_weight),
        spread_rows(outer_bias),
    )
    mlp_gain_f = mlp_gain.astype(jnp.float32)
    outer_delta = clipped.astype(jnp.bfloat16)
    outer_bias_grad = column_sums(outer_delta)
    outer_weight_grad = jnp.einsum(
        "nk,nm->km", active_low, outer_delta, preferred_element_type=jnp.float32
    )
    active_delta = jnp.einsum(
        "nm,km->nk", outer_delta, outer_full, preferred_element_type=jnp.float32
    )
    (inner_grad_pre,) = gelu_pull(active_delta)
    inner_delta = inner_grad_pre.astype(jnp.bfloat16)
    inner_bias_grad = column_sums(inner_delta)
    inner_weight_grad = jnp.einsum(
        "nd,nf->df", normed_mid, inner_delta, preferred_element_type=jnp.float32
    )
    mid_delta = jnp.einsum("nf,df->nd", inner_delta, inner_full, preferred_element_type=jnp.float32)
    norm_out, norm_pull = jax.vjp(layer_norm, hidden, mlp_gain_f, mlp_shift_f)
    hidden_part, mlp_gain_grad, mlp_shift_grad = norm_pull(mid_delta)
    hidden_delta = clipped + hidden_part
    (
        attn_gain,
        attn_shift,
        query_full,
        key_full,
        value_full,
        relative_full,
        content_full,
        position_full,
        exit_full,
        exit_bias,
    ) = (
        spread_rows(attn_norm_gain),
        spread_rows(attn_norm_shift),
        spread_rows(query_weight),
        spread_rows(key_weight),
        spread_rows(value_weight),
        spread_rows(relative_weight),
        spread_rows(content_bias),
        spread_rows(position_bias),
        spread_rows(out_weight),
        spread_rows(out_bias),
    )
    attn_gain_f = attn_gain.astype(jnp.float32)
    branch_delta = hidden_delta.astype(jnp.bfloat16)
    out_bias_grad = column_sums(branch_delta)
    out_weight_grad = jnp.einsum(
        "nk,nd->kd", mixed_heads, branch_delta, preferred_element_type=jnp.float32
    )
    mixed_delta = jnp.einsum(
        "nd,kd->nk", branch_delta, exit_full, preferred_element_type=jnp.float32
    )
    mixed_delta = mixed_delta.astype(jnp.bfloat16).reshape(seq_count, length, H, VAL)
    logits = attention_logits()
    soft_rows = jnp.exp(logits - log_total)
    attention = soft_rows.astype(jnp.bfloat16)
    attention_delta = jnp.einsum(
        "bihd,bjhd->bhij", mixed_delta, value_rows, preferred_element_type=jnp.float32
    )
    value_delta = jnp.einsum(
        "bhij,bihd->bjhd", attention, mixed_delta, preferred_element_type=jnp.float32
    )
    value_delta = value_delta.astype(jnp.bfloat16).reshape(row_count, H * VAL)
    logit_delta = soft_rows * (
        attention_delta - jnp.sum(soft_rows * attention_delta, axis=-1, keepdims=True)
    )
    logit_delta = logit_delta.astype(jnp.bfloat16)
    content_delta = jnp.einsum(
        "bhij,bjhe->bihe", logit_delta, key_rows, preferred_element_type=jnp.float32
    )
    key_delta = jnp.einsum(
        "bhij,bihe->bjhe", logit_delta, content_query, preferred_element_type=jnp.float32
    )
    key_delta = key_delta.astype(jnp.bfloat16).reshape(row_count, H * KEY)
    offset_delta = unshift_offsets(logit_delta, length)
    position_delta = jnp.einsum(
        "bhit,the->bihe", offset_delta, rel_keys, preferred_element_type=jnp.float32
    )
    rel_delta = jnp.einsum(
        "bhit,bihe->the", offset_delta, position_query, preferred_element_type=jnp.float32
    )
    rel_delta = rel_delta.astype(jnp.bfloat16).reshape(span, H * KEY)
    relative_weight_grad = jnp.einsum(
        "tf,tk->fk", basis, rel_delta, preferred_element_type=jnp.float32
    )
    content_delta = content_delta.reshape(row_count, H * KEY)
    position_delta = position_delta.reshape(row_count, H * KEY)
    content_bias_grad = jnp.sum(content_delta, axis=0)
    position_bias_grad = jnp.sum(position_delta, axis=0)
    query_delta = (content_delta + position_delta).astype(jnp.bfloat16) * jnp.asarray(
        query_scale, jnp.bfloat16
    )
    query_weight_grad = jnp.einsum(
        "nd,nk->dk", normed, query_delta, preferred_element_type=jnp.float32
    )
    key_weight_grad = jnp.einsum("nd,nk->dk", normed, key_delta, preferred_element_type=jnp.float32)
    value_weight_grad = jnp.einsum(
        "nd,nk->dk", normed, value_delta, preferred_element_type=jnp.float32
    )
    normed_delta = (
        jnp.einsum("nk,dk->nd", query_delta, query_full, preferred_element_type=jnp.float32)
        + jnp.einsum("nk,dk->nd", key_delta, key_full, preferred_element_type=jnp.float32)
        + jnp.einsum("nk,dk->nd", value_delta, value_full, preferred_element_type=jnp.float32)
    )
    first_out, first_pull = jax.vjp(layer_norm, flat_tokens, attn_gain_f, attn_shift_f)
    tokens_part, attn_gain_grad, attn_shift_grad = first_pull(normed_delta)
    tokens_grad = (
        (hidden_delta + tokens_part).astype(jnp.bfloat16).reshape(seq_count, length, model_width)
    )
    (
        query_weight_grad,
        key_weight_grad,
        value_weight_grad,
        relative_weight_grad,
        out_weight_grad,
        inner_weight_grad,
        outer_weight_grad,
    ) = (
        sum_columns(query_weight_grad),
        sum_columns(key_weight_grad),
        sum_columns(value_weight_grad),
        sum_columns(relative_weight_grad),
        sum_columns(out_weight_grad),
        sum_columns(inner_weight_grad),
        sum_columns(outer_weight_grad),
    )
    (
        query_weight_grad,
        key_weight_grad,
        value_weight_grad,
        relative_weight_grad,
        out_weight_grad,
        inner_weight_grad,
        outer_weight_grad,
        attn_gain_grad,
        attn_shift_grad,
        content_bias_grad,
        position_bias_grad,
        out_bias_grad,
        mlp_gain_grad,
        mlp_shift_grad,
        inner_bias_grad,
        outer_bias_grad,
    ) = (
        sum_rows(query_weight_grad),
        sum_rows(key_weight_grad),
        sum_rows(value_weight_grad),
        sum_rows(relative_weight_grad),
        sum_rows(out_weight_grad),
        sum_rows(inner_weight_grad),
        sum_rows(outer_weight_grad),
        sum_rows(attn_gain_grad),
        sum_rows(attn_shift_grad),
        sum_rows(content_bias_grad),
        sum_rows(position_bias_grad),
        sum_rows(out_bias_grad),
        sum_rows(mlp_gain_grad),
        sum_rows(mlp_shift_grad),
        sum_rows(inner_bias_grad),
        sum_rows(outer_bias_grad),
    )
    (
        query_weight_grad,
        key_weight_grad,
        value_weight_grad,
        relative_weight_grad,
        out_weight_grad,
        inner_weight_grad,
        outer_weight_grad,
    ) = (
        spread_columns(query_weight_grad),
        spread_columns(key_weight_grad),
        spread_columns(value_weight_grad),
        spread_columns(relative_weight_grad),
        spread_columns(out_weight_grad),
        spread_columns(inner_weight_grad),
        spread_columns(outer_weight_grad),
    )
    (
        attn_gain_grad,
        attn_shift_grad,
        content_bias_grad,
        position_bias_grad,
        out_bias_grad,
        mlp_gain_grad,
        mlp_shift_grad,
        inner_bias_grad,
        outer_bias_grad,
    ) = lax.psum(
        (
            attn_gain_grad,
            attn_shift_grad,
            content_bias_grad,
            position_bias_grad,
            out_bias_grad,
            mlp_gain_grad,
            mlp_shift_grad,
            inner_bias_grad,
            outer_bias_grad,
        ),
        WIDE,
    )
    return (
        layer_out,
        tokens_grad,
        attn_gain_grad,
        attn_shift_grad,
        query_weight_grad,
        key_weight_grad,
        value_weight_grad,
        relative_weight_grad,
        content_bias_grad,
        position_bias_grad,
        out_weight_grad,
        out_bias_grad,
        mlp_gain_grad,
        mlp_shift_grad,
        inner_weight_grad,
        inner_bias_grad,
        outer_weight_grad,
        outer_bias_grad,
    )


MESH = pl.DeviceIdType.MESH
NARROW = 4


def position():
    w = lax.axis_index(WIDE)
    z = lax.axis_index(DEPTH)
    c = lax.rem(w, 2)
    p = lax.div(w, 2)
    x = lax.rem(p, 2)
    y = lax.div(p, 2)
    chip = (lambda q: q * 2 + c)
    return types.SimpleNamespace(
        w=w,
        z=z,
        c=c,
        p=p,
        x=x,
        y=y,
        px=p + 1 - 2 * x,
        py=p + 2 - 4 * y,
        pd=3 - p,
        sib=(w + 1 - 2 * c, z),
        xn=(chip(p + 1 - 2 * x), z),
        yn=(chip(p + 2 - 4 * y), z),
    )


def meet(partners):
    barrier = pltpu.get_barrier_semaphore()
    for partner in partners:
        pl.semaphore_signal(barrier, inc=1, device_id=partner, device_id_type=MESH)
    pl.semaphore_wait(barrier, len(partners))


def remote(src, dst, send, recv, target):
    return pltpu.make_async_remote_copy(
        src_ref=src,
        dst_ref=dst,
        send_sem=send,
        recv_sem=recv,
        device_id=target,
        device_id_type=MESH,
    )


HBM = pl.BlockSpec(memory_space=pltpu.HBM)
DMA = pltpu.SemaphoreType.DMA
SMEM = pl.BlockSpec(memory_space=pltpu.SMEM)


def dot_nn(a, b):
    return jnp.dot(a, b, preferred_element_type=jnp.float32)


def dot_nt(a, b):
    return lax.dot_general(a, b, (((1,), (1,)), ((), ())), preferred_element_type=jnp.float32)


def dot_tn(a, b):
    return lax.dot_general(a, b, (((0,), (0,)), ((), ())), preferred_element_type=jnp.float32)


def low(v):
    return v.astype(jnp.bfloat16)


def wide(v):
    return v.astype(jnp.float32)


def lanes(start, size):
    return pl.ds(pl.multiple_of(start, 128), size)


def arrive(ref, sem):
    me = (lax.axis_index(WIDE), lax.axis_index(DEPTH))
    remote(ref, ref, sem, sem, me).wait_recv()


def left(ref, sem):
    me = (lax.axis_index(WIDE), lax.axis_index(DEPTH))
    remote(ref, ref, sem, sem, me).wait_send()


def forward_refs(
    tok_h,
    cot_h,
    lim_h,
    wq,
    wk,
    wv,
    wo,
    wi,
    wu,
    rel_h,
    small_h,
    basis_h,
    flip_h,
    p_h,
    cq_h,
    pq_h,
    k_h,
    v_h,
    rr_h,
    hid_h,
    act_h,
    slope_h,
    od_h,
    nn_h,
    nm_h,
    mx_h,
    fq,
    fk,
    fv,
    fo,
    fi0,
    fi1,
    fu0,
    fu1,
    vec_h,
    gu0,
    gu1,
    sums_h,
    q,
    k,
    v,
    o,
    i0,
    i1,
    rel,
    small,
    vec,
    tok,
    normed,
    cq,
    pq,
    kr,
    vr,
    basis,
    flip,
    rk,
    rr,
    p,
    mixed,
    hidden,
    nmid,
    cot,
    od,
    odc,
    act,
    slope,
    gst,
    sums,
    zr,
    zs,
    xr,
    yr,
    fxr,
    fyr,
    sr,
    snd,
    own,
    ld,
    mr,
    ms,
    ps,
    pr,
    st,
    gs,
):
    return types.SimpleNamespace(**locals())


def forward_kernel(*refs):
    t = forward_refs(*refs)
    at = position()
    w, z, c, p = at.w, at.z, at.c, at.p
    depth = [(w, lax.rem(z + d, NARROW)) for d in range(1, NARROW)]
    meet([at.sib, at.xn, at.yn] + depth)
    rows_all = t.tok.shape[0]
    width = t.tok.shape[1]

    keys_all = H * KEY
    quarter = width // 4
    plan = (
        (t.wq, 0, 0, t.fq, keys_all),
        (t.wk, 0, 0, t.fk, keys_all),
        (t.wv, 0, 0, t.fv, width),
        (t.wo, 0, 0, t.fo, width),
        (t.wi, 0, 0, t.fi0, width),
        (t.wi, 0, width, t.fi1, width),
        (t.wu, 0, 0, t.fu0, width),
        (t.wu, quarter, 0, t.fu1, width),
    )

    def rows_of(m, pp, part=None):
        rows = quarter // 4
        start = pp * rows
        if part is not None:
            rows = rows // 2
            start = start + part * rows
        return start, rows

    def block(m, zz, pp, part=None):
        start, rows = rows_of(m, pp, part)
        cols = plan[m][4] // 2
        return plan[m][3].at[zz, pl.ds(pl.multiple_of(start, 16), rows), lanes(c * cols, cols)]

    def send(m, ref, recv, target):
        remote(ref, ref, t.snd.at[m], recv, target).start()

    loads = [
        pltpu.make_async_copy(src, dst, t.ld.at[k])
        for k, (src, dst) in enumerate(
            (
                (t.tok_h, t.tok),
                (t.small_h, t.small.at[z]),
                (t.rel_h, t.rel.at[z]),
                (t.basis_h, t.basis),
                (t.cot_h, t.cot),
                (t.flip_h, t.flip),
            )
        )
    ]
    def over_z(k, src, dst):
        for d in (1, 3, 2):
            remote(src, dst.at[z], t.ms.at[k], t.mr.at[k], depth[d - 1]).start()

    over_z(0, t.small_h, t.small)
    for copy in loads:
        copy.start()

    above, below = (w, jnp.minimum(z + 1, NARROW - 1)), (w, jnp.maximum(z - 1, 0))
    can_rise, can_sink = z < NARROW - 1, z > 0

    def own_piece(m):
        shard, r0, c0, _, span = plan[m]
        start, rows = rows_of(m, p)
        cols = span // 2
        return shard.at[pl.ds(pl.multiple_of(r0 + start, 16), rows), lanes(c0 + c * cols, cols)]

    def depart(m):
        @pl.when(can_rise)
        def _():
            remote(
                own_piece(m), block(m, z, p), t.zs.at[m, 3], t.zr.at[m, 0], above
            ).start()

        @pl.when(can_sink)
        def _():
            remote(
                own_piece(m), block(m, z, p), t.zs.at[m, 4], t.zr.at[m, 2], below
            ).start()

    def hop(k):
        first, last = z == 0, z == NARROW - 1
        if k == 0:
            return jnp.where(first, 3, 1)
        if k == 1:
            return jnp.where(first | last, 2, 3)
        return jnp.where(first, 1, jnp.where(last, 3, 2))

    def source(k):
        return lax.rem(z + NARROW - hop(k), NARROW)

    def relay(m, k):
        d = hop(k)
        mine = block(m, source(k), p)
        rise = can_rise & (d <= z)
        sink = can_sink & (d > z)
        return mine, d, rise, sink

    def spread(m, k):
        mine, d, rise, sink = relay(m, k)
        arrive(mine, t.zr.at[m, d - 1])

        @pl.when(rise)
        def _():
            remote(mine, mine, t.zs.at[m, k], t.zr.at[m, jnp.minimum(d, 2)], above).start()

        @pl.when(sink)
        def _():
            remote(mine, mine, t.zs.at[m, k], t.zr.at[m, jnp.maximum(d - 2, 0)], below).start()

        send(m, mine, t.xr.at[m, k], at.xn)
        send(m, mine, t.yr.at[m, k], at.yn)
        send(m, mine, t.sr.at[m], at.sib)
        if k == 2 and m + 3 < len(plan):
            depart(m + 3)

    def forward(m, k):
        zz = source(k)
        arrive(block(m, zz, at.px), t.xr.at[m, k])
        send(m, block(m, zz, at.px, 0), t.fxr.at[m, k], at.yn)
        send(m, block(m, zz, at.px), t.sr.at[m], at.sib)
        arrive(block(m, zz, at.py), t.yr.at[m, k])
        send(m, block(m, zz, at.py, 1), t.fyr.at[m, k], at.xn)
        send(m, block(m, zz, at.py), t.sr.at[m], at.sib)

    def finish(m, k):
        zz = source(k)
        arrive(block(m, zz, at.pd, 0), t.fxr.at[m, k])
        arrive(block(m, zz, at.pd, 1), t.fyr.at[m, k])
        send(m, block(m, zz, at.pd), t.sr.at[m], at.sib)

    for m in range(3):
        depart(m)
    over_z(1, t.rel_h, t.rel)
    units = [(m, k) for m in range(len(plan)) for k in range(3)]
    steps = ((spread, 0), (forward, 2), (finish, 4))
    events = []
    for u in range(len(units) + 4):
        for step, lag in steps:
            if 0 <= u - lag < len(units):
                events.append((step, units[u - lag]))
    progress = [0]

    def pump(count):
        for _ in range(count):
            if progress[0] < len(events):
                step, unit = events[progress[0]]
                step(*unit)
                progress[0] += 1

    def complete(m):
        goal = events.index((finish, (m, 2))) + 1
        pump(goal - progress[0])
        arrive(plan[m][3].at[pl.ds(0, 3), :, pl.ds(0, plan[m][4] // 2)], t.sr.at[m])

    def fetch(m, held):
        shard, r0, c0, full, span = plan[m]
        copies = [
            pltpu.make_async_copy(
                shard.at[pl.ds(r0, quarter), pl.ds(c0, span)], held.at[z], t.own.at[m, 0]
            )
        ]
        for d in range(1, NARROW):
            zz = lax.rem(z + d, NARROW)
            copies.append(pltpu.make_async_copy(full.at[zz], held.at[zz], t.own.at[m, d]))
        for copy in copies:
            copy.start()
        return copies

    def use(copies):
        for copy in copies:
            copy.wait()

    def vectors():
        loads[1].wait()
        arrive(t.small.at[pl.ds(0, 3)], t.mr.at[0])
        for zz in range(NARROW):
            rows = wide(t.small[zz])
            for r in range(6):
                t.vec[r : r + 1, zz * 384 : (zz + 1) * 384] = rows[r : r + 1, 0:384]
            for r in range(2):
                spot = slice(zz * 768 + r * 384, zz * 768 + (r + 1) * 384)
                t.vec[6:7, spot] = rows[6 + r : 7 + r, 0:384]
                t.vec[7 + r : 8 + r, zz * 128 : (zz + 1) * 128] = rows[r : r + 1, 384:512]

    def norm_rows(src, dst, gain_row):
        def one(i, _):
            rows = pl.ds(pl.multiple_of(i * 32, 32), 32)
            v = wide(src[rows, :])
            center = v - jnp.mean(v, axis=1, keepdims=True)
            var = jnp.mean(center * center, axis=1, keepdims=True)
            gain = t.vec[gain_row : gain_row + 1, 0:width]
            shift = t.vec[gain_row + 1 : gain_row + 2, 0:width]
            dst[rows, :] = low(center * lax.rsqrt(var + EPSILON) * gain + shift)
            return 0

        lax.fori_loop(0, rows_all // 32, one, 0)

    def flat(full):
        return full[...].reshape(full.shape[0] * full.shape[1], full.shape[2])

    def columns(full, start, size):
        part = full[:, :, lanes(start, size)]
        return part.reshape(full.shape[0] * full.shape[1], size)

    def make_queries():
        queries = dot_nn(t.normed[...], flat(t.q)) * (KEY ** (-0.5))
        size = H * KEY
        t.cq[...] = low(queries + t.vec[7:8, 0:size])
        t.pq[...] = low(queries + t.vec[8:9, 0:size])

    def make_keys():
        t.kr[...] = low(dot_nn(t.normed[...], flat(t.k)))
        loads[2].wait()
        arrive(t.rel.at[pl.ds(0, 3)], t.mr.at[1])
        loads[3].wait()
        table = t.rel[...].reshape(t.rel.shape[0] * t.rel.shape[1], t.rel.shape[2])
        t.rk[...] = low(dot_nn(t.basis[...], table))
        loads[5].wait()
        t.rr[...] = low(dot_nn(t.flip[...], table))

    def make_values():
        def one(n, _):
            t.vr[:, lanes(n * 512, 512)] = low(dot_nn(t.normed[...], columns(t.v, n * 512, 512)))
            return 0

        lax.fori_loop(0, 3, one, 0)

    def pair_mask(size, split):
        return lax.broadcasted_iota(jnp.int32, (rows_all, size), 1) < split

    def heads(pair):
        qs = slice(pair * 2 * KEY, (pair + 1) * 2 * KEY)
        vs = slice(pair * 2 * VAL, (pair + 1) * 2 * VAL)
        first = pair_mask(2 * KEY, KEY)
        keys, rel, vals = t.kr[:, qs], t.rk[:, qs], t.vr[:, vs]
        mixed = []
        for side in range(2):
            keep = first if side == 0 else jnp.logical_not(first)
            cq = jnp.where(keep, t.cq[:, qs], jnp.zeros_like(t.cq[:, qs]))
            pq = jnp.where(keep, t.pq[:, qs], jnp.zeros_like(t.pq[:, qs]))
            raw = dot_nt(pq, rel)
            shifted = pltpu.roll(raw, rows_all + 1, axis=1, stride=1, stride_axis=0)
            logits = dot_nt(cq, keys) + shifted[:, :rows_all]
            grown = jnp.exp(logits - jnp.max(logits, axis=1, keepdims=True))
            soft = low(grown / jnp.sum(grown, axis=1, keepdims=True))
            t.p[2 * pair + side] = soft
            mixed.append(dot_nn(soft, vals))
        t.mixed[:, vs] = low(jnp.where(pair_mask(2 * VAL, VAL), mixed[0], mixed[1]))

    def give(k, src, dst):
        remote(src, dst, t.ps.at[k], t.pr.at[k], at.sib).start()

    stored = []

    def store(src, dst):
        copy = pltpu.make_async_copy(src, dst, t.st.at[len(stored)])
        copy.start()
        stored.append(copy)

    def attend_out():
        def one(n, _):
            cols = lanes(n * 512, 512)
            t.hidden[:, cols] = (
                wide(t.tok[:, cols])
                + dot_nn(t.mixed[...], columns(t.o, n * 512, 512))
                + t.vec[2:3, cols]
            )
            return 0

        lax.fori_loop(0, 3, one, 0)
        norm_rows(t.hidden, t.nmid, 3)
        give(2, t.nmid, t.nm_h.at[1])

    def clip_rows():
        loads[4].wait()

        def one(i, total):
            rows = pl.ds(pl.multiple_of(i * 32, 32), 32)
            clipped = low(clip(i * 32, wide(t.cot[rows, :])))
            t.od[rows, :] = clipped
            return total + jnp.sum(wide(clipped), axis=0, keepdims=True)

        total = lax.fori_loop(0, rows_all // 32, one, jnp.zeros((1, width), jnp.float32))
        t.sums[5:6, 0:width] = total
        half = width // 2
        t.odc[0] = t.od[:, lanes(c * half, half)]
        give(0, t.od.at[:, lanes((1 - c) * half, half)], t.odc.at[1])

    def clip(row, values):
        limit = jnp.where(row < WIN, t.lim_h[0, 0], t.lim_h[0, 1])
        return jnp.minimum(jnp.maximum(values, -limit), limit)

    def inner(h):
        full = (t.i0, t.i1)[h]

        def one(n, _):
            local = n * 256
            cols = lanes(h * width + local, 256)
            pre = dot_nn(t.nmid[...], columns(full, local, 256)) + t.vec[6:7, cols]
            cdf = 0.5 + 0.5 * lax.erf(pre * (0.5**0.5))
            slope = cdf + pre * jnp.exp(-0.5 * pre * pre) * (2.0 * math.pi) ** -0.5
            t.act[0, :, cols] = low(pre * cdf)
            t.slope[:, cols] = low(slope)
            return 0

        lax.fori_loop(0, 6, one, 0)
        cols = pl.ds(h * width, width)
        give(3 + h, t.act.at[0, :, cols], t.act.at[1, :, cols])

    def outer_product(left_ref, right_ref, dst, start, size):
        steps = left_ref.shape[2] // 256
        right = right_ref[:, :, start : start + size].reshape(2 * rows_all, size)

        def tile(slot, n):
            return pltpu.make_async_copy(
                t.gst.at[slot, :, 0:size],
                dst.at[pl.ds(pl.multiple_of(n * 256, 256), 256)],
                t.gs.at[slot],
            )

        def one(n, _):
            slot = lax.rem(n, 2)

            @pl.when(n >= 2)
            def _():
                tile(slot, n - 2).wait()

            lhs = left_ref[:, :, lanes(n * 256, 256)].reshape(2 * rows_all, 256)
            t.gst[slot, :, 0:size] = low(dot_tn(lhs, right))
            tile(slot, n).start()
            return 0

        lax.fori_loop(0, steps, one, 0)
        tile(0, steps - 2).wait()
        tile(1, steps - 1).wait()

    t.sums[...] = jnp.zeros_like(t.sums)
    t.vec[...] = jnp.zeros_like(t.vec)
    loads[0].wait()
    vectors()
    pump(1)
    norm_rows(t.tok, t.normed, 0)
    give(1, t.normed, t.nn_h.at[1])
    store(t.normed, t.nn_h.at[0])
    store(t.vec, t.vec_h)
    complete(0)
    queries_here = fetch(0, t.q)
    pump(2)
    clip_rows()
    store(t.od, t.od_h)
    use(queries_here)
    make_queries()
    store(t.cq, t.cq_h)
    store(t.pq, t.pq_h)
    complete(1)
    keys_here = fetch(1, t.k)
    pump(3)
    use(keys_here)
    make_keys()
    store(t.kr, t.k_h)
    store(t.rr, t.rr_h)
    complete(2)
    values_here = fetch(2, t.v)
    pump(2)
    use(values_here)
    make_values()
    store(t.vr, t.v_h)
    for pair in range(4):
        heads(pair)
        pump(2)
    store(t.p, t.p_h)
    give(5, t.mixed, t.mx_h.at[1])
    store(t.mixed, t.mx_h.at[0])
    complete(3)
    out_here = fetch(3, t.o)
    pump(2)
    use(out_here)
    attend_out()
    store(t.hidden, t.hid_h)
    store(t.nmid, t.nm_h.at[0])
    complete(4)
    inner_here = fetch(4, t.i0)
    pump(2)
    use(inner_here)
    inner(0)
    complete(5)
    inner_here = fetch(5, t.i1)
    pump(2)
    use(inner_here)
    inner(1)
    store(t.act.at[0], t.act_h)
    store(t.slope, t.slope_h)
    pump(2)
    arrive(t.odc.at[1], t.pr.at[0])
    for h in range(2):
        arrive(t.act.at[1, :, pl.ds(0, width)], t.pr.at[3 + h])
    outer_product(t.act, t.odc, t.gu0, 0, 384)
    pump(2)
    outer_product(t.act, t.odc, t.gu1, 384, 384)
    store(t.sums, t.sums_h)
    complete(6)
    complete(7)

    arrive(t.nn_h.at[1], t.pr.at[1])
    arrive(t.nm_h.at[1], t.pr.at[2])
    arrive(t.mx_h.at[1], t.pr.at[5])
    left(t.odc.at[1], t.ps.at[0])
    left(t.normed, t.ps.at[1])
    left(t.nmid, t.ps.at[2])
    for h in range(2):
        left(t.act.at[0, :, pl.ds(0, width)], t.ps.at[3 + h])
    left(t.mixed, t.ps.at[5])
    for k, full in enumerate((t.small, t.rel)):
        left(full.at[pl.ds(0, 3)], t.ms.at[k])
    for m in range(len(plan)):
        mine = block(m, z, p)
        for k in range(3):
            _, _, rise, sink = relay(m, k)

            @pl.when(rise | sink)
            def _():
                left(mine, t.zs.at[m, k])

        @pl.when(can_rise)
        def _():
            left(mine, t.zs.at[m, 3])

        @pl.when(can_sink)
        def _():
            left(mine, t.zs.at[m, 4])

        full, cols = plan[m][3], plan[m][4] // 2
        left(full.at[pl.ds(0, 3), :, pl.ds(0, cols)], t.snd.at[m])
        left(full.at[pl.ds(0, 3), pl.ds(0, 3 * quarter // 4), pl.ds(0, cols)], t.snd.at[m])
    for copy in stored:
        copy.wait()


def forward_pass(tokens, cotangent, limits, shards, rel, small, basis, flip):
    rows, width = tokens.shape
    bf, f32 = jnp.bfloat16, jnp.float32
    keys = H * KEY
    quarter = width // 4
    full = ((NARROW, quarter, width), bf)
    thin = ((NARROW, quarter, keys), bf)
    out_shape = (
        ((H, rows, rows), bf),
        ((rows, keys), bf),
        ((rows, keys), bf),
        ((rows, keys), bf),
        ((rows, width), bf),
        ((2 * rows, keys), bf),
        ((rows, width), f32),
        ((rows, 2 * width), bf),
        ((rows, 2 * width), bf),
        ((rows, width), bf),
        ((2, rows, width), bf),
        ((2, rows, width), bf),
        ((2, rows, width), bf),
        thin,
        thin,
        full,
        full,
        full,
        full,
        full,
        full,
        ((16, 2 * width), f32),
        ((2 * width, width // 4), bf),
        ((2 * width, width // 4), bf),
        ((8, 2 * width), f32),
    )
    vmem = (
        thin,
        thin,
        full,
        full,
        full,
        full,
        ((NARROW,) + rel.shape, bf),
        ((NARROW,) + small.shape, bf),
        ((16, 2 * width), f32),
        ((rows, width), bf),
        ((rows, width), bf),
        ((rows, keys), bf),
        ((rows, keys), bf),
        ((rows, keys), bf),
        ((rows, width), bf),
        (basis.shape, bf),
        (flip.shape, bf),
        ((2 * rows, keys), bf),
        ((2 * rows, keys), bf),
        ((H, rows, rows), bf),
        ((rows, width), bf),
        ((rows, width), f32),
        ((rows, width), bf),
        ((rows, width), bf),
        ((rows, width), bf),
        ((2, rows, width // 2), bf),
        ((2, rows, 2 * width), bf),
        ((rows, 2 * width), bf),
        ((2, rows, width // 2), bf),
        ((8, 2 * width), f32),
    )
    sems = [
        DMA((8, 3)),
        DMA((8, 5)),
        DMA((8, 3)),
        DMA((8, 3)),
        DMA((8, 3)),
        DMA((8, 3)),
        DMA((8,)),
        DMA((8,)),
        DMA((8, 4)),
        DMA((7,)),
        DMA((2,)),
        DMA((2,)),
        DMA((6,)),
        DMA((6,)),
        DMA((20,)),
        DMA((2,)),
    ]
    ins = (tokens, cotangent, limits, *shards, rel, small, basis, flip)
    return pl.pallas_call(
        forward_kernel,
        out_shape=tuple(jax.ShapeDtypeStruct(s, d) for s, d in out_shape),
        in_specs=[HBM, HBM, SMEM] + [HBM] * (len(ins) - 3),
        out_specs=(HBM,) * len(out_shape),
        scratch_shapes=[pltpu.VMEM(s, d) for s, d in vmem] + sems,
        compiler_params=pltpu.CompilerParams(
            collective_id=1, has_side_effects=True, vmem_limit_bytes=60 << 20
        ),
        name="forward_pass",
    )(*ins)


UNITS = 8
CHAINS = (0, 3)


def backward_refs(
    gu0,
    gu1,
    p_h,
    cq_h,
    pq_h,
    k_h,
    v_h,
    rr_h,
    hid_h,
    act_h,
    slope_h,
    od_h,
    nn_h,
    nm_h,
    mx_h,
    fq,
    fk,
    fv,
    fo,
    fi0,
    fi1,
    fu0,
    fu1,
    wq,
    wk,
    wv,
    wo,
    wi,
    wu,
    tok_h,
    cot_h,
    lim_h,
    vec_h,
    sums_h,
    flipt_h,
    turn_h,
    ou,
    oi,
    oo,
    ov,
    ok,
    oq,
    out_h,
    tg_h,
    e_h,
    rg_h,
    gi0,
    gi1,
    go,
    gv,
    gk,
    gq,
    s0,
    s1,
    p,
    cq,
    pq,
    kr,
    vr,
    rr,
    hid,
    act,
    slope,
    od,
    cat,
    idc,
    cot,
    vec,
    sums,
    flipt,
    turn,
    bdc,
    qdc,
    kdc,
    vdc,
    nd,
    rg,
    rgk,
    rgg,
    rgs,
    rgo,
    eb,
    ek,
    eg,
    es,
    eo,
    ld,
    own,
    s1s,
    r1,
    l1,
    s2,
    r2,
    s3,
    r3,
    s4,
    r4,
    lo,
    zu,
    zd,
    zs,
    ps,
    pr,
    xs,
    xr,
    ws,
    wr,
    st,
):
    return types.SimpleNamespace(**locals())


def backward_kernel(*refs):
    head = 46
    held = 2
    t = backward_refs(*refs[:head], *refs[head + held + 4 * UNITS :])
    spare = refs[head : head + held + 4 * UNITS]
    keep = spare[:held]
    got1, got2, got3, last = (
        spare[held + k * UNITS : held + (k + 1) * UNITS] for k in range(4)
    )
    at = position()
    w, z, c, p, x, y = at.w, at.z, at.c, at.p, at.x, at.y
    depth = [(w, lax.rem(z + d, NARROW)) for d in range(1, NARROW)]
    rows_all, width = t.cot.shape
    meet([at.sib, at.xn, at.yn] + depth)

    plan = (
        (t.gu0, False, t.ou, 0, width // 2),
        (t.gu1, False, t.ou, width // 4, width // 2),
        (t.gi0, True, t.oi, 0, width),
        (t.gi1, True, t.oi, width // 2, width),
        (t.go, True, t.oo, 0, width // 2),
        (t.gv, True, t.ov, 0, width // 2),
        (t.gk, True, t.ok, 0, H * KEY // 2),
        (t.gq, True, t.oq, 0, H * KEY // 2),
    )

    def half(m, h, mine):
        g = plan[m][0]
        if h == 0:
            return g.at[:, :, x if mine else 1 - x, 0]
        return g.at[:, y if mine else 1 - y, :, 1]

    def stage1(m):
        for h, target in ((0, at.xn), (1, at.yn)):
            remote(half(m, h, False), got1[m].at[h], t.s1s.at[m, h], t.r1.at[m, h], target).start()
            if not plan[m][1]:
                pltpu.make_async_copy(half(m, h, True), keep[m].at[h], t.l1.at[m, h]).start()

    def kept(m, h, zz, o):
        if not plan[m][1]:
            return keep[m].at[h, zz, o]
        if h == 0:
            return plan[m][0].at[zz, o, x, 0]
        return plan[m][0].at[zz, y, o, 1]

    def stage2(m):
        for h, target, mine in ((0, at.yn, y), (1, at.xn, x)):
            arrive(got1[m].at[h], t.r1.at[m, h])
            if not plan[m][1]:
                arrive(keep[m].at[h], t.l1.at[m, h])

            def add(k, _, h=h):
                zz, o = lax.div(k, 2), lax.rem(k, 2)
                spot = kept(m, h, zz, o)
                spot[...] = low(wide(spot[...]) + wide(got1[m][h, zz, o]))
                return 0

            lax.fori_loop(0, 2 * NARROW, add, 0)
            every = pl.ds(0, NARROW)
            remote(
                kept(m, h, every, 1 - mine), got2[m].at[h], t.s2.at[m, h], t.r2.at[m, h], target
            ).start()

    def stage3(m):
        for h, mine in ((0, y), (1, x)):
            arrive(got2[m].at[h], t.r2.at[m, h])

            def add(zz, _, h=h, mine=mine):
                got2[m][h, zz] = low(wide(kept(m, h, zz, mine)[...]) + wide(got2[m][h, zz]))
                return 0

            lax.fori_loop(0, NARROW, add, 0)
        for d in (1, 3, 2):
            zz = lax.rem(z + d, NARROW)
            remote(
                got2[m].at[:, zz],
                got3[m].at[d - 1],
                t.s3.at[m, d - 1],
                t.r3.at[m, d - 1],
                depth[d - 1],
            ).start()

    def piece(m, pp, part=None):
        _, _, out, start, span = plan[m]
        rows, cols = out.shape[0] // 4, last[m].shape[1]
        first = pp * rows
        if part is not None:
            rows = rows // 2
            first = first + part * rows
        return out.at[pl.ds(pl.multiple_of(first, 16), rows), lanes(c * span + start, cols)]

    def stage4(m):
        for d in (1, 3, 2):
            arrive(got3[m].at[d - 1], t.r3.at[m, d - 1])
        rows = last[m].shape[0] // 2
        for h in range(2):
            total = wide(got2[m][h, z])
            for d in range(3):
                total = total + wide(got3[m][d, h])
            last[m][h * rows : (h + 1) * rows, :] = low(total)
        share(m)

    def share(m):
        mine = piece(m, p)
        remote(last[m], mine, t.s4.at[m], t.r4.at[m, 0], at.xn).start()
        remote(last[m], mine, t.s4.at[m], t.r4.at[m, 1], at.yn).start()
        remote(last[m], mine, t.s4.at[m], t.r4.at[m, 4], at.sib).start()
        pltpu.make_async_copy(last[m], mine, t.lo.at[m]).start()

    def stage5(m):
        for pp, part, slot, target in ((at.px, 0, 0, at.yn), (at.py, 1, 1, at.xn)):
            arrive(piece(m, pp), t.r4.at[m, slot])
            some = piece(m, pp, part)
            remote(some, some, t.s4.at[m], t.r4.at[m, 2 + slot], target).start()
            some = piece(m, pp)
            remote(some, some, t.s4.at[m], t.r4.at[m, 4], at.sib).start()

    def stage6(m):
        arrive(piece(m, at.pd, 0), t.r4.at[m, 2])
        arrive(piece(m, at.pd, 1), t.r4.at[m, 3])
        some = piece(m, at.pd)
        remote(some, some, t.s4.at[m], t.r4.at[m, 4], at.sib).start()

    above, under = (w, jnp.minimum(z + 1, NARROW - 1)), (w, jnp.maximum(z - 1, 0))
    top = NARROW - 1

    def chain_start(m):
        g, room = plan[m][0], got1[m]
        bring(m, 0, rise_to(1))
        bring(m, 1, sink_to(1))

        @pl.when(z == 0)
        def _():
            for i in range(top):
                there = top - i
                remote(
                    g.at[there], room.at[there], t.zs.at[m, i], t.zu.at[m, there], above
                ).start()

        @pl.when(z == top)
        def _():
            for i in range(top):
                spot = NARROW if i == top - 1 else i
                remote(g.at[i], room.at[spot], t.zs.at[m, i], t.zd.at[m, i], under).start()

    def bring(m, spot, there):
        if not plan[m][1]:
            pltpu.make_async_copy(
                plan[m][0].at[there], keep[m].at[spot], t.l1.at[m, spot]
            ).start()

    def brought(m, spot):
        if not plan[m][1]:
            pltpu.make_async_copy(keep[m].at[spot], keep[m].at[spot], t.l1.at[m, spot]).wait()

    def own_part(m, spot, there):
        return plan[m][0].at[there] if plan[m][1] else keep[m].at[spot]

    def join(m, spot, there):
        own = own_part(m, spot, there)

        def add(k, _):
            a, b, h = lax.div(k, 4), lax.rem(lax.div(k, 2), 2), lax.rem(k, 2)
            got1[m][there, a, b, h] = low(wide(got1[m][there, a, b, h]) + wide(own[a, b, h]))
            return 0

        lax.fori_loop(0, 8, add, 0)

    def rising(slot):
        return (z >= 1) & (z <= slot)

    def sinking(slot):
        return (z < top) & (z >= top - slot)

    def rise_to(slot):
        return jnp.minimum(top + z - slot, top)

    def sink_to(slot):
        return jnp.maximum(slot - top + z, 0)

    def chain_step(m, slot):
        room = got1[m]
        brought(m, 0)
        brought(m, 1)

        @pl.when(rising(slot))
        def _():
            there = rise_to(slot)
            arrive(room.at[there], t.zu.at[m, there])
            join(m, 0, there)
            remote(
                room.at[there], room.at[there], t.zs.at[m, 2 + slot], t.zu.at[m, there], above
            ).start()

        @pl.when(sinking(slot))
        def _():
            there = sink_to(slot)
            arrive(room.at[there], t.zd.at[m, there])
            join(m, 1, there)
            spot = NARROW if slot == 2 else there
            remote(
                room.at[there], room.at[spot], t.zs.at[m, 4 + slot], t.zd.at[m, there], under
            ).start()

        if slot == 1:
            bring(m, 0, rise_to(2))
            bring(m, 1, sink_to(2))
        else:
            bring(m, 0, z)

    def chain_end(m):
        room = got1[m]
        brought(m, 0)

        @pl.when(z > 0)
        def _():
            arrive(room.at[z], t.zu.at[m, z])
            join(m, 0, z)

        @pl.when(z < top)
        def _():
            arrive(room.at[NARROW], t.zd.at[m, z])

        def add(k, _, fresh=False):
            a, b, h = lax.div(k, 4), lax.rem(lax.div(k, 2), 2), lax.rem(k, 2)
            own = own_part(m, 0, z)[a, b, h] if fresh else room[z, a, b, h]
            room[z, a, b, h] = low(wide(own) + wide(room[NARROW, a, b, h]))
            return 0

        @pl.when((z > 0) & (z < top))
        def _():
            lax.fori_loop(0, 8, add, 0)

        @pl.when(z == 0)
        def _():
            lax.fori_loop(0, 8, functools.partial(add, fresh=True), 0)

        remote(
            room.at[z, :, 1 - x, 0], got2[m].at[0], t.s1s.at[m, 0], t.r1.at[m, 0], at.xn
        ).start()
        remote(
            room.at[z, 1 - y, :, 1], got2[m].at[1], t.s1s.at[m, 1], t.r1.at[m, 1], at.yn
        ).start()

    def chain_plane(m):
        room = got1[m]
        for h, target in ((0, at.yn), (1, at.xn)):
            arrive(got2[m].at[h], t.r1.at[m, h])
            for o in range(2):
                spot = room.at[z, o, x, 0] if h == 0 else room.at[z, y, o, 1]
                spot[...] = low(wide(spot[...]) + wide(got2[m][h, o]))
            away = room.at[z, 1 - y, x, 0] if h == 0 else room.at[z, y, 1 - x, 1]
            remote(away, got3[m].at[h], t.s2.at[m, h], t.r2.at[m, h], target).start()

    def chain_last(m):
        rows = last[m].shape[0] // 2
        for h in range(2):
            arrive(got3[m].at[h], t.r2.at[m, h])
            last[m][h * rows : (h + 1) * rows, :] = low(
                wide(got1[m][z, y, x, h]) + wide(got3[m][h])
            )
        share(m)

    sources = (
        (t.act_h, t.act),
        (t.od_h, t.od),
        (t.slope_h, t.slope),
        (t.hid_h, t.hid),
        (t.vec_h, t.vec),
        (t.sums_h, t.sums),
        (t.cot_h, t.cot),
        (t.nm_h, t.cat),
        (t.p_h, t.p),
        (t.v_h, t.vr),
        (t.k_h, t.kr),
        (t.cq_h, t.cq),
        (t.pq_h, t.pq),
        (t.rr_h, t.rr),
        (t.turn_h, t.turn),
        (t.flipt_h, t.flipt),
        (t.tok_h, t.cot),
        (t.mx_h, t.cat),
        (t.nn_h, t.idc),
    )
    quarter = width // 4

    def fetch(k, full, shard, held, row=0, col=0):
        span = held.shape[2]
        copies = [
            pltpu.make_async_copy(
                shard.at[pl.ds(row, quarter), pl.ds(col, span)], held.at[z], t.own.at[k, 0]
            )
        ]
        for d in range(1, NARROW):
            zz = lax.rem(z + d, NARROW)
            copies.append(pltpu.make_async_copy(full.at[zz], held.at[zz], t.own.at[k, d]))
        for copy in copies:
            copy.start()
        return copies

    def use(copies):
        for copy in copies:
            copy.wait()

    chain_start(0)
    stage1(1)
    here0 = fetch(0, t.fu0, t.wu, t.s0)
    here1 = fetch(1, t.fu1, t.wu, t.s1, row=quarter)
    loads = [pltpu.make_async_copy(s, d, t.ld.at[k]) for k, (s, d) in enumerate(sources)]
    for k in (*range(9), *range(10, 16)):
        loads[k].start()

    def give(k, src, dst):
        remote(src, dst, t.ps.at[k], t.pr.at[k], at.sib).start()

    def clip(row, values):
        limit = jnp.where(row < WIN, t.lim_h[0, 0], t.lim_h[0, 1])
        return jnp.minimum(jnp.maximum(values, -limit), limit)

    def leave_mlp(h):
        full = (t.s0, t.s1)[h]
        spots = [
            slice(2 * quarter * zz + quarter * h, 2 * quarter * zz + quarter * (h + 1))
            for zz in range(NARROW)
        ]
        active = jnp.concatenate([t.act[:, spot] for spot in spots], axis=1)

        def one(n, _):
            cols = lanes(n * 512, 512)
            part = dot_nn(active, full[:, :, cols].reshape(width, 512))
            if h == 0:
                t.nd[:, cols] = t.hid[:, cols] + part + t.vec[5:6, cols]
            else:
                t.vr[:, cols] = low(t.nd[:, cols] + part)
            return 0

        lax.fori_loop(0, 3, one, 0)
        for zz, spot in enumerate(spots):
            delta = low(dot_nt(t.od[...], full[zz]) * wide(t.slope[:, spot]))
            t.act[:, spot] = delta
            t.sums[6:7, spot] = jnp.sum(wide(delta), axis=0, keepdims=True)

    def pull_mid():
        for zz in range(NARROW):
            t.nd[:, zz * quarter : (zz + 1) * quarter] = dot_nt(
                t.act[:, 0:width], t.s0[zz]
            ) + dot_nt(t.act[:, width : 2 * width], t.s1[zz])

        def one(i, carry):
            gain_total, shift_total, bias_total = carry
            rows = pl.ds(pl.multiple_of(i * 32, 32), 32)
            v = t.hid[rows, :]
            center = v - jnp.mean(v, axis=1, keepdims=True)
            scale = lax.rsqrt(jnp.mean(center * center, axis=1, keepdims=True) + EPSILON)
            n = center * scale
            delta = t.nd[rows, :]
            e = delta * t.vec[3:4, 0:width]
            back = scale * (
                e
                - jnp.mean(e, axis=1, keepdims=True)
                - n * jnp.mean(e * n, axis=1, keepdims=True)
            )
            full = clip(i * 32, wide(t.cot[rows, :])) + back
            t.hid[rows, :] = full
            rounded = low(full)
            bd[rows, :] = rounded
            return (
                gain_total + jnp.sum(delta * n, axis=0, keepdims=True),
                shift_total + jnp.sum(delta, axis=0, keepdims=True),
                bias_total + jnp.sum(wide(rounded), axis=0, keepdims=True),
            )

        zero = jnp.zeros((1, width), jnp.float32)
        gain_total, shift_total, bias_total = lax.fori_loop(
            0, rows_all // 32, one, (zero, zero, zero)
        )
        t.sums[3:4, 0:width] = gain_total
        t.sums[4:5, 0:width] = shift_total
        t.sums[2:3, 0:width] = bias_total
        half = width // 2
        give(1, bd.at[:, lanes((1 - c) * half, half)], t.bdc.at[1])
        t.bdc[0] = bd[:, lanes(c * half, half)]

    def pull_mixed():
        for zz in range(NARROW):
            md[:, zz * quarter : (zz + 1) * quarter] = low(dot_nt(bd[...], t.s0[zz]))

    bd = t.slope.at[:, 0:width]
    md = t.od
    vd = t.act.at[:, 0:width]
    qd = t.act.at[:, width : width + H * KEY]
    kd = t.act.at[:, width + H * KEY : width + 2 * H * KEY]

    def lane_mask(size, split, rows=rows_all):
        return lax.broadcasted_iota(jnp.int32, (rows, size), 1) < split

    def heads(pair):
        qs = slice(pair * 2 * KEY, (pair + 1) * 2 * KEY)
        vs = slice(pair * 2 * VAL, (pair + 1) * 2 * VAL)
        vals, mixed = t.vr[:, vs], md[:, vs]
        keys, rel, cq, pq = t.kr[:, qs], t.rr[:, qs], t.cq[:, qs], t.pq[:, qs]
        first = lane_mask(2 * VAL, VAL)
        parts = []
        for side in range(2):
            mask = first if side == 0 else jnp.logical_not(first)
            soft = t.p[2 * pair + side]
            pull = dot_nt(jnp.where(mask, mixed, jnp.zeros_like(mixed)), vals)
            full = wide(soft)
            delta = low(full * (pull - jnp.sum(full * pull, axis=1, keepdims=True)))
            turned = dot_nn(delta, t.turn[...])
            padded = jnp.concatenate([turned, jnp.zeros_like(turned)], axis=1)
            slid = low(pltpu.roll(padded, 2 * rows_all, axis=1, stride=1, stride_axis=0))
            parts.append(
                (
                    dot_tn(soft, mixed),
                    dot_nn(delta, keys),
                    dot_tn(delta, cq),
                    dot_nn(slid, rel),
                    dot_tn(slid, pq),
                )
            )
        vd[:, vs] = low(jnp.where(first, parts[0][0], parts[1][0]))
        narrow = lane_mask(2 * KEY, KEY)
        content = jnp.where(narrow, parts[0][1], parts[1][1])
        place = jnp.where(narrow, parts[0][3], parts[1][3])
        kd[:, qs] = low(jnp.where(narrow, parts[0][2], parts[1][2]))
        rel_delta = low(
            jnp.where(lane_mask(2 * KEY, KEY, 2 * rows_all), parts[0][4], parts[1][4])
        )
        qd[:, qs] = low(content + place) * jnp.asarray(KEY ** (-0.5), jnp.bfloat16)
        t.rg[:, qs] = dot_nn(t.flipt[...], rel_delta)
        t.sums[7:8, qs] = jnp.sum(content, axis=0, keepdims=True)
        there = slice(keys_all + pair * 2 * KEY, keys_all + (pair + 1) * 2 * KEY)
        t.sums[7:8, there] = jnp.sum(place, axis=0, keepdims=True)

    def trade():
        for k, (full, pair) in enumerate(((vd, t.vdc), (kd, t.kdc), (qd, t.qdc))):
            cols = full.shape[1] // 2
            away = full.at[:, lanes((1 - c) * cols, cols)]
            give(2 + k, away, pair.at[1])
            pair[0] = full[:, lanes(c * cols, cols)]
        cols = t.rg.shape[1] // 2
        t.rgo[...] = low(t.rg[:, lanes((1 - c) * cols, cols)]).reshape(t.rgo.shape)
        remote(t.rgo, t.rgg.at[0], t.xs.at[0], t.xr.at[0], at.sib).start()
        t.rgk[0] = low(t.rg[:, lanes(c * cols, cols)]).reshape(t.rgo.shape)

    def outer_product(rows_from, pair, dst, start=0):
        size = dst.shape[5]

        def one(zz, _):
            lhs = rows_from[:, :, lanes(zz * quarter, quarter)].reshape(2 * rows_all, quarter)
            rhs = pair[:, :, start : start + size].reshape(2 * rows_all, size)
            dst[zz] = low(dot_tn(lhs, rhs)).reshape(dst.shape[1:])
            return 0

        lax.fori_loop(0, NARROW, one, 0)

    keys_all = H * KEY

    def pull_tokens():
        for zz in range(NARROW):
            t.nd[:, zz * 384 : (zz + 1) * 384] = (
                dot_nt(qd[...], t.s0[zz, :, 0:keys_all])
                + dot_nt(kd[...], t.s0[zz, :, keys_all : 2 * keys_all])
                + dot_nt(vd[...], t.s1[zz])
            )

        def one(i, carry):
            gain_total, shift_total = carry
            rows = pl.ds(pl.multiple_of(i * 32, 32), 32)
            v = wide(t.cot[rows, :])
            center = v - jnp.mean(v, axis=1, keepdims=True)
            scale = lax.rsqrt(jnp.mean(center * center, axis=1, keepdims=True) + EPSILON)
            n = center * scale
            delta = t.nd[rows, :]
            e = delta * t.vec[0:1, 0:width]
            back = scale * (
                e
                - jnp.mean(e, axis=1, keepdims=True)
                - n * jnp.mean(e * n, axis=1, keepdims=True)
            )
            t.od[rows, :] = low(t.hid[rows, :] + back)
            return (
                gain_total + jnp.sum(delta * n, axis=0, keepdims=True),
                shift_total + jnp.sum(delta, axis=0, keepdims=True),
            )

        zero = jnp.zeros((1, width), jnp.float32)
        gain_total, shift_total = lax.fori_loop(0, rows_all // 32, one, (zero, zero))
        t.sums[0:1, 0:width] = gain_total
        t.sums[1:2, 0:width] = shift_total
        for zz in range(NARROW):
            t.eb[zz] = jnp.zeros(t.eb.shape[1:], jnp.float32)
            t.eb[zz, 0:6, 0:384] = t.sums[0:6, zz * 384 : (zz + 1) * 384]
            t.eb[zz, 6:7, :] = t.sums[6:7, zz * 768 : (zz + 1) * 768]
            t.eb[zz, 7:8, 0:128] = t.sums[7:8, zz * 128 : (zz + 1) * 128]
            t.eb[zz, 7:8, 128:256] = t.sums[7:8, 512 + zz * 128 : 512 + (zz + 1) * 128]

    def sum_steps(keep, got, over, out, sends, recvs):
        def begin():
            remote(keep.at[0], got.at[0], sends.at[0], recvs.at[0], at.sib).start()

        def step(k):
            arrive(got.at[k], recvs.at[k])
            total = wide(keep[k]) + wide(got[k])
            keep[k + 1] = total.astype(keep.dtype)
            if k < 2:
                target = (at.xn, at.yn)[k]
                remote(
                    keep.at[k + 1], got.at[k + 1], sends.at[k + 1], recvs.at[k + 1], target
                ).start()
            else:
                for d in (1, 3, 2):
                    zz = lax.rem(z + d, NARROW)
                    remote(
                        keep.at[3, zz],
                        over.at[d - 1],
                        sends.at[2 + d],
                        recvs.at[2 + d],
                        depth[d - 1],
                    ).start()

        def end():
            total = wide(keep[3, z])
            for d in (1, 3, 2):
                arrive(over.at[d - 1], recvs.at[2 + d])
                total = total + wide(over[d - 1])
            out[...] = total

        return begin, step, end

    rel_sums = sum_steps(t.rgk, t.rgg, t.rgs, t.rg.at[0:48, 0:256], t.xs, t.xr)
    row_sums = sum_steps(t.ek, t.eg, t.es, t.eo, t.ws, t.wr)

    stored = []

    def store(src, dst):
        copy = pltpu.make_async_copy(src, dst, t.st.at[len(stored)])
        copy.start()
        stored.append(copy)

    for copy in loads[:6]:
        copy.wait()
    use(here0)
    leave_mlp(0)
    use(here1)
    leave_mlp(1)
    store(t.vr, t.out_h)
    give(0, t.act.at[:, lanes((1 - c) * width, width)], t.idc.at[1])
    t.idc[0] = t.act[:, lanes(c * width, width)]
    here0 = fetch(2, t.fi0, t.wi, t.s0)
    here1 = fetch(3, t.fi1, t.wi, t.s1, col=width)
    loads[7].wait()
    arrive(t.idc.at[1], t.pr.at[0])
    outer_product(t.cat, t.idc, t.gi0)
    stage1(2)
    chain_step(0, 1)
    outer_product(t.cat, t.idc, t.gi1, width // 2)
    loads[17].start()
    loads[18].start()
    stage2(1)
    loads[6].wait()
    use(here0)
    use(here1)
    pull_mid()
    stored[0].wait()
    loads[9].start()
    loads[16].start()
    here0 = fetch(4, t.fo, t.wo, t.s0)
    here1 = fetch(5, t.fv, t.wv, t.s1)
    use(here0)
    pull_mixed()
    here0 = fetch(6, t.fq, t.wq, t.s0.at[:, :, 0:keys_all])
    here2 = fetch(7, t.fk, t.wk, t.s0.at[:, :, keys_all : 2 * keys_all])
    loads[17].wait()
    arrive(t.bdc.at[1], t.pr.at[1])
    outer_product(t.cat, t.bdc, t.go)
    stage1(4)
    stage3(1)
    chain_start(3)
    for copy in loads[8:16]:
        copy.wait()
    left(t.idc.at[1], t.ps.at[0])
    heads(0)
    chain_step(0, 2)
    stage2(2)
    heads(1)
    heads(2)
    chain_end(0)
    heads(3)
    trade()
    loads[18].wait()
    loads[16].wait()
    for k, (pair, dst) in enumerate(((t.vdc, t.gv), (t.kdc, t.gk), (t.qdc, t.gq))):
        arrive(pair.at[1], t.pr.at[2 + k])
        outer_product(t.idc, pair, dst)
        stage1(5 + k)
    stage2(4)
    rel_sums[1](0)
    use(here0)
    use(here1)
    use(here2)
    pull_tokens()
    store(t.od, t.tg_h)
    t.ek[0] = t.eb[...]
    row_sums[0]()
    stage3(2)
    chain_step(3, 1)
    chain_plane(0)
    stage4(1)
    rel_sums[1](1)
    row_sums[1](0)
    stage2(5)
    stage3(4)
    chain_last(0)
    stage5(1)
    rel_sums[1](2)
    row_sums[1](1)
    chain_step(3, 2)
    stage2(6)
    stage2(7)
    stage6(1)
    stage5(0)
    row_sums[1](2)
    stage3(5)
    stage3(6)
    stage3(7)
    stage4(2)
    stage6(0)
    chain_end(3)
    rel_sums[2]()
    row_sums[2]()
    store(t.eo, t.e_h)
    store(t.rg.at[0:48, 0:256], t.rg_h.at[c])
    remote(t.rg.at[0:48, 0:256], t.rg_h.at[c], t.xs.at[6], t.xr.at[6], at.sib).start()
    stage4(4)
    stage5(2)
    chain_plane(3)
    stage4(5)
    stage5(4)
    stage6(2)
    chain_last(3)
    stage4(6)
    stage4(7)
    stage5(5)
    stage6(4)
    stage5(3)
    stage5(6)
    stage5(7)
    stage6(5)
    stage6(3)
    stage6(6)
    stage6(7)

    for m in range(UNITS):
        _, _, out, _, _ = plan[m]
        cols = last[m].shape[1]
        arrive(out.at[:, pl.ds(0, cols)], t.r4.at[m, 4])
        arrive(last[m], t.lo.at[m])
        if m in CHAINS:
            room = got1[m]
            for i in range(top):

                @pl.when((z == 0) | (z == top))
                def _():
                    left(room.at[0], t.zs.at[m, i])

            for slot in (1, 2):

                @pl.when(rising(slot))
                def _():
                    left(room.at[0], t.zs.at[m, 2 + slot])

                @pl.when(sinking(slot))
                def _():
                    left(room.at[0], t.zs.at[m, 4 + slot])

            for h in range(2):
                left(got2[m].at[h], t.s1s.at[m, h])
                left(got3[m].at[h], t.s2.at[m, h])
        else:
            for h in range(2):
                left(got1[m].at[h], t.s1s.at[m, h])
                left(got2[m].at[h], t.s2.at[m, h])
            for d in range(3):
                left(got3[m].at[d], t.s3.at[m, d])
        left(out.at[:, pl.ds(0, cols)], t.s4.at[m])
        left(out.at[pl.ds(0, 3 * (out.shape[0] // 4)), pl.ds(0, cols)], t.s4.at[m])
    for k, pair in enumerate((t.bdc, t.vdc, t.kdc, t.qdc)):
        left(pair.at[1], t.ps.at[1 + k])
    for got, over, sends in ((t.rgg, t.rgs, t.xs), (t.eg, t.es, t.ws)):
        for k in range(3):
            left(got.at[k], sends.at[k])
            left(over.at[k], sends.at[3 + k])
    left(t.rg.at[0:48, 0:256], t.xs.at[6])
    arrive(t.rg_h.at[1 - c], t.xr.at[6])
    for copy in stored[1:]:
        copy.wait()


def backward_pass(grads, saved, weights, shards, rest):
    bf, f32 = jnp.bfloat16, jnp.float32
    rows, width = rest[0].shape
    keys = H * KEY
    views = [g.reshape(4, 2, 2, 2, g.shape[0] // 32, g.shape[1]) for g in grads]
    shapes = [(g.shape[0], g.shape[1]) for g in grads] + [(width, width // 2)] * 4
    shapes += [(width, keys // 2)] * 2
    out_shape = (
        ((width // 2, width), bf),
        ((width // 4, 2 * width), bf),
        ((width // 4, width), bf),
        ((width // 4, width), bf),
        ((width // 4, keys), bf),
        ((width // 4, keys), bf),
        ((rows, width), bf),
        ((rows, width), bf),
        ((8, 768), f32),
        ((2, 48, 256), f32),
    )
    vmem = [
        (((2, 2, 2, 2) if m in CHAINS else (2, 4, 2)) + (r // 32, n), bf)
        for m, (r, n) in enumerate(shapes[: len(grads)])
    ]
    for plain, chain in (
        ((2, 4, 2), (5, 2, 2, 2)),
        ((2, 4), (2, 2)),
        ((3, 2), (2,)),
    ):
        vmem += [
            ((chain if m in CHAINS else plain) + (r // 32, n), bf)
            for m, (r, n) in enumerate(shapes)
        ]
    vmem += [((r // 16, n), bf) for r, n in shapes]
    vmem += [((4, 2, 2, 2, r // 32, n), bf) for r, n in shapes[len(grads) :]]
    vmem += [((NARROW, width // 4, width), bf)] * 2
    vmem += [(a.shape, a.dtype) for a in saved[:10]]
    vmem += [((2, rows, width), bf)] * 2
    vmem += [(a.shape, a.dtype) for a in rest[1:] if a.size > 2]
    vmem += [
        ((2, rows, width // 2), bf),
        ((2, rows, keys // 2), bf),
        ((2, rows, keys // 2), bf),
        ((2, rows, width // 2), bf),
        ((rows, width), f32),
        ((F, keys), f32),
        ((4, 4, 48, 256), bf),
        ((3, 4, 48, 256), bf),
        ((3, 48, 256), bf),
        ((4, 48, 256), bf),
        ((4, 8, 768), f32),
        ((4, 4, 8, 768), f32),
        ((3, 4, 8, 768), f32),
        ((3, 8, 768), f32),
        ((8, 768), f32),
    ]
    sems = [
        DMA((20,)),
        DMA((8, 4)),
        DMA((UNITS, 2)),
        DMA((UNITS, 2)),
        DMA((UNITS, 2)),
        DMA((UNITS, 2)),
        DMA((UNITS, 2)),
        DMA((UNITS, 3)),
        DMA((UNITS, 3)),
        DMA((UNITS,)),
        DMA((UNITS, 5)),
        DMA((UNITS,)),
        DMA((UNITS, NARROW)),
        DMA((UNITS, NARROW)),
        DMA((UNITS, 7)),
        DMA((5,)),
        DMA((5,)),
        DMA((7,)),
        DMA((7,)),
        DMA((6,)),
        DMA((6,)),
        DMA((4,)),
    ]
    ins = (*views, *saved, *weights, *shards, *rest)
    return pl.pallas_call(
        backward_kernel,
        out_shape=tuple(jax.ShapeDtypeStruct(s, d) for s, d in out_shape),
        in_specs=[SMEM if a.size == 2 else HBM for a in ins],
        out_specs=(HBM,) * len(out_shape),
        scratch_shapes=[pltpu.VMEM(s, d) for s, d in vmem] + sems,
        compiler_params=pltpu.CompilerParams(
            collective_id=2, has_side_effects=True, vmem_limit_bytes=60 << 20
        ),
        name="backward_pass",
    )(*ins)


def finish_kernel(count, *refs):
    ins, (rows_h, rel_h), passed = refs[:count], refs[count : count + 2], refs[count + 2 : count + 4]
    refs = refs[count + 4 :]
    outs, relative, kept, vectors = (
        refs[:count],
        refs[count],
        refs[count + 1 : count + 3],
        refs[count + 3 : count + 12],
    )
    refs = refs[count + 12 :]
    low_in, f32_out, through = refs[:count], refs[count : 2 * count], refs[2 * count : 2 * count + 2]
    into, out = refs[2 * count + 2 :]
    loads = [
        pltpu.make_async_copy(src, dst, into.at[k])
        for k, (src, dst) in enumerate(zip((*ins, *passed), (*low_in, *through)))
    ]
    for copy in loads:
        copy.start()
    stored = []

    def store(src, dst):
        copy = pltpu.make_async_copy(src, dst, out.at[len(stored)])
        copy.start()
        stored.append(copy)

    size = relative.shape[1] // 2
    relative[:, 0:size] = rel_h[0]
    relative[:, size : 2 * size] = rel_h[1]
    for k, vector in enumerate(vectors):
        n = vector.shape[0]
        row, start = (7, 128 * (k - 7)) if k >= 7 else (k, 0)
        vector[...] = rows_h[row : row + 1, start : start + n].reshape(n)
    for k in (count, count + 1):
        loads[k].wait()
        store(through[k - count], kept[k - count])
    for k in range(count):
        loads[k].wait()
        src, dst, res = low_in[k], f32_out[k], outs[k]
        half = src.shape[0] // 2
        for part in range(2):

            def one(i, _):
                spot = pl.ds(pl.multiple_of(part * half + i * 32, 32), 32)
                dst[spot, :] = wide(src[spot, :])
                return 0

            lax.fori_loop(0, half // 32, one, 0)
            spot = pl.ds(part * half, half)
            store(dst.at[spot], res.at[spot])
    for copy in stored:
        copy.wait()


def finish_grads(sums, rows, rel, layer_out, tokens_grad):
    f32 = jnp.float32
    vmem = pl.BlockSpec(memory_space=pltpu.VMEM)
    count = len(sums)
    lengths = (384, 384, 384, 384, 384, 384, 768, 128, 128)
    shapes = [(a.shape, f32) for a in sums] + [((rel.shape[1], 2 * rel.shape[2]), f32)]
    shapes += [(a.shape, a.dtype) for a in (layer_out, tokens_grad)]
    shapes += [((n,), f32) for n in lengths]
    through = [(a.shape, a.dtype) for a in (layer_out, tokens_grad)]
    scratch = [(a.shape, a.dtype) for a in sums] + [(a.shape, f32) for a in sums] + through
    return pl.pallas_call(
        lambda *refs: finish_kernel(count, *refs),
        out_shape=tuple(jax.ShapeDtypeStruct(s, d) for s, d in shapes),
        in_specs=[HBM] * count + [vmem] * 2 + [HBM] * 2,
        out_specs=(HBM,) * count + (vmem,) + (HBM,) * 2 + (vmem,) * len(lengths),
        scratch_shapes=[pltpu.VMEM(s, d) for s, d in scratch]
        + [DMA((count + 2,)), DMA((2 * count + 2,))],
        compiler_params=pltpu.CompilerParams(vmem_limit_bytes=60 << 20),
        name="finish_grads",
    )(*sums, rows, rel, layer_out, tokens_grad)


def basis_rows(length, features):
    f32 = np.float32
    family = features // 6
    offsets = np.arange(2 * length - 1, dtype=f32) - f32(length - 1)
    distance = np.abs(offsets)[:, None]
    halves = f32(2.0) ** np.linspace(3.0, math.log2(length), family, dtype=f32)
    decays = np.exp(f32(-math.log(2.0)) / halves[None, :] * distance)
    widths = f32(2.0) ** np.arange(1, family + 1, dtype=f32) - f32(1.0)
    central = np.where(widths[None, :] > distance, f32(1.0), f32(0.0))
    centers = np.linspace(0.0, float(length), family, dtype=f32)
    spread = f32(length / family)
    bump_rows = np.exp(f32(-0.5) * ((distance - centers[None, :]) / spread) ** 2)
    positive = np.concatenate([decays, central, bump_rows], axis=1)
    return np.concatenate([positive, np.sign(offsets)[:, None] * positive], axis=1)


def per_device_linked(
    tokens,
    cotangent,
    thresholds,
    attn_norm_gain,
    attn_norm_shift,
    query_weight,
    key_weight,
    value_weight,
    relative_weight,
    content_bias,
    position_bias,
    out_weight,
    out_bias,
    mlp_norm_gain,
    mlp_norm_shift,
    inner_weight,
    inner_bias,
    outer_weight,
    outer_bias,
):
    _, length, width = tokens.shape
    bf = jnp.bfloat16
    vectors = (
        (attn_norm_gain, 0, 0),
        (attn_norm_shift, 1, 0),
        (out_bias, 2, 0),
        (mlp_norm_gain, 3, 0),
        (mlp_norm_shift, 4, 0),
        (outer_bias, 5, 0),
        (inner_bias, 6, 0),
        (content_bias, 0, 384),
        (position_bias, 1, 384),
    )
    small = jnp.zeros((8, 512), bf)
    for vector, row, col in vectors:
        table = vector.reshape(-1, min(vector.shape[0], 384))
        n, m = table.shape
        small = small + jnp.pad(table, ((row, 8 - row - n), (col, 512 - col - m)))
    limits = thresholds
    table = basis_rows(length, F)
    empty = np.zeros((1, F), np.float32)
    basis = jnp.asarray(np.concatenate([table, empty]), bf)
    flip = jnp.asarray(np.concatenate([table[::-1], empty]), bf)
    flip_t = jnp.asarray(np.concatenate([table[::-1], empty]).T, bf)
    turn = jnp.asarray(np.eye(length)[::-1], bf)
    flat_tokens = tokens.reshape(length, width)
    flat_cotangent = cotangent.reshape(length, width)
    shards = (query_weight, key_weight, value_weight, out_weight, inner_weight, outer_weight)
    outs = forward_pass(
        flat_tokens, flat_cotangent, limits, shards, relative_weight, small, basis, flip
    )
    saved, weights, (vec, gu0, gu1, sums) = outs[:13], outs[13:21], outs[21:]
    ou, oi, oo, ov, ok, oq, layer_out, tokens_grad, rows, rel = backward_pass(
        (gu0, gu1),
        saved,
        weights,
        shards,
        (flat_tokens, flat_cotangent, limits, vec, sums, flip_t, turn),
    )
    outer, inner, out, value, key, query, relative, layer_out, tokens_grad, *vectors = finish_grads(
        (ou, oi, oo, ov, ok, oq), rows, rel, layer_out, tokens_grad
    )
    gain, shift, out_b, mlp_gain, mlp_shift, outer_b, inner_b, content_b, position_b = vectors
    return (
        layer_out[None],
        tokens_grad[None],
        gain,
        shift,
        query,
        key,
        value,
        relative,
        content_b,
        position_b,
        out,
        out_b,
        mlp_gain,
        mlp_shift,
        inner,
        inner_b,
        outer,
        outer_b,
    )


def solution(mesh):
    body = per_device_generic
    if mesh.shape[WIDE] == 8 and mesh.shape[DEPTH] == 4:
        body = per_device_linked
    in_specs = (
        P((WIDE, DEPTH), None, None),
        P((WIDE, DEPTH), None, None),
        P((WIDE, DEPTH), None),
        P(DEPTH),
        P(DEPTH),
        P(DEPTH, None),
        P(DEPTH, None),
        P(DEPTH, None),
        P(DEPTH, None),
        P(DEPTH),
        P(DEPTH),
        P(DEPTH, None),
        P(DEPTH),
        P(DEPTH),
        P(DEPTH),
        P(DEPTH, None),
        P(DEPTH),
        P(DEPTH, None),
        P(DEPTH),
    )
    out_specs = (
        P((WIDE, DEPTH), None, None),
        P((WIDE, DEPTH), None, None),
        P(DEPTH),
        P(DEPTH),
        P(DEPTH, None),
        P(DEPTH, None),
        P(DEPTH, None),
        P(DEPTH, None),
        P(DEPTH),
        P(DEPTH),
        P(DEPTH, None),
        P(DEPTH),
        P(DEPTH),
        P(DEPTH),
        P(DEPTH, None),
        P(DEPTH),
        P(DEPTH, None),
        P(DEPTH),
    )
    return jax.shard_map(
        body, mesh=mesh, in_specs=in_specs, out_specs=out_specs, check_vma=False
    )
```

```python
import functools
import math
import types

import jax
import jax.numpy as jnp
import numpy as np
from jax import lax
from jax.experimental import pallas as pl
from jax.experimental.pallas import tpu as pltpu
from jax.sharding import PartitionSpec as P

H = 8
KEY = 64
VAL = 192
F = 192
WIN = 128


EPSILON = 1e-05


def basis_table(length, features):
    family = features // 6
    offsets = jnp.arange(2 * length - 1, dtype=jnp.float32) - (length - 1)
    distance = jnp.abs(offsets)[:, None]
    halves = 2.0 ** jnp.linspace(3.0, math.log2(length), family, dtype=jnp.float32)
    decays = jnp.exp(-math.log(2.0) / halves[None, :] * distance)
    widths = 2.0 ** jnp.arange(1, family + 1, dtype=jnp.float32) - 1.0
    central = jnp.where(widths[None, :] > distance, 1.0, 0.0).astype(jnp.float32)
    centers = jnp.linspace(0.0, float(length), family, dtype=jnp.float32)
    spread = length / family
    bump_rows = jnp.exp(-0.5 * ((distance - centers[None, :]) / spread) ** 2)
    positive = jnp.concatenate([decays, central, bump_rows], axis=1)
    return jnp.concatenate([positive, jnp.sign(offsets)[:, None] * positive], axis=1)


def shift_offsets(raw_scores, length):
    leading = raw_scores.shape[:-2]
    padded = jnp.pad(raw_scores, [(0, 0)] * len(leading) + [(0, 0), (0, 1)])
    flatten = padded.reshape(leading + (2 * length * length,))
    window = flatten[..., length - 1 : length - 1 + length * (2 * length - 1)]
    return window.reshape(leading + (length, 2 * length - 1))[..., :length]


def unshift_offsets(grad_scores, length):
    leading = grad_scores.shape[:-2]
    widened = jnp.pad(grad_scores, [(0, 0)] * len(leading) + [(0, 0), (0, length - 1)])
    flatten = widened.reshape(leading + (length * (2 * length - 1),))
    flatten = jnp.pad(flatten, [(0, 0)] * len(leading) + [(length - 1, 1)])
    return flatten.reshape(leading + (length, 2 * length))[..., : 2 * length - 1]


def layer_norm(values, gain, shift):
    center = values - jnp.mean(values, axis=-1, keepdims=True)
    spread = jnp.mean(center * center, axis=-1, keepdims=True)
    return center * lax.rsqrt(spread + EPSILON) * gain + shift


def gelu_exact(values):
    return jax.nn.gelu(values, approximate=False)


def column_sums(values):
    return jnp.sum(values.astype(jnp.float32), axis=0)


WIDE = "wide"
DEPTH = "narrow"


def spread_rows(shard):
    return lax.all_gather(shard, DEPTH, axis=0, tiled=True)


def sum_columns(part):
    low = part.astype(jnp.bfloat16)
    return lax.psum_scatter(low, WIDE, scatter_dimension=1, tiled=True).astype(jnp.float32)


def sum_rows(part):
    low = part.astype(jnp.bfloat16)
    return lax.psum_scatter(low, DEPTH, scatter_dimension=0, tiled=True).astype(jnp.float32)


def spread_columns(part):
    low = part.astype(jnp.bfloat16)
    return lax.all_gather(low, WIDE, axis=1, tiled=True).astype(jnp.float32)


def per_device_generic(
    tokens,
    cotangent,
    thresholds,
    attn_norm_gain,
    attn_norm_shift,
    query_weight,
    key_weight,
    value_weight,
    relative_weight,
    content_bias,
    position_bias,
    out_weight,
    out_bias,
    mlp_norm_gain,
    mlp_norm_shift,
    inner_weight,
    inner_bias,
    outer_weight,
    outer_bias,
):
    seq_count, length, model_width = tokens.shape
    row_count = seq_count * length
    span = 2 * length - 1
    query_scale = KEY ** (-0.5)
    (
        attn_gain,
        attn_shift,
        query_full,
        key_full,
        value_full,
        relative_full,
        content_full,
        position_full,
        exit_full,
        exit_bias,
    ) = (
        spread_rows(attn_norm_gain),
        spread_rows(attn_norm_shift),
        spread_rows(query_weight),
        spread_rows(key_weight),
        spread_rows(value_weight),
        spread_rows(relative_weight),
        spread_rows(content_bias),
        spread_rows(position_bias),
        spread_rows(out_weight),
        spread_rows(out_bias),
    )
    mlp_gain, mlp_shift, inner_full, inner_offset, outer_full, outer_offset = (
        spread_rows(mlp_norm_gain),
        spread_rows(mlp_norm_shift),
        spread_rows(inner_weight),
        spread_rows(inner_bias),
        spread_rows(outer_weight),
        spread_rows(outer_bias),
    )
    flat_tokens = tokens.reshape(row_count, model_width).astype(jnp.float32)
    attn_gain_f = attn_gain.astype(jnp.float32)
    attn_shift_f = attn_shift.astype(jnp.float32)
    normed = layer_norm(flat_tokens, attn_gain_f, attn_shift_f).astype(jnp.bfloat16)
    queries = jnp.dot(normed, query_full, preferred_element_type=jnp.float32) * query_scale
    content_query = (
        (queries + content_full.astype(jnp.float32))
        .astype(jnp.bfloat16)
        .reshape(seq_count, length, H, KEY)
    )
    position_query = (
        (queries + position_full.astype(jnp.float32))
        .astype(jnp.bfloat16)
        .reshape(seq_count, length, H, KEY)
    )
    key_rows = (
        jnp.dot(normed, key_full, preferred_element_type=jnp.float32)
        .astype(jnp.bfloat16)
        .reshape(seq_count, length, H, KEY)
    )
    value_rows = (
        jnp.dot(normed, value_full, preferred_element_type=jnp.float32)
        .astype(jnp.bfloat16)
        .reshape(seq_count, length, H, VAL)
    )
    basis = basis_table(length, F).astype(jnp.bfloat16)
    rel_keys = (
        jnp.dot(basis, relative_full, preferred_element_type=jnp.float32)
        .astype(jnp.bfloat16)
        .reshape(span, H, KEY)
    )

    def attention_logits():
        content = jnp.einsum(
            "bihe,bjhe->bhij", content_query, key_rows, preferred_element_type=jnp.float32
        )
        raw_scores = jnp.einsum(
            "bihe,the->bhit", position_query, rel_keys, preferred_element_type=jnp.float32
        )
        return content + shift_offsets(raw_scores, length)

    logits = attention_logits()
    row_peak = jnp.max(logits, axis=-1, keepdims=True)
    log_total = row_peak + jnp.log(jnp.sum(jnp.exp(logits - row_peak), axis=-1, keepdims=True))
    attention = jnp.exp(logits - log_total).astype(jnp.bfloat16)
    mixed_heads = jnp.einsum(
        "bhij,bjhd->bihd", attention, value_rows, preferred_element_type=jnp.float32
    )
    mixed_heads = mixed_heads.astype(jnp.bfloat16).reshape(row_count, H * VAL)
    hidden = flat_tokens + (
        jnp.dot(mixed_heads, exit_full, preferred_element_type=jnp.float32)
        + exit_bias.astype(jnp.float32)
    )
    mlp_gain_f = mlp_gain.astype(jnp.float32)
    mlp_shift_f = mlp_shift.astype(jnp.float32)
    normed_mid = layer_norm(hidden, mlp_gain_f, mlp_shift_f).astype(jnp.bfloat16)
    inner_pre = jnp.dot(
        normed_mid, inner_full, preferred_element_type=jnp.float32
    ) + inner_offset.astype(jnp.float32)
    active, gelu_pull = jax.vjp(gelu_exact, inner_pre)
    active_low = active.astype(jnp.bfloat16)
    result = hidden + (
        jnp.dot(active_low, outer_full, preferred_element_type=jnp.float32)
        + outer_offset.astype(jnp.float32)
    )
    layer_out = result.astype(jnp.bfloat16).reshape(seq_count, length, model_width)
    clip_limit = jnp.repeat(thresholds, WIN, axis=1).reshape(row_count, 1)
    clipped = jnp.clip(
        cotangent.reshape(row_count, model_width).astype(jnp.float32), -clip_limit, clip_limit
    )
    mlp_gain, mlp_shift, inner_full, inner_offset, outer_full, outer_offset = (
        spread_rows(mlp_norm_gain),
        spread_rows(mlp_norm_shift),
        spread_rows(inner_weight),
        spread_rows(inner_bias),
        spread_rows(outer_weight),
        spread_rows(outer_bias),
    )
    mlp_gain_f = mlp_gain.astype(jnp.float32)
    outer_delta = clipped.astype(jnp.bfloat16)
    outer_bias_grad = column_sums(outer_delta)
    outer_weight_grad = jnp.einsum(
        "nk,nm->km", active_low, outer_delta, preferred_element_type=jnp.float32
    )
    active_delta = jnp.einsum(
        "nm,km->nk", outer_delta, outer_full, preferred_element_type=jnp.float32
    )
    (inner_grad_pre,) = gelu_pull(active_delta)
    inner_delta = inner_grad_pre.astype(jnp.bfloat16)
    inner_bias_grad = column_sums(inner_delta)
    inner_weight_grad = jnp.einsum(
        "nd,nf->df", normed_mid, inner_delta, preferred_element_type=jnp.float32
    )
    mid_delta = jnp.einsum("nf,df->nd", inner_delta, inner_full, preferred_element_type=jnp.float32)
    norm_out, norm_pull = jax.vjp(layer_norm, hidden, mlp_gain_f, mlp_shift_f)
    hidden_part, mlp_gain_grad, mlp_shift_grad = norm_pull(mid_delta)
    hidden_delta = clipped + hidden_part
    (
        attn_gain,
        attn_shift,
        query_full,
        key_full,
        value_full,
        relative_full,
        content_full,
        position_full,
        exit_full,
        exit_bias,
    ) = (
        spread_rows(attn_norm_gain),
        spread_rows(attn_norm_shift),
        spread_rows(query_weight),
        spread_rows(key_weight),
        spread_rows(value_weight),
        spread_rows(relative_weight),
        spread_rows(content_bias),
        spread_rows(position_bias),
        spread_rows(out_weight),
        spread_rows(out_bias),
    )
    attn_gain_f = attn_gain.astype(jnp.float32)
    branch_delta = hidden_delta.astype(jnp.bfloat16)
    out_bias_grad = column_sums(branch_delta)
    out_weight_grad = jnp.einsum(
        "nk,nd->kd", mixed_heads, branch_delta, preferred_element_type=jnp.float32
    )
    mixed_delta = jnp.einsum(
        "nd,kd->nk", branch_delta, exit_full, preferred_element_type=jnp.float32
    )
    mixed_delta = mixed_delta.astype(jnp.bfloat16).reshape(seq_count, length, H, VAL)
    logits = attention_logits()
    soft_rows = jnp.exp(logits - log_total)
    attention = soft_rows.astype(jnp.bfloat16)
    attention_delta = jnp.einsum(
        "bihd,bjhd->bhij", mixed_delta, value_rows, preferred_element_type=jnp.float32
    )
    value_delta = jnp.einsum(
        "bhij,bihd->bjhd", attention, mixed_delta, preferred_element_type=jnp.float32
    )
    value_delta = value_delta.astype(jnp.bfloat16).reshape(row_count, H * VAL)
    logit_delta = soft_rows * (
        attention_delta - jnp.sum(soft_rows * attention_delta, axis=-1, keepdims=True)
    )
    logit_delta = logit_delta.astype(jnp.bfloat16)
    content_delta = jnp.einsum(
        "bhij,bjhe->bihe", logit_delta, key_rows, preferred_element_type=jnp.float32
    )
    key_delta = jnp.einsum(
        "bhij,bihe->bjhe", logit_delta, content_query, preferred_element_type=jnp.float32
    )
    key_delta = key_delta.astype(jnp.bfloat16).reshape(row_count, H * KEY)
    offset_delta = unshift_offsets(logit_delta, length)
    position_delta = jnp.einsum(
        "bhit,the->bihe", offset_delta, rel_keys, preferred_element_type=jnp.float32
    )
    rel_delta = jnp.einsum(
        "bhit,bihe->the", offset_delta, position_query, preferred_element_type=jnp.float32
    )
    rel_delta = rel_delta.astype(jnp.bfloat16).reshape(span, H * KEY)
    relative_weight_grad = jnp.einsum(
        "tf,tk->fk", basis, rel_delta, preferred_element_type=jnp.float32
    )
    content_delta = content_delta.reshape(row_count, H * KEY)
    position_delta = position_delta.reshape(row_count, H * KEY)
    content_bias_grad = jnp.sum(content_delta, axis=0)
    position_bias_grad = jnp.sum(position_delta, axis=0)
    query_delta = (content_delta + position_delta).astype(jnp.bfloat16) * jnp.asarray(
        query_scale, jnp.bfloat16
    )
    query_weight_grad = jnp.einsum(
        "nd,nk->dk", normed, query_delta, preferred_element_type=jnp.float32
    )
    key_weight_grad = jnp.einsum("nd,nk->dk", normed, key_delta, preferred_element_type=jnp.float32)
    value_weight_grad = jnp.einsum(
        "nd,nk->dk", normed, value_delta, preferred_element_type=jnp.float32
    )
    normed_delta = (
        jnp.einsum("nk,dk->nd", query_delta, query_full, preferred_element_type=jnp.float32)
        + jnp.einsum("nk,dk->nd", key_delta, key_full, preferred_element_type=jnp.float32)
        + jnp.einsum("nk,dk->nd", value_delta, value_full, preferred_element_type=jnp.float32)
    )
    first_out, first_pull = jax.vjp(layer_norm, flat_tokens, attn_gain_f, attn_shift_f)
    tokens_part, attn_gain_grad, attn_shift_grad = first_pull(normed_delta)
    tokens_grad = (
        (hidden_delta + tokens_part).astype(jnp.bfloat16).reshape(seq_count, length, model_width)
    )
    (
        query_weight_grad,
        key_weight_grad,
        value_weight_grad,
        relative_weight_grad,
        out_weight_grad,
        inner_weight_grad,
        outer_weight_grad,
    ) = (
        sum_columns(query_weight_grad),
        sum_columns(key_weight_grad),
        sum_columns(value_weight_grad),
        sum_columns(relative_weight_grad),
        sum_columns(out_weight_grad),
        sum_columns(inner_weight_grad),
        sum_columns(outer_weight_grad),
    )
    (
        query_weight_grad,
        key_weight_grad,
        value_weight_grad,
        relative_weight_grad,
        out_weight_grad,
        inner_weight_grad,
        outer_weight_grad,
        attn_gain_grad,
        attn_shift_grad,
        content_bias_grad,
        position_bias_grad,
        out_bias_grad,
        mlp_gain_grad,
        mlp_shift_grad,
        inner_bias_grad,
        outer_bias_grad,
    ) = (
        sum_rows(query_weight_grad),
        sum_rows(key_weight_grad),
        sum_rows(value_weight_grad),
        sum_rows(relative_weight_grad),
        sum_rows(out_weight_grad),
        sum_rows(inner_weight_grad),
        sum_rows(outer_weight_grad),
        sum_rows(attn_gain_grad),
        sum_rows(attn_shift_grad),
        sum_rows(content_bias_grad),
        sum_rows(position_bias_grad),
        sum_rows(out_bias_grad),
        sum_rows(mlp_gain_grad),
        sum_rows(mlp_shift_grad),
        sum_rows(inner_bias_grad),
        sum_rows(outer_bias_grad),
    )
    (
        query_weight_grad,
        key_weight_grad,
        value_weight_grad,
        relative_weight_grad,
        out_weight_grad,
        inner_weight_grad,
        outer_weight_grad,
    ) = (
        spread_columns(query_weight_grad),
        spread_columns(key_weight_grad),
        spread_columns(value_weight_grad),
        spread_columns(relative_weight_grad),
        spread_columns(out_weight_grad),
        spread_columns(inner_weight_grad),
        spread_columns(outer_weight_grad),
    )
    (
        attn_gain_grad,
        attn_shift_grad,
        content_bias_grad,
        position_bias_grad,
        out_bias_grad,
        mlp_gain_grad,
        mlp_shift_grad,
        inner_bias_grad,
        outer_bias_grad,
    ) = lax.psum(
        (
            attn_gain_grad,
            attn_shift_grad,
            content_bias_grad,
            position_bias_grad,
            out_bias_grad,
            mlp_gain_grad,
            mlp_shift_grad,
            inner_bias_grad,
            outer_bias_grad,
        ),
        WIDE,
    )
    return (
        layer_out,
        tokens_grad,
        attn_gain_grad,
        attn_shift_grad,
        query_weight_grad,
        key_weight_grad,
        value_weight_grad,
        relative_weight_grad,
        content_bias_grad,
        position_bias_grad,
        out_weight_grad,
        out_bias_grad,
        mlp_gain_grad,
        mlp_shift_grad,
        inner_weight_grad,
        inner_bias_grad,
        outer_weight_grad,
        outer_bias_grad,
    )


MESH = pl.DeviceIdType.MESH
NARROW = 4


def position():
    w = lax.axis_index(WIDE)
    z = lax.axis_index(DEPTH)
    c = lax.rem(w, 2)
    p = lax.div(w, 2)
    x = lax.rem(p, 2)
    y = lax.div(p, 2)
    chip = (lambda q: q * 2 + c)
    return types.SimpleNamespace(
        w=w,
        z=z,
        c=c,
        p=p,
        x=x,
        y=y,
        px=p + 1 - 2 * x,
        py=p + 2 - 4 * y,
        pd=3 - p,
        sib=(w + 1 - 2 * c, z),
        xn=(chip(p + 1 - 2 * x), z),
        yn=(chip(p + 2 - 4 * y), z),
    )


def meet(partners):
    barrier = pltpu.get_barrier_semaphore()
    for partner in partners:
        pl.semaphore_signal(barrier, inc=1, device_id=partner, device_id_type=MESH)
    pl.semaphore_wait(barrier, len(partners))


def remote(src, dst, send, recv, target):
    return pltpu.make_async_remote_copy(
        src_ref=src,
        dst_ref=dst,
        send_sem=send,
        recv_sem=recv,
        device_id=target,
        device_id_type=MESH,
    )


HBM = pl.BlockSpec(memory_space=pltpu.HBM)
DMA = pltpu.SemaphoreType.DMA
SMEM = pl.BlockSpec(memory_space=pltpu.SMEM)


def dot_nn(a, b):
    return jnp.dot(a, b, preferred_element_type=jnp.float32)


def dot_nt(a, b):
    return lax.dot_general(a, b, (((1,), (1,)), ((), ())), preferred_element_type=jnp.float32)


def dot_tn(a, b):
    return lax.dot_general(a, b, (((0,), (0,)), ((), ())), preferred_element_type=jnp.float32)


def low(v):
    return v.astype(jnp.bfloat16)


def wide(v):
    return v.astype(jnp.float32)


def lanes(start, size):
    return pl.ds(pl.multiple_of(start, 128), size)


def arrive(ref, sem):
    me = (lax.axis_index(WIDE), lax.axis_index(DEPTH))
    remote(ref, ref, sem, sem, me).wait_recv()


def left(ref, sem):
    me = (lax.axis_index(WIDE), lax.axis_index(DEPTH))
    remote(ref, ref, sem, sem, me).wait_send()


def forward_refs(
    tok_h,
    cot_h,
    lim_h,
    wq,
    wk,
    wv,
    wo,
    wi,
    wu,
    rel_h,
    small_h,
    basis_h,
    flip_h,
    p_h,
    cq_h,
    pq_h,
    k_h,
    v_h,
    rr_h,
    hid_h,
    act_h,
    slope_h,
    od_h,
    nn_h,
    nm_h,
    mx_h,
    fq,
    fk,
    fv,
    fo,
    fi0,
    fi1,
    fu0,
    fu1,
    vec_h,
    gu0,
    gu1,
    sums_h,
    q,
    k,
    v,
    o,
    i0,
    i1,
    rel,
    small,
    vec,
    tok,
    normed,
    cq,
    pq,
    kr,
    vr,
    basis,
    flip,
    rk,
    rr,
    p,
    mixed,
    hidden,
    nmid,
    cot,
    od,
    odc,
    act,
    slope,
    gst,
    sums,
    zr,
    zs,
    xr,
    yr,
    fxr,
    fyr,
    sr,
    snd,
    own,
    ld,
    mr,
    ms,
    ps,
    pr,
    st,
    gs,
):
    return types.SimpleNamespace(**locals())


def forward_kernel(*refs):
    t = forward_refs(*refs)
    at = position()
    w, z, c, p = at.w, at.z, at.c, at.p
    depth = [(w, lax.rem(z + d, NARROW)) for d in range(1, NARROW)]
    meet([at.sib, at.xn, at.yn] + depth)
    rows_all = t.tok.shape[0]
    width = t.tok.shape[1]

    keys_all = H * KEY
    quarter = width // 4
    plan = (
        (t.wq, 0, 0, t.fq, keys_all),
        (t.wk, 0, 0, t.fk, keys_all),
        (t.wv, 0, 0, t.fv, width),
        (t.wo, 0, 0, t.fo, width),
        (t.wi, 0, 0, t.fi0, width),
        (t.wi, 0, width, t.fi1, width),
        (t.wu, 0, 0, t.fu0, width),
        (t.wu, quarter, 0, t.fu1, width),
    )

    def rows_of(m, pp, part=None):
        rows = quarter // 4
        start = pp * rows
        if part is not None:
            rows = rows // 2
            start = start + part * rows
        return start, rows

    def block(m, zz, pp, part=None):
        start, rows = rows_of(m, pp, part)
        cols = plan[m][4] // 2
        return plan[m][3].at[zz, pl.ds(pl.multiple_of(start, 16), rows), lanes(c * cols, cols)]

    def send(m, ref, recv, target):
        remote(ref, ref, t.snd.at[m], recv, target).start()

    loads = [
        pltpu.make_async_copy(src, dst, t.ld.at[k])
        for k, (src, dst) in enumerate(
            (
                (t.tok_h, t.tok),
                (t.small_h, t.small.at[z]),
                (t.rel_h, t.rel.at[z]),
                (t.basis_h, t.basis),
                (t.cot_h, t.cot),
                (t.flip_h, t.flip),
            )
        )
    ]
    def over_z(k, src, dst):
        for d in (1, 3, 2):
            remote(src, dst.at[z], t.ms.at[k], t.mr.at[k], depth[d - 1]).start()

    over_z(0, t.small_h, t.small)
    for copy in loads:
        copy.start()

    above, below = (w, jnp.minimum(z + 1, NARROW - 1)), (w, jnp.maximum(z - 1, 0))
    can_rise, can_sink = z < NARROW - 1, z > 0

    def own_piece(m):
        shard, r0, c0, _, span = plan[m]
        start, rows = rows_of(m, p)
        cols = span // 2
        return shard.at[pl.ds(pl.multiple_of(r0 + start, 16), rows), lanes(c0 + c * cols, cols)]

    def depart(m):
        @pl.when(can_rise)
        def _():
            remote(
                own_piece(m), block(m, z, p), t.zs.at[m, 3], t.zr.at[m, 0], above
            ).start()

        @pl.when(can_sink)
        def _():
            remote(
                own_piece(m), block(m, z, p), t.zs.at[m, 4], t.zr.at[m, 2], below
            ).start()

    def hop(k):
        first, last = z == 0, z == NARROW - 1
        if k == 0:
            return jnp.where(first, 3, 1)
        if k == 1:
            return jnp.where(first | last, 2, 3)
        return jnp.where(first, 1, jnp.where(last, 3, 2))

    def source(k):
        return lax.rem(z + NARROW - hop(k), NARROW)

    def relay(m, k):
        d = hop(k)
        mine = block(m, source(k), p)
        rise = can_rise & (d <= z)
        sink = can_sink & (d > z)
        return mine, d, rise, sink

    def spread(m, k):
        mine, d, rise, sink = relay(m, k)
        arrive(mine, t.zr.at[m, d - 1])

        @pl.when(rise)
        def _():
            remote(mine, mine, t.zs.at[m, k], t.zr.at[m, jnp.minimum(d, 2)], above).start()

        @pl.when(sink)
        def _():
            remote(mine, mine, t.zs.at[m, k], t.zr.at[m, jnp.maximum(d - 2, 0)], below).start()

        send(m, mine, t.xr.at[m, k], at.xn)
        send(m, mine, t.yr.at[m, k], at.yn)
        send(m, mine, t.sr.at[m], at.sib)

    def forward(m, k):
        zz = source(k)
        arrive(block(m, zz, at.px), t.xr.at[m, k])
        send(m, block(m, zz, at.px, 0), t.fxr.at[m, k], at.yn)
        send(m, block(m, zz, at.px), t.sr.at[m], at.sib)
        arrive(block(m, zz, at.py), t.yr.at[m, k])
        send(m, block(m, zz, at.py, 1), t.fyr.at[m, k], at.xn)
        send(m, block(m, zz, at.py), t.sr.at[m], at.sib)

    def finish(m, k):
        zz = source(k)
        arrive(block(m, zz, at.pd, 0), t.fxr.at[m, k])
        arrive(block(m, zz, at.pd, 1), t.fyr.at[m, k])
        send(m, block(m, zz, at.pd), t.sr.at[m], at.sib)

    depart(2)
    depart(0)
    over_z(1, t.rel_h, t.rel)
    def all_here(m):
        arrive(plan[m][3].at[pl.ds(0, 3), :, pl.ds(0, plan[m][4] // 2)], t.sr.at[m])

    def fetch(m, held):
        all_here(m)
        shard, r0, c0, full, span = plan[m]
        copies = [
            pltpu.make_async_copy(
                shard.at[pl.ds(r0, quarter), pl.ds(c0, span)], held.at[z], t.own.at[m, 0]
            )
        ]
        for d in range(1, NARROW):
            zz = lax.rem(z + d, NARROW)
            copies.append(pltpu.make_async_copy(full.at[zz], held.at[zz], t.own.at[m, d]))
        for copy in copies:
            copy.start()
        return copies

    def use(copies):
        for copy in copies:
            copy.wait()

    def vectors():
        loads[1].wait()
        arrive(t.small.at[pl.ds(0, 3)], t.mr.at[0])
        for zz in range(NARROW):
            rows = wide(t.small[zz])
            for r in range(6):
                t.vec[r : r + 1, zz * 384 : (zz + 1) * 384] = rows[r : r + 1, 0:384]
            for r in range(2):
                spot = slice(zz * 768 + r * 384, zz * 768 + (r + 1) * 384)
                t.vec[6:7, spot] = rows[6 + r : 7 + r, 0:384]
                t.vec[7 + r : 8 + r, zz * 128 : (zz + 1) * 128] = rows[r : r + 1, 384:512]

    def norm_rows(src, dst, gain_row):
        def one(i, _):
            rows = pl.ds(pl.multiple_of(i * 32, 32), 32)
            v = wide(src[rows, :])
            center = v - jnp.mean(v, axis=1, keepdims=True)
            var = jnp.mean(center * center, axis=1, keepdims=True)
            gain = t.vec[gain_row : gain_row + 1, 0:width]
            shift = t.vec[gain_row + 1 : gain_row + 2, 0:width]
            dst[rows, :] = low(center * lax.rsqrt(var + EPSILON) * gain + shift)
            return 0

        lax.fori_loop(0, rows_all // 32, one, 0)

    def flat(full):
        return full[...].reshape(full.shape[0] * full.shape[1], full.shape[2])

    def columns(full, start, size):
        part = full[:, :, lanes(start, size)]
        return part.reshape(full.shape[0] * full.shape[1], size)

    def make_queries():
        queries = dot_nn(t.normed[...], flat(t.q)) * (KEY ** (-0.5))
        size = H * KEY
        t.cq[...] = low(queries + t.vec[7:8, 0:size])
        t.pq[...] = low(queries + t.vec[8:9, 0:size])

    def make_keys():
        t.kr[...] = low(dot_nn(t.normed[...], flat(t.k)))
        loads[2].wait()
        arrive(t.rel.at[pl.ds(0, 3)], t.mr.at[1])
        loads[3].wait()
        table = t.rel[...].reshape(t.rel.shape[0] * t.rel.shape[1], t.rel.shape[2])
        t.rk[...] = low(dot_nn(t.basis[...], table))
        loads[5].wait()
        t.rr[...] = low(dot_nn(t.flip[...], table))

    def make_values():
        def one(n, _):
            t.vr[:, lanes(n * 512, 512)] = low(dot_nn(t.normed[...], columns(t.v, n * 512, 512)))
            return 0

        lax.fori_loop(0, 3, one, 0)

    def pair_mask(size, split):
        return lax.broadcasted_iota(jnp.int32, (rows_all, size), 1) < split

    def heads(pair):
        qs = slice(pair * 2 * KEY, (pair + 1) * 2 * KEY)
        vs = slice(pair * 2 * VAL, (pair + 1) * 2 * VAL)
        first = pair_mask(2 * KEY, KEY)
        keys, rel, vals = t.kr[:, qs], t.rk[:, qs], t.vr[:, vs]
        mixed = []
        for side in range(2):
            keep = first if side == 0 else jnp.logical_not(first)
            cq = jnp.where(keep, t.cq[:, qs], jnp.zeros_like(t.cq[:, qs]))
            pq = jnp.where(keep, t.pq[:, qs], jnp.zeros_like(t.pq[:, qs]))
            raw = dot_nt(pq, rel)
            shifted = pltpu.roll(raw, rows_all + 1, axis=1, stride=1, stride_axis=0)
            logits = dot_nt(cq, keys) + shifted[:, :rows_all]
            grown = jnp.exp(logits - jnp.max(logits, axis=1, keepdims=True))
            soft = low(grown / jnp.sum(grown, axis=1, keepdims=True))
            t.p[2 * pair + side] = soft
            mixed.append(dot_nn(soft, vals))
        t.mixed[:, vs] = low(jnp.where(pair_mask(2 * VAL, VAL), mixed[0], mixed[1]))

    def give(k, src, dst):
        remote(src, dst, t.ps.at[k], t.pr.at[k], at.sib).start()

    stored = []

    def store(src, dst):
        copy = pltpu.make_async_copy(src, dst, t.st.at[len(stored)])
        copy.start()
        stored.append(copy)

    def attend_out():
        def one(n, _):
            cols = lanes(n * 512, 512)
            t.hidden[:, cols] = (
                wide(t.tok[:, cols])
                + dot_nn(t.mixed[...], columns(t.o, n * 512, 512))
                + t.vec[2:3, cols]
            )
            return 0

        lax.fori_loop(0, 3, one, 0)
        norm_rows(t.hidden, t.nmid, 3)
        give(2, t.nmid, t.nm_h.at[1])

    def clip_rows():
        loads[4].wait()

        def one(i, total):
            rows = pl.ds(pl.multiple_of(i * 32, 32), 32)
            clipped = low(clip(i * 32, wide(t.cot[rows, :])))
            t.od[rows, :] = clipped
            return total + jnp.sum(wide(clipped), axis=0, keepdims=True)

        total = lax.fori_loop(0, rows_all // 32, one, jnp.zeros((1, width), jnp.float32))
        t.sums[5:6, 0:width] = total
        half = width // 2
        t.odc[0] = t.od[:, lanes(c * half, half)]
        give(0, t.od.at[:, lanes((1 - c) * half, half)], t.odc.at[1])

    def clip(row, values):
        limit = jnp.where(row < WIN, t.lim_h[0, 0], t.lim_h[0, 1])
        return jnp.minimum(jnp.maximum(values, -limit), limit)

    def inner(h):
        full = (t.i0, t.i1)[h]

        def one(n, _):
            local = n * 256
            cols = lanes(h * width + local, 256)
            pre = dot_nn(t.nmid[...], columns(full, local, 256)) + t.vec[6:7, cols]
            cdf = 0.5 + 0.5 * lax.erf(pre * (0.5**0.5))
            slope = cdf + pre * jnp.exp(-0.5 * pre * pre) * (2.0 * math.pi) ** -0.5
            t.act[0, :, cols] = low(pre * cdf)
            t.slope[:, cols] = low(slope)
            return 0

        lax.fori_loop(0, 6, one, 0)
        cols = pl.ds(h * width, width)
        give(3 + h, t.act.at[0, :, cols], t.act.at[1, :, cols])

    def outer_product(left_ref, right_ref, dst, start, size):
        steps = left_ref.shape[2] // 256
        right = right_ref[:, :, start : start + size].reshape(2 * rows_all, size)

        def tile(slot, n):
            return pltpu.make_async_copy(
                t.gst.at[slot, :, 0:size],
                dst.at[pl.ds(pl.multiple_of(n * 256, 256), 256)],
                t.gs.at[slot],
            )

        def one(n, _):
            slot = lax.rem(n, 2)

            @pl.when(n >= 2)
            def _():
                tile(slot, n - 2).wait()

            lhs = left_ref[:, :, lanes(n * 256, 256)].reshape(2 * rows_all, 256)
            t.gst[slot, :, 0:size] = low(dot_tn(lhs, right))
            tile(slot, n).start()
            return 0

        lax.fori_loop(0, steps, one, 0)
        tile(0, steps - 2).wait()
        tile(1, steps - 1).wait()

    t.sums[...] = jnp.zeros_like(t.sums)
    t.vec[...] = jnp.zeros_like(t.vec)
    here = {}
    spread(2, 0)
    spread(2, 1)
    spread(0, 0)
    depart(1)
    spread(0, 1)
    spread(2, 2)
    spread(0, 2)
    spread(1, 0)
    depart(3)
    spread(1, 1)
    spread(1, 2)
    forward(0, 2)
    forward(2, 0)
    depart(5)
    forward(0, 0)
    depart(4)
    forward(2, 2)
    forward(0, 1)
    loads[0].wait()
    vectors()
    norm_rows(t.tok, t.normed, 0)
    give(1, t.normed, t.nn_h.at[1])
    store(t.normed, t.nn_h.at[0])
    store(t.vec, t.vec_h)
    clip_rows()
    store(t.od, t.od_h)
    forward(1, 0)
    forward(1, 1)
    forward(1, 2)
    spread(3, 0)
    forward(2, 1)
    finish(2, 2)
    finish(0, 2)
    finish(0, 0)
    finish(0, 1)
    spread(3, 1)
    here[0] = fetch(0, t.q)
    finish(1, 1)
    spread(5, 0)
    use(here[0])
    make_queries()
    store(t.cq, t.cq_h)
    store(t.pq, t.pq_h)
    finish(1, 2)
    spread(5, 1)
    finish(2, 0)
    finish(1, 0)
    here[1] = fetch(1, t.k)
    use(here[1])
    make_keys()
    store(t.kr, t.k_h)
    store(t.rr, t.rr_h)
    finish(2, 1)
    here[2] = fetch(2, t.v)
    spread(3, 2)
    use(here[2])
    make_values()
    store(t.vr, t.v_h)
    forward(3, 1)
    forward(3, 0)
    spread(5, 2)
    spread(4, 0)
    depart(7)
    heads(0)
    spread(4, 1)
    finish(3, 1)
    depart(6)
    heads(1)
    spread(4, 2)
    forward(3, 2)
    finish(3, 0)
    spread(7, 0)
    heads(2)
    forward(5, 2)
    forward(4, 1)
    forward(4, 0)
    forward(5, 0)
    forward(4, 2)
    forward(5, 1)
    spread(6, 0)
    spread(6, 1)
    heads(3)
    store(t.p, t.p_h)
    give(5, t.mixed, t.mx_h.at[1])
    store(t.mixed, t.mx_h.at[0])
    finish(3, 2)
    here[3] = fetch(3, t.o)
    spread(6, 2)
    use(here[3])
    attend_out()
    store(t.hidden, t.hid_h)
    store(t.nmid, t.nm_h.at[0])
    finish(4, 0)
    finish(5, 0)
    finish(4, 1)
    finish(4, 2)
    here[4] = fetch(4, t.i0)
    spread(7, 1)
    use(here[4])
    inner(0)
    finish(5, 2)
    forward(7, 0)
    spread(7, 2)
    forward(6, 2)
    finish(5, 1)
    here[5] = fetch(5, t.i1)
    forward(6, 0)
    use(here[5])
    inner(1)
    store(t.act.at[0], t.act_h)
    store(t.slope, t.slope_h)
    finish(7, 0)
    forward(7, 1)
    forward(6, 1)
    arrive(t.odc.at[1], t.pr.at[0])
    for h in range(2):
        arrive(t.act.at[1, :, pl.ds(0, width)], t.pr.at[3 + h])
    outer_product(t.act, t.odc, t.gu0, 0, 384)
    forward(7, 2)
    outer_product(t.act, t.odc, t.gu1, 384, 384)
    store(t.sums, t.sums_h)
    finish(6, 2)
    finish(6, 1)
    finish(6, 0)
    finish(7, 1)
    finish(7, 2)
    all_here(6)
    all_here(7)

    arrive(t.nn_h.at[1], t.pr.at[1])
    arrive(t.nm_h.at[1], t.pr.at[2])
    arrive(t.mx_h.at[1], t.pr.at[5])
    left(t.odc.at[1], t.ps.at[0])
    left(t.normed, t.ps.at[1])
    left(t.nmid, t.ps.at[2])
    for h in range(2):
        left(t.act.at[0, :, pl.ds(0, width)], t.ps.at[3 + h])
    left(t.mixed, t.ps.at[5])
    for k, full in enumerate((t.small, t.rel)):
        left(full.at[pl.ds(0, 3)], t.ms.at[k])
    for m in range(len(plan)):
        mine = block(m, z, p)
        for k in range(3):
            _, _, rise, sink = relay(m, k)

            @pl.when(rise | sink)
            def _():
                left(mine, t.zs.at[m, k])

        @pl.when(can_rise)
        def _():
            left(mine, t.zs.at[m, 3])

        @pl.when(can_sink)
        def _():
            left(mine, t.zs.at[m, 4])

        full, cols = plan[m][3], plan[m][4] // 2
        left(full.at[pl.ds(0, 3), :, pl.ds(0, cols)], t.snd.at[m])
        left(full.at[pl.ds(0, 3), pl.ds(0, 3 * quarter // 4), pl.ds(0, cols)], t.snd.at[m])
    for copy in stored:
        copy.wait()


def forward_pass(tokens, cotangent, limits, shards, rel, small, basis, flip):
    rows, width = tokens.shape
    bf, f32 = jnp.bfloat16, jnp.float32
    keys = H * KEY
    quarter = width // 4
    full = ((NARROW, quarter, width), bf)
    thin = ((NARROW, quarter, keys), bf)
    out_shape = (
        ((H, rows, rows), bf),
        ((rows, keys), bf),
        ((rows, keys), bf),
        ((rows, keys), bf),
        ((rows, width), bf),
        ((2 * rows, keys), bf),
        ((rows, width), f32),
        ((rows, 2 * width), bf),
        ((rows, 2 * width), bf),
        ((rows, width), bf),
        ((2, rows, width), bf),
        ((2, rows, width), bf),
        ((2, rows, width), bf),
        thin,
        thin,
        full,
        full,
        full,
        full,
        full,
        full,
        ((16, 2 * width), f32),
        ((2 * width, width // 4), bf),
        ((2 * width, width // 4), bf),
        ((8, 2 * width), f32),
    )
    vmem = (
        thin,
        thin,
        full,
        full,
        full,
        full,
        ((NARROW,) + rel.shape, bf),
        ((NARROW,) + small.shape, bf),
        ((16, 2 * width), f32),
        ((rows, width), bf),
        ((rows, width), bf),
        ((rows, keys), bf),
        ((rows, keys), bf),
        ((rows, keys), bf),
        ((rows, width), bf),
        (basis.shape, bf),
        (flip.shape, bf),
        ((2 * rows, keys), bf),
        ((2 * rows, keys), bf),
        ((H, rows, rows), bf),
        ((rows, width), bf),
        ((rows, width), f32),
        ((rows, width), bf),
        ((rows, width), bf),
        ((rows, width), bf),
        ((2, rows, width // 2), bf),
        ((2, rows, 2 * width), bf),
        ((rows, 2 * width), bf),
        ((2, rows, width // 2), bf),
        ((8, 2 * width), f32),
    )
    sems = [
        DMA((8, 3)),
        DMA((8, 5)),
        DMA((8, 3)),
        DMA((8, 3)),
        DMA((8, 3)),
        DMA((8, 3)),
        DMA((8,)),
        DMA((8,)),
        DMA((8, 4)),
        DMA((7,)),
        DMA((2,)),
        DMA((2,)),
        DMA((6,)),
        DMA((6,)),
        DMA((20,)),
        DMA((2,)),
    ]
    ins = (tokens, cotangent, limits, *shards, rel, small, basis, flip)
    return pl.pallas_call(
        forward_kernel,
        out_shape=tuple(jax.ShapeDtypeStruct(s, d) for s, d in out_shape),
        in_specs=[HBM, HBM, SMEM] + [HBM] * (len(ins) - 3),
        out_specs=(HBM,) * len(out_shape),
        scratch_shapes=[pltpu.VMEM(s, d) for s, d in vmem] + sems,
        compiler_params=pltpu.CompilerParams(
            collective_id=1, has_side_effects=True, vmem_limit_bytes=60 << 20
        ),
        name="forward_pass",
    )(*ins)


UNITS = 8
CHAINS = (0, 3)


def backward_refs(
    gu0,
    gu1,
    p_h,
    cq_h,
    pq_h,
    k_h,
    v_h,
    rr_h,
    hid_h,
    act_h,
    slope_h,
    od_h,
    nn_h,
    nm_h,
    mx_h,
    fq,
    fk,
    fv,
    fo,
    fi0,
    fi1,
    fu0,
    fu1,
    wq,
    wk,
    wv,
    wo,
    wi,
    wu,
    tok_h,
    cot_h,
    lim_h,
    vec_h,
    sums_h,
    flipt_h,
    turn_h,
    ou,
    oi,
    oo,
    ov,
    ok,
    oq,
    out_h,
    tg_h,
    e_h,
    rg_h,
    gi0,
    gi1,
    go,
    gv,
    gk,
    gq,
    s0,
    s1,
    p,
    cq,
    pq,
    kr,
    vr,
    rr,
    hid,
    act,
    slope,
    od,
    cat,
    idc,
    cot,
    vec,
    sums,
    flipt,
    turn,
    bdc,
    qdc,
    kdc,
    vdc,
    nd,
    rg,
    rgk,
    rgg,
    rgs,
    rgo,
    eb,
    ek,
    eg,
    es,
    eo,
    ld,
    own,
    s1s,
    r1,
    l1,
    s2,
    r2,
    s3,
    r3,
    s4,
    r4,
    lo,
    zu,
    zd,
    zs,
    ps,
    pr,
    xs,
    xr,
    ws,
    wr,
    st,
):
    return types.SimpleNamespace(**locals())


def backward_kernel(*refs):
    head = 46
    held = 2
    t = backward_refs(*refs[:head], *refs[head + held + 4 * UNITS :])
    spare = refs[head : head + held + 4 * UNITS]
    keep = spare[:held]
    got1, got2, got3, last = (
        spare[held + k * UNITS : held + (k + 1) * UNITS] for k in range(4)
    )
    at = position()
    w, z, c, p, x, y = at.w, at.z, at.c, at.p, at.x, at.y
    depth = [(w, lax.rem(z + d, NARROW)) for d in range(1, NARROW)]
    rows_all, width = t.cot.shape
    meet([at.sib, at.xn, at.yn] + depth)

    plan = (
        (t.gu0, False, t.ou, 0, width // 2),
        (t.gu1, False, t.ou, width // 4, width // 2),
        (t.gi0, True, t.oi, 0, width),
        (t.gi1, True, t.oi, width // 2, width),
        (t.go, True, t.oo, 0, width // 2),
        (t.gv, True, t.ov, 0, width // 2),
        (t.gk, True, t.ok, 0, H * KEY // 2),
        (t.gq, True, t.oq, 0, H * KEY // 2),
    )

    def half(m, h, mine):
        g = plan[m][0]
        if h == 0:
            return g.at[:, :, x if mine else 1 - x, 0]
        return g.at[:, y if mine else 1 - y, :, 1]

    def stage1(m):
        for h, target in ((0, at.xn), (1, at.yn)):
            remote(half(m, h, False), got1[m].at[h], t.s1s.at[m, h], t.r1.at[m, h], target).start()
            if not plan[m][1]:
                pltpu.make_async_copy(half(m, h, True), keep[m].at[h], t.l1.at[m, h]).start()

    def kept(m, h, zz, o):
        if not plan[m][1]:
            return keep[m].at[h, zz, o]
        if h == 0:
            return plan[m][0].at[zz, o, x, 0]
        return plan[m][0].at[zz, y, o, 1]

    def stage2(m):
        for h, target, mine in ((0, at.yn, y), (1, at.xn, x)):
            arrive(got1[m].at[h], t.r1.at[m, h])
            if not plan[m][1]:
                arrive(keep[m].at[h], t.l1.at[m, h])

            def add(k, _, h=h):
                zz, o = lax.div(k, 2), lax.rem(k, 2)
                spot = kept(m, h, zz, o)
                spot[...] = low(wide(spot[...]) + wide(got1[m][h, zz, o]))
                return 0

            lax.fori_loop(0, 2 * NARROW, add, 0)
            every = pl.ds(0, NARROW)
            remote(
                kept(m, h, every, 1 - mine), got2[m].at[h], t.s2.at[m, h], t.r2.at[m, h], target
            ).start()

    def stage3(m):
        for h, mine in ((0, y), (1, x)):
            arrive(got2[m].at[h], t.r2.at[m, h])

            def add(zz, _, h=h, mine=mine):
                got2[m][h, zz] = low(wide(kept(m, h, zz, mine)[...]) + wide(got2[m][h, zz]))
                return 0

            lax.fori_loop(0, NARROW, add, 0)
        for d in (1, 3, 2):
            zz = lax.rem(z + d, NARROW)
            remote(
                got2[m].at[:, zz],
                got3[m].at[d - 1],
                t.s3.at[m, d - 1],
                t.r3.at[m, d - 1],
                depth[d - 1],
            ).start()

    def piece(m, pp, part=None):
        _, _, out, start, span = plan[m]
        rows, cols = out.shape[0] // 4, last[m].shape[1]
        first = pp * rows
        if part is not None:
            rows = rows // 2
            first = first + part * rows
        return out.at[pl.ds(pl.multiple_of(first, 16), rows), lanes(c * span + start, cols)]

    def stage4(m):
        for d in (1, 3, 2):
            arrive(got3[m].at[d - 1], t.r3.at[m, d - 1])
        rows = last[m].shape[0] // 2
        for h in range(2):
            total = wide(got2[m][h, z])
            for d in range(3):
                total = total + wide(got3[m][d, h])
            last[m][h * rows : (h + 1) * rows, :] = low(total)
        share(m)

    def share(m):
        mine = piece(m, p)
        remote(last[m], mine, t.s4.at[m], t.r4.at[m, 0], at.xn).start()
        remote(last[m], mine, t.s4.at[m], t.r4.at[m, 1], at.yn).start()
        remote(last[m], mine, t.s4.at[m], t.r4.at[m, 4], at.sib).start()
        pltpu.make_async_copy(last[m], mine, t.lo.at[m]).start()

    def stage5(m):
        for pp, part, slot, target in ((at.px, 0, 0, at.yn), (at.py, 1, 1, at.xn)):
            arrive(piece(m, pp), t.r4.at[m, slot])
            some = piece(m, pp, part)
            remote(some, some, t.s4.at[m], t.r4.at[m, 2 + slot], target).start()
            some = piece(m, pp)
            remote(some, some, t.s4.at[m], t.r4.at[m, 4], at.sib).start()

    def stage6(m):
        arrive(piece(m, at.pd, 0), t.r4.at[m, 2])
        arrive(piece(m, at.pd, 1), t.r4.at[m, 3])
        some = piece(m, at.pd)
        remote(some, some, t.s4.at[m], t.r4.at[m, 4], at.sib).start()

    above, under = (w, jnp.minimum(z + 1, NARROW - 1)), (w, jnp.maximum(z - 1, 0))
    top = NARROW - 1

    def chain_start(m):
        g, room = plan[m][0], got1[m]
        bring(m, 0, rise_to(1))
        bring(m, 1, sink_to(1))

        @pl.when(z == 0)
        def _():
            for i in range(top):
                there = top - i
                remote(
                    g.at[there], room.at[there], t.zs.at[m, i], t.zu.at[m, there], above
                ).start()

        @pl.when(z == top)
        def _():
            for i in range(top):
                spot = NARROW if i == top - 1 else i
                remote(g.at[i], room.at[spot], t.zs.at[m, i], t.zd.at[m, i], under).start()

    def bring(m, spot, there):
        if not plan[m][1]:
            pltpu.make_async_copy(
                plan[m][0].at[there], keep[m].at[spot], t.l1.at[m, spot]
            ).start()

    def brought(m, spot):
        if not plan[m][1]:
            pltpu.make_async_copy(keep[m].at[spot], keep[m].at[spot], t.l1.at[m, spot]).wait()

    def own_part(m, spot, there):
        return plan[m][0].at[there] if plan[m][1] else keep[m].at[spot]

    def join(m, spot, there):
        own = own_part(m, spot, there)

        def add(k, _):
            a, b, h = lax.div(k, 4), lax.rem(lax.div(k, 2), 2), lax.rem(k, 2)
            got1[m][there, a, b, h] = low(wide(got1[m][there, a, b, h]) + wide(own[a, b, h]))
            return 0

        lax.fori_loop(0, 8, add, 0)

    def rising(slot):
        return (z >= 1) & (z <= slot)

    def sinking(slot):
        return (z < top) & (z >= top - slot)

    def rise_to(slot):
        return jnp.minimum(top + z - slot, top)

    def sink_to(slot):
        return jnp.maximum(slot - top + z, 0)

    def chain_step(m, slot):
        room = got1[m]
        brought(m, 0)
        brought(m, 1)

        @pl.when(rising(slot))
        def _():
            there = rise_to(slot)
            arrive(room.at[there], t.zu.at[m, there])
            join(m, 0, there)
            remote(
                room.at[there], room.at[there], t.zs.at[m, 2 + slot], t.zu.at[m, there], above
            ).start()

        @pl.when(sinking(slot))
        def _():
            there = sink_to(slot)
            arrive(room.at[there], t.zd.at[m, there])
            join(m, 1, there)
            spot = NARROW if slot == 2 else there
            remote(
                room.at[there], room.at[spot], t.zs.at[m, 4 + slot], t.zd.at[m, there], under
            ).start()

        if slot == 1:
            bring(m, 0, rise_to(2))
            bring(m, 1, sink_to(2))
        else:
            bring(m, 0, z)

    def chain_end(m):
        room = got1[m]
        brought(m, 0)

        @pl.when(z > 0)
        def _():
            arrive(room.at[z], t.zu.at[m, z])
            join(m, 0, z)

        @pl.when(z < top)
        def _():
            arrive(room.at[NARROW], t.zd.at[m, z])

        def add(k, _, fresh=False):
            a, b, h = lax.div(k, 4), lax.rem(lax.div(k, 2), 2), lax.rem(k, 2)
            own = own_part(m, 0, z)[a, b, h] if fresh else room[z, a, b, h]
            room[z, a, b, h] = low(wide(own) + wide(room[NARROW, a, b, h]))
            return 0

        @pl.when((z > 0) & (z < top))
        def _():
            lax.fori_loop(0, 8, add, 0)

        @pl.when(z == 0)
        def _():
            lax.fori_loop(0, 8, functools.partial(add, fresh=True), 0)

        remote(
            room.at[z, :, 1 - x, 0], got2[m].at[0], t.s1s.at[m, 0], t.r1.at[m, 0], at.xn
        ).start()
        remote(
            room.at[z, 1 - y, :, 1], got2[m].at[1], t.s1s.at[m, 1], t.r1.at[m, 1], at.yn
        ).start()

    def chain_plane(m):
        room = got1[m]
        for h, target in ((0, at.yn), (1, at.xn)):
            arrive(got2[m].at[h], t.r1.at[m, h])
            for o in range(2):
                spot = room.at[z, o, x, 0] if h == 0 else room.at[z, y, o, 1]
                spot[...] = low(wide(spot[...]) + wide(got2[m][h, o]))
            away = room.at[z, 1 - y, x, 0] if h == 0 else room.at[z, y, 1 - x, 1]
            remote(away, got3[m].at[h], t.s2.at[m, h], t.r2.at[m, h], target).start()

    def chain_last(m):
        rows = last[m].shape[0] // 2
        for h in range(2):
            arrive(got3[m].at[h], t.r2.at[m, h])
            last[m][h * rows : (h + 1) * rows, :] = low(
                wide(got1[m][z, y, x, h]) + wide(got3[m][h])
            )
        share(m)

    sources = (
        (t.act_h, t.act),
        (t.od_h, t.od),
        (t.slope_h, t.slope),
        (t.hid_h, t.hid),
        (t.vec_h, t.vec),
        (t.sums_h, t.sums),
        (t.cot_h, t.cot),
        (t.nm_h, t.cat),
        (t.p_h, t.p),
        (t.v_h, t.vr),
        (t.k_h, t.kr),
        (t.cq_h, t.cq),
        (t.pq_h, t.pq),
        (t.rr_h, t.rr),
        (t.turn_h, t.turn),
        (t.flipt_h, t.flipt),
        (t.tok_h, t.cot),
        (t.mx_h, t.cat),
        (t.nn_h, t.idc),
    )
    quarter = width // 4

    def fetch(k, full, shard, held, row=0, col=0):
        span = held.shape[2]
        copies = [
            pltpu.make_async_copy(
                shard.at[pl.ds(row, quarter), pl.ds(col, span)], held.at[z], t.own.at[k, 0]
            )
        ]
        for d in range(1, NARROW):
            zz = lax.rem(z + d, NARROW)
            copies.append(pltpu.make_async_copy(full.at[zz], held.at[zz], t.own.at[k, d]))
        for copy in copies:
            copy.start()
        return copies

    def use(copies):
        for copy in copies:
            copy.wait()

    here0 = fetch(0, t.fu0, t.wu, t.s0)
    here1 = fetch(1, t.fu1, t.wu, t.s1, row=quarter)
    loads = [pltpu.make_async_copy(s, d, t.ld.at[k]) for k, (s, d) in enumerate(sources)]
    for k in (*range(9), *range(10, 16)):
        loads[k].start()

    def give(k, src, dst):
        remote(src, dst, t.ps.at[k], t.pr.at[k], at.sib).start()

    def clip(row, values):
        limit = jnp.where(row < WIN, t.lim_h[0, 0], t.lim_h[0, 1])
        return jnp.minimum(jnp.maximum(values, -limit), limit)

    def leave_mlp(h):
        full = (t.s0, t.s1)[h]
        spots = [
            slice(2 * quarter * zz + quarter * h, 2 * quarter * zz + quarter * (h + 1))
            for zz in range(NARROW)
        ]
        active = jnp.concatenate([t.act[:, spot] for spot in spots], axis=1)

        def one(n, _):
            cols = lanes(n * 512, 512)
            part = dot_nn(active, full[:, :, cols].reshape(width, 512))
            if h == 0:
                t.nd[:, cols] = t.hid[:, cols] + part + t.vec[5:6, cols]
            else:
                t.vr[:, cols] = low(t.nd[:, cols] + part)
            return 0

        lax.fori_loop(0, 3, one, 0)
        for zz, spot in enumerate(spots):
            delta = low(dot_nt(t.od[...], full[zz]) * wide(t.slope[:, spot]))
            t.act[:, spot] = delta
            t.sums[6:7, spot] = jnp.sum(wide(delta), axis=0, keepdims=True)

    def pull_mid():
        for zz in range(NARROW):
            t.nd[:, zz * quarter : (zz + 1) * quarter] = dot_nt(
                t.act[:, 0:width], t.s0[zz]
            ) + dot_nt(t.act[:, width : 2 * width], t.s1[zz])

        def one(i, carry):
            gain_total, shift_total, bias_total = carry
            rows = pl.ds(pl.multiple_of(i * 32, 32), 32)
            v = t.hid[rows, :]
            center = v - jnp.mean(v, axis=1, keepdims=True)
            scale = lax.rsqrt(jnp.mean(center * center, axis=1, keepdims=True) + EPSILON)
            n = center * scale
            delta = t.nd[rows, :]
            e = delta * t.vec[3:4, 0:width]
            back = scale * (
                e
                - jnp.mean(e, axis=1, keepdims=True)
                - n * jnp.mean(e * n, axis=1, keepdims=True)
            )
            full = clip(i * 32, wide(t.cot[rows, :])) + back
            t.hid[rows, :] = full
            rounded = low(full)
            bd[rows, :] = rounded
            return (
                gain_total + jnp.sum(delta * n, axis=0, keepdims=True),
                shift_total + jnp.sum(delta, axis=0, keepdims=True),
                bias_total + jnp.sum(wide(rounded), axis=0, keepdims=True),
            )

        zero = jnp.zeros((1, width), jnp.float32)
        gain_total, shift_total, bias_total = lax.fori_loop(
            0, rows_all // 32, one, (zero, zero, zero)
        )
        t.sums[3:4, 0:width] = gain_total
        t.sums[4:5, 0:width] = shift_total
        t.sums[2:3, 0:width] = bias_total
        half = width // 2
        give(1, bd.at[:, lanes((1 - c) * half, half)], t.bdc.at[1])
        t.bdc[0] = bd[:, lanes(c * half, half)]

    def pull_mixed():
        for zz in range(NARROW):
            md[:, zz * quarter : (zz + 1) * quarter] = low(dot_nt(bd[...], t.s0[zz]))

    bd = t.slope.at[:, 0:width]
    md = t.od
    vd = t.act.at[:, 0:width]
    qd = t.act.at[:, width : width + H * KEY]
    kd = t.act.at[:, width + H * KEY : width + 2 * H * KEY]

    def lane_mask(size, split, rows=rows_all):
        return lax.broadcasted_iota(jnp.int32, (rows, size), 1) < split

    def heads(pair):
        qs = slice(pair * 2 * KEY, (pair + 1) * 2 * KEY)
        vs = slice(pair * 2 * VAL, (pair + 1) * 2 * VAL)
        vals, mixed = t.vr[:, vs], md[:, vs]
        keys, rel, cq, pq = t.kr[:, qs], t.rr[:, qs], t.cq[:, qs], t.pq[:, qs]
        first = lane_mask(2 * VAL, VAL)
        parts = []
        for side in range(2):
            mask = first if side == 0 else jnp.logical_not(first)
            soft = t.p[2 * pair + side]
            pull = dot_nt(jnp.where(mask, mixed, jnp.zeros_like(mixed)), vals)
            full = wide(soft)
            delta = low(full * (pull - jnp.sum(full * pull, axis=1, keepdims=True)))
            turned = dot_nn(delta, t.turn[...])
            padded = jnp.concatenate([turned, jnp.zeros_like(turned)], axis=1)
            slid = low(pltpu.roll(padded, 2 * rows_all, axis=1, stride=1, stride_axis=0))
            parts.append(
                (
                    dot_tn(soft, mixed),
                    dot_nn(delta, keys),
                    dot_tn(delta, cq),
                    dot_nn(slid, rel),
                    dot_tn(slid, pq),
                )
            )
        vd[:, vs] = low(jnp.where(first, parts[0][0], parts[1][0]))
        narrow = lane_mask(2 * KEY, KEY)
        content = jnp.where(narrow, parts[0][1], parts[1][1])
        place = jnp.where(narrow, parts[0][3], parts[1][3])
        kd[:, qs] = low(jnp.where(narrow, parts[0][2], parts[1][2]))
        rel_delta = low(
            jnp.where(lane_mask(2 * KEY, KEY, 2 * rows_all), parts[0][4], parts[1][4])
        )
        qd[:, qs] = low(content + place) * jnp.asarray(KEY ** (-0.5), jnp.bfloat16)
        t.rg[:, qs] = dot_nn(t.flipt[...], rel_delta)
        t.sums[7:8, qs] = jnp.sum(content, axis=0, keepdims=True)
        there = slice(keys_all + pair * 2 * KEY, keys_all + (pair + 1) * 2 * KEY)
        t.sums[7:8, there] = jnp.sum(place, axis=0, keepdims=True)

    def trade():
        for k, (full, pair) in enumerate(((vd, t.vdc), (kd, t.kdc), (qd, t.qdc))):
            cols = full.shape[1] // 2
            away = full.at[:, lanes((1 - c) * cols, cols)]
            give(2 + k, away, pair.at[1])
            pair[0] = full[:, lanes(c * cols, cols)]
        cols = t.rg.shape[1] // 2
        t.rgo[...] = low(t.rg[:, lanes((1 - c) * cols, cols)]).reshape(t.rgo.shape)
        remote(t.rgo, t.rgg.at[0], t.xs.at[0], t.xr.at[0], at.sib).start()
        t.rgk[0] = low(t.rg[:, lanes(c * cols, cols)]).reshape(t.rgo.shape)

    def outer_product(rows_from, pair, dst, start=0):
        size = dst.shape[5]

        def one(zz, _):
            lhs = rows_from[:, :, lanes(zz * quarter, quarter)].reshape(2 * rows_all, quarter)
            rhs = pair[:, :, start : start + size].reshape(2 * rows_all, size)
            dst[zz] = low(dot_tn(lhs, rhs)).reshape(dst.shape[1:])
            return 0

        lax.fori_loop(0, NARROW, one, 0)

    keys_all = H * KEY

    def pull_tokens():
        for zz in range(NARROW):
            t.nd[:, zz * 384 : (zz + 1) * 384] = (
                dot_nt(qd[...], t.s0[zz, :, 0:keys_all])
                + dot_nt(kd[...], t.s0[zz, :, keys_all : 2 * keys_all])
                + dot_nt(vd[...], t.s1[zz])
            )

        def one(i, carry):
            gain_total, shift_total = carry
            rows = pl.ds(pl.multiple_of(i * 32, 32), 32)
            v = wide(t.cot[rows, :])
            center = v - jnp.mean(v, axis=1, keepdims=True)
            scale = lax.rsqrt(jnp.mean(center * center, axis=1, keepdims=True) + EPSILON)
            n = center * scale
            delta = t.nd[rows, :]
            e = delta * t.vec[0:1, 0:width]
            back = scale * (
                e
                - jnp.mean(e, axis=1, keepdims=True)
                - n * jnp.mean(e * n, axis=1, keepdims=True)
            )
            t.od[rows, :] = low(t.hid[rows, :] + back)
            return (
                gain_total + jnp.sum(delta * n, axis=0, keepdims=True),
                shift_total + jnp.sum(delta, axis=0, keepdims=True),
            )

        zero = jnp.zeros((1, width), jnp.float32)
        gain_total, shift_total = lax.fori_loop(0, rows_all // 32, one, (zero, zero))
        t.sums[0:1, 0:width] = gain_total
        t.sums[1:2, 0:width] = shift_total
        for zz in range(NARROW):
            t.eb[zz] = jnp.zeros(t.eb.shape[1:], jnp.float32)
            t.eb[zz, 0:6, 0:384] = t.sums[0:6, zz * 384 : (zz + 1) * 384]
            t.eb[zz, 6:7, :] = t.sums[6:7, zz * 768 : (zz + 1) * 768]
            t.eb[zz, 7:8, 0:128] = t.sums[7:8, zz * 128 : (zz + 1) * 128]
            t.eb[zz, 7:8, 128:256] = t.sums[7:8, 512 + zz * 128 : 512 + (zz + 1) * 128]

    def sum_steps(keep, got, over, out, sends, recvs):
        def begin():
            remote(keep.at[0], got.at[0], sends.at[0], recvs.at[0], at.sib).start()

        def step(k):
            arrive(got.at[k], recvs.at[k])
            total = wide(keep[k]) + wide(got[k])
            keep[k + 1] = total.astype(keep.dtype)
            if k < 2:
                target = (at.xn, at.yn)[k]
                remote(
                    keep.at[k + 1], got.at[k + 1], sends.at[k + 1], recvs.at[k + 1], target
                ).start()
            else:
                for d in (1, 3, 2):
                    zz = lax.rem(z + d, NARROW)
                    remote(
                        keep.at[3, zz],
                        over.at[d - 1],
                        sends.at[2 + d],
                        recvs.at[2 + d],
                        depth[d - 1],
                    ).start()

        def end():
            total = wide(keep[3, z])
            for d in (1, 3, 2):
                arrive(over.at[d - 1], recvs.at[2 + d])
                total = total + wide(over[d - 1])
            out[...] = total

        return begin, step, end

    rel_sums = sum_steps(t.rgk, t.rgg, t.rgs, t.rg.at[0:48, 0:256], t.xs, t.xr)
    row_sums = sum_steps(t.ek, t.eg, t.es, t.eo, t.ws, t.wr)

    stored = []

    def store(src, dst):
        copy = pltpu.make_async_copy(src, dst, t.st.at[len(stored)])
        copy.start()
        stored.append(copy)

    chain_start(0)
    stage1(1)
    for copy in loads[:6]:
        copy.wait()
    use(here0)
    leave_mlp(0)
    use(here1)
    leave_mlp(1)
    store(t.vr, t.out_h)
    give(0, t.act.at[:, lanes((1 - c) * width, width)], t.idc.at[1])
    t.idc[0] = t.act[:, lanes(c * width, width)]
    here0 = fetch(2, t.fi0, t.wi, t.s0)
    here1 = fetch(3, t.fi1, t.wi, t.s1, col=width)
    stage2(1)
    loads[7].wait()
    arrive(t.idc.at[1], t.pr.at[0])
    outer_product(t.cat, t.idc, t.gi0)
    stage1(2)
    chain_step(0, 1)
    outer_product(t.cat, t.idc, t.gi1, width // 2)
    loads[17].start()
    loads[18].start()
    stage3(1)
    loads[6].wait()
    use(here0)
    use(here1)
    pull_mid()
    stored[0].wait()
    loads[9].start()
    loads[16].start()
    here0 = fetch(4, t.fo, t.wo, t.s0)
    here1 = fetch(5, t.fv, t.wv, t.s1)
    use(here0)
    pull_mixed()
    here0 = fetch(6, t.fq, t.wq, t.s0.at[:, :, 0:keys_all])
    here2 = fetch(7, t.fk, t.wk, t.s0.at[:, :, keys_all : 2 * keys_all])
    loads[17].wait()
    arrive(t.bdc.at[1], t.pr.at[1])
    outer_product(t.cat, t.bdc, t.go)
    chain_step(0, 2)
    stage1(4)
    chain_start(3)
    for copy in loads[8:16]:
        copy.wait()
    left(t.idc.at[1], t.ps.at[0])
    heads(0)
    heads(1)
    stage2(2)
    heads(2)
    stage4(1)
    chain_end(0)
    chain_step(3, 1)
    stage2(4)
    heads(3)
    trade()
    loads[18].wait()
    loads[16].wait()
    arrive(t.vdc.at[1], t.pr.at[2])
    outer_product(t.idc, t.vdc, t.gv)
    stage1(5)
    arrive(t.kdc.at[1], t.pr.at[3])
    outer_product(t.idc, t.kdc, t.gk)
    stage3(4)
    chain_step(3, 2)
    arrive(t.qdc.at[1], t.pr.at[4])
    outer_product(t.idc, t.qdc, t.gq)
    stage3(2)
    stage5(1)
    stage1(6)
    use(here0)
    use(here1)
    use(here2)
    pull_tokens()
    store(t.od, t.tg_h)
    t.ek[0] = t.eb[...]
    row_sums[0]()
    rel_sums[1](0)
    stage2(5)
    row_sums[1](0)
    stage1(7)
    stage3(5)
    stage2(6)
    chain_end(3)
    chain_plane(0)
    stage2(7)
    rel_sums[1](1)
    stage4(4)
    row_sums[1](1)
    chain_last(0)
    chain_plane(3)
    stage5(4)
    stage5(0)
    stage3(6)
    chain_last(3)
    stage4(2)
    rel_sums[1](2)
    stage3(7)
    row_sums[1](2)
    stage4(5)
    stage6(0)
    stage5(3)
    stage4(6)
    stage5(5)
    stage6(1)
    stage5(6)
    stage4(7)
    rel_sums[2]()
    store(t.rg.at[0:48, 0:256], t.rg_h.at[c])
    remote(t.rg.at[0:48, 0:256], t.rg_h.at[c], t.xs.at[6], t.xr.at[6], at.sib).start()
    stage5(2)
    row_sums[2]()
    store(t.eo, t.e_h)
    stage5(7)
    stage6(6)
    stage6(5)
    stage6(2)
    stage6(3)
    stage6(4)
    stage6(7)

    for m in range(UNITS):
        _, _, out, _, _ = plan[m]
        cols = last[m].shape[1]
        arrive(out.at[:, pl.ds(0, cols)], t.r4.at[m, 4])
        arrive(last[m], t.lo.at[m])
        if m in CHAINS:
            room = got1[m]
            for i in range(top):

                @pl.when((z == 0) | (z == top))
                def _():
                    left(room.at[0], t.zs.at[m, i])

            for slot in (1, 2):

                @pl.when(rising(slot))
                def _():
                    left(room.at[0], t.zs.at[m, 2 + slot])

                @pl.when(sinking(slot))
                def _():
                    left(room.at[0], t.zs.at[m, 4 + slot])

            for h in range(2):
                left(got2[m].at[h], t.s1s.at[m, h])
                left(got3[m].at[h], t.s2.at[m, h])
        else:
            for h in range(2):
                left(got1[m].at[h], t.s1s.at[m, h])
                left(got2[m].at[h], t.s2.at[m, h])
            for d in range(3):
                left(got3[m].at[d], t.s3.at[m, d])
        left(out.at[:, pl.ds(0, cols)], t.s4.at[m])
        left(out.at[pl.ds(0, 3 * (out.shape[0] // 4)), pl.ds(0, cols)], t.s4.at[m])
    for k, pair in enumerate((t.bdc, t.vdc, t.kdc, t.qdc)):
        left(pair.at[1], t.ps.at[1 + k])
    for got, over, sends in ((t.rgg, t.rgs, t.xs), (t.eg, t.es, t.ws)):
        for k in range(3):
            left(got.at[k], sends.at[k])
            left(over.at[k], sends.at[3 + k])
    left(t.rg.at[0:48, 0:256], t.xs.at[6])
    arrive(t.rg_h.at[1 - c], t.xr.at[6])
    for copy in stored[1:]:
        copy.wait()


def backward_pass(grads, saved, weights, shards, rest):
    bf, f32 = jnp.bfloat16, jnp.float32
    rows, width = rest[0].shape
    keys = H * KEY
    views = [g.reshape(4, 2, 2, 2, g.shape[0] // 32, g.shape[1]) for g in grads]
    shapes = [(g.shape[0], g.shape[1]) for g in grads] + [(width, width // 2)] * 4
    shapes += [(width, keys // 2)] * 2
    out_shape = (
        ((width // 2, width), bf),
        ((width // 4, 2 * width), bf),
        ((width // 4, width), bf),
        ((width // 4, width), bf),
        ((width // 4, keys), bf),
        ((width // 4, keys), bf),
        ((rows, width), bf),
        ((rows, width), bf),
        ((8, 768), f32),
        ((2, 48, 256), f32),
    )
    vmem = [
        (((2, 2, 2, 2) if m in CHAINS else (2, 4, 2)) + (r // 32, n), bf)
        for m, (r, n) in enumerate(shapes[: len(grads)])
    ]
    for plain, chain in (
        ((2, 4, 2), (5, 2, 2, 2)),
        ((2, 4), (2, 2)),
        ((3, 2), (2,)),
    ):
        vmem += [
            ((chain if m in CHAINS else plain) + (r // 32, n), bf)
            for m, (r, n) in enumerate(shapes)
        ]
    vmem += [((r // 16, n), bf) for r, n in shapes]
    vmem += [((4, 2, 2, 2, r // 32, n), bf) for r, n in shapes[len(grads) :]]
    vmem += [((NARROW, width // 4, width), bf)] * 2
    vmem += [(a.shape, a.dtype) for a in saved[:10]]
    vmem += [((2, rows, width), bf)] * 2
    vmem += [(a.shape, a.dtype) for a in rest[1:] if a.size > 2]
    vmem += [
        ((2, rows, width // 2), bf),
        ((2, rows, keys // 2), bf),
        ((2, rows, keys // 2), bf),
        ((2, rows, width // 2), bf),
        ((rows, width), f32),
        ((F, keys), f32),
        ((4, 4, 48, 256), bf),
        ((3, 4, 48, 256), bf),
        ((3, 48, 256), bf),
        ((4, 48, 256), bf),
        ((4, 8, 768), f32),
        ((4, 4, 8, 768), f32),
        ((3, 4, 8, 768), f32),
        ((3, 8, 768), f32),
        ((8, 768), f32),
    ]
    sems = [
        DMA((20,)),
        DMA((8, 4)),
        DMA((UNITS, 2)),
        DMA((UNITS, 2)),
        DMA((UNITS, 2)),
        DMA((UNITS, 2)),
        DMA((UNITS, 2)),
        DMA((UNITS, 3)),
        DMA((UNITS, 3)),
        DMA((UNITS,)),
        DMA((UNITS, 5)),
        DMA((UNITS,)),
        DMA((UNITS, NARROW)),
        DMA((UNITS, NARROW)),
        DMA((UNITS, 7)),
        DMA((5,)),
        DMA((5,)),
        DMA((7,)),
        DMA((7,)),
        DMA((6,)),
        DMA((6,)),
        DMA((4,)),
    ]
    ins = (*views, *saved, *weights, *shards, *rest)
    return pl.pallas_call(
        backward_kernel,
        out_shape=tuple(jax.ShapeDtypeStruct(s, d) for s, d in out_shape),
        in_specs=[SMEM if a.size == 2 else HBM for a in ins],
        out_specs=(HBM,) * len(out_shape),
        scratch_shapes=[pltpu.VMEM(s, d) for s, d in vmem] + sems,
        compiler_params=pltpu.CompilerParams(
            collective_id=2, has_side_effects=True, vmem_limit_bytes=60 << 20
        ),
        name="backward_pass",
    )(*ins)


def finish_kernel(count, *refs):
    ins, (rows_h, rel_h), passed = refs[:count], refs[count : count + 2], refs[count + 2 : count + 4]
    refs = refs[count + 4 :]
    outs, relative, kept, vectors = (
        refs[:count],
        refs[count],
        refs[count + 1 : count + 3],
        refs[count + 3 : count + 12],
    )
    refs = refs[count + 12 :]
    low_in, f32_out, through = refs[:count], refs[count : 2 * count], refs[2 * count : 2 * count + 2]
    into, out = refs[2 * count + 2 :]
    loads = [
        pltpu.make_async_copy(src, dst, into.at[k])
        for k, (src, dst) in enumerate(zip((*ins, *passed), (*low_in, *through)))
    ]
    for copy in loads:
        copy.start()
    stored = []

    def store(src, dst):
        copy = pltpu.make_async_copy(src, dst, out.at[len(stored)])
        copy.start()
        stored.append(copy)

    size = relative.shape[1] // 2
    relative[:, 0:size] = rel_h[0]
    relative[:, size : 2 * size] = rel_h[1]
    for k, vector in enumerate(vectors):
        n = vector.shape[0]
        row, start = (7, 128 * (k - 7)) if k >= 7 else (k, 0)
        vector[...] = rows_h[row : row + 1, start : start + n].reshape(n)
    for k in (count, count + 1):
        loads[k].wait()
        store(through[k - count], kept[k - count])
    for k in range(count):
        loads[k].wait()
        src, dst, res = low_in[k], f32_out[k], outs[k]
        half = src.shape[0] // 2
        for part in range(2):

            def one(i, _):
                spot = pl.ds(pl.multiple_of(part * half + i * 32, 32), 32)
                dst[spot, :] = wide(src[spot, :])
                return 0

            lax.fori_loop(0, half // 32, one, 0)
            spot = pl.ds(part * half, half)
            store(dst.at[spot], res.at[spot])
    for copy in stored:
        copy.wait()


def finish_grads(sums, rows, rel, layer_out, tokens_grad):
    f32 = jnp.float32
    vmem = pl.BlockSpec(memory_space=pltpu.VMEM)
    count = len(sums)
    lengths = (384, 384, 384, 384, 384, 384, 768, 128, 128)
    shapes = [(a.shape, f32) for a in sums] + [((rel.shape[1], 2 * rel.shape[2]), f32)]
    shapes += [(a.shape, a.dtype) for a in (layer_out, tokens_grad)]
    shapes += [((n,), f32) for n in lengths]
    through = [(a.shape, a.dtype) for a in (layer_out, tokens_grad)]
    scratch = [(a.shape, a.dtype) for a in sums] + [(a.shape, f32) for a in sums] + through
    return pl.pallas_call(
        lambda *refs: finish_kernel(count, *refs),
        out_shape=tuple(jax.ShapeDtypeStruct(s, d) for s, d in shapes),
        in_specs=[HBM] * count + [vmem] * 2 + [HBM] * 2,
        out_specs=(HBM,) * count + (vmem,) + (HBM,) * 2 + (vmem,) * len(lengths),
        scratch_shapes=[pltpu.VMEM(s, d) for s, d in scratch]
        + [DMA((count + 2,)), DMA((2 * count + 2,))],
        compiler_params=pltpu.CompilerParams(vmem_limit_bytes=60 << 20),
        name="finish_grads",
    )(*sums, rows, rel, layer_out, tokens_grad)


def basis_rows(length, features):
    f32 = np.float32
    family = features // 6
    offsets = np.arange(2 * length - 1, dtype=f32) - f32(length - 1)
    distance = np.abs(offsets)[:, None]
    halves = f32(2.0) ** np.linspace(3.0, math.log2(length), family, dtype=f32)
    decays = np.exp(f32(-math.log(2.0)) / halves[None, :] * distance)
    widths = f32(2.0) ** np.arange(1, family + 1, dtype=f32) - f32(1.0)
    central = np.where(widths[None, :] > distance, f32(1.0), f32(0.0))
    centers = np.linspace(0.0, float(length), family, dtype=f32)
    spread = f32(length / family)
    bump_rows = np.exp(f32(-0.5) * ((distance - centers[None, :]) / spread) ** 2)
    positive = np.concatenate([decays, central, bump_rows], axis=1)
    return np.concatenate([positive, np.sign(offsets)[:, None] * positive], axis=1)


def per_device_linked(
    tokens,
    cotangent,
    thresholds,
    attn_norm_gain,
    attn_norm_shift,
    query_weight,
    key_weight,
    value_weight,
    relative_weight,
    content_bias,
    position_bias,
    out_weight,
    out_bias,
    mlp_norm_gain,
    mlp_norm_shift,
    inner_weight,
    inner_bias,
    outer_weight,
    outer_bias,
):
    _, length, width = tokens.shape
    bf = jnp.bfloat16
    vectors = (
        (attn_norm_gain, 0, 0),
        (attn_norm_shift, 1, 0),
        (out_bias, 2, 0),
        (mlp_norm_gain, 3, 0),
        (mlp_norm_shift, 4, 0),
        (outer_bias, 5, 0),
        (inner_bias, 6, 0),
        (content_bias, 0, 384),
        (position_bias, 1, 384),
    )
    small = jnp.zeros((8, 512), bf)
    for vector, row, col in vectors:
        table = vector.reshape(-1, min(vector.shape[0], 384))
        n, m = table.shape
        small = small + jnp.pad(table, ((row, 8 - row - n), (col, 512 - col - m)))
    limits = thresholds
    table = basis_rows(length, F)
    empty = np.zeros((1, F), np.float32)
    basis = jnp.asarray(np.concatenate([table, empty]), bf)
    flip = jnp.asarray(np.concatenate([table[::-1], empty]), bf)
    flip_t = jnp.asarray(np.concatenate([table[::-1], empty]).T, bf)
    turn = jnp.asarray(np.eye(length)[::-1], bf)
    flat_tokens = tokens.reshape(length, width)
    flat_cotangent = cotangent.reshape(length, width)
    shards = (query_weight, key_weight, value_weight, out_weight, inner_weight, outer_weight)
    outs = forward_pass(
        flat_tokens, flat_cotangent, limits, shards, relative_weight, small, basis, flip
    )
    saved, weights, (vec, gu0, gu1, sums) = outs[:13], outs[13:21], outs[21:]
    ou, oi, oo, ov, ok, oq, layer_out, tokens_grad, rows, rel = backward_pass(
        (gu0, gu1),
        saved,
        weights,
        shards,
        (flat_tokens, flat_cotangent, limits, vec, sums, flip_t, turn),
    )
    outer, inner, out, value, key, query, relative, layer_out, tokens_grad, *vectors = finish_grads(
        (ou, oi, oo, ov, ok, oq), rows, rel, layer_out, tokens_grad
    )
    gain, shift, out_b, mlp_gain, mlp_shift, outer_b, inner_b, content_b, position_b = vectors
    return (
        layer_out[None],
        tokens_grad[None],
        gain,
        shift,
        query,
        key,
        value,
        relative,
        content_b,
        position_b,
        out,
        out_b,
        mlp_gain,
        mlp_shift,
        inner,
        inner_b,
        outer,
        outer_b,
    )


def solution(mesh):
    body = per_device_generic
    if mesh.shape[WIDE] == 8 and mesh.shape[DEPTH] == 4:
        body = per_device_linked
    in_specs = (
        P((WIDE, DEPTH), None, None),
        P((WIDE, DEPTH), None, None),
        P((WIDE, DEPTH), None),
        P(DEPTH),
        P(DEPTH),
        P(DEPTH, None),
        P(DEPTH, None),
        P(DEPTH, None),
        P(DEPTH, None),
        P(DEPTH),
        P(DEPTH),
        P(DEPTH, None),
        P(DEPTH),
        P(DEPTH),
        P(DEPTH),
        P(DEPTH, None),
        P(DEPTH),
        P(DEPTH, None),
        P(DEPTH),
    )
    out_specs = (
        P((WIDE, DEPTH), None, None),
        P((WIDE, DEPTH), None, None),
        P(DEPTH),
        P(DEPTH),
        P(DEPTH, None),
        P(DEPTH, None),
        P(DEPTH, None),
        P(DEPTH, None),
        P(DEPTH),
        P(DEPTH),
        P(DEPTH, None),
        P(DEPTH),
        P(DEPTH),
        P(DEPTH),
        P(DEPTH, None),
        P(DEPTH),
        P(DEPTH, None),
        P(DEPTH),
    )
    return jax.shard_map(
        body, mesh=mesh, in_specs=in_specs, out_specs=out_specs, check_vma=False
    )
```

```python
import functools
import math
import types

import jax
import jax.numpy as jnp
import numpy as np
from jax import lax
from jax.experimental import pallas as pl
from jax.experimental.pallas import tpu as pltpu
from jax.sharding import PartitionSpec as P

H = 8
KEY = 64
VAL = 192
F = 192
WIN = 128


EPSILON = 1e-05


def basis_table(length, features):
    family = features // 6
    offsets = jnp.arange(2 * length - 1, dtype=jnp.float32) - (length - 1)
    distance = jnp.abs(offsets)[:, None]
    halves = 2.0 ** jnp.linspace(3.0, math.log2(length), family, dtype=jnp.float32)
    decays = jnp.exp(-math.log(2.0) / halves[None, :] * distance)
    widths = 2.0 ** jnp.arange(1, family + 1, dtype=jnp.float32) - 1.0
    central = jnp.where(widths[None, :] > distance, 1.0, 0.0).astype(jnp.float32)
    centers = jnp.linspace(0.0, float(length), family, dtype=jnp.float32)
    spread = length / family
    bump_rows = jnp.exp(-0.5 * ((distance - centers[None, :]) / spread) ** 2)
    positive = jnp.concatenate([decays, central, bump_rows], axis=1)
    return jnp.concatenate([positive, jnp.sign(offsets)[:, None] * positive], axis=1)


def shift_offsets(raw_scores, length):
    leading = raw_scores.shape[:-2]
    padded = jnp.pad(raw_scores, [(0, 0)] * len(leading) + [(0, 0), (0, 1)])
    flatten = padded.reshape(leading + (2 * length * length,))
    window = flatten[..., length - 1 : length - 1 + length * (2 * length - 1)]
    return window.reshape(leading + (length, 2 * length - 1))[..., :length]


def unshift_offsets(grad_scores, length):
    leading = grad_scores.shape[:-2]
    widened = jnp.pad(grad_scores, [(0, 0)] * len(leading) + [(0, 0), (0, length - 1)])
    flatten = widened.reshape(leading + (length * (2 * length - 1),))
    flatten = jnp.pad(flatten, [(0, 0)] * len(leading) + [(length - 1, 1)])
    return flatten.reshape(leading + (length, 2 * length))[..., : 2 * length - 1]


def layer_norm(values, gain, shift):
    center = values - jnp.mean(values, axis=-1, keepdims=True)
    spread = jnp.mean(center * center, axis=-1, keepdims=True)
    return center * lax.rsqrt(spread + EPSILON) * gain + shift


def gelu_exact(values):
    return jax.nn.gelu(values, approximate=False)


def column_sums(values):
    return jnp.sum(values.astype(jnp.float32), axis=0)


WIDE = "wide"
DEPTH = "narrow"


def spread_rows(shard):
    return lax.all_gather(shard, DEPTH, axis=0, tiled=True)


def sum_columns(part):
    low = part.astype(jnp.bfloat16)
    return lax.psum_scatter(low, WIDE, scatter_dimension=1, tiled=True).astype(jnp.float32)


def sum_rows(part):
    low = part.astype(jnp.bfloat16)
    return lax.psum_scatter(low, DEPTH, scatter_dimension=0, tiled=True).astype(jnp.float32)


def spread_columns(part):
    low = part.astype(jnp.bfloat16)
    return lax.all_gather(low, WIDE, axis=1, tiled=True).astype(jnp.float32)


def per_device_generic(
    tokens,
    cotangent,
    thresholds,
    attn_norm_gain,
    attn_norm_shift,
    query_weight,
    key_weight,
    value_weight,
    relative_weight,
    content_bias,
    position_bias,
    out_weight,
    out_bias,
    mlp_norm_gain,
    mlp_norm_shift,
    inner_weight,
    inner_bias,
    outer_weight,
    outer_bias,
):
    seq_count, length, model_width = tokens.shape
    row_count = seq_count * length
    span = 2 * length - 1
    query_scale = KEY ** (-0.5)
    (
        attn_gain,
        attn_shift,
        query_full,
        key_full,
        value_full,
        relative_full,
        content_full,
        position_full,
        exit_full,
        exit_bias,
    ) = (
        spread_rows(attn_norm_gain),
        spread_rows(attn_norm_shift),
        spread_rows(query_weight),
        spread_rows(key_weight),
        spread_rows(value_weight),
        spread_rows(relative_weight),
        spread_rows(content_bias),
        spread_rows(position_bias),
        spread_rows(out_weight),
        spread_rows(out_bias),
    )
    mlp_gain, mlp_shift, inner_full, inner_offset, outer_full, outer_offset = (
        spread_rows(mlp_norm_gain),
        spread_rows(mlp_norm_shift),
        spread_rows(inner_weight),
        spread_rows(inner_bias),
        spread_rows(outer_weight),
        spread_rows(outer_bias),
    )
    flat_tokens = tokens.reshape(row_count, model_width).astype(jnp.float32)
    attn_gain_f = attn_gain.astype(jnp.float32)
    attn_shift_f = attn_shift.astype(jnp.float32)
    normed = layer_norm(flat_tokens, attn_gain_f, attn_shift_f).astype(jnp.bfloat16)
    queries = jnp.dot(normed, query_full, preferred_element_type=jnp.float32) * query_scale
    content_query = (
        (queries + content_full.astype(jnp.float32))
        .astype(jnp.bfloat16)
        .reshape(seq_count, length, H, KEY)
    )
    position_query = (
        (queries + position_full.astype(jnp.float32))
        .astype(jnp.bfloat16)
        .reshape(seq_count, length, H, KEY)
    )
    key_rows = (
        jnp.dot(normed, key_full, preferred_element_type=jnp.float32)
        .astype(jnp.bfloat16)
        .reshape(seq_count, length, H, KEY)
    )
    value_rows = (
        jnp.dot(normed, value_full, preferred_element_type=jnp.float32)
        .astype(jnp.bfloat16)
        .reshape(seq_count, length, H, VAL)
    )
    basis = basis_table(length, F).astype(jnp.bfloat16)
    rel_keys = (
        jnp.dot(basis, relative_full, preferred_element_type=jnp.float32)
        .astype(jnp.bfloat16)
        .reshape(span, H, KEY)
    )

    def attention_logits():
        content = jnp.einsum(
            "bihe,bjhe->bhij", content_query, key_rows, preferred_element_type=jnp.float32
        )
        raw_scores = jnp.einsum(
            "bihe,the->bhit", position_query, rel_keys, preferred_element_type=jnp.float32
        )
        return content + shift_offsets(raw_scores, length)

    logits = attention_logits()
    row_peak = jnp.max(logits, axis=-1, keepdims=True)
    log_total = row_peak + jnp.log(jnp.sum(jnp.exp(logits - row_peak), axis=-1, keepdims=True))
    attention = jnp.exp(logits - log_total).astype(jnp.bfloat16)
    mixed_heads = jnp.einsum(
        "bhij,bjhd->bihd", attention, value_rows, preferred_element_type=jnp.float32
    )
    mixed_heads = mixed_heads.astype(jnp.bfloat16).reshape(row_count, H * VAL)
    hidden = flat_tokens + (
        jnp.dot(mixed_heads, exit_full, preferred_element_type=jnp.float32)
        + exit_bias.astype(jnp.float32)
    )
    mlp_gain_f = mlp_gain.astype(jnp.float32)
    mlp_shift_f = mlp_shift.astype(jnp.float32)
    normed_mid = layer_norm(hidden, mlp_gain_f, mlp_shift_f).astype(jnp.bfloat16)
    inner_pre = jnp.dot(
        normed_mid, inner_full, preferred_element_type=jnp.float32
    ) + inner_offset.astype(jnp.float32)
    active, gelu_pull = jax.vjp(gelu_exact, inner_pre)
    active_low = active.astype(jnp.bfloat16)
    result = hidden + (
        jnp.dot(active_low, outer_full, preferred_element_type=jnp.float32)
        + outer_offset.astype(jnp.float32)
    )
    layer_out = result.astype(jnp.bfloat16).reshape(seq_count, length, model_width)
    clip_limit = jnp.repeat(thresholds, WIN, axis=1).reshape(row_count, 1)
    clipped = jnp.clip(
        cotangent.reshape(row_count, model_width).astype(jnp.float32), -clip_limit, clip_limit
    )
    mlp_gain, mlp_shift, inner_full, inner_offset, outer_full, outer_offset = (
        spread_rows(mlp_norm_gain),
        spread_rows(mlp_norm_shift),
        spread_rows(inner_weight),
        spread_rows(inner_bias),
        spread_rows(outer_weight),
        spread_rows(outer_bias),
    )
    mlp_gain_f = mlp_gain.astype(jnp.float32)
    outer_delta = clipped.astype(jnp.bfloat16)
    outer_bias_grad = column_sums(outer_delta)
    outer_weight_grad = jnp.einsum(
        "nk,nm->km", active_low, outer_delta, preferred_element_type=jnp.float32
    )
    active_delta = jnp.einsum(
        "nm,km->nk", outer_delta, outer_full, preferred_element_type=jnp.float32
    )
    (inner_grad_pre,) = gelu_pull(active_delta)
    inner_delta = inner_grad_pre.astype(jnp.bfloat16)
    inner_bias_grad = column_sums(inner_delta)
    inner_weight_grad = jnp.einsum(
        "nd,nf->df", normed_mid, inner_delta, preferred_element_type=jnp.float32
    )
    mid_delta = jnp.einsum("nf,df->nd", inner_delta, inner_full, preferred_element_type=jnp.float32)
    norm_out, norm_pull = jax.vjp(layer_norm, hidden, mlp_gain_f, mlp_shift_f)
    hidden_part, mlp_gain_grad, mlp_shift_grad = norm_pull(mid_delta)
    hidden_delta = clipped + hidden_part
    (
        attn_gain,
        attn_shift,
        query_full,
        key_full,
        value_full,
        relative_full,
        content_full,
        position_full,
        exit_full,
        exit_bias,
    ) = (
        spread_rows(attn_norm_gain),
        spread_rows(attn_norm_shift),
        spread_rows(query_weight),
        spread_rows(key_weight),
        spread_rows(value_weight),
        spread_rows(relative_weight),
        spread_rows(content_bias),
        spread_rows(position_bias),
        spread_rows(out_weight),
        spread_rows(out_bias),
    )
    attn_gain_f = attn_gain.astype(jnp.float32)
    branch_delta = hidden_delta.astype(jnp.bfloat16)
    out_bias_grad = column_sums(branch_delta)
    out_weight_grad = jnp.einsum(
        "nk,nd->kd", mixed_heads, branch_delta, preferred_element_type=jnp.float32
    )
    mixed_delta = jnp.einsum(
        "nd,kd->nk", branch_delta, exit_full, preferred_element_type=jnp.float32
    )
    mixed_delta = mixed_delta.astype(jnp.bfloat16).reshape(seq_count, length, H, VAL)
    logits = attention_logits()
    soft_rows = jnp.exp(logits - log_total)
    attention = soft_rows.astype(jnp.bfloat16)
    attention_delta = jnp.einsum(
        "bihd,bjhd->bhij", mixed_delta, value_rows, preferred_element_type=jnp.float32
    )
    value_delta = jnp.einsum(
        "bhij,bihd->bjhd", attention, mixed_delta, preferred_element_type=jnp.float32
    )
    value_delta = value_delta.astype(jnp.bfloat16).reshape(row_count, H * VAL)
    logit_delta = soft_rows * (
        attention_delta - jnp.sum(soft_rows * attention_delta, axis=-1, keepdims=True)
    )
    logit_delta = logit_delta.astype(jnp.bfloat16)
    content_delta = jnp.einsum(
        "bhij,bjhe->bihe", logit_delta, key_rows, preferred_element_type=jnp.float32
    )
    key_delta = jnp.einsum(
        "bhij,bihe->bjhe", logit_delta, content_query, preferred_element_type=jnp.float32
    )
    key_delta = key_delta.astype(jnp.bfloat16).reshape(row_count, H * KEY)
    offset_delta = unshift_offsets(logit_delta, length)
    position_delta = jnp.einsum(
        "bhit,the->bihe", offset_delta, rel_keys, preferred_element_type=jnp.float32
    )
    rel_delta = jnp.einsum(
        "bhit,bihe->the", offset_delta, position_query, preferred_element_type=jnp.float32
    )
    rel_delta = rel_delta.astype(jnp.bfloat16).reshape(span, H * KEY)
    relative_weight_grad = jnp.einsum(
        "tf,tk->fk", basis, rel_delta, preferred_element_type=jnp.float32
    )
    content_delta = content_delta.reshape(row_count, H * KEY)
    position_delta = position_delta.reshape(row_count, H * KEY)
    content_bias_grad = jnp.sum(content_delta, axis=0)
    position_bias_grad = jnp.sum(position_delta, axis=0)
    query_delta = (content_delta + position_delta).astype(jnp.bfloat16) * jnp.asarray(
        query_scale, jnp.bfloat16
    )
    query_weight_grad = jnp.einsum(
        "nd,nk->dk", normed, query_delta, preferred_element_type=jnp.float32
    )
    key_weight_grad = jnp.einsum("nd,nk->dk", normed, key_delta, preferred_element_type=jnp.float32)
    value_weight_grad = jnp.einsum(
        "nd,nk->dk", normed, value_delta, preferred_element_type=jnp.float32
    )
    normed_delta = (
        jnp.einsum("nk,dk->nd", query_delta, query_full, preferred_element_type=jnp.float32)
        + jnp.einsum("nk,dk->nd", key_delta, key_full, preferred_element_type=jnp.float32)
        + jnp.einsum("nk,dk->nd", value_delta, value_full, preferred_element_type=jnp.float32)
    )
    first_out, first_pull = jax.vjp(layer_norm, flat_tokens, attn_gain_f, attn_shift_f)
    tokens_part, attn_gain_grad, attn_shift_grad = first_pull(normed_delta)
    tokens_grad = (
        (hidden_delta + tokens_part).astype(jnp.bfloat16).reshape(seq_count, length, model_width)
    )
    (
        query_weight_grad,
        key_weight_grad,
        value_weight_grad,
        relative_weight_grad,
        out_weight_grad,
        inner_weight_grad,
        outer_weight_grad,
    ) = (
        sum_columns(query_weight_grad),
        sum_columns(key_weight_grad),
        sum_columns(value_weight_grad),
        sum_columns(relative_weight_grad),
        sum_columns(out_weight_grad),
        sum_columns(inner_weight_grad),
        sum_columns(outer_weight_grad),
    )
    (
        query_weight_grad,
        key_weight_grad,
        value_weight_grad,
        relative_weight_grad,
        out_weight_grad,
        inner_weight_grad,
        outer_weight_grad,
        attn_gain_grad,
        attn_shift_grad,
        content_bias_grad,
        position_bias_grad,
        out_bias_grad,
        mlp_gain_grad,
        mlp_shift_grad,
        inner_bias_grad,
        outer_bias_grad,
    ) = (
        sum_rows(query_weight_grad),
        sum_rows(key_weight_grad),
        sum_rows(value_weight_grad),
        sum_rows(relative_weight_grad),
        sum_rows(out_weight_grad),
        sum_rows(inner_weight_grad),
        sum_rows(outer_weight_grad),
        sum_rows(attn_gain_grad),
        sum_rows(attn_shift_grad),
        sum_rows(content_bias_grad),
        sum_rows(position_bias_grad),
        sum_rows(out_bias_grad),
        sum_rows(mlp_gain_grad),
        sum_rows(mlp_shift_grad),
        sum_rows(inner_bias_grad),
        sum_rows(outer_bias_grad),
    )
    (
        query_weight_grad,
        key_weight_grad,
        value_weight_grad,
        relative_weight_grad,
        out_weight_grad,
        inner_weight_grad,
        outer_weight_grad,
    ) = (
        spread_columns(query_weight_grad),
        spread_columns(key_weight_grad),
        spread_columns(value_weight_grad),
        spread_columns(relative_weight_grad),
        spread_columns(out_weight_grad),
        spread_columns(inner_weight_grad),
        spread_columns(outer_weight_grad),
    )
    (
        attn_gain_grad,
        attn_shift_grad,
        content_bias_grad,
        position_bias_grad,
        out_bias_grad,
        mlp_gain_grad,
        mlp_shift_grad,
        inner_bias_grad,
        outer_bias_grad,
    ) = lax.psum(
        (
            attn_gain_grad,
            attn_shift_grad,
            content_bias_grad,
            position_bias_grad,
            out_bias_grad,
            mlp_gain_grad,
            mlp_shift_grad,
            inner_bias_grad,
            outer_bias_grad,
        ),
        WIDE,
    )
    return (
        layer_out,
        tokens_grad,
        attn_gain_grad,
        attn_shift_grad,
        query_weight_grad,
        key_weight_grad,
        value_weight_grad,
        relative_weight_grad,
        content_bias_grad,
        position_bias_grad,
        out_weight_grad,
        out_bias_grad,
        mlp_gain_grad,
        mlp_shift_grad,
        inner_weight_grad,
        inner_bias_grad,
        outer_weight_grad,
        outer_bias_grad,
    )


MESH = pl.DeviceIdType.MESH
NARROW = 4


def position():
    w = lax.axis_index(WIDE)
    z = lax.axis_index(DEPTH)
    c = lax.rem(w, 2)
    p = lax.div(w, 2)
    x = lax.rem(p, 2)
    y = lax.div(p, 2)
    chip = (lambda q: q * 2 + c)
    return types.SimpleNamespace(
        w=w,
        z=z,
        c=c,
        p=p,
        x=x,
        y=y,
        px=p + 1 - 2 * x,
        py=p + 2 - 4 * y,
        pd=3 - p,
        sib=(w + 1 - 2 * c, z),
        xn=(chip(p + 1 - 2 * x), z),
        yn=(chip(p + 2 - 4 * y), z),
    )


def meet(partners):
    barrier = pltpu.get_barrier_semaphore()
    for partner in partners:
        pl.semaphore_signal(barrier, inc=1, device_id=partner, device_id_type=MESH)
    pl.semaphore_wait(barrier, len(partners))


def remote(src, dst, send, recv, target):
    return pltpu.make_async_remote_copy(
        src_ref=src,
        dst_ref=dst,
        send_sem=send,
        recv_sem=recv,
        device_id=target,
        device_id_type=MESH,
    )


HBM = pl.BlockSpec(memory_space=pltpu.HBM)
DMA = pltpu.SemaphoreType.DMA
SMEM = pl.BlockSpec(memory_space=pltpu.SMEM)


def dot_nn(a, b):
    return jnp.dot(a, b, preferred_element_type=jnp.float32)


def dot_nt(a, b):
    return lax.dot_general(a, b, (((1,), (1,)), ((), ())), preferred_element_type=jnp.float32)


def dot_tn(a, b):
    return lax.dot_general(a, b, (((0,), (0,)), ((), ())), preferred_element_type=jnp.float32)


def low(v):
    return v.astype(jnp.bfloat16)


def wide(v):
    return v.astype(jnp.float32)


def lanes(start, size):
    return pl.ds(pl.multiple_of(start, 128), size)


def arrive(ref, sem):
    me = (lax.axis_index(WIDE), lax.axis_index(DEPTH))
    remote(ref, ref, sem, sem, me).wait_recv()


def left(ref, sem):
    me = (lax.axis_index(WIDE), lax.axis_index(DEPTH))
    remote(ref, ref, sem, sem, me).wait_send()


def forward_refs(
    tok_h,
    cot_h,
    lim_h,
    wq,
    wk,
    wv,
    wo,
    wi,
    wu,
    rel_h,
    small_h,
    basis_h,
    flip_h,
    p_h,
    cq_h,
    pq_h,
    k_h,
    v_h,
    rr_h,
    hid_h,
    act_h,
    slope_h,
    od_h,
    nn_h,
    nm_h,
    mx_h,
    fq,
    fk,
    fv,
    fo,
    fi0,
    fi1,
    fu0,
    fu1,
    vec_h,
    gu0,
    gu1,
    sums_h,
    q,
    k,
    v,
    o,
    i0,
    i1,
    rel,
    small,
    vec,
    tok,
    normed,
    cq,
    pq,
    kr,
    vr,
    basis,
    flip,
    rk,
    rr,
    p,
    mixed,
    hidden,
    nmid,
    cot,
    od,
    odc,
    act,
    slope,
    gst,
    sums,
    zr,
    zs,
    xr,
    yr,
    fxr,
    fyr,
    sr,
    snd,
    own,
    ld,
    mr,
    ms,
    ps,
    pr,
    st,
    gs,
):
    return types.SimpleNamespace(**locals())


def forward_kernel(*refs):
    t = forward_refs(*refs)
    at = position()
    w, z, c, p = at.w, at.z, at.c, at.p
    depth = [(w, lax.rem(z + d, NARROW)) for d in range(1, NARROW)]
    meet([at.sib, at.xn, at.yn] + depth)
    rows_all = t.tok.shape[0]
    width = t.tok.shape[1]

    keys_all = H * KEY
    quarter = width // 4
    plan = (
        (t.wq, 0, 0, t.fq, keys_all),
        (t.wk, 0, 0, t.fk, keys_all),
        (t.wv, 0, 0, t.fv, width),
        (t.wo, 0, 0, t.fo, width),
        (t.wi, 0, 0, t.fi0, width),
        (t.wi, 0, width, t.fi1, width),
        (t.wu, 0, 0, t.fu0, width),
        (t.wu, quarter, 0, t.fu1, width),
    )

    def rows_of(m, pp, part=None):
        rows = quarter // 4
        start = pp * rows
        if part is not None:
            rows = rows // 2
            start = start + part * rows
        return start, rows

    def block(m, zz, pp, part=None):
        start, rows = rows_of(m, pp, part)
        cols = plan[m][4] // 2
        return plan[m][3].at[zz, pl.ds(pl.multiple_of(start, 16), rows), lanes(c * cols, cols)]

    def send(m, ref, recv, target):
        remote(ref, ref, t.snd.at[m], recv, target).start()

    loads = [
        pltpu.make_async_copy(src, dst, t.ld.at[k])
        for k, (src, dst) in enumerate(
            (
                (t.tok_h, t.tok),
                (t.small_h, t.small.at[z]),
                (t.rel_h, t.rel.at[z]),
                (t.basis_h, t.basis),
                (t.cot_h, t.cot),
                (t.flip_h, t.flip),
            )
        )
    ]
    def over_z(k, src, dst):
        for d in (1, 3, 2):
            remote(src, dst.at[z], t.ms.at[k], t.mr.at[k], depth[d - 1]).start()

    over_z(0, t.small_h, t.small)
    for copy in loads:
        copy.start()

    above, below = (w, jnp.minimum(z + 1, NARROW - 1)), (w, jnp.maximum(z - 1, 0))
    can_rise, can_sink = z < NARROW - 1, z > 0

    def own_piece(m):
        shard, r0, c0, _, span = plan[m]
        start, rows = rows_of(m, p)
        cols = span // 2
        return shard.at[pl.ds(pl.multiple_of(r0 + start, 16), rows), lanes(c0 + c * cols, cols)]

    def depart(m):
        @pl.when(can_rise)
        def _():
            remote(
                own_piece(m), block(m, z, p), t.zs.at[m, 3], t.zr.at[m, 0], above
            ).start()

        @pl.when(can_sink)
        def _():
            remote(
                own_piece(m), block(m, z, p), t.zs.at[m, 4], t.zr.at[m, 2], below
            ).start()

    def hop(k):
        first, last = z == 0, z == NARROW - 1
        if k == 0:
            return jnp.where(first, 3, 1)
        if k == 1:
            return jnp.where(first | last, 2, 3)
        return jnp.where(first, 1, jnp.where(last, 3, 2))

    def source(k):
        return lax.rem(z + NARROW - hop(k), NARROW)

    def relay(m, k):
        d = hop(k)
        mine = block(m, source(k), p)
        rise = can_rise & (d <= z)
        sink = can_sink & (d > z)
        return mine, d, rise, sink

    def spread(m, k):
        mine, d, rise, sink = relay(m, k)
        arrive(mine, t.zr.at[m, d - 1])

        @pl.when(rise)
        def _():
            remote(mine, mine, t.zs.at[m, k], t.zr.at[m, jnp.minimum(d, 2)], above).start()

        @pl.when(sink)
        def _():
            remote(mine, mine, t.zs.at[m, k], t.zr.at[m, jnp.maximum(d - 2, 0)], below).start()

        send(m, mine, t.xr.at[m, k], at.xn)
        send(m, mine, t.yr.at[m, k], at.yn)
        send(m, mine, t.sr.at[m], at.sib)

    def forward(m, k):
        zz = source(k)
        arrive(block(m, zz, at.px), t.xr.at[m, k])
        send(m, block(m, zz, at.px, 0), t.fxr.at[m, k], at.yn)
        send(m, block(m, zz, at.px), t.sr.at[m], at.sib)
        arrive(block(m, zz, at.py), t.yr.at[m, k])
        send(m, block(m, zz, at.py, 1), t.fyr.at[m, k], at.xn)
        send(m, block(m, zz, at.py), t.sr.at[m], at.sib)

    def finish(m, k):
        zz = source(k)
        arrive(block(m, zz, at.pd, 0), t.fxr.at[m, k])
        arrive(block(m, zz, at.pd, 1), t.fyr.at[m, k])
        send(m, block(m, zz, at.pd), t.sr.at[m], at.sib)

    depart(0)
    depart(1)
    depart(2)
    over_z(1, t.rel_h, t.rel)
    def all_here(m):
        arrive(plan[m][3].at[pl.ds(0, 3), :, pl.ds(0, plan[m][4] // 2)], t.sr.at[m])

    def fetch(m, held):
        all_here(m)
        shard, r0, c0, full, span = plan[m]
        copies = [
            pltpu.make_async_copy(
                shard.at[pl.ds(r0, quarter), pl.ds(c0, span)], held.at[z], t.own.at[m, 0]
            )
        ]
        for d in range(1, NARROW):
            zz = lax.rem(z + d, NARROW)
            copies.append(pltpu.make_async_copy(full.at[zz], held.at[zz], t.own.at[m, d]))
        for copy in copies:
            copy.start()
        return copies

    def use(copies):
        for copy in copies:
            copy.wait()

    def vectors():
        loads[1].wait()
        arrive(t.small.at[pl.ds(0, 3)], t.mr.at[0])
        for zz in range(NARROW):
            rows = wide(t.small[zz])
            for r in range(6):
                t.vec[r : r + 1, zz * 384 : (zz + 1) * 384] = rows[r : r + 1, 0:384]
            for r in range(2):
                spot = slice(zz * 768 + r * 384, zz * 768 + (r + 1) * 384)
                t.vec[6:7, spot] = rows[6 + r : 7 + r, 0:384]
                t.vec[7 + r : 8 + r, zz * 128 : (zz + 1) * 128] = rows[r : r + 1, 384:512]

    def norm_rows(src, dst, gain_row):
        def one(i, _):
            rows = pl.ds(pl.multiple_of(i * 32, 32), 32)
            v = wide(src[rows, :])
            center = v - jnp.mean(v, axis=1, keepdims=True)
            var = jnp.mean(center * center, axis=1, keepdims=True)
            gain = t.vec[gain_row : gain_row + 1, 0:width]
            shift = t.vec[gain_row + 1 : gain_row + 2, 0:width]
            dst[rows, :] = low(center * lax.rsqrt(var + EPSILON) * gain + shift)
            return 0

        lax.fori_loop(0, rows_all // 32, one, 0)

    def flat(full):
        return full[...].reshape(full.shape[0] * full.shape[1], full.shape[2])

    def columns(full, start, size):
        part = full[:, :, lanes(start, size)]
        return part.reshape(full.shape[0] * full.shape[1], size)

    def make_queries():
        queries = dot_nn(t.normed[...], flat(t.q)) * (KEY ** (-0.5))
        size = H * KEY
        t.cq[...] = low(queries + t.vec[7:8, 0:size])
        t.pq[...] = low(queries + t.vec[8:9, 0:size])

    def make_keys():
        t.kr[...] = low(dot_nn(t.normed[...], flat(t.k)))
        loads[2].wait()
        arrive(t.rel.at[pl.ds(0, 3)], t.mr.at[1])
        loads[3].wait()
        table = t.rel[...].reshape(t.rel.shape[0] * t.rel.shape[1], t.rel.shape[2])
        t.rk[...] = low(dot_nn(t.basis[...], table))
        loads[5].wait()
        t.rr[...] = low(dot_nn(t.flip[...], table))

    def make_values():
        def one(n, _):
            t.vr[:, lanes(n * 512, 512)] = low(dot_nn(t.normed[...], columns(t.v, n * 512, 512)))
            return 0

        lax.fori_loop(0, 3, one, 0)

    def pair_mask(size, split):
        return lax.broadcasted_iota(jnp.int32, (rows_all, size), 1) < split

    def heads(pair):
        qs = slice(pair * 2 * KEY, (pair + 1) * 2 * KEY)
        vs = slice(pair * 2 * VAL, (pair + 1) * 2 * VAL)
        first = pair_mask(2 * KEY, KEY)
        keys, rel, vals = t.kr[:, qs], t.rk[:, qs], t.vr[:, vs]
        mixed = []
        for side in range(2):
            keep = first if side == 0 else jnp.logical_not(first)
            cq = jnp.where(keep, t.cq[:, qs], jnp.zeros_like(t.cq[:, qs]))
            pq = jnp.where(keep, t.pq[:, qs], jnp.zeros_like(t.pq[:, qs]))
            raw = dot_nt(pq, rel)
            shifted = pltpu.roll(raw, rows_all + 1, axis=1, stride=1, stride_axis=0)
            logits = dot_nt(cq, keys) + shifted[:, :rows_all]
            grown = jnp.exp(logits - jnp.max(logits, axis=1, keepdims=True))
            soft = low(grown / jnp.sum(grown, axis=1, keepdims=True))
            t.p[2 * pair + side] = soft
            mixed.append(dot_nn(soft, vals))
        t.mixed[:, vs] = low(jnp.where(pair_mask(2 * VAL, VAL), mixed[0], mixed[1]))

    def give(k, src, dst):
        remote(src, dst, t.ps.at[k], t.pr.at[k], at.sib).start()

    stored = []

    def store(src, dst):
        copy = pltpu.make_async_copy(src, dst, t.st.at[len(stored)])
        copy.start()
        stored.append(copy)

    def attend_out():
        def one(n, _):
            cols = lanes(n * 512, 512)
            t.hidden[:, cols] = (
                wide(t.tok[:, cols])
                + dot_nn(t.mixed[...], columns(t.o, n * 512, 512))
                + t.vec[2:3, cols]
            )
            return 0

        lax.fori_loop(0, 3, one, 0)
        norm_rows(t.hidden, t.nmid, 3)
        give(2, t.nmid, t.nm_h.at[1])

    def clip_rows():
        loads[4].wait()

        def one(i, total):
            rows = pl.ds(pl.multiple_of(i * 32, 32), 32)
            clipped = low(clip(i * 32, wide(t.cot[rows, :])))
            t.od[rows, :] = clipped
            return total + jnp.sum(wide(clipped), axis=0, keepdims=True)

        total = lax.fori_loop(0, rows_all // 32, one, jnp.zeros((1, width), jnp.float32))
        t.sums[5:6, 0:width] = total
        half = width // 2
        t.odc[0] = t.od[:, lanes(c * half, half)]
        give(0, t.od.at[:, lanes((1 - c) * half, half)], t.odc.at[1])

    def clip(row, values):
        limit = jnp.where(row < WIN, t.lim_h[0, 0], t.lim_h[0, 1])
        return jnp.minimum(jnp.maximum(values, -limit), limit)

    def inner(h):
        full = (t.i0, t.i1)[h]

        def one(n, _):
            local = n * 256
            cols = lanes(h * width + local, 256)
            pre = dot_nn(t.nmid[...], columns(full, local, 256)) + t.vec[6:7, cols]
            cdf = 0.5 + 0.5 * lax.erf(pre * (0.5**0.5))
            slope = cdf + pre * jnp.exp(-0.5 * pre * pre) * (2.0 * math.pi) ** -0.5
            t.act[0, :, cols] = low(pre * cdf)
            t.slope[:, cols] = low(slope)
            return 0

        lax.fori_loop(0, 6, one, 0)
        cols = pl.ds(h * width, width)
        give(3 + h, t.act.at[0, :, cols], t.act.at[1, :, cols])

    def outer_product(left_ref, right_ref, dst, start, size):
        steps = left_ref.shape[2] // 256
        right = right_ref[:, :, start : start + size].reshape(2 * rows_all, size)

        def tile(slot, n):
            return pltpu.make_async_copy(
                t.gst.at[slot, :, 0:size],
                dst.at[pl.ds(pl.multiple_of(n * 256, 256), 256)],
                t.gs.at[slot],
            )

        def one(n, _):
            slot = lax.rem(n, 2)

            @pl.when(n >= 2)
            def _():
                tile(slot, n - 2).wait()

            lhs = left_ref[:, :, lanes(n * 256, 256)].reshape(2 * rows_all, 256)
            t.gst[slot, :, 0:size] = low(dot_tn(lhs, right))
            tile(slot, n).start()
            return 0

        lax.fori_loop(0, steps, one, 0)
        tile(0, steps - 2).wait()
        tile(1, steps - 1).wait()

    t.sums[...] = jnp.zeros_like(t.sums)
    t.vec[...] = jnp.zeros_like(t.vec)
    here = {}
    spread(0, 0)
    spread(1, 0)
    spread(0, 1)
    forward(0, 0)
    spread(1, 1)
    spread(2, 0)
    forward(1, 0)
    spread(0, 2)
    spread(2, 1)
    spread(1, 2)
    depart(3)
    forward(0, 1)
    loads[0].wait()
    vectors()
    norm_rows(t.tok, t.normed, 0)
    give(1, t.normed, t.nn_h.at[1])
    store(t.normed, t.nn_h.at[0])
    store(t.vec, t.vec_h)
    clip_rows()
    store(t.od, t.od_h)
    forward(0, 2)
    forward(1, 1)
    spread(2, 2)
    forward(1, 2)
    forward(2, 1)
    finish(1, 1)
    depart(4)
    finish(0, 0)
    finish(0, 1)
    finish(0, 2)
    finish(1, 0)
    here[0] = fetch(0, t.q)
    forward(2, 0)
    depart(5)
    use(here[0])
    make_queries()
    store(t.cq, t.cq_h)
    store(t.pq, t.pq_h)
    spread(3, 0)
    finish(1, 2)
    here[1] = fetch(1, t.k)
    forward(2, 2)
    spread(3, 1)
    use(here[1])
    make_keys()
    store(t.kr, t.k_h)
    store(t.rr, t.rr_h)
    finish(2, 1)
    spread(4, 0)
    spread(5, 0)
    spread(4, 1)
    finish(2, 2)
    depart(6)
    finish(2, 0)
    here[2] = fetch(2, t.v)
    use(here[2])
    make_values()
    store(t.vr, t.v_h)
    forward(3, 0)
    spread(5, 1)
    heads(0)
    spread(3, 2)
    heads(1)
    forward(3, 1)
    forward(4, 1)
    spread(4, 2)
    heads(2)
    forward(3, 2)
    spread(5, 2)
    depart(7)
    finish(3, 1)
    forward(5, 1)
    forward(4, 0)
    heads(3)
    store(t.p, t.p_h)
    give(5, t.mixed, t.mx_h.at[1])
    store(t.mixed, t.mx_h.at[0])
    forward(4, 2)
    finish(3, 2)
    spread(6, 0)
    spread(6, 1)
    forward(5, 0)
    finish(3, 0)
    here[3] = fetch(3, t.o)
    use(here[3])
    attend_out()
    store(t.hidden, t.hid_h)
    store(t.nmid, t.nm_h.at[0])
    spread(6, 2)
    finish(4, 1)
    finish(4, 0)
    forward(5, 2)
    spread(7, 0)
    finish(4, 2)
    here[4] = fetch(4, t.i0)
    use(here[4])
    inner(0)
    finish(5, 1)
    forward(6, 0)
    spread(7, 1)
    forward(6, 1)
    finish(5, 0)
    forward(6, 2)
    finish(5, 2)
    here[5] = fetch(5, t.i1)
    use(here[5])
    inner(1)
    store(t.act.at[0], t.act_h)
    store(t.slope, t.slope_h)
    spread(7, 2)
    forward(7, 1)
    finish(6, 1)
    forward(7, 0)
    arrive(t.odc.at[1], t.pr.at[0])
    for h in range(2):
        arrive(t.act.at[1, :, pl.ds(0, width)], t.pr.at[3 + h])
    outer_product(t.act, t.odc, t.gu0, 0, 384)
    finish(6, 2)
    finish(6, 0)
    forward(7, 2)
    outer_product(t.act, t.odc, t.gu1, 384, 384)
    store(t.sums, t.sums_h)
    finish(7, 0)
    finish(7, 1)
    finish(7, 2)
    all_here(6)
    all_here(7)

    arrive(t.nn_h.at[1], t.pr.at[1])
    arrive(t.nm_h.at[1], t.pr.at[2])
    arrive(t.mx_h.at[1], t.pr.at[5])
    left(t.odc.at[1], t.ps.at[0])
    left(t.normed, t.ps.at[1])
    left(t.nmid, t.ps.at[2])
    for h in range(2):
        left(t.act.at[0, :, pl.ds(0, width)], t.ps.at[3 + h])
    left(t.mixed, t.ps.at[5])
    for k, full in enumerate((t.small, t.rel)):
        left(full.at[pl.ds(0, 3)], t.ms.at[k])
    for m in range(len(plan)):
        mine = block(m, z, p)
        for k in range(3):
            _, _, rise, sink = relay(m, k)

            @pl.when(rise | sink)
            def _():
                left(mine, t.zs.at[m, k])

        @pl.when(can_rise)
        def _():
            left(mine, t.zs.at[m, 3])

        @pl.when(can_sink)
        def _():
            left(mine, t.zs.at[m, 4])

        full, cols = plan[m][3], plan[m][4] // 2
        left(full.at[pl.ds(0, 3), :, pl.ds(0, cols)], t.snd.at[m])
        left(full.at[pl.ds(0, 3), pl.ds(0, 3 * quarter // 4), pl.ds(0, cols)], t.snd.at[m])
    for copy in stored:
        copy.wait()


def forward_pass(tokens, cotangent, limits, shards, rel, small, basis, flip):
    rows, width = tokens.shape
    bf, f32 = jnp.bfloat16, jnp.float32
    keys = H * KEY
    quarter = width // 4
    full = ((NARROW, quarter, width), bf)
    thin = ((NARROW, quarter, keys), bf)
    out_shape = (
        ((H, rows, rows), bf),
        ((rows, keys), bf),
        ((rows, keys), bf),
        ((rows, keys), bf),
        ((rows, width), bf),
        ((2 * rows, keys), bf),
        ((rows, width), f32),
        ((rows, 2 * width), bf),
        ((rows, 2 * width), bf),
        ((rows, width), bf),
        ((2, rows, width), bf),
        ((2, rows, width), bf),
        ((2, rows, width), bf),
        thin,
        thin,
        full,
        full,
        full,
        full,
        full,
        full,
        ((16, 2 * width), f32),
        ((2 * width, width // 4), bf),
        ((2 * width, width // 4), bf),
        ((8, 2 * width), f32),
    )
    vmem = (
        thin,
        thin,
        full,
        full,
        full,
        full,
        ((NARROW,) + rel.shape, bf),
        ((NARROW,) + small.shape, bf),
        ((16, 2 * width), f32),
        ((rows, width), bf),
        ((rows, width), bf),
        ((rows, keys), bf),
        ((rows, keys), bf),
        ((rows, keys), bf),
        ((rows, width), bf),
        (basis.shape, bf),
        (flip.shape, bf),
        ((2 * rows, keys), bf),
        ((2 * rows, keys), bf),
        ((H, rows, rows), bf),
        ((rows, width), bf),
        ((rows, width), f32),
        ((rows, width), bf),
        ((rows, width), bf),
        ((rows, width), bf),
        ((2, rows, width // 2), bf),
        ((2, rows, 2 * width), bf),
        ((rows, 2 * width), bf),
        ((2, rows, width // 2), bf),
        ((8, 2 * width), f32),
    )
    sems = [
        DMA((8, 3)),
        DMA((8, 5)),
        DMA((8, 3)),
        DMA((8, 3)),
        DMA((8, 3)),
        DMA((8, 3)),
        DMA((8,)),
        DMA((8,)),
        DMA((8, 4)),
        DMA((7,)),
        DMA((2,)),
        DMA((2,)),
        DMA((6,)),
        DMA((6,)),
        DMA((20,)),
        DMA((2,)),
    ]
    ins = (tokens, cotangent, limits, *shards, rel, small, basis, flip)
    return pl.pallas_call(
        forward_kernel,
        out_shape=tuple(jax.ShapeDtypeStruct(s, d) for s, d in out_shape),
        in_specs=[HBM, HBM, SMEM] + [HBM] * (len(ins) - 3),
        out_specs=(HBM,) * len(out_shape),
        scratch_shapes=[pltpu.VMEM(s, d) for s, d in vmem] + sems,
        compiler_params=pltpu.CompilerParams(
            collective_id=1, has_side_effects=True, vmem_limit_bytes=60 << 20
        ),
        name="forward_pass",
    )(*ins)


UNITS = 8
CHAINS = (0, 3)


def backward_refs(
    gu0,
    gu1,
    p_h,
    cq_h,
    pq_h,
    k_h,
    v_h,
    rr_h,
    hid_h,
    act_h,
    slope_h,
    od_h,
    nn_h,
    nm_h,
    mx_h,
    fq,
    fk,
    fv,
    fo,
    fi0,
    fi1,
    fu0,
    fu1,
    wq,
    wk,
    wv,
    wo,
    wi,
    wu,
    tok_h,
    cot_h,
    lim_h,
    vec_h,
    sums_h,
    flipt_h,
    turn_h,
    ou,
    oi,
    oo,
    ov,
    ok,
    oq,
    out_h,
    tg_h,
    e_h,
    rg_h,
    gi0,
    gi1,
    go,
    gv,
    gk,
    gq,
    s0,
    s1,
    p,
    cq,
    pq,
    kr,
    vr,
    rr,
    hid,
    act,
    slope,
    od,
    cat,
    idc,
    cot,
    vec,
    sums,
    flipt,
    turn,
    bdc,
    qdc,
    kdc,
    vdc,
    nd,
    rg,
    rgk,
    rgg,
    rgs,
    rgo,
    eb,
    ek,
    eg,
    es,
    eo,
    ld,
    own,
    s1s,
    r1,
    l1,
    s2,
    r2,
    s3,
    r3,
    s4,
    r4,
    lo,
    zu,
    zd,
    zs,
    ps,
    pr,
    xs,
    xr,
    ws,
    wr,
    st,
):
    return types.SimpleNamespace(**locals())


def backward_kernel(*refs):
    head = 46
    held = 2
    t = backward_refs(*refs[:head], *refs[head + held + 4 * UNITS :])
    spare = refs[head : head + held + 4 * UNITS]
    keep = spare[:held]
    got1, got2, got3, last = (
        spare[held + k * UNITS : held + (k + 1) * UNITS] for k in range(4)
    )
    at = position()
    w, z, c, p, x, y = at.w, at.z, at.c, at.p, at.x, at.y
    depth = [(w, lax.rem(z + d, NARROW)) for d in range(1, NARROW)]
    rows_all, width = t.cot.shape
    meet([at.sib, at.xn, at.yn] + depth)

    plan = (
        (t.gu0, False, t.ou, 0, width // 2),
        (t.gu1, False, t.ou, width // 4, width // 2),
        (t.gi0, True, t.oi, 0, width),
        (t.gi1, True, t.oi, width // 2, width),
        (t.go, True, t.oo, 0, width // 2),
        (t.gv, True, t.ov, 0, width // 2),
        (t.gk, True, t.ok, 0, H * KEY // 2),
        (t.gq, True, t.oq, 0, H * KEY // 2),
    )

    def half(m, h, mine):
        g = plan[m][0]
        if h == 0:
            return g.at[:, :, x if mine else 1 - x, 0]
        return g.at[:, y if mine else 1 - y, :, 1]

    def stage1(m):
        for h, target in ((0, at.xn), (1, at.yn)):
            remote(half(m, h, False), got1[m].at[h], t.s1s.at[m, h], t.r1.at[m, h], target).start()
            if not plan[m][1]:
                pltpu.make_async_copy(half(m, h, True), keep[m].at[h], t.l1.at[m, h]).start()

    def kept(m, h, zz, o):
        if not plan[m][1]:
            return keep[m].at[h, zz, o]
        if h == 0:
            return plan[m][0].at[zz, o, x, 0]
        return plan[m][0].at[zz, y, o, 1]

    def stage2(m):
        for h, target, mine in ((0, at.yn, y), (1, at.xn, x)):
            arrive(got1[m].at[h], t.r1.at[m, h])
            if not plan[m][1]:
                arrive(keep[m].at[h], t.l1.at[m, h])

            def add(k, _, h=h):
                zz, o = lax.div(k, 2), lax.rem(k, 2)
                spot = kept(m, h, zz, o)
                spot[...] = low(wide(spot[...]) + wide(got1[m][h, zz, o]))
                return 0

            lax.fori_loop(0, 2 * NARROW, add, 0)
            every = pl.ds(0, NARROW)
            remote(
                kept(m, h, every, 1 - mine), got2[m].at[h], t.s2.at[m, h], t.r2.at[m, h], target
            ).start()

    def stage3(m):
        for h, mine in ((0, y), (1, x)):
            arrive(got2[m].at[h], t.r2.at[m, h])

            def add(zz, _, h=h, mine=mine):
                got2[m][h, zz] = low(wide(kept(m, h, zz, mine)[...]) + wide(got2[m][h, zz]))
                return 0

            lax.fori_loop(0, NARROW, add, 0)
        for d in (1, 3, 2):
            zz = lax.rem(z + d, NARROW)
            remote(
                got2[m].at[:, zz],
                got3[m].at[d - 1],
                t.s3.at[m, d - 1],
                t.r3.at[m, d - 1],
                depth[d - 1],
            ).start()

    def piece(m, pp, part=None):
        _, _, out, start, span = plan[m]
        rows, cols = out.shape[0] // 4, last[m].shape[1]
        first = pp * rows
        if part is not None:
            rows = rows // 2
            first = first + part * rows
        return out.at[pl.ds(pl.multiple_of(first, 16), rows), lanes(c * span + start, cols)]

    def stage4(m):
        for d in (1, 3, 2):
            arrive(got3[m].at[d - 1], t.r3.at[m, d - 1])
        rows = last[m].shape[0] // 2
        for h in range(2):
            total = wide(got2[m][h, z])
            for d in range(3):
                total = total + wide(got3[m][d, h])
            last[m][h * rows : (h + 1) * rows, :] = low(total)
        share(m)

    def share(m):
        mine = piece(m, p)
        remote(last[m], mine, t.s4.at[m], t.r4.at[m, 0], at.xn).start()
        remote(last[m], mine, t.s4.at[m], t.r4.at[m, 1], at.yn).start()
        remote(last[m], mine, t.s4.at[m], t.r4.at[m, 4], at.sib).start()
        pltpu.make_async_copy(last[m], mine, t.lo.at[m]).start()

    def stage5(m):
        for pp, part, slot, target in ((at.px, 0, 0, at.yn), (at.py, 1, 1, at.xn)):
            arrive(piece(m, pp), t.r4.at[m, slot])
            some = piece(m, pp, part)
            remote(some, some, t.s4.at[m], t.r4.at[m, 2 + slot], target).start()
            some = piece(m, pp)
            remote(some, some, t.s4.at[m], t.r4.at[m, 4], at.sib).start()

    def stage6(m):
        arrive(piece(m, at.pd, 0), t.r4.at[m, 2])
        arrive(piece(m, at.pd, 1), t.r4.at[m, 3])
        some = piece(m, at.pd)
        remote(some, some, t.s4.at[m], t.r4.at[m, 4], at.sib).start()

    above, under = (w, jnp.minimum(z + 1, NARROW - 1)), (w, jnp.maximum(z - 1, 0))
    top = NARROW - 1

    def chain_start(m):
        g, room = plan[m][0], got1[m]
        bring(m, 0, rise_to(1))
        bring(m, 1, sink_to(1))

        @pl.when(z == 0)
        def _():
            for i in range(top):
                there = top - i
                remote(
                    g.at[there], room.at[there], t.zs.at[m, i], t.zu.at[m, there], above
                ).start()

        @pl.when(z == top)
        def _():
            for i in range(top):
                spot = NARROW if i == top - 1 else i
                remote(g.at[i], room.at[spot], t.zs.at[m, i], t.zd.at[m, i], under).start()

    def bring(m, spot, there):
        if not plan[m][1]:
            pltpu.make_async_copy(
                plan[m][0].at[there], keep[m].at[spot], t.l1.at[m, spot]
            ).start()

    def brought(m, spot):
        if not plan[m][1]:
            pltpu.make_async_copy(keep[m].at[spot], keep[m].at[spot], t.l1.at[m, spot]).wait()

    def own_part(m, spot, there):
        return plan[m][0].at[there] if plan[m][1] else keep[m].at[spot]

    def join(m, spot, there):
        own = own_part(m, spot, there)

        def add(k, _):
            a, b, h = lax.div(k, 4), lax.rem(lax.div(k, 2), 2), lax.rem(k, 2)
            got1[m][there, a, b, h] = low(wide(got1[m][there, a, b, h]) + wide(own[a, b, h]))
            return 0

        lax.fori_loop(0, 8, add, 0)

    def rising(slot):
        return (z >= 1) & (z <= slot)

    def sinking(slot):
        return (z < top) & (z >= top - slot)

    def rise_to(slot):
        return jnp.minimum(top + z - slot, top)

    def sink_to(slot):
        return jnp.maximum(slot - top + z, 0)

    def chain_step(m, slot):
        room = got1[m]
        brought(m, 0)
        brought(m, 1)

        @pl.when(rising(slot))
        def _():
            there = rise_to(slot)
            arrive(room.at[there], t.zu.at[m, there])
            join(m, 0, there)
            remote(
                room.at[there], room.at[there], t.zs.at[m, 2 + slot], t.zu.at[m, there], above
            ).start()

        @pl.when(sinking(slot))
        def _():
            there = sink_to(slot)
            arrive(room.at[there], t.zd.at[m, there])
            join(m, 1, there)
            spot = NARROW if slot == 2 else there
            remote(
                room.at[there], room.at[spot], t.zs.at[m, 4 + slot], t.zd.at[m, there], under
            ).start()

        if slot == 1:
            bring(m, 0, rise_to(2))
            bring(m, 1, sink_to(2))
        else:
            bring(m, 0, z)

    def chain_end(m):
        room = got1[m]
        brought(m, 0)

        @pl.when(z > 0)
        def _():
            arrive(room.at[z], t.zu.at[m, z])
            join(m, 0, z)

        @pl.when(z < top)
        def _():
            arrive(room.at[NARROW], t.zd.at[m, z])

        def add(k, _, fresh=False):
            a, b, h = lax.div(k, 4), lax.rem(lax.div(k, 2), 2), lax.rem(k, 2)
            own = own_part(m, 0, z)[a, b, h] if fresh else room[z, a, b, h]
            room[z, a, b, h] = low(wide(own) + wide(room[NARROW, a, b, h]))
            return 0

        @pl.when((z > 0) & (z < top))
        def _():
            lax.fori_loop(0, 8, add, 0)

        @pl.when(z == 0)
        def _():
            lax.fori_loop(0, 8, functools.partial(add, fresh=True), 0)

        remote(
            room.at[z, :, 1 - x, 0], got2[m].at[0], t.s1s.at[m, 0], t.r1.at[m, 0], at.xn
        ).start()
        remote(
            room.at[z, 1 - y, :, 1], got2[m].at[1], t.s1s.at[m, 1], t.r1.at[m, 1], at.yn
        ).start()

    def chain_plane(m):
        room = got1[m]
        for h, target in ((0, at.yn), (1, at.xn)):
            arrive(got2[m].at[h], t.r1.at[m, h])
            for o in range(2):
                spot = room.at[z, o, x, 0] if h == 0 else room.at[z, y, o, 1]
                spot[...] = low(wide(spot[...]) + wide(got2[m][h, o]))
            away = room.at[z, 1 - y, x, 0] if h == 0 else room.at[z, y, 1 - x, 1]
            remote(away, got3[m].at[h], t.s2.at[m, h], t.r2.at[m, h], target).start()

    def chain_last(m):
        rows = last[m].shape[0] // 2
        for h in range(2):
            arrive(got3[m].at[h], t.r2.at[m, h])
            last[m][h * rows : (h + 1) * rows, :] = low(
                wide(got1[m][z, y, x, h]) + wide(got3[m][h])
            )
        share(m)

    sources = (
        (t.act_h, t.act),
        (t.od_h, t.od),
        (t.slope_h, t.slope),
        (t.hid_h, t.hid),
        (t.vec_h, t.vec),
        (t.sums_h, t.sums),
        (t.cot_h, t.cot),
        (t.nm_h, t.cat),
        (t.p_h, t.p),
        (t.v_h, t.vr),
        (t.k_h, t.kr),
        (t.cq_h, t.cq),
        (t.pq_h, t.pq),
        (t.rr_h, t.rr),
        (t.turn_h, t.turn),
        (t.flipt_h, t.flipt),
        (t.tok_h, t.cot),
        (t.mx_h, t.cat),
        (t.nn_h, t.idc),
    )
    quarter = width // 4

    def fetch(k, full, shard, held, row=0, col=0):
        span = held.shape[2]
        copies = [
            pltpu.make_async_copy(
                shard.at[pl.ds(row, quarter), pl.ds(col, span)], held.at[z], t.own.at[k, 0]
            )
        ]
        for d in range(1, NARROW):
            zz = lax.rem(z + d, NARROW)
            copies.append(pltpu.make_async_copy(full.at[zz], held.at[zz], t.own.at[k, d]))
        for copy in copies:
            copy.start()
        return copies

    def use(copies):
        for copy in copies:
            copy.wait()

    here0 = fetch(0, t.fu0, t.wu, t.s0)
    here1 = fetch(1, t.fu1, t.wu, t.s1, row=quarter)
    loads = [pltpu.make_async_copy(s, d, t.ld.at[k]) for k, (s, d) in enumerate(sources)]
    for k in (*range(9), *range(10, 16)):
        loads[k].start()

    def give(k, src, dst):
        remote(src, dst, t.ps.at[k], t.pr.at[k], at.sib).start()

    def clip(row, values):
        limit = jnp.where(row < WIN, t.lim_h[0, 0], t.lim_h[0, 1])
        return jnp.minimum(jnp.maximum(values, -limit), limit)

    def leave_mlp(h):
        full = (t.s0, t.s1)[h]
        spots = [
            slice(2 * quarter * zz + quarter * h, 2 * quarter * zz + quarter * (h + 1))
            for zz in range(NARROW)
        ]
        active = jnp.concatenate([t.act[:, spot] for spot in spots], axis=1)

        def one(n, _):
            cols = lanes(n * 512, 512)
            part = dot_nn(active, full[:, :, cols].reshape(width, 512))
            if h == 0:
                t.nd[:, cols] = t.hid[:, cols] + part + t.vec[5:6, cols]
            else:
                t.vr[:, cols] = low(t.nd[:, cols] + part)
            return 0

        lax.fori_loop(0, 3, one, 0)
        for zz, spot in enumerate(spots):
            delta = low(dot_nt(t.od[...], full[zz]) * wide(t.slope[:, spot]))
            t.act[:, spot] = delta
            t.sums[6:7, spot] = jnp.sum(wide(delta), axis=0, keepdims=True)

    def pull_mid():
        for zz in range(NARROW):
            t.nd[:, zz * quarter : (zz + 1) * quarter] = dot_nt(
                t.act[:, 0:width], t.s0[zz]
            ) + dot_nt(t.act[:, width : 2 * width], t.s1[zz])

        def one(i, carry):
            gain_total, shift_total, bias_total = carry
            rows = pl.ds(pl.multiple_of(i * 32, 32), 32)
            v = t.hid[rows, :]
            center = v - jnp.mean(v, axis=1, keepdims=True)
            scale = lax.rsqrt(jnp.mean(center * center, axis=1, keepdims=True) + EPSILON)
            n = center * scale
            delta = t.nd[rows, :]
            e = delta * t.vec[3:4, 0:width]
            back = scale * (
                e
                - jnp.mean(e, axis=1, keepdims=True)
                - n * jnp.mean(e * n, axis=1, keepdims=True)
            )
            full = clip(i * 32, wide(t.cot[rows, :])) + back
            t.hid[rows, :] = full
            rounded = low(full)
            bd[rows, :] = rounded
            return (
                gain_total + jnp.sum(delta * n, axis=0, keepdims=True),
                shift_total + jnp.sum(delta, axis=0, keepdims=True),
                bias_total + jnp.sum(wide(rounded), axis=0, keepdims=True),
            )

        zero = jnp.zeros((1, width), jnp.float32)
        gain_total, shift_total, bias_total = lax.fori_loop(
            0, rows_all // 32, one, (zero, zero, zero)
        )
        t.sums[3:4, 0:width] = gain_total
        t.sums[4:5, 0:width] = shift_total
        t.sums[2:3, 0:width] = bias_total
        half = width // 2
        give(1, bd.at[:, lanes((1 - c) * half, half)], t.bdc.at[1])
        t.bdc[0] = bd[:, lanes(c * half, half)]

    def pull_mixed():
        for zz in range(NARROW):
            md[:, zz * quarter : (zz + 1) * quarter] = low(dot_nt(bd[...], t.s0[zz]))

    bd = t.slope.at[:, 0:width]
    md = t.od
    vd = t.act.at[:, 0:width]
    qd = t.act.at[:, width : width + H * KEY]
    kd = t.act.at[:, width + H * KEY : width + 2 * H * KEY]

    def lane_mask(size, split, rows=rows_all):
        return lax.broadcasted_iota(jnp.int32, (rows, size), 1) < split

    def heads(pair):
        qs = slice(pair * 2 * KEY, (pair + 1) * 2 * KEY)
        vs = slice(pair * 2 * VAL, (pair + 1) * 2 * VAL)
        vals, mixed = t.vr[:, vs], md[:, vs]
        keys, rel, cq, pq = t.kr[:, qs], t.rr[:, qs], t.cq[:, qs], t.pq[:, qs]
        first = lane_mask(2 * VAL, VAL)
        parts = []
        for side in range(2):
            mask = first if side == 0 else jnp.logical_not(first)
            soft = t.p[2 * pair + side]
            pull = dot_nt(jnp.where(mask, mixed, jnp.zeros_like(mixed)), vals)
            full = wide(soft)
            delta = low(full * (pull - jnp.sum(full * pull, axis=1, keepdims=True)))
            turned = dot_nn(delta, t.turn[...])
            padded = jnp.concatenate([turned, jnp.zeros_like(turned)], axis=1)
            slid = low(pltpu.roll(padded, 2 * rows_all, axis=1, stride=1, stride_axis=0))
            parts.append(
                (
                    dot_tn(soft, mixed),
                    dot_nn(delta, keys),
                    dot_tn(delta, cq),
                    dot_nn(slid, rel),
                    dot_tn(slid, pq),
                )
            )
        vd[:, vs] = low(jnp.where(first, parts[0][0], parts[1][0]))
        narrow = lane_mask(2 * KEY, KEY)
        content = jnp.where(narrow, parts[0][1], parts[1][1])
        place = jnp.where(narrow, parts[0][3], parts[1][3])
        kd[:, qs] = low(jnp.where(narrow, parts[0][2], parts[1][2]))
        rel_delta = low(
            jnp.where(lane_mask(2 * KEY, KEY, 2 * rows_all), parts[0][4], parts[1][4])
        )
        qd[:, qs] = low(content + place) * jnp.asarray(KEY ** (-0.5), jnp.bfloat16)
        t.rg[:, qs] = dot_nn(t.flipt[...], rel_delta)
        t.sums[7:8, qs] = jnp.sum(content, axis=0, keepdims=True)
        there = slice(keys_all + pair * 2 * KEY, keys_all + (pair + 1) * 2 * KEY)
        t.sums[7:8, there] = jnp.sum(place, axis=0, keepdims=True)

    def trade():
        for k, (full, pair) in enumerate(((vd, t.vdc), (kd, t.kdc), (qd, t.qdc))):
            cols = full.shape[1] // 2
            away = full.at[:, lanes((1 - c) * cols, cols)]
            give(2 + k, away, pair.at[1])
            pair[0] = full[:, lanes(c * cols, cols)]
        cols = t.rg.shape[1] // 2
        t.rgo[...] = low(t.rg[:, lanes((1 - c) * cols, cols)]).reshape(t.rgo.shape)
        remote(t.rgo, t.rgg.at[0], t.xs.at[0], t.xr.at[0], at.sib).start()
        t.rgk[0] = low(t.rg[:, lanes(c * cols, cols)]).reshape(t.rgo.shape)

    def outer_product(rows_from, pair, dst, start=0):
        size = dst.shape[5]

        def one(zz, _):
            lhs = rows_from[:, :, lanes(zz * quarter, quarter)].reshape(2 * rows_all, quarter)
            rhs = pair[:, :, start : start + size].reshape(2 * rows_all, size)
            dst[zz] = low(dot_tn(lhs, rhs)).reshape(dst.shape[1:])
            return 0

        lax.fori_loop(0, NARROW, one, 0)

    keys_all = H * KEY

    def pull_tokens():
        for zz in range(NARROW):
            t.nd[:, zz * 384 : (zz + 1) * 384] = (
                dot_nt(qd[...], t.s0[zz, :, 0:keys_all])
                + dot_nt(kd[...], t.s0[zz, :, keys_all : 2 * keys_all])
                + dot_nt(vd[...], t.s1[zz])
            )

        def one(i, carry):
            gain_total, shift_total = carry
            rows = pl.ds(pl.multiple_of(i * 32, 32), 32)
            v = wide(t.cot[rows, :])
            center = v - jnp.mean(v, axis=1, keepdims=True)
            scale = lax.rsqrt(jnp.mean(center * center, axis=1, keepdims=True) + EPSILON)
            n = center * scale
            delta = t.nd[rows, :]
            e = delta * t.vec[0:1, 0:width]
            back = scale * (
                e
                - jnp.mean(e, axis=1, keepdims=True)
                - n * jnp.mean(e * n, axis=1, keepdims=True)
            )
            t.od[rows, :] = low(t.hid[rows, :] + back)
            return (
                gain_total + jnp.sum(delta * n, axis=0, keepdims=True),
                shift_total + jnp.sum(delta, axis=0, keepdims=True),
            )

        zero = jnp.zeros((1, width), jnp.float32)
        gain_total, shift_total = lax.fori_loop(0, rows_all // 32, one, (zero, zero))
        t.sums[0:1, 0:width] = gain_total
        t.sums[1:2, 0:width] = shift_total
        for zz in range(NARROW):
            t.eb[zz] = jnp.zeros(t.eb.shape[1:], jnp.float32)
            t.eb[zz, 0:6, 0:384] = t.sums[0:6, zz * 384 : (zz + 1) * 384]
            t.eb[zz, 6:7, :] = t.sums[6:7, zz * 768 : (zz + 1) * 768]
            t.eb[zz, 7:8, 0:128] = t.sums[7:8, zz * 128 : (zz + 1) * 128]
            t.eb[zz, 7:8, 128:256] = t.sums[7:8, 512 + zz * 128 : 512 + (zz + 1) * 128]

    def sum_steps(keep, got, over, out, sends, recvs):
        def begin():
            remote(keep.at[0], got.at[0], sends.at[0], recvs.at[0], at.sib).start()

        def step(k):
            arrive(got.at[k], recvs.at[k])
            total = wide(keep[k]) + wide(got[k])
            keep[k + 1] = total.astype(keep.dtype)
            if k < 2:
                target = (at.xn, at.yn)[k]
                remote(
                    keep.at[k + 1], got.at[k + 1], sends.at[k + 1], recvs.at[k + 1], target
                ).start()
            else:
                for d in (1, 3, 2):
                    zz = lax.rem(z + d, NARROW)
                    remote(
                        keep.at[3, zz],
                        over.at[d - 1],
                        sends.at[2 + d],
                        recvs.at[2 + d],
                        depth[d - 1],
                    ).start()

        def end():
            total = wide(keep[3, z])
            for d in (1, 3, 2):
                arrive(over.at[d - 1], recvs.at[2 + d])
                total = total + wide(over[d - 1])
            out[...] = total

        return begin, step, end

    rel_sums = sum_steps(t.rgk, t.rgg, t.rgs, t.rg.at[0:48, 0:256], t.xs, t.xr)
    row_sums = sum_steps(t.ek, t.eg, t.es, t.eo, t.ws, t.wr)

    stored = []

    def store(src, dst):
        copy = pltpu.make_async_copy(src, dst, t.st.at[len(stored)])
        copy.start()
        stored.append(copy)

    stage1(1)
    chain_start(0)
    for copy in loads[:6]:
        copy.wait()
    use(here0)
    leave_mlp(0)
    use(here1)
    leave_mlp(1)
    store(t.vr, t.out_h)
    give(0, t.act.at[:, lanes((1 - c) * width, width)], t.idc.at[1])
    t.idc[0] = t.act[:, lanes(c * width, width)]
    here0 = fetch(2, t.fi0, t.wi, t.s0)
    here1 = fetch(3, t.fi1, t.wi, t.s1, col=width)
    stage2(1)
    chain_step(0, 1)
    loads[7].wait()
    arrive(t.idc.at[1], t.pr.at[0])
    outer_product(t.cat, t.idc, t.gi0)
    stage1(2)
    outer_product(t.cat, t.idc, t.gi1, width // 2)
    loads[17].start()
    loads[18].start()
    stage3(1)
    loads[6].wait()
    use(here0)
    use(here1)
    pull_mid()
    stored[0].wait()
    loads[9].start()
    loads[16].start()
    here0 = fetch(4, t.fo, t.wo, t.s0)
    here1 = fetch(5, t.fv, t.wv, t.s1)
    use(here0)
    pull_mixed()
    here0 = fetch(6, t.fq, t.wq, t.s0.at[:, :, 0:keys_all])
    here2 = fetch(7, t.fk, t.wk, t.s0.at[:, :, keys_all : 2 * keys_all])
    chain_start(3)
    chain_step(0, 2)
    stage2(2)
    loads[17].wait()
    arrive(t.bdc.at[1], t.pr.at[1])
    outer_product(t.cat, t.bdc, t.go)
    stage1(4)
    for copy in loads[8:16]:
        copy.wait()
    left(t.idc.at[1], t.ps.at[0])
    heads(0)
    heads(1)
    chain_end(0)
    stage3(2)
    stage4(1)
    heads(2)
    chain_plane(0)
    chain_step(3, 1)
    stage5(1)
    stage2(4)
    heads(3)
    trade()
    loads[18].wait()
    loads[16].wait()
    chain_last(0)
    arrive(t.vdc.at[1], t.pr.at[2])
    outer_product(t.idc, t.vdc, t.gv)
    stage1(5)
    stage3(4)
    arrive(t.kdc.at[1], t.pr.at[3])
    outer_product(t.idc, t.kdc, t.gk)
    arrive(t.qdc.at[1], t.pr.at[4])
    outer_product(t.idc, t.qdc, t.gq)
    chain_step(3, 2)
    stage1(7)
    stage1(6)
    stage2(5)
    stage2(7)
    use(here0)
    use(here1)
    use(here2)
    pull_tokens()
    store(t.od, t.tg_h)
    t.ek[0] = t.eb[...]
    row_sums[0]()
    rel_sums[1](0)
    stage6(1)
    row_sums[1](0)
    chain_end(3)
    stage2(6)
    stage3(5)
    stage5(0)
    stage4(4)
    stage3(6)
    rel_sums[1](1)
    chain_plane(3)
    row_sums[1](1)
    stage4(2)
    chain_last(3)
    stage5(4)
    stage5(2)
    stage3(7)
    stage4(5)
    stage4(6)
    rel_sums[1](2)
    stage5(3)
    row_sums[1](2)
    stage6(0)
    stage4(7)
    stage6(2)
    stage5(6)
    stage5(5)
    stage5(7)
    stage6(4)
    stage6(3)
    rel_sums[2]()
    store(t.rg.at[0:48, 0:256], t.rg_h.at[c])
    remote(t.rg.at[0:48, 0:256], t.rg_h.at[c], t.xs.at[6], t.xr.at[6], at.sib).start()
    stage6(5)
    row_sums[2]()
    store(t.eo, t.e_h)
    stage6(6)
    stage6(7)

    for m in range(UNITS):
        _, _, out, _, _ = plan[m]
        cols = last[m].shape[1]
        arrive(out.at[:, pl.ds(0, cols)], t.r4.at[m, 4])
        arrive(last[m], t.lo.at[m])
        if m in CHAINS:
            room = got1[m]
            for i in range(top):

                @pl.when((z == 0) | (z == top))
                def _():
                    left(room.at[0], t.zs.at[m, i])

            for slot in (1, 2):

                @pl.when(rising(slot))
                def _():
                    left(room.at[0], t.zs.at[m, 2 + slot])

                @pl.when(sinking(slot))
                def _():
                    left(room.at[0], t.zs.at[m, 4 + slot])

            for h in range(2):
                left(got2[m].at[h], t.s1s.at[m, h])
                left(got3[m].at[h], t.s2.at[m, h])
        else:
            for h in range(2):
                left(got1[m].at[h], t.s1s.at[m, h])
                left(got2[m].at[h], t.s2.at[m, h])
            for d in range(3):
                left(got3[m].at[d], t.s3.at[m, d])
        left(out.at[:, pl.ds(0, cols)], t.s4.at[m])
        left(out.at[pl.ds(0, 3 * (out.shape[0] // 4)), pl.ds(0, cols)], t.s4.at[m])
    for k, pair in enumerate((t.bdc, t.vdc, t.kdc, t.qdc)):
        left(pair.at[1], t.ps.at[1 + k])
    for got, over, sends in ((t.rgg, t.rgs, t.xs), (t.eg, t.es, t.ws)):
        for k in range(3):
            left(got.at[k], sends.at[k])
            left(over.at[k], sends.at[3 + k])
    left(t.rg.at[0:48, 0:256], t.xs.at[6])
    arrive(t.rg_h.at[1 - c], t.xr.at[6])
    for copy in stored[1:]:
        copy.wait()


def backward_pass(grads, saved, weights, shards, rest):
    bf, f32 = jnp.bfloat16, jnp.float32
    rows, width = rest[0].shape
    keys = H * KEY
    views = [g.reshape(4, 2, 2, 2, g.shape[0] // 32, g.shape[1]) for g in grads]
    shapes = [(g.shape[0], g.shape[1]) for g in grads] + [(width, width // 2)] * 4
    shapes += [(width, keys // 2)] * 2
    out_shape = (
        ((width // 2, width), bf),
        ((width // 4, 2 * width), bf),
        ((width // 4, width), bf),
        ((width // 4, width), bf),
        ((width // 4, keys), bf),
        ((width // 4, keys), bf),
        ((rows, width), bf),
        ((rows, width), bf),
        ((8, 768), f32),
        ((2, 48, 256), f32),
    )
    vmem = [
        (((2, 2, 2, 2) if m in CHAINS else (2, 4, 2)) + (r // 32, n), bf)
        for m, (r, n) in enumerate(shapes[: len(grads)])
    ]
    for plain, chain in (
        ((2, 4, 2), (5, 2, 2, 2)),
        ((2, 4), (2, 2)),
        ((3, 2), (2,)),
    ):
        vmem += [
            ((chain if m in CHAINS else plain) + (r // 32, n), bf)
            for m, (r, n) in enumerate(shapes)
        ]
    vmem += [((r // 16, n), bf) for r, n in shapes]
    vmem += [((4, 2, 2, 2, r // 32, n), bf) for r, n in shapes[len(grads) :]]
    vmem += [((NARROW, width // 4, width), bf)] * 2
    vmem += [(a.shape, a.dtype) for a in saved[:10]]
    vmem += [((2, rows, width), bf)] * 2
    vmem += [(a.shape, a.dtype) for a in rest[1:] if a.size > 2]
    vmem += [
        ((2, rows, width // 2), bf),
        ((2, rows, keys // 2), bf),
        ((2, rows, keys // 2), bf),
        ((2, rows, width // 2), bf),
        ((rows, width), f32),
        ((F, keys), f32),
        ((4, 4, 48, 256), bf),
        ((3, 4, 48, 256), bf),
        ((3, 48, 256), bf),
        ((4, 48, 256), bf),
        ((4, 8, 768), f32),
        ((4, 4, 8, 768), f32),
        ((3, 4, 8, 768), f32),
        ((3, 8, 768), f32),
        ((8, 768), f32),
    ]
    sems = [
        DMA((20,)),
        DMA((8, 4)),
        DMA((UNITS, 2)),
        DMA((UNITS, 2)),
        DMA((UNITS, 2)),
        DMA((UNITS, 2)),
        DMA((UNITS, 2)),
        DMA((UNITS, 3)),
        DMA((UNITS, 3)),
        DMA((UNITS,)),
        DMA((UNITS, 5)),
        DMA((UNITS,)),
        DMA((UNITS, NARROW)),
        DMA((UNITS, NARROW)),
        DMA((UNITS, 7)),
        DMA((5,)),
        DMA((5,)),
        DMA((7,)),
        DMA((7,)),
        DMA((6,)),
        DMA((6,)),
        DMA((4,)),
    ]
    ins = (*views, *saved, *weights, *shards, *rest)
    return pl.pallas_call(
        backward_kernel,
        out_shape=tuple(jax.ShapeDtypeStruct(s, d) for s, d in out_shape),
        in_specs=[SMEM if a.size == 2 else HBM for a in ins],
        out_specs=(HBM,) * len(out_shape),
        scratch_shapes=[pltpu.VMEM(s, d) for s, d in vmem] + sems,
        compiler_params=pltpu.CompilerParams(
            collective_id=2, has_side_effects=True, vmem_limit_bytes=60 << 20
        ),
        name="backward_pass",
    )(*ins)


def finish_kernel(count, *refs):
    ins, (rows_h, rel_h), passed = refs[:count], refs[count : count + 2], refs[count + 2 : count + 4]
    refs = refs[count + 4 :]
    outs, relative, kept, vectors = (
        refs[:count],
        refs[count],
        refs[count + 1 : count + 3],
        refs[count + 3 : count + 12],
    )
    refs = refs[count + 12 :]
    low_in, f32_out, through = refs[:count], refs[count : 2 * count], refs[2 * count : 2 * count + 2]
    into, out = refs[2 * count + 2 :]
    loads = [
        pltpu.make_async_copy(src, dst, into.at[k])
        for k, (src, dst) in enumerate(zip((*ins, *passed), (*low_in, *through)))
    ]
    for copy in loads:
        copy.start()
    stored = []

    def store(src, dst):
        copy = pltpu.make_async_copy(src, dst, out.at[len(stored)])
        copy.start()
        stored.append(copy)

    size = relative.shape[1] // 2
    relative[:, 0:size] = rel_h[0]
    relative[:, size : 2 * size] = rel_h[1]
    for k, vector in enumerate(vectors):
        n = vector.shape[0]
        row, start = (7, 128 * (k - 7)) if k >= 7 else (k, 0)
        vector[...] = rows_h[row : row + 1, start : start + n].reshape(n)
    for k in (count, count + 1):
        loads[k].wait()
        store(through[k - count], kept[k - count])
    for k in range(count):
        loads[k].wait()
        src, dst, res = low_in[k], f32_out[k], outs[k]
        half = src.shape[0] // 2
        for part in range(2):

            def one(i, _):
                spot = pl.ds(pl.multiple_of(part * half + i * 32, 32), 32)
                dst[spot, :] = wide(src[spot, :])
                return 0

            lax.fori_loop(0, half // 32, one, 0)
            spot = pl.ds(part * half, half)
            store(dst.at[spot], res.at[spot])
    for copy in stored:
        copy.wait()


def finish_grads(sums, rows, rel, layer_out, tokens_grad):
    f32 = jnp.float32
    vmem = pl.BlockSpec(memory_space=pltpu.VMEM)
    count = len(sums)
    lengths = (384, 384, 384, 384, 384, 384, 768, 128, 128)
    shapes = [(a.shape, f32) for a in sums] + [((rel.shape[1], 2 * rel.shape[2]), f32)]
    shapes += [(a.shape, a.dtype) for a in (layer_out, tokens_grad)]
    shapes += [((n,), f32) for n in lengths]
    through = [(a.shape, a.dtype) for a in (layer_out, tokens_grad)]
    scratch = [(a.shape, a.dtype) for a in sums] + [(a.shape, f32) for a in sums] + through
    return pl.pallas_call(
        lambda *refs: finish_kernel(count, *refs),
        out_shape=tuple(jax.ShapeDtypeStruct(s, d) for s, d in shapes),
        in_specs=[HBM] * count + [vmem] * 2 + [HBM] * 2,
        out_specs=(HBM,) * count + (vmem,) + (HBM,) * 2 + (vmem,) * len(lengths),
        scratch_shapes=[pltpu.VMEM(s, d) for s, d in scratch]
        + [DMA((count + 2,)), DMA((2 * count + 2,))],
        compiler_params=pltpu.CompilerParams(vmem_limit_bytes=60 << 20),
        name="finish_grads",
    )(*sums, rows, rel, layer_out, tokens_grad)


def basis_rows(length, features):
    f32 = np.float32
    family = features // 6
    offsets = np.arange(2 * length - 1, dtype=f32) - f32(length - 1)
    distance = np.abs(offsets)[:, None]
    halves = f32(2.0) ** np.linspace(3.0, math.log2(length), family, dtype=f32)
    decays = np.exp(f32(-math.log(2.0)) / halves[None, :] * distance)
    widths = f32(2.0) ** np.arange(1, family + 1, dtype=f32) - f32(1.0)
    central = np.where(widths[None, :] > distance, f32(1.0), f32(0.0))
    centers = np.linspace(0.0, float(length), family, dtype=f32)
    spread = f32(length / family)
    bump_rows = np.exp(f32(-0.5) * ((distance - centers[None, :]) / spread) ** 2)
    positive = np.concatenate([decays, central, bump_rows], axis=1)
    return np.concatenate([positive, np.sign(offsets)[:, None] * positive], axis=1)


def per_device_linked(
    tokens,
    cotangent,
    thresholds,
    attn_norm_gain,
    attn_norm_shift,
    query_weight,
    key_weight,
    value_weight,
    relative_weight,
    content_bias,
    position_bias,
    out_weight,
    out_bias,
    mlp_norm_gain,
    mlp_norm_shift,
    inner_weight,
    inner_bias,
    outer_weight,
    outer_bias,
):
    _, length, width = tokens.shape
    bf = jnp.bfloat16
    vectors = (
        (attn_norm_gain, 0, 0),
        (attn_norm_shift, 1, 0),
        (out_bias, 2, 0),
        (mlp_norm_gain, 3, 0),
        (mlp_norm_shift, 4, 0),
        (outer_bias, 5, 0),
        (inner_bias, 6, 0),
        (content_bias, 0, 384),
        (position_bias, 1, 384),
    )
    small = jnp.zeros((8, 512), bf)
    for vector, row, col in vectors:
        table = vector.reshape(-1, min(vector.shape[0], 384))
        n, m = table.shape
        small = small + jnp.pad(table, ((row, 8 - row - n), (col, 512 - col - m)))
    limits = thresholds
    table = basis_rows(length, F)
    empty = np.zeros((1, F), np.float32)
    basis = jnp.asarray(np.concatenate([table, empty]), bf)
    flip = jnp.asarray(np.concatenate([table[::-1], empty]), bf)
    flip_t = jnp.asarray(np.concatenate([table[::-1], empty]).T, bf)
    turn = jnp.asarray(np.eye(length)[::-1], bf)
    flat_tokens = tokens.reshape(length, width)
    flat_cotangent = cotangent.reshape(length, width)
    shards = (query_weight, key_weight, value_weight, out_weight, inner_weight, outer_weight)
    outs = forward_pass(
        flat_tokens, flat_cotangent, limits, shards, relative_weight, small, basis, flip
    )
    saved, weights, (vec, gu0, gu1, sums) = outs[:13], outs[13:21], outs[21:]
    ou, oi, oo, ov, ok, oq, layer_out, tokens_grad, rows, rel = backward_pass(
        (gu0, gu1),
        saved,
        weights,
        shards,
        (flat_tokens, flat_cotangent, limits, vec, sums, flip_t, turn),
    )
    outer, inner, out, value, key, query, relative, layer_out, tokens_grad, *vectors = finish_grads(
        (ou, oi, oo, ov, ok, oq), rows, rel, layer_out, tokens_grad
    )
    gain, shift, out_b, mlp_gain, mlp_shift, outer_b, inner_b, content_b, position_b = vectors
    return (
        layer_out[None],
        tokens_grad[None],
        gain,
        shift,
        query,
        key,
        value,
        relative,
        content_b,
        position_b,
        out,
        out_b,
        mlp_gain,
        mlp_shift,
        inner,
        inner_b,
        outer,
        outer_b,
    )


def solution(mesh):
    body = per_device_generic
    if mesh.shape[WIDE] == 8 and mesh.shape[DEPTH] == 4:
        body = per_device_linked
    in_specs = (
        P((WIDE, DEPTH), None, None),
        P((WIDE, DEPTH), None, None),
        P((WIDE, DEPTH), None),
        P(DEPTH),
        P(DEPTH),
        P(DEPTH, None),
        P(DEPTH, None),
        P(DEPTH, None),
        P(DEPTH, None),
        P(DEPTH),
        P(DEPTH),
        P(DEPTH, None),
        P(DEPTH),
        P(DEPTH),
        P(DEPTH),
        P(DEPTH, None),
        P(DEPTH),
        P(DEPTH, None),
        P(DEPTH),
    )
    out_specs = (
        P((WIDE, DEPTH), None, None),
        P((WIDE, DEPTH), None, None),
        P(DEPTH),
        P(DEPTH),
        P(DEPTH, None),
        P(DEPTH, None),
        P(DEPTH, None),
        P(DEPTH, None),
        P(DEPTH),
        P(DEPTH),
        P(DEPTH, None),
        P(DEPTH),
        P(DEPTH),
        P(DEPTH),
        P(DEPTH, None),
        P(DEPTH),
        P(DEPTH, None),
        P(DEPTH),
    )
    return jax.shard_map(
        body, mesh=mesh, in_specs=in_specs, out_specs=out_specs, check_vma=False
    )
```

```python
import functools
import math
import types

import jax
import jax.numpy as jnp
import numpy as np
from jax import lax
from jax.experimental import pallas as pl
from jax.experimental.pallas import tpu as pltpu
from jax.sharding import PartitionSpec as P

H = 8
KEY = 64
VAL = 192
F = 192
WIN = 128


EPSILON = 1e-05


def basis_table(length, features):
    family = features // 6
    offsets = jnp.arange(2 * length - 1, dtype=jnp.float32) - (length - 1)
    distance = jnp.abs(offsets)[:, None]
    halves = 2.0 ** jnp.linspace(3.0, math.log2(length), family, dtype=jnp.float32)
    decays = jnp.exp(-math.log(2.0) / halves[None, :] * distance)
    widths = 2.0 ** jnp.arange(1, family + 1, dtype=jnp.float32) - 1.0
    central = jnp.where(widths[None, :] > distance, 1.0, 0.0).astype(jnp.float32)
    centers = jnp.linspace(0.0, float(length), family, dtype=jnp.float32)
    spread = length / family
    bump_rows = jnp.exp(-0.5 * ((distance - centers[None, :]) / spread) ** 2)
    positive = jnp.concatenate([decays, central, bump_rows], axis=1)
    return jnp.concatenate([positive, jnp.sign(offsets)[:, None] * positive], axis=1)


def shift_offsets(raw_scores, length):
    leading = raw_scores.shape[:-2]
    padded = jnp.pad(raw_scores, [(0, 0)] * len(leading) + [(0, 0), (0, 1)])
    flatten = padded.reshape(leading + (2 * length * length,))
    window = flatten[..., length - 1 : length - 1 + length * (2 * length - 1)]
    return window.reshape(leading + (length, 2 * length - 1))[..., :length]


def unshift_offsets(grad_scores, length):
    leading = grad_scores.shape[:-2]
    widened = jnp.pad(grad_scores, [(0, 0)] * len(leading) + [(0, 0), (0, length - 1)])
    flatten = widened.reshape(leading + (length * (2 * length - 1),))
    flatten = jnp.pad(flatten, [(0, 0)] * len(leading) + [(length - 1, 1)])
    return flatten.reshape(leading + (length, 2 * length))[..., : 2 * length - 1]


def layer_norm(values, gain, shift):
    center = values - jnp.mean(values, axis=-1, keepdims=True)
    spread = jnp.mean(center * center, axis=-1, keepdims=True)
    return center * lax.rsqrt(spread + EPSILON) * gain + shift


def gelu_exact(values):
    return jax.nn.gelu(values, approximate=False)


def column_sums(values):
    return jnp.sum(values.astype(jnp.float32), axis=0)


WIDE = "wide"
DEPTH = "narrow"


def spread_rows(shard):
    return lax.all_gather(shard, DEPTH, axis=0, tiled=True)


def sum_columns(part):
    low = part.astype(jnp.bfloat16)
    return lax.psum_scatter(low, WIDE, scatter_dimension=1, tiled=True).astype(jnp.float32)


def sum_rows(part):
    low = part.astype(jnp.bfloat16)
    return lax.psum_scatter(low, DEPTH, scatter_dimension=0, tiled=True).astype(jnp.float32)


def spread_columns(part):
    low = part.astype(jnp.bfloat16)
    return lax.all_gather(low, WIDE, axis=1, tiled=True).astype(jnp.float32)


def per_device_generic(
    tokens,
    cotangent,
    thresholds,
    attn_norm_gain,
    attn_norm_shift,
    query_weight,
    key_weight,
    value_weight,
    relative_weight,
    content_bias,
    position_bias,
    out_weight,
    out_bias,
    mlp_norm_gain,
    mlp_norm_shift,
    inner_weight,
    inner_bias,
    outer_weight,
    outer_bias,
):
    seq_count, length, model_width = tokens.shape
    row_count = seq_count * length
    span = 2 * length - 1
    query_scale = KEY ** (-0.5)
    (
        attn_gain,
        attn_shift,
        query_full,
        key_full,
        value_full,
        relative_full,
        content_full,
        position_full,
        exit_full,
        exit_bias,
    ) = (
        spread_rows(attn_norm_gain),
        spread_rows(attn_norm_shift),
        spread_rows(query_weight),
        spread_rows(key_weight),
        spread_rows(value_weight),
        spread_rows(relative_weight),
        spread_rows(content_bias),
        spread_rows(position_bias),
        spread_rows(out_weight),
        spread_rows(out_bias),
    )
    mlp_gain, mlp_shift, inner_full, inner_offset, outer_full, outer_offset = (
        spread_rows(mlp_norm_gain),
        spread_rows(mlp_norm_shift),
        spread_rows(inner_weight),
        spread_rows(inner_bias),
        spread_rows(outer_weight),
        spread_rows(outer_bias),
    )
    flat_tokens = tokens.reshape(row_count, model_width).astype(jnp.float32)
    attn_gain_f = attn_gain.astype(jnp.float32)
    attn_shift_f = attn_shift.astype(jnp.float32)
    normed = layer_norm(flat_tokens, attn_gain_f, attn_shift_f).astype(jnp.bfloat16)
    queries = jnp.dot(normed, query_full, preferred_element_type=jnp.float32) * query_scale
    content_query = (
        (queries + content_full.astype(jnp.float32))
        .astype(jnp.bfloat16)
        .reshape(seq_count, length, H, KEY)
    )
    position_query = (
        (queries + position_full.astype(jnp.float32))
        .astype(jnp.bfloat16)
        .reshape(seq_count, length, H, KEY)
    )
    key_rows = (
        jnp.dot(normed, key_full, preferred_element_type=jnp.float32)
        .astype(jnp.bfloat16)
        .reshape(seq_count, length, H, KEY)
    )
    value_rows = (
        jnp.dot(normed, value_full, preferred_element_type=jnp.float32)
        .astype(jnp.bfloat16)
        .reshape(seq_count, length, H, VAL)
    )
    basis = basis_table(length, F).astype(jnp.bfloat16)
    rel_keys = (
        jnp.dot(basis, relative_full, preferred_element_type=jnp.float32)
        .astype(jnp.bfloat16)
        .reshape(span, H, KEY)
    )

    def attention_logits():
        content = jnp.einsum(
            "bihe,bjhe->bhij", content_query, key_rows, preferred_element_type=jnp.float32
        )
        raw_scores = jnp.einsum(
            "bihe,the->bhit", position_query, rel_keys, preferred_element_type=jnp.float32
        )
        return content + shift_offsets(raw_scores, length)

    logits = attention_logits()
    row_peak = jnp.max(logits, axis=-1, keepdims=True)
    log_total = row_peak + jnp.log(jnp.sum(jnp.exp(logits - row_peak), axis=-1, keepdims=True))
    attention = jnp.exp(logits - log_total).astype(jnp.bfloat16)
    mixed_heads = jnp.einsum(
        "bhij,bjhd->bihd", attention, value_rows, preferred_element_type=jnp.float32
    )
    mixed_heads = mixed_heads.astype(jnp.bfloat16).reshape(row_count, H * VAL)
    hidden = flat_tokens + (
        jnp.dot(mixed_heads, exit_full, preferred_element_type=jnp.float32)
        + exit_bias.astype(jnp.float32)
    )
    mlp_gain_f = mlp_gain.astype(jnp.float32)
    mlp_shift_f = mlp_shift.astype(jnp.float32)
    normed_mid = layer_norm(hidden, mlp_gain_f, mlp_shift_f).astype(jnp.bfloat16)
    inner_pre = jnp.dot(
        normed_mid, inner_full, preferred_element_type=jnp.float32
    ) + inner_offset.astype(jnp.float32)
    active, gelu_pull = jax.vjp(gelu_exact, inner_pre)
    active_low = active.astype(jnp.bfloat16)
    result = hidden + (
        jnp.dot(active_low, outer_full, preferred_element_type=jnp.float32)
        + outer_offset.astype(jnp.float32)
    )
    layer_out = result.astype(jnp.bfloat16).reshape(seq_count, length, model_width)
    clip_limit = jnp.repeat(thresholds, WIN, axis=1).reshape(row_count, 1)
    clipped = jnp.clip(
        cotangent.reshape(row_count, model_width).astype(jnp.float32), -clip_limit, clip_limit
    )
    mlp_gain, mlp_shift, inner_full, inner_offset, outer_full, outer_offset = (
        spread_rows(mlp_norm_gain),
        spread_rows(mlp_norm_shift),
        spread_rows(inner_weight),
        spread_rows(inner_bias),
        spread_rows(outer_weight),
        spread_rows(outer_bias),
    )
    mlp_gain_f = mlp_gain.astype(jnp.float32)
    outer_delta = clipped.astype(jnp.bfloat16)
    outer_bias_grad = column_sums(outer_delta)
    outer_weight_grad = jnp.einsum(
        "nk,nm->km", active_low, outer_delta, preferred_element_type=jnp.float32
    )
    active_delta = jnp.einsum(
        "nm,km->nk", outer_delta, outer_full, preferred_element_type=jnp.float32
    )
    (inner_grad_pre,) = gelu_pull(active_delta)
    inner_delta = inner_grad_pre.astype(jnp.bfloat16)
    inner_bias_grad = column_sums(inner_delta)
    inner_weight_grad = jnp.einsum(
        "nd,nf->df", normed_mid, inner_delta, preferred_element_type=jnp.float32
    )
    mid_delta = jnp.einsum("nf,df->nd", inner_delta, inner_full, preferred_element_type=jnp.float32)
    norm_out, norm_pull = jax.vjp(layer_norm, hidden, mlp_gain_f, mlp_shift_f)
    hidden_part, mlp_gain_grad, mlp_shift_grad = norm_pull(mid_delta)
    hidden_delta = clipped + hidden_part
    (
        attn_gain,
        attn_shift,
        query_full,
        key_full,
        value_full,
        relative_full,
        content_full,
        position_full,
        exit_full,
        exit_bias,
    ) = (
        spread_rows(attn_norm_gain),
        spread_rows(attn_norm_shift),
        spread_rows(query_weight),
        spread_rows(key_weight),
        spread_rows(value_weight),
        spread_rows(relative_weight),
        spread_rows(content_bias),
        spread_rows(position_bias),
        spread_rows(out_weight),
        spread_rows(out_bias),
    )
    attn_gain_f = attn_gain.astype(jnp.float32)
    branch_delta = hidden_delta.astype(jnp.bfloat16)
    out_bias_grad = column_sums(branch_delta)
    out_weight_grad = jnp.einsum(
        "nk,nd->kd", mixed_heads, branch_delta, preferred_element_type=jnp.float32
    )
    mixed_delta = jnp.einsum(
        "nd,kd->nk", branch_delta, exit_full, preferred_element_type=jnp.float32
    )
    mixed_delta = mixed_delta.astype(jnp.bfloat16).reshape(seq_count, length, H, VAL)
    logits = attention_logits()
    soft_rows = jnp.exp(logits - log_total)
    attention = soft_rows.astype(jnp.bfloat16)
    attention_delta = jnp.einsum(
        "bihd,bjhd->bhij", mixed_delta, value_rows, preferred_element_type=jnp.float32
    )
    value_delta = jnp.einsum(
        "bhij,bihd->bjhd", attention, mixed_delta, preferred_element_type=jnp.float32
    )
    value_delta = value_delta.astype(jnp.bfloat16).reshape(row_count, H * VAL)
    logit_delta = soft_rows * (
        attention_delta - jnp.sum(soft_rows * attention_delta, axis=-1, keepdims=True)
    )
    logit_delta = logit_delta.astype(jnp.bfloat16)
    content_delta = jnp.einsum(
        "bhij,bjhe->bihe", logit_delta, key_rows, preferred_element_type=jnp.float32
    )
    key_delta = jnp.einsum(
        "bhij,bihe->bjhe", logit_delta, content_query, preferred_element_type=jnp.float32
    )
    key_delta = key_delta.astype(jnp.bfloat16).reshape(row_count, H * KEY)
    offset_delta = unshift_offsets(logit_delta, length)
    position_delta = jnp.einsum(
        "bhit,the->bihe", offset_delta, rel_keys, preferred_element_type=jnp.float32
    )
    rel_delta = jnp.einsum(
        "bhit,bihe->the", offset_delta, position_query, preferred_element_type=jnp.float32
    )
    rel_delta = rel_delta.astype(jnp.bfloat16).reshape(span, H * KEY)
    relative_weight_grad = jnp.einsum(
        "tf,tk->fk", basis, rel_delta, preferred_element_type=jnp.float32
    )
    content_delta = content_delta.reshape(row_count, H * KEY)
    position_delta = position_delta.reshape(row_count, H * KEY)
    content_bias_grad = jnp.sum(content_delta, axis=0)
    position_bias_grad = jnp.sum(position_delta, axis=0)
    query_delta = (content_delta + position_delta).astype(jnp.bfloat16) * jnp.asarray(
        query_scale, jnp.bfloat16
    )
    query_weight_grad = jnp.einsum(
        "nd,nk->dk", normed, query_delta, preferred_element_type=jnp.float32
    )
    key_weight_grad = jnp.einsum("nd,nk->dk", normed, key_delta, preferred_element_type=jnp.float32)
    value_weight_grad = jnp.einsum(
        "nd,nk->dk", normed, value_delta, preferred_element_type=jnp.float32
    )
    normed_delta = (
        jnp.einsum("nk,dk->nd", query_delta, query_full, preferred_element_type=jnp.float32)
        + jnp.einsum("nk,dk->nd", key_delta, key_full, preferred_element_type=jnp.float32)
        + jnp.einsum("nk,dk->nd", value_delta, value_full, preferred_element_type=jnp.float32)
    )
    first_out, first_pull = jax.vjp(layer_norm, flat_tokens, attn_gain_f, attn_shift_f)
    tokens_part, attn_gain_grad, attn_shift_grad = first_pull(normed_delta)
    tokens_grad = (
        (hidden_delta + tokens_part).astype(jnp.bfloat16).reshape(seq_count, length, model_width)
    )
    (
        query_weight_grad,
        key_weight_grad,
        value_weight_grad,
        relative_weight_grad,
        out_weight_grad,
        inner_weight_grad,
        outer_weight_grad,
    ) = (
        sum_columns(query_weight_grad),
        sum_columns(key_weight_grad),
        sum_columns(value_weight_grad),
        sum_columns(relative_weight_grad),
        sum_columns(out_weight_grad),
        sum_columns(inner_weight_grad),
        sum_columns(outer_weight_grad),
    )
    (
        query_weight_grad,
        key_weight_grad,
        value_weight_grad,
        relative_weight_grad,
        out_weight_grad,
        inner_weight_grad,
        outer_weight_grad,
        attn_gain_grad,
        attn_shift_grad,
        content_bias_grad,
        position_bias_grad,
        out_bias_grad,
        mlp_gain_grad,
        mlp_shift_grad,
        inner_bias_grad,
        outer_bias_grad,
    ) = (
        sum_rows(query_weight_grad),
        sum_rows(key_weight_grad),
        sum_rows(value_weight_grad),
        sum_rows(relative_weight_grad),
        sum_rows(out_weight_grad),
        sum_rows(inner_weight_grad),
        sum_rows(outer_weight_grad),
        sum_rows(attn_gain_grad),
        sum_rows(attn_shift_grad),
        sum_rows(content_bias_grad),
        sum_rows(position_bias_grad),
        sum_rows(out_bias_grad),
        sum_rows(mlp_gain_grad),
        sum_rows(mlp_shift_grad),
        sum_rows(inner_bias_grad),
        sum_rows(outer_bias_grad),
    )
    (
        query_weight_grad,
        key_weight_grad,
        value_weight_grad,
        relative_weight_grad,
        out_weight_grad,
        inner_weight_grad,
        outer_weight_grad,
    ) = (
        spread_columns(query_weight_grad),
        spread_columns(key_weight_grad),
        spread_columns(value_weight_grad),
        spread_columns(relative_weight_grad),
        spread_columns(out_weight_grad),
        spread_columns(inner_weight_grad),
        spread_columns(outer_weight_grad),
    )
    (
        attn_gain_grad,
        attn_shift_grad,
        content_bias_grad,
        position_bias_grad,
        out_bias_grad,
        mlp_gain_grad,
        mlp_shift_grad,
        inner_bias_grad,
        outer_bias_grad,
    ) = lax.psum(
        (
            attn_gain_grad,
            attn_shift_grad,
            content_bias_grad,
            position_bias_grad,
            out_bias_grad,
            mlp_gain_grad,
            mlp_shift_grad,
            inner_bias_grad,
            outer_bias_grad,
        ),
        WIDE,
    )
    return (
        layer_out,
        tokens_grad,
        attn_gain_grad,
        attn_shift_grad,
        query_weight_grad,
        key_weight_grad,
        value_weight_grad,
        relative_weight_grad,
        content_bias_grad,
        position_bias_grad,
        out_weight_grad,
        out_bias_grad,
        mlp_gain_grad,
        mlp_shift_grad,
        inner_weight_grad,
        inner_bias_grad,
        outer_weight_grad,
        outer_bias_grad,
    )


MESH = pl.DeviceIdType.MESH
NARROW = 4


def position():
    w = lax.axis_index(WIDE)
    z = lax.axis_index(DEPTH)
    c = lax.rem(w, 2)
    p = lax.div(w, 2)
    x = lax.rem(p, 2)
    y = lax.div(p, 2)
    chip = (lambda q: q * 2 + c)
    return types.SimpleNamespace(
        w=w,
        z=z,
        c=c,
        p=p,
        x=x,
        y=y,
        px=p + 1 - 2 * x,
        py=p + 2 - 4 * y,
        pd=3 - p,
        sib=(w + 1 - 2 * c, z),
        xn=(chip(p + 1 - 2 * x), z),
        yn=(chip(p + 2 - 4 * y), z),
    )


def meet(partners):
    barrier = pltpu.get_barrier_semaphore()
    for partner in partners:
        pl.semaphore_signal(barrier, inc=1, device_id=partner, device_id_type=MESH)
    pl.semaphore_wait(barrier, len(partners))


def remote(src, dst, send, recv, target):
    return pltpu.make_async_remote_copy(
        src_ref=src,
        dst_ref=dst,
        send_sem=send,
        recv_sem=recv,
        device_id=target,
        device_id_type=MESH,
    )


HBM = pl.BlockSpec(memory_space=pltpu.HBM)
DMA = pltpu.SemaphoreType.DMA
SMEM = pl.BlockSpec(memory_space=pltpu.SMEM)


def dot_nn(a, b):
    return jnp.dot(a, b, preferred_element_type=jnp.float32)


def dot_nt(a, b):
    return lax.dot_general(a, b, (((1,), (1,)), ((), ())), preferred_element_type=jnp.float32)


def dot_tn(a, b):
    return lax.dot_general(a, b, (((0,), (0,)), ((), ())), preferred_element_type=jnp.float32)


def low(v):
    return v.astype(jnp.bfloat16)


def wide(v):
    return v.astype(jnp.float32)


def lanes(start, size):
    return pl.ds(pl.multiple_of(start, 128), size)


def arrive(ref, sem):
    me = (lax.axis_index(WIDE), lax.axis_index(DEPTH))
    remote(ref, ref, sem, sem, me).wait_recv()


def left(ref, sem):
    me = (lax.axis_index(WIDE), lax.axis_index(DEPTH))
    remote(ref, ref, sem, sem, me).wait_send()


def forward_refs(
    tok_h,
    cot_h,
    lim_h,
    wq,
    wk,
    wv,
    wo,
    wi,
    wu,
    rel_h,
    small_h,
    basis_h,
    flip_h,
    p_h,
    cq_h,
    pq_h,
    k_h,
    v_h,
    rr_h,
    hid_h,
    act_h,
    slope_h,
    od_h,
    nn_h,
    nm_h,
    mx_h,
    fq,
    fk,
    fv,
    fo,
    fi0,
    fi1,
    fu0,
    fu1,
    vec_h,
    gu0,
    gu1,
    sums_h,
    q,
    k,
    v,
    o,
    i0,
    i1,
    rel,
    small,
    vec,
    tok,
    normed,
    cq,
    pq,
    kr,
    vr,
    basis,
    flip,
    rk,
    rr,
    p,
    mixed,
    hidden,
    nmid,
    cot,
    od,
    odc,
    act,
    slope,
    gst,
    sums,
    zr,
    zs,
    xr,
    yr,
    fxr,
    fyr,
    sr,
    snd,
    own,
    ld,
    mr,
    ms,
    ps,
    pr,
    st,
    gs,
):
    return types.SimpleNamespace(**locals())


def forward_kernel(*refs):
    t = forward_refs(*refs)
    at = position()
    w, z, c, p = at.w, at.z, at.c, at.p
    depth = [(w, lax.rem(z + d, NARROW)) for d in range(1, NARROW)]
    meet([at.sib, at.xn, at.yn] + depth)
    rows_all = t.tok.shape[0]
    width = t.tok.shape[1]

    keys_all = H * KEY
    quarter = width // 4
    half_width = width // 2
    plan = (
        (t.wq, 0, 0, t.fq, 0, keys_all, False),
        (t.wk, 0, 0, t.fk, 0, keys_all, False),
        (t.wv, 0, 0, t.fv, 0, width, False),
        (t.wo, 0, 0, t.fo, 0, width, False),
        (t.wi, 0, 0, t.fi0, 0, width, False),
        (t.wi, 0, width, t.fi1, 0, width, False),
        (t.wu, quarter, half_width, t.fu1, half_width, half_width, True),
        (t.wu, quarter, 0, t.fu1, 0, half_width, False),
        (t.wu, 0, 0, t.fu0, 0, width, False),
    )

    def rows_of(m, pp, part=None):
        if plan[m][6]:
            return 0, quarter
        rows = quarter // 4
        start = pp * rows
        if part is not None:
            rows = rows // 2
            start = start + part * rows
        return start, rows

    def block(m, zz, pp, part=None):
        start, rows = rows_of(m, pp, part)
        _, _, _, full, first, span, _ = plan[m]
        cols = span // 2
        rows = pl.ds(pl.multiple_of(start, 16), rows)
        return full.at[zz, rows, lanes(first + c * cols, cols)]

    def send(m, ref, recv, target):
        remote(ref, ref, t.snd.at[m], recv, target).start()

    loads = [
        pltpu.make_async_copy(src, dst, t.ld.at[k])
        for k, (src, dst) in enumerate(
            (
                (t.tok_h, t.tok),
                (t.small_h, t.small.at[z]),
                (t.rel_h, t.rel.at[z]),
                (t.basis_h, t.basis),
                (t.cot_h, t.cot),
                (t.flip_h, t.flip),
            )
        )
    ]
    def over_z(k, src, dst):
        for d in (1, 3, 2):
            remote(src, dst.at[z], t.ms.at[k], t.mr.at[k], depth[d - 1]).start()

    over_z(0, t.small_h, t.small)
    for copy in loads:
        copy.start()

    above, below = (w, jnp.minimum(z + 1, NARROW - 1)), (w, jnp.maximum(z - 1, 0))
    can_rise, can_sink = z < NARROW - 1, z > 0

    def own_piece(m):
        shard, r0, c0, _, _, span, _ = plan[m]
        start, rows = rows_of(m, p)
        cols = span // 2
        return shard.at[pl.ds(pl.multiple_of(r0 + start, 16), rows), lanes(c0 + c * cols, cols)]

    def depart(m):
        @pl.when(can_rise)
        def _():
            remote(
                own_piece(m), block(m, z, p), t.zs.at[m, 3], t.zr.at[m, 0], above
            ).start()

        @pl.when(can_sink)
        def _():
            remote(
                own_piece(m), block(m, z, p), t.zs.at[m, 4], t.zr.at[m, 2], below
            ).start()

    def hop(k):
        first, last = z == 0, z == NARROW - 1
        if k == 0:
            return jnp.where(first, 3, 1)
        if k == 1:
            return jnp.where(first | last, 2, 3)
        return jnp.where(first, 1, jnp.where(last, 3, 2))

    def source(k):
        return lax.rem(z + NARROW - hop(k), NARROW)

    def relay(m, k):
        d = hop(k)
        mine = block(m, source(k), p)
        rise = can_rise & (d <= z)
        sink = can_sink & (d > z)
        return mine, d, rise, sink

    def spread(m, k):
        mine, d, rise, sink = relay(m, k)
        arrive(mine, t.zr.at[m, d - 1])

        @pl.when(rise)
        def _():
            remote(mine, mine, t.zs.at[m, k], t.zr.at[m, jnp.minimum(d, 2)], above).start()

        @pl.when(sink)
        def _():
            remote(mine, mine, t.zs.at[m, k], t.zr.at[m, jnp.maximum(d - 2, 0)], below).start()

        if not plan[m][6]:
            send(m, mine, t.xr.at[m, k], at.xn)
            send(m, mine, t.yr.at[m, k], at.yn)
        send(m, mine, t.sr.at[m], at.sib)

    def forward(m, k):
        zz = source(k)
        arrive(block(m, zz, at.px), t.xr.at[m, k])
        send(m, block(m, zz, at.px, 0), t.fxr.at[m, k], at.yn)
        send(m, block(m, zz, at.px), t.sr.at[m], at.sib)
        arrive(block(m, zz, at.py), t.yr.at[m, k])
        send(m, block(m, zz, at.py, 1), t.fyr.at[m, k], at.xn)
        send(m, block(m, zz, at.py), t.sr.at[m], at.sib)

    def finish(m, k):
        zz = source(k)
        arrive(block(m, zz, at.pd, 0), t.fxr.at[m, k])
        arrive(block(m, zz, at.pd, 1), t.fyr.at[m, k])
        send(m, block(m, zz, at.pd), t.sr.at[m], at.sib)

    depart(0)
    depart(1)
    depart(2)
    over_z(1, t.rel_h, t.rel)
    def all_here(m):
        arrive(plan[m][3].at[pl.ds(0, 3), :, pl.ds(0, plan[m][5] // 2)], t.sr.at[m])

    def fetch(m, held):
        all_here(m)
        shard, r0, c0, full, _, span, _ = plan[m]
        copies = [
            pltpu.make_async_copy(
                shard.at[pl.ds(r0, quarter), pl.ds(c0, span)], held.at[z], t.own.at[m, 0]
            )
        ]
        for d in range(1, NARROW):
            zz = lax.rem(z + d, NARROW)
            copies.append(pltpu.make_async_copy(full.at[zz], held.at[zz], t.own.at[m, d]))
        for copy in copies:
            copy.start()
        return copies

    def use(copies):
        for copy in copies:
            copy.wait()

    def vectors():
        loads[1].wait()
        arrive(t.small.at[pl.ds(0, 3)], t.mr.at[0])
        for zz in range(NARROW):
            rows = wide(t.small[zz])
            for r in range(6):
                t.vec[r : r + 1, zz * 384 : (zz + 1) * 384] = rows[r : r + 1, 0:384]
            for r in range(2):
                spot = slice(zz * 768 + r * 384, zz * 768 + (r + 1) * 384)
                t.vec[6:7, spot] = rows[6 + r : 7 + r, 0:384]
                t.vec[7 + r : 8 + r, zz * 128 : (zz + 1) * 128] = rows[r : r + 1, 384:512]

    def norm_rows(src, dst, gain_row):
        def one(i, _):
            rows = pl.ds(pl.multiple_of(i * 32, 32), 32)
            v = wide(src[rows, :])
            center = v - jnp.mean(v, axis=1, keepdims=True)
            var = jnp.mean(center * center, axis=1, keepdims=True)
            gain = t.vec[gain_row : gain_row + 1, 0:width]
            shift = t.vec[gain_row + 1 : gain_row + 2, 0:width]
            dst[rows, :] = low(center * lax.rsqrt(var + EPSILON) * gain + shift)
            return 0

        lax.fori_loop(0, rows_all // 32, one, 0)

    def flat(full):
        return full[...].reshape(full.shape[0] * full.shape[1], full.shape[2])

    def columns(full, start, size):
        part = full[:, :, lanes(start, size)]
        return part.reshape(full.shape[0] * full.shape[1], size)

    def make_queries():
        queries = dot_nn(t.normed[...], flat(t.q)) * (KEY ** (-0.5))
        size = H * KEY
        t.cq[...] = low(queries + t.vec[7:8, 0:size])
        t.pq[...] = low(queries + t.vec[8:9, 0:size])

    def make_keys():
        t.kr[...] = low(dot_nn(t.normed[...], flat(t.k)))
        loads[2].wait()
        arrive(t.rel.at[pl.ds(0, 3)], t.mr.at[1])
        loads[3].wait()
        table = t.rel[...].reshape(t.rel.shape[0] * t.rel.shape[1], t.rel.shape[2])
        t.rk[...] = low(dot_nn(t.basis[...], table))
        loads[5].wait()
        t.rr[...] = low(dot_nn(t.flip[...], table))

    def make_values():
        def one(n, _):
            t.vr[:, lanes(n * 512, 512)] = low(dot_nn(t.normed[...], columns(t.v, n * 512, 512)))
            return 0

        lax.fori_loop(0, 3, one, 0)

    def pair_mask(size, split):
        return lax.broadcasted_iota(jnp.int32, (rows_all, size), 1) < split

    def heads(pair):
        qs = slice(pair * 2 * KEY, (pair + 1) * 2 * KEY)
        vs = slice(pair * 2 * VAL, (pair + 1) * 2 * VAL)
        first = pair_mask(2 * KEY, KEY)
        keys, rel, vals = t.kr[:, qs], t.rk[:, qs], t.vr[:, vs]
        mixed = []
        for side in range(2):
            keep = first if side == 0 else jnp.logical_not(first)
            cq = jnp.where(keep, t.cq[:, qs], jnp.zeros_like(t.cq[:, qs]))
            pq = jnp.where(keep, t.pq[:, qs], jnp.zeros_like(t.pq[:, qs]))
            raw = dot_nt(pq, rel)
            shifted = pltpu.roll(raw, rows_all + 1, axis=1, stride=1, stride_axis=0)
            logits = dot_nt(cq, keys) + shifted[:, :rows_all]
            grown = jnp.exp(logits - jnp.max(logits, axis=1, keepdims=True))
            soft = low(grown / jnp.sum(grown, axis=1, keepdims=True))
            t.p[2 * pair + side] = soft
            mixed.append(dot_nn(soft, vals))
        t.mixed[:, vs] = low(jnp.where(pair_mask(2 * VAL, VAL), mixed[0], mixed[1]))

    def give(k, src, dst):
        remote(src, dst, t.ps.at[k], t.pr.at[k], at.sib).start()

    stored = []

    def store(src, dst):
        copy = pltpu.make_async_copy(src, dst, t.st.at[len(stored)])
        copy.start()
        stored.append(copy)

    def attend_out():
        def one(n, _):
            cols = lanes(n * 512, 512)
            t.hidden[:, cols] = (
                wide(t.tok[:, cols])
                + dot_nn(t.mixed[...], columns(t.o, n * 512, 512))
                + t.vec[2:3, cols]
            )
            return 0

        lax.fori_loop(0, 3, one, 0)
        norm_rows(t.hidden, t.nmid, 3)
        give(2, t.nmid, t.nm_h.at[1])

    def clip_rows():
        loads[4].wait()

        def one(i, total):
            rows = pl.ds(pl.multiple_of(i * 32, 32), 32)
            clipped = low(clip(i * 32, wide(t.cot[rows, :])))
            t.od[rows, :] = clipped
            return total + jnp.sum(wide(clipped), axis=0, keepdims=True)

        total = lax.fori_loop(0, rows_all // 32, one, jnp.zeros((1, width), jnp.float32))
        t.sums[5:6, 0:width] = total
        half = width // 2
        t.odc[0] = t.od[:, lanes(c * half, half)]
        give(0, t.od.at[:, lanes((1 - c) * half, half)], t.odc.at[1])

    def clip(row, values):
        limit = jnp.where(row < WIN, t.lim_h[0, 0], t.lim_h[0, 1])
        return jnp.minimum(jnp.maximum(values, -limit), limit)

    def inner(h):
        full = (t.i0, t.i1)[h]

        def one(n, _):
            local = n * 256
            cols = lanes(h * width + local, 256)
            pre = dot_nn(t.nmid[...], columns(full, local, 256)) + t.vec[6:7, cols]
            cdf = 0.5 + 0.5 * lax.erf(pre * (0.5**0.5))
            slope = cdf + pre * jnp.exp(-0.5 * pre * pre) * (2.0 * math.pi) ** -0.5
            t.act[0, :, cols] = low(pre * cdf)
            t.slope[:, cols] = low(slope)
            return 0

        lax.fori_loop(0, 6, one, 0)
        cols = pl.ds(h * width, width)
        give(3 + h, t.act.at[0, :, cols], t.act.at[1, :, cols])

    def outer_product(left_ref, right_ref, dst, start, size):
        steps = left_ref.shape[2] // 256
        right = right_ref[:, :, start : start + size].reshape(2 * rows_all, size)

        def tile(slot, n):
            return pltpu.make_async_copy(
                t.gst.at[slot, :, 0:size],
                dst.at[pl.ds(pl.multiple_of(n * 256, 256), 256)],
                t.gs.at[slot],
            )

        def one(n, _):
            slot = lax.rem(n, 2)

            @pl.when(n >= 2)
            def _():
                tile(slot, n - 2).wait()

            lhs = left_ref[:, :, lanes(n * 256, 256)].reshape(2 * rows_all, 256)
            t.gst[slot, :, 0:size] = low(dot_tn(lhs, right))
            tile(slot, n).start()
            return 0

        lax.fori_loop(0, steps, one, 0)
        tile(0, steps - 2).wait()
        tile(1, steps - 1).wait()

    t.sums[...] = jnp.zeros_like(t.sums)
    t.vec[...] = jnp.zeros_like(t.vec)
    here = {}
    spread(0, 0)
    spread(1, 0)
    spread(1, 1)
    forward(0, 0)
    spread(0, 1)
    spread(2, 0)
    spread(2, 1)
    spread(0, 2)
    forward(0, 1)
    depart(3)
    spread(1, 2)
    loads[0].wait()
    vectors()
    norm_rows(t.tok, t.normed, 0)
    give(1, t.normed, t.nn_h.at[1])
    store(t.normed, t.nn_h.at[0])
    store(t.vec, t.vec_h)
    clip_rows()
    store(t.od, t.od_h)
    spread(2, 2)
    forward(1, 1)
    finish(0, 0)
    forward(0, 2)
    depart(4)
    forward(1, 0)
    forward(1, 2)
    depart(5)
    finish(0, 1)
    depart(8)
    forward(2, 2)
    finish(1, 0)
    spread(3, 0)
    finish(0, 2)
    here[0] = fetch(0, t.q)
    forward(2, 0)
    forward(2, 1)
    use(here[0])
    make_queries()
    store(t.cq, t.cq_h)
    store(t.pq, t.pq_h)
    finish(1, 2)
    spread(3, 1)
    finish(1, 1)
    here[1] = fetch(1, t.k)
    finish(2, 2)
    use(here[1])
    make_keys()
    store(t.kr, t.k_h)
    store(t.rr, t.rr_h)
    finish(2, 0)
    forward(3, 0)
    finish(2, 1)
    spread(3, 2)
    here[2] = fetch(2, t.v)
    spread(4, 0)
    spread(4, 1)
    use(here[2])
    make_values()
    store(t.vr, t.v_h)
    forward(3, 1)
    spread(4, 2)
    depart(6)
    heads(0)
    forward(3, 2)
    depart(7)
    spread(5, 0)
    forward(4, 0)
    heads(1)
    finish(3, 0)
    finish(3, 1)
    heads(2)
    spread(5, 1)
    heads(3)
    store(t.p, t.p_h)
    give(5, t.mixed, t.mx_h.at[1])
    store(t.mixed, t.mx_h.at[0])
    spread(5, 2)
    forward(4, 2)
    finish(3, 2)
    forward(4, 1)
    here[3] = fetch(3, t.o)
    spread(7, 0)
    spread(7, 1)
    use(here[3])
    attend_out()
    store(t.hidden, t.hid_h)
    store(t.nmid, t.nm_h.at[0])
    finish(4, 0)
    forward(5, 1)
    forward(5, 2)
    forward(5, 0)
    spread(7, 2)
    spread(8, 0)
    spread(6, 0)
    spread(8, 1)
    finish(4, 2)
    finish(4, 1)
    here[4] = fetch(4, t.i0)
    use(here[4])
    inner(0)
    spread(8, 2)
    finish(5, 2)
    finish(5, 1)
    finish(5, 0)
    here[5] = fetch(5, t.i1)
    use(here[5])
    inner(1)
    store(t.act.at[0], t.act_h)
    store(t.slope, t.slope_h)
    forward(7, 0)
    spread(6, 1)
    forward(8, 0)
    forward(7, 2)
    forward(7, 1)
    forward(8, 1)
    arrive(t.odc.at[1], t.pr.at[0])
    for h in range(2):
        arrive(t.act.at[1, :, pl.ds(0, width)], t.pr.at[3 + h])
    outer_product(t.act, t.odc, t.gu0, 0, 384)
    forward(8, 2)
    finish(7, 0)
    outer_product(t.act, t.odc, t.gu1, 384, 384)
    store(t.sums, t.sums_h)
    finish(7, 1)
    finish(8, 0)
    spread(6, 2)
    finish(8, 2)
    finish(8, 1)
    finish(7, 2)
    all_here(6)
    all_here(7)
    all_here(8)

    arrive(t.nn_h.at[1], t.pr.at[1])
    arrive(t.nm_h.at[1], t.pr.at[2])
    arrive(t.mx_h.at[1], t.pr.at[5])
    left(t.odc.at[1], t.ps.at[0])
    left(t.normed, t.ps.at[1])
    left(t.nmid, t.ps.at[2])
    for h in range(2):
        left(t.act.at[0, :, pl.ds(0, width)], t.ps.at[3 + h])
    left(t.mixed, t.ps.at[5])
    for k, full in enumerate((t.small, t.rel)):
        left(full.at[pl.ds(0, 3)], t.ms.at[k])
    for m in range(len(plan)):
        mine = block(m, z, p)
        for k in range(3):
            _, _, rise, sink = relay(m, k)

            @pl.when(rise | sink)
            def _():
                left(mine, t.zs.at[m, k])

        @pl.when(can_rise)
        def _():
            left(mine, t.zs.at[m, 3])

        @pl.when(can_sink)
        def _():
            left(mine, t.zs.at[m, 4])

        full, cols = plan[m][3], plan[m][5] // 2
        left(full.at[pl.ds(0, 3), :, pl.ds(0, cols)], t.snd.at[m])
        if not plan[m][6]:
            left(full.at[pl.ds(0, 3), pl.ds(0, 3 * quarter // 4), pl.ds(0, cols)], t.snd.at[m])
    for copy in stored:
        copy.wait()


def forward_pass(tokens, cotangent, limits, shards, rel, small, basis, flip):
    rows, width = tokens.shape
    bf, f32 = jnp.bfloat16, jnp.float32
    keys = H * KEY
    quarter = width // 4
    full = ((NARROW, quarter, width), bf)
    thin = ((NARROW, quarter, keys), bf)
    out_shape = (
        ((H, rows, rows), bf),
        ((rows, keys), bf),
        ((rows, keys), bf),
        ((rows, keys), bf),
        ((rows, width), bf),
        ((2 * rows, keys), bf),
        ((rows, width), f32),
        ((rows, 2 * width), bf),
        ((rows, 2 * width), bf),
        ((rows, width), bf),
        ((2, rows, width), bf),
        ((2, rows, width), bf),
        ((2, rows, width), bf),
        thin,
        thin,
        full,
        full,
        full,
        full,
        full,
        full,
        ((16, 2 * width), f32),
        ((2 * width, width // 4), bf),
        ((2 * width, width // 4), bf),
        ((8, 2 * width), f32),
    )
    vmem = (
        thin,
        thin,
        full,
        full,
        full,
        full,
        ((NARROW,) + rel.shape, bf),
        ((NARROW,) + small.shape, bf),
        ((16, 2 * width), f32),
        ((rows, width), bf),
        ((rows, width), bf),
        ((rows, keys), bf),
        ((rows, keys), bf),
        ((rows, keys), bf),
        ((rows, width), bf),
        (basis.shape, bf),
        (flip.shape, bf),
        ((2 * rows, keys), bf),
        ((2 * rows, keys), bf),
        ((H, rows, rows), bf),
        ((rows, width), bf),
        ((rows, width), f32),
        ((rows, width), bf),
        ((rows, width), bf),
        ((rows, width), bf),
        ((2, rows, width // 2), bf),
        ((2, rows, 2 * width), bf),
        ((rows, 2 * width), bf),
        ((2, rows, width // 2), bf),
        ((8, 2 * width), f32),
    )
    sems = [
        DMA((9, 3)),
        DMA((9, 5)),
        DMA((9, 3)),
        DMA((9, 3)),
        DMA((9, 3)),
        DMA((9, 3)),
        DMA((9,)),
        DMA((9,)),
        DMA((9, 4)),
        DMA((7,)),
        DMA((2,)),
        DMA((2,)),
        DMA((6,)),
        DMA((6,)),
        DMA((20,)),
        DMA((2,)),
    ]
    ins = (tokens, cotangent, limits, *shards, rel, small, basis, flip)
    return pl.pallas_call(
        forward_kernel,
        out_shape=tuple(jax.ShapeDtypeStruct(s, d) for s, d in out_shape),
        in_specs=[HBM, HBM, SMEM] + [HBM] * (len(ins) - 3),
        out_specs=(HBM,) * len(out_shape),
        scratch_shapes=[pltpu.VMEM(s, d) for s, d in vmem] + sems,
        compiler_params=pltpu.CompilerParams(
            collective_id=1, has_side_effects=True, vmem_limit_bytes=60 << 20
        ),
        name="forward_pass",
    )(*ins)


UNITS = 8
CHAINS = (0, 3)


def backward_refs(
    gu0,
    gu1,
    p_h,
    cq_h,
    pq_h,
    k_h,
    v_h,
    rr_h,
    hid_h,
    act_h,
    slope_h,
    od_h,
    nn_h,
    nm_h,
    mx_h,
    fq,
    fk,
    fv,
    fo,
    fi0,
    fi1,
    fu0,
    fu1,
    wq,
    wk,
    wv,
    wo,
    wi,
    wu,
    tok_h,
    cot_h,
    lim_h,
    vec_h,
    sums_h,
    flipt_h,
    turn_h,
    ou,
    oi,
    oo,
    ov,
    ok,
    oq,
    out_h,
    tg_h,
    e_h,
    rg_h,
    gi0,
    gi1,
    go,
    gv,
    gk,
    gq,
    s0,
    s1,
    p,
    cq,
    pq,
    kr,
    vr,
    rr,
    hid,
    act,
    slope,
    od,
    cat,
    idc,
    cot,
    vec,
    sums,
    flipt,
    turn,
    bdc,
    qdc,
    kdc,
    vdc,
    nd,
    rg,
    rgk,
    rgg,
    rgs,
    rgo,
    eb,
    ek,
    eg,
    es,
    eo,
    ld,
    own,
    s1s,
    r1,
    l1,
    s2,
    r2,
    s3,
    r3,
    s4,
    r4,
    lo,
    zu,
    zd,
    zs,
    ps,
    pr,
    xs,
    xr,
    ws,
    wr,
    st,
):
    return types.SimpleNamespace(**locals())


def backward_kernel(*refs):
    head = 46
    held = 2
    t = backward_refs(*refs[:head], *refs[head + held + 4 * UNITS :])
    spare = refs[head : head + held + 4 * UNITS]
    keep = spare[:held]
    got1, got2, got3, last = (
        spare[held + k * UNITS : held + (k + 1) * UNITS] for k in range(4)
    )
    at = position()
    w, z, c, p, x, y = at.w, at.z, at.c, at.p, at.x, at.y
    depth = [(w, lax.rem(z + d, NARROW)) for d in range(1, NARROW)]
    rows_all, width = t.cot.shape
    meet([at.sib, at.xn, at.yn] + depth)

    plan = (
        (t.gu0, False, t.ou, 0, width // 2),
        (t.gu1, False, t.ou, width // 4, width // 2),
        (t.gi0, True, t.oi, 0, width),
        (t.gi1, True, t.oi, width // 2, width),
        (t.go, True, t.oo, 0, width // 2),
        (t.gv, True, t.ov, 0, width // 2),
        (t.gk, True, t.ok, 0, H * KEY // 2),
        (t.gq, True, t.oq, 0, H * KEY // 2),
    )

    def half(m, h, mine):
        g = plan[m][0]
        if h == 0:
            return g.at[:, :, x if mine else 1 - x, 0]
        return g.at[:, y if mine else 1 - y, :, 1]

    def stage1(m):
        for h, target in ((0, at.xn), (1, at.yn)):
            remote(half(m, h, False), got1[m].at[h], t.s1s.at[m, h], t.r1.at[m, h], target).start()
            if not plan[m][1]:
                pltpu.make_async_copy(half(m, h, True), keep[m].at[h], t.l1.at[m, h]).start()

    def kept(m, h, zz, o):
        if not plan[m][1]:
            return keep[m].at[h, zz, o]
        if h == 0:
            return plan[m][0].at[zz, o, x, 0]
        return plan[m][0].at[zz, y, o, 1]

    def stage2(m):
        for h, target, mine in ((0, at.yn, y), (1, at.xn, x)):
            arrive(got1[m].at[h], t.r1.at[m, h])
            if not plan[m][1]:
                arrive(keep[m].at[h], t.l1.at[m, h])

            def add(k, _, h=h):
                zz, o = lax.div(k, 2), lax.rem(k, 2)
                spot = kept(m, h, zz, o)
                spot[...] = low(wide(spot[...]) + wide(got1[m][h, zz, o]))
                return 0

            lax.fori_loop(0, 2 * NARROW, add, 0)
            every = pl.ds(0, NARROW)
            remote(
                kept(m, h, every, 1 - mine), got2[m].at[h], t.s2.at[m, h], t.r2.at[m, h], target
            ).start()

    def stage3(m):
        for h, mine in ((0, y), (1, x)):
            arrive(got2[m].at[h], t.r2.at[m, h])

            def add(zz, _, h=h, mine=mine):
                got2[m][h, zz] = low(wide(kept(m, h, zz, mine)[...]) + wide(got2[m][h, zz]))
                return 0

            lax.fori_loop(0, NARROW, add, 0)
        for d in (1, 3, 2):
            zz = lax.rem(z + d, NARROW)
            remote(
                got2[m].at[:, zz],
                got3[m].at[d - 1],
                t.s3.at[m, d - 1],
                t.r3.at[m, d - 1],
                depth[d - 1],
            ).start()

    def piece(m, pp, part=None):
        _, _, out, start, span = plan[m]
        rows, cols = out.shape[0] // 4, last[m].shape[1]
        first = pp * rows
        if part is not None:
            rows = rows // 2
            first = first + part * rows
        return out.at[pl.ds(pl.multiple_of(first, 16), rows), lanes(c * span + start, cols)]

    def stage4(m):
        for d in (1, 3, 2):
            arrive(got3[m].at[d - 1], t.r3.at[m, d - 1])
        rows = last[m].shape[0] // 2
        for h in range(2):
            total = wide(got2[m][h, z])
            for d in range(3):
                total = total + wide(got3[m][d, h])
            last[m][h * rows : (h + 1) * rows, :] = low(total)
        share(m)

    def share(m):
        mine = piece(m, p)
        remote(last[m], mine, t.s4.at[m], t.r4.at[m, 0], at.xn).start()
        remote(last[m], mine, t.s4.at[m], t.r4.at[m, 1], at.yn).start()
        remote(last[m], mine, t.s4.at[m], t.r4.at[m, 4], at.sib).start()
        pltpu.make_async_copy(last[m], mine, t.lo.at[m]).start()

    def stage5(m):
        for pp, part, slot, target in ((at.px, 0, 0, at.yn), (at.py, 1, 1, at.xn)):
            arrive(piece(m, pp), t.r4.at[m, slot])
            some = piece(m, pp, part)
            remote(some, some, t.s4.at[m], t.r4.at[m, 2 + slot], target).start()
            some = piece(m, pp)
            remote(some, some, t.s4.at[m], t.r4.at[m, 4], at.sib).start()

    def stage6(m):
        arrive(piece(m, at.pd, 0), t.r4.at[m, 2])
        arrive(piece(m, at.pd, 1), t.r4.at[m, 3])
        some = piece(m, at.pd)
        remote(some, some, t.s4.at[m], t.r4.at[m, 4], at.sib).start()

    above, under = (w, jnp.minimum(z + 1, NARROW - 1)), (w, jnp.maximum(z - 1, 0))
    top = NARROW - 1

    def chain_start(m):
        g, room = plan[m][0], got1[m]
        bring(m, 0, rise_to(1))
        bring(m, 1, sink_to(1))

        @pl.when(z == 0)
        def _():
            for i in range(top):
                there = top - i
                remote(
                    g.at[there], room.at[there], t.zs.at[m, i], t.zu.at[m, there], above
                ).start()

        @pl.when(z == top)
        def _():
            for i in range(top):
                spot = NARROW if i == top - 1 else i
                remote(g.at[i], room.at[spot], t.zs.at[m, i], t.zd.at[m, i], under).start()

    def bring(m, spot, there):
        if not plan[m][1]:
            pltpu.make_async_copy(
                plan[m][0].at[there], keep[m].at[spot], t.l1.at[m, spot]
            ).start()

    def brought(m, spot):
        if not plan[m][1]:
            pltpu.make_async_copy(keep[m].at[spot], keep[m].at[spot], t.l1.at[m, spot]).wait()

    def own_part(m, spot, there):
        return plan[m][0].at[there] if plan[m][1] else keep[m].at[spot]

    def join(m, spot, there):
        own = own_part(m, spot, there)

        def add(k, _):
            a, b, h = lax.div(k, 4), lax.rem(lax.div(k, 2), 2), lax.rem(k, 2)
            got1[m][there, a, b, h] = low(wide(got1[m][there, a, b, h]) + wide(own[a, b, h]))
            return 0

        lax.fori_loop(0, 8, add, 0)

    def rising(slot):
        return (z >= 1) & (z <= slot)

    def sinking(slot):
        return (z < top) & (z >= top - slot)

    def rise_to(slot):
        return jnp.minimum(top + z - slot, top)

    def sink_to(slot):
        return jnp.maximum(slot - top + z, 0)

    def chain_step(m, slot):
        room = got1[m]
        brought(m, 0)
        brought(m, 1)

        @pl.when(rising(slot))
        def _():
            there = rise_to(slot)
            arrive(room.at[there], t.zu.at[m, there])
            join(m, 0, there)
            remote(
                room.at[there], room.at[there], t.zs.at[m, 2 + slot], t.zu.at[m, there], above
            ).start()

        @pl.when(sinking(slot))
        def _():
            there = sink_to(slot)
            arrive(room.at[there], t.zd.at[m, there])
            join(m, 1, there)
            spot = NARROW if slot == 2 else there
            remote(
                room.at[there], room.at[spot], t.zs.at[m, 4 + slot], t.zd.at[m, there], under
            ).start()

        if slot == 1:
            bring(m, 0, rise_to(2))
            bring(m, 1, sink_to(2))
        else:
            bring(m, 0, z)

    def chain_end(m):
        room = got1[m]
        brought(m, 0)

        @pl.when(z > 0)
        def _():
            arrive(room.at[z], t.zu.at[m, z])
            join(m, 0, z)

        @pl.when(z < top)
        def _():
            arrive(room.at[NARROW], t.zd.at[m, z])

        def add(k, _, fresh=False):
            a, b, h = lax.div(k, 4), lax.rem(lax.div(k, 2), 2), lax.rem(k, 2)
            own = own_part(m, 0, z)[a, b, h] if fresh else room[z, a, b, h]
            room[z, a, b, h] = low(wide(own) + wide(room[NARROW, a, b, h]))
            return 0

        @pl.when((z > 0) & (z < top))
        def _():
            lax.fori_loop(0, 8, add, 0)

        @pl.when(z == 0)
        def _():
            lax.fori_loop(0, 8, functools.partial(add, fresh=True), 0)

        remote(
            room.at[z, :, 1 - x, 0], got2[m].at[0], t.s1s.at[m, 0], t.r1.at[m, 0], at.xn
        ).start()
        remote(
            room.at[z, 1 - y, :, 1], got2[m].at[1], t.s1s.at[m, 1], t.r1.at[m, 1], at.yn
        ).start()

    def chain_plane(m):
        room = got1[m]
        for h, target in ((0, at.yn), (1, at.xn)):
            arrive(got2[m].at[h], t.r1.at[m, h])
            for o in range(2):
                spot = room.at[z, o, x, 0] if h == 0 else room.at[z, y, o, 1]
                spot[...] = low(wide(spot[...]) + wide(got2[m][h, o]))
            away = room.at[z, 1 - y, x, 0] if h == 0 else room.at[z, y, 1 - x, 1]
            remote(away, got3[m].at[h], t.s2.at[m, h], t.r2.at[m, h], target).start()

    def chain_last(m):
        rows = last[m].shape[0] // 2
        for h in range(2):
            arrive(got3[m].at[h], t.r2.at[m, h])
            last[m][h * rows : (h + 1) * rows, :] = low(
                wide(got1[m][z, y, x, h]) + wide(got3[m][h])
            )
        share(m)

    sources = (
        (t.act_h, t.act),
        (t.od_h, t.od),
        (t.slope_h, t.slope),
        (t.hid_h, t.hid),
        (t.vec_h, t.vec),
        (t.sums_h, t.sums),
        (t.cot_h, t.cot),
        (t.nm_h, t.cat),
        (t.p_h, t.p),
        (t.v_h, t.vr),
        (t.k_h, t.kr),
        (t.cq_h, t.cq),
        (t.pq_h, t.pq),
        (t.rr_h, t.rr),
        (t.turn_h, t.turn),
        (t.flipt_h, t.flipt),
        (t.tok_h, t.cot),
        (t.mx_h, t.cat),
        (t.nn_h, t.idc),
    )
    quarter = width // 4

    def fetch(k, full, shard, held, row=0, col=0):
        span = held.shape[2]
        copies = [
            pltpu.make_async_copy(
                shard.at[pl.ds(row, quarter), pl.ds(col, span)], held.at[z], t.own.at[k, 0]
            )
        ]
        for d in range(1, NARROW):
            zz = lax.rem(z + d, NARROW)
            copies.append(pltpu.make_async_copy(full.at[zz], held.at[zz], t.own.at[k, d]))
        for copy in copies:
            copy.start()
        return copies

    def use(copies):
        for copy in copies:
            copy.wait()

    here0 = fetch(0, t.fu0, t.wu, t.s0)
    here1 = fetch(1, t.fu1, t.wu, t.s1, row=quarter)
    loads = [pltpu.make_async_copy(s, d, t.ld.at[k]) for k, (s, d) in enumerate(sources)]
    for k in (*range(9), *range(10, 16)):
        loads[k].start()

    def give(k, src, dst):
        remote(src, dst, t.ps.at[k], t.pr.at[k], at.sib).start()

    def clip(row, values):
        limit = jnp.where(row < WIN, t.lim_h[0, 0], t.lim_h[0, 1])
        return jnp.minimum(jnp.maximum(values, -limit), limit)

    def leave_mlp(h):
        full = (t.s0, t.s1)[h]
        spots = [
            slice(2 * quarter * zz + quarter * h, 2 * quarter * zz + quarter * (h + 1))
            for zz in range(NARROW)
        ]
        active = jnp.concatenate([t.act[:, spot] for spot in spots], axis=1)

        def one(n, _):
            cols = lanes(n * 512, 512)
            part = dot_nn(active, full[:, :, cols].reshape(width, 512))
            if h == 0:
                t.nd[:, cols] = t.hid[:, cols] + part + t.vec[5:6, cols]
            else:
                t.vr[:, cols] = low(t.nd[:, cols] + part)
            return 0

        lax.fori_loop(0, 3, one, 0)
        for zz, spot in enumerate(spots):
            delta = low(dot_nt(t.od[...], full[zz]) * wide(t.slope[:, spot]))
            t.act[:, spot] = delta
            t.sums[6:7, spot] = jnp.sum(wide(delta), axis=0, keepdims=True)

    def pull_mid():
        for zz in range(NARROW):
            t.nd[:, zz * quarter : (zz + 1) * quarter] = dot_nt(
                t.act[:, 0:width], t.s0[zz]
            ) + dot_nt(t.act[:, width : 2 * width], t.s1[zz])

        def one(i, carry):
            gain_total, shift_total, bias_total = carry
            rows = pl.ds(pl.multiple_of(i * 32, 32), 32)
            v = t.hid[rows, :]
            center = v - jnp.mean(v, axis=1, keepdims=True)
            scale = lax.rsqrt(jnp.mean(center * center, axis=1, keepdims=True) + EPSILON)
            n = center * scale
            delta = t.nd[rows, :]
            e = delta * t.vec[3:4, 0:width]
            back = scale * (
                e
                - jnp.mean(e, axis=1, keepdims=True)
                - n * jnp.mean(e * n, axis=1, keepdims=True)
            )
            full = clip(i * 32, wide(t.cot[rows, :])) + back
            t.hid[rows, :] = full
            rounded = low(full)
            bd[rows, :] = rounded
            return (
                gain_total + jnp.sum(delta * n, axis=0, keepdims=True),
                shift_total + jnp.sum(delta, axis=0, keepdims=True),
                bias_total + jnp.sum(wide(rounded), axis=0, keepdims=True),
            )

        zero = jnp.zeros((1, width), jnp.float32)
        gain_total, shift_total, bias_total = lax.fori_loop(
            0, rows_all // 32, one, (zero, zero, zero)
        )
        t.sums[3:4, 0:width] = gain_total
        t.sums[4:5, 0:width] = shift_total
        t.sums[2:3, 0:width] = bias_total
        half = width // 2
        give(1, bd.at[:, lanes((1 - c) * half, half)], t.bdc.at[1])
        t.bdc[0] = bd[:, lanes(c * half, half)]

    def pull_mixed():
        for zz in range(NARROW):
            md[:, zz * quarter : (zz + 1) * quarter] = low(dot_nt(bd[...], t.s0[zz]))

    bd = t.slope.at[:, 0:width]
    md = t.od
    vd = t.act.at[:, 0:width]
    qd = t.act.at[:, width : width + H * KEY]
    kd = t.act.at[:, width + H * KEY : width + 2 * H * KEY]

    def lane_mask(size, split, rows=rows_all):
        return lax.broadcasted_iota(jnp.int32, (rows, size), 1) < split

    def heads(pair):
        qs = slice(pair * 2 * KEY, (pair + 1) * 2 * KEY)
        vs = slice(pair * 2 * VAL, (pair + 1) * 2 * VAL)
        vals, mixed = t.vr[:, vs], md[:, vs]
        keys, rel, cq, pq = t.kr[:, qs], t.rr[:, qs], t.cq[:, qs], t.pq[:, qs]
        first = lane_mask(2 * VAL, VAL)
        parts = []
        for side in range(2):
            mask = first if side == 0 else jnp.logical_not(first)
            soft = t.p[2 * pair + side]
            pull = dot_nt(jnp.where(mask, mixed, jnp.zeros_like(mixed)), vals)
            full = wide(soft)
            delta = low(full * (pull - jnp.sum(full * pull, axis=1, keepdims=True)))
            turned = dot_nn(delta, t.turn[...])
            padded = jnp.concatenate([turned, jnp.zeros_like(turned)], axis=1)
            slid = low(pltpu.roll(padded, 2 * rows_all, axis=1, stride=1, stride_axis=0))
            parts.append(
                (
                    dot_tn(soft, mixed),
                    dot_nn(delta, keys),
                    dot_tn(delta, cq),
                    dot_nn(slid, rel),
                    dot_tn(slid, pq),
                )
            )
        vd[:, vs] = low(jnp.where(first, parts[0][0], parts[1][0]))
        narrow = lane_mask(2 * KEY, KEY)
        content = jnp.where(narrow, parts[0][1], parts[1][1])
        place = jnp.where(narrow, parts[0][3], parts[1][3])
        kd[:, qs] = low(jnp.where(narrow, parts[0][2], parts[1][2]))
        rel_delta = low(
            jnp.where(lane_mask(2 * KEY, KEY, 2 * rows_all), parts[0][4], parts[1][4])
        )
        qd[:, qs] = low(content + place) * jnp.asarray(KEY ** (-0.5), jnp.bfloat16)
        t.rg[:, qs] = dot_nn(t.flipt[...], rel_delta)
        t.sums[7:8, qs] = jnp.sum(content, axis=0, keepdims=True)
        there = slice(keys_all + pair * 2 * KEY, keys_all + (pair + 1) * 2 * KEY)
        t.sums[7:8, there] = jnp.sum(place, axis=0, keepdims=True)

    def trade():
        for k, (full, pair) in enumerate(((vd, t.vdc), (kd, t.kdc), (qd, t.qdc))):
            cols = full.shape[1] // 2
            away = full.at[:, lanes((1 - c) * cols, cols)]
            give(2 + k, away, pair.at[1])
            pair[0] = full[:, lanes(c * cols, cols)]
        cols = t.rg.shape[1] // 2
        t.rgo[...] = low(t.rg[:, lanes((1 - c) * cols, cols)]).reshape(t.rgo.shape)
        remote(t.rgo, t.rgg.at[0], t.xs.at[0], t.xr.at[0], at.sib).start()
        t.rgk[0] = low(t.rg[:, lanes(c * cols, cols)]).reshape(t.rgo.shape)

    def outer_product(rows_from, pair, dst, start=0):
        size = dst.shape[5]

        def one(zz, _):
            lhs = rows_from[:, :, lanes(zz * quarter, quarter)].reshape(2 * rows_all, quarter)
            rhs = pair[:, :, start : start + size].reshape(2 * rows_all, size)
            dst[zz] = low(dot_tn(lhs, rhs)).reshape(dst.shape[1:])
            return 0

        lax.fori_loop(0, NARROW, one, 0)

    keys_all = H * KEY

    def pull_tokens():
        for zz in range(NARROW):
            t.nd[:, zz * 384 : (zz + 1) * 384] = (
                dot_nt(qd[...], t.s0[zz, :, 0:keys_all])
                + dot_nt(kd[...], t.s0[zz, :, keys_all : 2 * keys_all])
                + dot_nt(vd[...], t.s1[zz])
            )

        def one(i, carry):
            gain_total, shift_total = carry
            rows = pl.ds(pl.multiple_of(i * 32, 32), 32)
            v = wide(t.cot[rows, :])
            center = v - jnp.mean(v, axis=1, keepdims=True)
            scale = lax.rsqrt(jnp.mean(center * center, axis=1, keepdims=True) + EPSILON)
            n = center * scale
            delta = t.nd[rows, :]
            e = delta * t.vec[0:1, 0:width]
            back = scale * (
                e
                - jnp.mean(e, axis=1, keepdims=True)
                - n * jnp.mean(e * n, axis=1, keepdims=True)
            )
            t.od[rows, :] = low(t.hid[rows, :] + back)
            return (
                gain_total + jnp.sum(delta * n, axis=0, keepdims=True),
                shift_total + jnp.sum(delta, axis=0, keepdims=True),
            )

        zero = jnp.zeros((1, width), jnp.float32)
        gain_total, shift_total = lax.fori_loop(0, rows_all // 32, one, (zero, zero))
        t.sums[0:1, 0:width] = gain_total
        t.sums[1:2, 0:width] = shift_total
        for zz in range(NARROW):
            t.eb[zz] = jnp.zeros(t.eb.shape[1:], jnp.float32)
            t.eb[zz, 0:6, 0:384] = t.sums[0:6, zz * 384 : (zz + 1) * 384]
            t.eb[zz, 6:7, :] = t.sums[6:7, zz * 768 : (zz + 1) * 768]
            t.eb[zz, 7:8, 0:128] = t.sums[7:8, zz * 128 : (zz + 1) * 128]
            t.eb[zz, 7:8, 128:256] = t.sums[7:8, 512 + zz * 128 : 512 + (zz + 1) * 128]

    def sum_steps(keep, got, over, out, sends, recvs):
        def begin():
            remote(keep.at[0], got.at[0], sends.at[0], recvs.at[0], at.sib).start()

        def step(k):
            arrive(got.at[k], recvs.at[k])
            total = wide(keep[k]) + wide(got[k])
            keep[k + 1] = total.astype(keep.dtype)
            if k < 2:
                target = (at.xn, at.yn)[k]
                remote(
                    keep.at[k + 1], got.at[k + 1], sends.at[k + 1], recvs.at[k + 1], target
                ).start()
            else:
                for d in (1, 3, 2):
                    zz = lax.rem(z + d, NARROW)
                    remote(
                        keep.at[3, zz],
                        over.at[d - 1],
                        sends.at[2 + d],
                        recvs.at[2 + d],
                        depth[d - 1],
                    ).start()

        def end():
            total = wide(keep[3, z])
            for d in (1, 3, 2):
                arrive(over.at[d - 1], recvs.at[2 + d])
                total = total + wide(over[d - 1])
            out[...] = total

        return begin, step, end

    rel_sums = sum_steps(t.rgk, t.rgg, t.rgs, t.rg.at[0:48, 0:256], t.xs, t.xr)
    row_sums = sum_steps(t.ek, t.eg, t.es, t.eo, t.ws, t.wr)

    stored = []

    def store(src, dst):
        copy = pltpu.make_async_copy(src, dst, t.st.at[len(stored)])
        copy.start()
        stored.append(copy)

    stage1(1)
    chain_start(0)
    for copy in loads[:6]:
        copy.wait()
    use(here0)
    leave_mlp(0)
    use(here1)
    leave_mlp(1)
    store(t.vr, t.out_h)
    give(0, t.act.at[:, lanes((1 - c) * width, width)], t.idc.at[1])
    t.idc[0] = t.act[:, lanes(c * width, width)]
    here0 = fetch(2, t.fi0, t.wi, t.s0)
    here1 = fetch(3, t.fi1, t.wi, t.s1, col=width)
    stage2(1)
    chain_step(0, 1)
    loads[7].wait()
    arrive(t.idc.at[1], t.pr.at[0])
    outer_product(t.cat, t.idc, t.gi0)
    stage1(2)
    outer_product(t.cat, t.idc, t.gi1, width // 2)
    loads[17].start()
    loads[18].start()
    stage3(1)
    loads[6].wait()
    use(here0)
    use(here1)
    pull_mid()
    stored[0].wait()
    loads[9].start()
    loads[16].start()
    here0 = fetch(4, t.fo, t.wo, t.s0)
    here1 = fetch(5, t.fv, t.wv, t.s1)
    use(here0)
    pull_mixed()
    here0 = fetch(6, t.fq, t.wq, t.s0.at[:, :, 0:keys_all])
    here2 = fetch(7, t.fk, t.wk, t.s0.at[:, :, keys_all : 2 * keys_all])
    chain_start(3)
    chain_step(0, 2)
    stage2(2)
    loads[17].wait()
    arrive(t.bdc.at[1], t.pr.at[1])
    outer_product(t.cat, t.bdc, t.go)
    stage1(4)
    for copy in loads[8:16]:
        copy.wait()
    left(t.idc.at[1], t.ps.at[0])
    heads(0)
    heads(1)
    chain_end(0)
    stage3(2)
    stage4(1)
    heads(2)
    chain_plane(0)
    chain_step(3, 1)
    stage5(1)
    stage2(4)
    heads(3)
    trade()
    loads[18].wait()
    loads[16].wait()
    chain_last(0)
    arrive(t.vdc.at[1], t.pr.at[2])
    outer_product(t.idc, t.vdc, t.gv)
    stage1(5)
    stage3(4)
    arrive(t.kdc.at[1], t.pr.at[3])
    outer_product(t.idc, t.kdc, t.gk)
    arrive(t.qdc.at[1], t.pr.at[4])
    outer_product(t.idc, t.qdc, t.gq)
    chain_step(3, 2)
    stage1(7)
    stage1(6)
    stage2(5)
    stage2(7)
    use(here0)
    use(here1)
    use(here2)
    pull_tokens()
    store(t.od, t.tg_h)
    t.ek[0] = t.eb[...]
    row_sums[0]()
    rel_sums[1](0)
    stage6(1)
    row_sums[1](0)
    chain_end(3)
    stage2(6)
    stage3(5)
    stage5(0)
    stage4(4)
    stage3(6)
    rel_sums[1](1)
    chain_plane(3)
    row_sums[1](1)
    stage4(2)
    chain_last(3)
    stage5(4)
    stage5(2)
    stage3(7)
    stage4(5)
    stage4(6)
    rel_sums[1](2)
    stage5(3)
    row_sums[1](2)
    stage6(0)
    stage4(7)
    stage6(2)
    stage5(6)
    stage5(5)
    stage5(7)
    stage6(4)
    stage6(3)
    rel_sums[2]()
    store(t.rg.at[0:48, 0:256], t.rg_h.at[c])
    remote(t.rg.at[0:48, 0:256], t.rg_h.at[c], t.xs.at[6], t.xr.at[6], at.sib).start()
    stage6(5)
    row_sums[2]()
    store(t.eo, t.e_h)
    stage6(6)
    stage6(7)

    for m in range(UNITS):
        _, _, out, _, _ = plan[m]
        cols = last[m].shape[1]
        arrive(out.at[:, pl.ds(0, cols)], t.r4.at[m, 4])
        arrive(last[m], t.lo.at[m])
        if m in CHAINS:
            room = got1[m]
            for i in range(top):

                @pl.when((z == 0) | (z == top))
                def _():
                    left(room.at[0], t.zs.at[m, i])

            for slot in (1, 2):

                @pl.when(rising(slot))
                def _():
                    left(room.at[0], t.zs.at[m, 2 + slot])

                @pl.when(sinking(slot))
                def _():
                    left(room.at[0], t.zs.at[m, 4 + slot])

            for h in range(2):
                left(got2[m].at[h], t.s1s.at[m, h])
                left(got3[m].at[h], t.s2.at[m, h])
        else:
            for h in range(2):
                left(got1[m].at[h], t.s1s.at[m, h])
                left(got2[m].at[h], t.s2.at[m, h])
            for d in range(3):
                left(got3[m].at[d], t.s3.at[m, d])
        left(out.at[:, pl.ds(0, cols)], t.s4.at[m])
        left(out.at[pl.ds(0, 3 * (out.shape[0] // 4)), pl.ds(0, cols)], t.s4.at[m])
    for k, pair in enumerate((t.bdc, t.vdc, t.kdc, t.qdc)):
        left(pair.at[1], t.ps.at[1 + k])
    for got, over, sends in ((t.rgg, t.rgs, t.xs), (t.eg, t.es, t.ws)):
        for k in range(3):
            left(got.at[k], sends.at[k])
            left(over.at[k], sends.at[3 + k])
    left(t.rg.at[0:48, 0:256], t.xs.at[6])
    arrive(t.rg_h.at[1 - c], t.xr.at[6])
    for copy in stored[1:]:
        copy.wait()


def backward_pass(grads, saved, weights, shards, rest):
    bf, f32 = jnp.bfloat16, jnp.float32
    rows, width = rest[0].shape
    keys = H * KEY
    views = [g.reshape(4, 2, 2, 2, g.shape[0] // 32, g.shape[1]) for g in grads]
    shapes = [(g.shape[0], g.shape[1]) for g in grads] + [(width, width // 2)] * 4
    shapes += [(width, keys // 2)] * 2
    out_shape = (
        ((width // 2, width), bf),
        ((width // 4, 2 * width), bf),
        ((width // 4, width), bf),
        ((width // 4, width), bf),
        ((width // 4, keys), bf),
        ((width // 4, keys), bf),
        ((rows, width), bf),
        ((rows, width), bf),
        ((8, 768), f32),
        ((2, 48, 256), f32),
    )
    vmem = [
        (((2, 2, 2, 2) if m in CHAINS else (2, 4, 2)) + (r // 32, n), bf)
        for m, (r, n) in enumerate(shapes[: len(grads)])
    ]
    for plain, chain in (
        ((2, 4, 2), (5, 2, 2, 2)),
        ((2, 4), (2, 2)),
        ((3, 2), (2,)),
    ):
        vmem += [
            ((chain if m in CHAINS else plain) + (r // 32, n), bf)
            for m, (r, n) in enumerate(shapes)
        ]
    vmem += [((r // 16, n), bf) for r, n in shapes]
    vmem += [((4, 2, 2, 2, r // 32, n), bf) for r, n in shapes[len(grads) :]]
    vmem += [((NARROW, width // 4, width), bf)] * 2
    vmem += [(a.shape, a.dtype) for a in saved[:10]]
    vmem += [((2, rows, width), bf)] * 2
    vmem += [(a.shape, a.dtype) for a in rest[1:] if a.size > 2]
    vmem += [
        ((2, rows, width // 2), bf),
        ((2, rows, keys // 2), bf),
        ((2, rows, keys // 2), bf),
        ((2, rows, width // 2), bf),
        ((rows, width), f32),
        ((F, keys), f32),
        ((4, 4, 48, 256), bf),
        ((3, 4, 48, 256), bf),
        ((3, 48, 256), bf),
        ((4, 48, 256), bf),
        ((4, 8, 768), f32),
        ((4, 4, 8, 768), f32),
        ((3, 4, 8, 768), f32),
        ((3, 8, 768), f32),
        ((8, 768), f32),
    ]
    sems = [
        DMA((20,)),
        DMA((8, 4)),
        DMA((UNITS, 2)),
        DMA((UNITS, 2)),
        DMA((UNITS, 2)),
        DMA((UNITS, 2)),
        DMA((UNITS, 2)),
        DMA((UNITS, 3)),
        DMA((UNITS, 3)),
        DMA((UNITS,)),
        DMA((UNITS, 5)),
        DMA((UNITS,)),
        DMA((UNITS, NARROW)),
        DMA((UNITS, NARROW)),
        DMA((UNITS, 7)),
        DMA((5,)),
        DMA((5,)),
        DMA((7,)),
        DMA((7,)),
        DMA((6,)),
        DMA((6,)),
        DMA((4,)),
    ]
    ins = (*views, *saved, *weights, *shards, *rest)
    return pl.pallas_call(
        backward_kernel,
        out_shape=tuple(jax.ShapeDtypeStruct(s, d) for s, d in out_shape),
        in_specs=[SMEM if a.size == 2 else HBM for a in ins],
        out_specs=(HBM,) * len(out_shape),
        scratch_shapes=[pltpu.VMEM(s, d) for s, d in vmem] + sems,
        compiler_params=pltpu.CompilerParams(
            collective_id=2, has_side_effects=True, vmem_limit_bytes=60 << 20
        ),
        name="backward_pass",
    )(*ins)


def finish_kernel(count, *refs):
    ins, (rows_h, rel_h), passed = refs[:count], refs[count : count + 2], refs[count + 2 : count + 4]
    refs = refs[count + 4 :]
    outs, relative, kept, vectors = (
        refs[:count],
        refs[count],
        refs[count + 1 : count + 3],
        refs[count + 3 : count + 12],
    )
    refs = refs[count + 12 :]
    low_in, f32_out, through = refs[:count], refs[count : 2 * count], refs[2 * count : 2 * count + 2]
    into, out = refs[2 * count + 2 :]
    loads = [
        pltpu.make_async_copy(src, dst, into.at[k])
        for k, (src, dst) in enumerate(zip((*ins, *passed), (*low_in, *through)))
    ]
    for copy in loads:
        copy.start()
    stored = []

    def store(src, dst):
        copy = pltpu.make_async_copy(src, dst, out.at[len(stored)])
        copy.start()
        stored.append(copy)

    size = relative.shape[1] // 2
    relative[:, 0:size] = rel_h[0]
    relative[:, size : 2 * size] = rel_h[1]
    for k, vector in enumerate(vectors):
        n = vector.shape[0]
        row, start = (7, 128 * (k - 7)) if k >= 7 else (k, 0)
        vector[...] = rows_h[row : row + 1, start : start + n].reshape(n)
    for k in (count, count + 1):
        loads[k].wait()
        store(through[k - count], kept[k - count])
    for k in range(count):
        loads[k].wait()
        src, dst, res = low_in[k], f32_out[k], outs[k]
        half = src.shape[0] // 2
        for part in range(2):

            def one(i, _):
                spot = pl.ds(pl.multiple_of(part * half + i * 32, 32), 32)
                dst[spot, :] = wide(src[spot, :])
                return 0

            lax.fori_loop(0, half // 32, one, 0)
            spot = pl.ds(part * half, half)
            store(dst.at[spot], res.at[spot])
    for copy in stored:
        copy.wait()


def finish_grads(sums, rows, rel, layer_out, tokens_grad):
    f32 = jnp.float32
    vmem = pl.BlockSpec(memory_space=pltpu.VMEM)
    count = len(sums)
    lengths = (384, 384, 384, 384, 384, 384, 768, 128, 128)
    shapes = [(a.shape, f32) for a in sums] + [((rel.shape[1], 2 * rel.shape[2]), f32)]
    shapes += [(a.shape, a.dtype) for a in (layer_out, tokens_grad)]
    shapes += [((n,), f32) for n in lengths]
    through = [(a.shape, a.dtype) for a in (layer_out, tokens_grad)]
    scratch = [(a.shape, a.dtype) for a in sums] + [(a.shape, f32) for a in sums] + through
    return pl.pallas_call(
        lambda *refs: finish_kernel(count, *refs),
        out_shape=tuple(jax.ShapeDtypeStruct(s, d) for s, d in shapes),
        in_specs=[HBM] * count + [vmem] * 2 + [HBM] * 2,
        out_specs=(HBM,) * count + (vmem,) + (HBM,) * 2 + (vmem,) * len(lengths),
        scratch_shapes=[pltpu.VMEM(s, d) for s, d in scratch]
        + [DMA((count + 2,)), DMA((2 * count + 2,))],
        compiler_params=pltpu.CompilerParams(vmem_limit_bytes=60 << 20),
        name="finish_grads",
    )(*sums, rows, rel, layer_out, tokens_grad)


def basis_rows(length, features):
    f32 = np.float32
    family = features // 6
    offsets = np.arange(2 * length - 1, dtype=f32) - f32(length - 1)
    distance = np.abs(offsets)[:, None]
    halves = f32(2.0) ** np.linspace(3.0, math.log2(length), family, dtype=f32)
    decays = np.exp(f32(-math.log(2.0)) / halves[None, :] * distance)
    widths = f32(2.0) ** np.arange(1, family + 1, dtype=f32) - f32(1.0)
    central = np.where(widths[None, :] > distance, f32(1.0), f32(0.0))
    centers = np.linspace(0.0, float(length), family, dtype=f32)
    spread = f32(length / family)
    bump_rows = np.exp(f32(-0.5) * ((distance - centers[None, :]) / spread) ** 2)
    positive = np.concatenate([decays, central, bump_rows], axis=1)
    return np.concatenate([positive, np.sign(offsets)[:, None] * positive], axis=1)


def per_device_linked(
    tokens,
    cotangent,
    thresholds,
    attn_norm_gain,
    attn_norm_shift,
    query_weight,
    key_weight,
    value_weight,
    relative_weight,
    content_bias,
    position_bias,
    out_weight,
    out_bias,
    mlp_norm_gain,
    mlp_norm_shift,
    inner_weight,
    inner_bias,
    outer_weight,
    outer_bias,
):
    _, length, width = tokens.shape
    bf = jnp.bfloat16
    vectors = (
        (attn_norm_gain, 0, 0),
        (attn_norm_shift, 1, 0),
        (out_bias, 2, 0),
        (mlp_norm_gain, 3, 0),
        (mlp_norm_shift, 4, 0),
        (outer_bias, 5, 0),
        (inner_bias, 6, 0),
        (content_bias, 0, 384),
        (position_bias, 1, 384),
    )
    small = jnp.zeros((8, 512), bf)
    for vector, row, col in vectors:
        table = vector.reshape(-1, min(vector.shape[0], 384))
        n, m = table.shape
        small = small + jnp.pad(table, ((row, 8 - row - n), (col, 512 - col - m)))
    limits = thresholds
    table = basis_rows(length, F)
    empty = np.zeros((1, F), np.float32)
    basis = jnp.asarray(np.concatenate([table, empty]), bf)
    flip = jnp.asarray(np.concatenate([table[::-1], empty]), bf)
    flip_t = jnp.asarray(np.concatenate([table[::-1], empty]).T, bf)
    turn = jnp.asarray(np.eye(length)[::-1], bf)
    flat_tokens = tokens.reshape(length, width)
    flat_cotangent = cotangent.reshape(length, width)
    shards = (query_weight, key_weight, value_weight, out_weight, inner_weight, outer_weight)
    outs = forward_pass(
        flat_tokens, flat_cotangent, limits, shards, relative_weight, small, basis, flip
    )
    saved, weights, (vec, gu0, gu1, sums) = outs[:13], outs[13:21], outs[21:]
    ou, oi, oo, ov, ok, oq, layer_out, tokens_grad, rows, rel = backward_pass(
        (gu0, gu1),
        saved,
        weights,
        shards,
        (flat_tokens, flat_cotangent, limits, vec, sums, flip_t, turn),
    )
    outer, inner, out, value, key, query, relative, layer_out, tokens_grad, *vectors = finish_grads(
        (ou, oi, oo, ov, ok, oq), rows, rel, layer_out, tokens_grad
    )
    gain, shift, out_b, mlp_gain, mlp_shift, outer_b, inner_b, content_b, position_b = vectors
    return (
        layer_out[None],
        tokens_grad[None],
        gain,
        shift,
        query,
        key,
        value,
        relative,
        content_b,
        position_b,
        out,
        out_b,
        mlp_gain,
        mlp_shift,
        inner,
        inner_b,
        outer,
        outer_b,
    )


def solution(mesh):
    body = per_device_generic
    if mesh.shape[WIDE] == 8 and mesh.shape[DEPTH] == 4:
        body = per_device_linked
    in_specs = (
        P((WIDE, DEPTH), None, None),
        P((WIDE, DEPTH), None, None),
        P((WIDE, DEPTH), None),
        P(DEPTH),
        P(DEPTH),
        P(DEPTH, None),
        P(DEPTH, None),
        P(DEPTH, None),
        P(DEPTH, None),
        P(DEPTH),
        P(DEPTH),
        P(DEPTH, None),
        P(DEPTH),
        P(DEPTH),
        P(DEPTH),
        P(DEPTH, None),
        P(DEPTH),
        P(DEPTH, None),
        P(DEPTH),
    )
    out_specs = (
        P((WIDE, DEPTH), None, None),
        P((WIDE, DEPTH), None, None),
        P(DEPTH),
        P(DEPTH),
        P(DEPTH, None),
        P(DEPTH, None),
        P(DEPTH, None),
        P(DEPTH, None),
        P(DEPTH),
        P(DEPTH),
        P(DEPTH, None),
        P(DEPTH),
        P(DEPTH),
        P(DEPTH),
        P(DEPTH, None),
        P(DEPTH),
        P(DEPTH, None),
        P(DEPTH),
    )
    return jax.shard_map(
        body, mesh=mesh, in_specs=in_specs, out_specs=out_specs, check_vma=False
    )
```
